32 devices in a mesh: dp: 8 (over y, x, core), seq: 4 (over z).
Axes of the slice: x: 2, y: 2, z: 4, core: 2. Of those that a mesh axis runs over, the one named last changes fastest.
Arguments:
- hidden_in: bfloat16 [8, 1024, 2048], P('dp', 'seq'), may hold values from -6 to 6
- doc_lengths: int32 [8, 3], P('dp'), may hold values from 1 to 768, 1024 in all within a row
- norm_gain: bfloat16 [2048], replicated, may hold values from 0.5 to 1.5
- in_weight: bfloat16 [8192, 2048], P(('dp', 'seq')), may hold values from -0.125 to 0.125
- conv_weight: bfloat16 [4, 4096], P(None, ('dp', 'seq')), may hold values from -3 to 3
- conv_bias: bfloat16 [4096], P(('dp', 'seq')), may hold values from -3 to 3
- x_weight: bfloat16 [4096, 160], P(('dp', 'seq'))
- dt_weight: bfloat16 [4096, 128], P(('dp', 'seq')), may hold values from -0.5 to 0.5
- dt_bias: bfloat16 [4096], P(('dp', 'seq')), may hold values from -8 to -1
- skip_gain: bfloat16 [4096], P(('dp', 'seq')), may hold values from 0.5 to 1.5
- out_weight: bfloat16 [4096, 2048], P(('dp', 'seq')), may hold values from -0.25 to 0.25
- out_cotangent: bfloat16 [8, 1024, 2048], P('dp', 'seq'), may hold values from -6 to 6
Outputs:
- output: bfloat16 [8, 1024, 2048], P('dp', 'seq')
- grad_in: bfloat16 [8, 1024, 2048], P('dp', 'seq')
- grad_norm_gain: float32 [2048], replicated
- grad_in_weight: float32 [8192, 2048], P(('dp', 'seq'))
- grad_conv_weight: float32 [4, 4096], P(None, ('dp', 'seq'))
- grad_conv_bias: float32 [4096], P(('dp', 'seq'))
- grad_x_weight: float32 [4096, 160], P(('dp', 'seq'))
- grad_dt_weight: float32 [4096, 128], P(('dp', 'seq'))
- grad_dt_bias: float32 [4096], P(('dp', 'seq'))
- grad_skip_gain: float32 [4096], P(('dp', 'seq'))
- grad_out_weight: float32 [4096, 2048], P(('dp', 'seq'))
The draws below stay inside these ranges and needn't reach their ends.
Inputs may be any that keep to these rules, and one draw needn't show every extreme that they name: `doc_lengths`: each row holds the lengths of 3 packed documents in order, summing to 1024; the longest is 768.
All inputs are finite; a program needn't handle non-finite values.
Results may differ from the reference program's by a relative error of at most 0.012.
Values may be sent and summed in bfloat16 or wider, within the bound.
A program may use at most 320 MiB of HBM per device.

```python
import math
import jax
import jax.numpy as jnp
import numpy as np
from jax import lax

D = 2048
E = 4096
N = 16
R = 128
KCONV = 4
SEQ_LEN = 1024
DOCS = 3
SEQS_ALL = 8
DOC_MOST = 768


def draw_x_weight(key, part):
    normal_draw = jnp.clip(jax.random.normal(key, (E, R + 2 * N), jnp.float32), -6.0, 6.0)
    columns = jnp.arange(R + 2 * N)
    factor = jnp.where(columns >= R + N, 4.0, 1.0)
    return (normal_draw * factor * E ** (-0.5)).astype(jnp.bfloat16)


def levels(stream_key, shape, cuts, low, high):
    gain = 1.0
    for dim, blocks in cuts:
        steps = jax.random.uniform(jax.random.fold_in(jax.random.fold_in(stream_key, 6), dim), (blocks,), jnp.float32, low / len(cuts), high / len(cuts))
        gain = gain * jnp.repeat(jnp.exp(steps), shape[dim] // blocks).reshape((-1,) + (1,) * (len(shape) - 1 - dim))
    return gain


def split_up(count, total, reach, lean):
    portions = [(1 << 20) // math.isqrt(grade ** lean) + 1 for grade in range(2, count + 1)]
    surplus, counts = total - reach - (count - 1), [1] * (count - 1)
    while surplus > 0:
        free = [i for i in range(count - 1) if counts[i] < reach]
        pool, remaining = sum([portions[i] for i in free]), surplus
        for i in free:
            more = min(reach - counts[i], max(1, remaining * portions[i] // pool), surplus)
            counts[i] = counts[i] + more
            surplus = surplus - more
    return np.array([reach] + counts)


def ragged(rng, amount, total, most, skew):
    if amount == 2:
        one = jax.random.randint(rng, (), max(1, total - most), min(most, total - 1) + 1)
        return jnp.stack([one, total - one])
    sizes = jnp.asarray(split_up(amount, total, most, skew), jnp.int32)
    couples = (amount - 1) // 2
    donor, taker = sizes[1:1 + 2 * couples:2], sizes[2:2 + 2 * couples:2]
    room = jnp.minimum(donor - 1, most - taker)
    shifted = jax.random.randint(jax.random.fold_in(rng, 1), (couples,), 0, 1 << 20) % (room + 1)
    sizes = sizes.at[1:1 + 2 * couples:2].set(donor - shifted).at[2:2 + 2 * couples:2].set(taker + shifted)
    return sizes[jax.random.permutation(jax.random.fold_in(rng, 2), amount)]


def bell_draw(rng, extent, spread, most, shards=(), kind=jnp.bfloat16):
    values = spread * jax.random.normal(rng, extent, jnp.float32)
    if shards:
        values = values * levels(rng, extent, shards, -0.22, 0.18)
    return jnp.clip(values, -most, most).astype(kind)


def setup_inputs(seed: int = 0) -> dict:
    keys = jax.random.split(jax.random.key(seed), 13)
    hidden_in = bell_draw(keys[0], (SEQS_ALL, SEQ_LEN, D), 1.0, 6.0, ((0, 8), (1, 4)))
    doc_lengths = jax.vmap(lambda own: ragged(own, DOCS, SEQ_LEN, DOC_MOST, 0))(jax.random.split(keys[1], SEQS_ALL)).reshape((SEQS_ALL, DOCS)).astype(jnp.int32)
    norm_gain = jnp.clip(1.0 + 0.1 * jax.random.normal(keys[2], (D,), jnp.float32), 0.5, 1.5).astype(jnp.bfloat16)
    in_weight = bell_draw(keys[3], (2 * E, D), D ** -0.5, 0.125, ((0, 32),))
    conv_weight = bell_draw(keys[4], (KCONV, E), KCONV ** -0.5, 3.0, ((1, 32),))
    conv_bias = bell_draw(keys[5], (E,), 0.5, 3.0, ((0, 32),))
    x_weight = draw_x_weight(jax.random.fold_in(keys[12], 71), 0)
    dt_weight = bell_draw(keys[7], (E, R), R ** -0.5, 0.5, ((0, 32),))
    dt_bias = jnp.clip(-8.0 + 7.0 * jax.random.uniform(keys[8], (E,), jnp.float32) ** levels(keys[8], (E,), ((0, 32),), -0.2, 0.2), -8.0, -1.0).astype(jnp.bfloat16)
    skip_gain = jnp.clip(0.5 + 1.0 * jax.random.uniform(keys[9], (E,), jnp.float32) ** levels(keys[9], (E,), ((0, 32),), -0.2, 0.2), 0.5, 1.5).astype(jnp.bfloat16)
    out_weight = bell_draw(keys[10], (E, D), (E // 8) ** -0.5, 0.25, ((0, 32),))
    out_cotangent = bell_draw(keys[11], (SEQS_ALL, SEQ_LEN, D), 1.0, 6.0, ((0, 8), (1, 4)))
    return dict(hidden_in=hidden_in, doc_lengths=doc_lengths, norm_gain=norm_gain, in_weight=in_weight, conv_weight=conv_weight, conv_bias=conv_bias, x_weight=x_weight, dt_weight=dt_weight, dt_bias=dt_bias, skip_gain=skip_gain, out_weight=out_weight, out_cotangent=out_cotangent)


@jax.custom_vjp
def low(v):
    return lax.optimization_barrier(v.astype(jnp.bfloat16)).astype(jnp.float32)

@jax.custom_vjp
def low_back(v):
    return v

def low_keep(v):
    return (low(v), None)

def low_pass(kept, grad):
    return (grad,)

def back_keep(v):
    return (v, None)

def back_low(kept, grad):
    return (low(grad),)
low.defvjp(low_keep, low_pass)
low_back.defvjp(back_keep, back_low)
norm_eps = 1e-05
highest = lax.Precision.HIGHEST

def token_begins(lengths, position_count):
    doc_ends = jnp.cumsum(lengths, axis=1)
    doc_starts = doc_ends - lengths
    places = jnp.arange(position_count, dtype=jnp.int32)
    inside = doc_starts[:, None, :] <= places[None, :, None]
    return (lax.optimization_barrier(jnp.max(jnp.where(inside, doc_starts[:, None, :], 0), axis=2)), places)

def run_block(state_in, block_inputs):

    def advance_one(carried, token_in):
        step_t, inject_t, key_t, query_t, keep_t = token_in
        decay_now = keep_t[:, None, None] * (1.0 - step_t[:, None, :] * (key_t * key_t)[:, :, None])
        carried = decay_now * carried + inject_t[:, None, :] * key_t[:, :, None]
        return (carried, lax.optimization_barrier(jnp.sum(carried * query_t[:, :, None], axis=1)))
    return lax.scan(advance_one, state_in, block_inputs)

def layer(x_part, norm_scale, w_in, conv_taps, conv_shift, w_proj, w_rate, rate_shift, skip_scale, w_out, lengths):
    group_size, seq_len, model_width = x_part.shape
    inv_rms = lax.rsqrt(lax.optimization_barrier(jnp.mean(x_part * x_part, axis=2, keepdims=True)) + norm_eps)
    normed = low(x_part * inv_rms * norm_scale)
    pre_act = low(low_back(jnp.einsum('gld,fd->glf', normed, w_in, precision=highest)))
    x_inner = pre_act[..., :E]
    z_inner = pre_act[..., E:]
    begins, places = token_begins(lengths, seq_len)
    padded = jnp.pad(x_inner, ((0, 0), (KCONV - 1, 0), (0, 0)))
    conv_sum = jnp.zeros_like(x_inner) + conv_shift
    for tap_idx in range(KCONV):
        lag_len = KCONV - 1 - tap_idx
        tap_valid = places[None, :] - lag_len >= begins
        conv_sum = conv_sum + jnp.where(tap_valid[:, :, None], padded[:, tap_idx:tap_idx + seq_len, :] * conv_taps[tap_idx], 0.0)
    conv_out = low(jax.nn.silu(conv_sum))
    projected = low_back(jnp.einsum('gle,er->glr', conv_out, w_proj, precision=highest))
    rate_low = low(projected[..., :R])
    key_rows = projected[..., R:R + N]
    query_rows = projected[..., R + N:]
    beta_rate = jax.nn.sigmoid(low_back(jnp.einsum('glr,er->gle', rate_low, w_rate, precision=highest) + rate_shift))
    step_size = beta_rate / (1.0 + beta_rate * lax.optimization_barrier(jnp.sum(key_rows * key_rows, axis=2, keepdims=True)))
    inject = step_size * conv_out
    keep_mask = (places[None, :] != begins).astype(jnp.float32)
    block_len = math.gcd(seq_len, 64)

    def to_blocks(values):
        moved = jnp.moveaxis(values, 1, 0)
        return moved.reshape((seq_len // block_len, block_len) + moved.shape[1:])
    zero_state = jnp.zeros((group_size, N, E), jnp.float32)
    block_inputs = (to_blocks(step_size), to_blocks(inject), to_blocks(key_rows), to_blocks(query_rows), to_blocks(keep_mask))
    final_state, mixed = lax.scan(jax.checkpoint(run_block), zero_state, block_inputs)
    mixed = jnp.moveaxis(mixed.reshape(seq_len, group_size, E), 0, 1)
    y_full = mixed + skip_scale * conv_out
    gated = low(y_full * jax.nn.silu(z_inner))
    return x_part + jnp.einsum('gle,ed->gld', gated, w_out, precision=highest)

def reference(hidden_in, doc_lengths, norm_gain, in_weight, conv_weight, conv_bias, x_weight, dt_weight, dt_bias, skip_gain, out_weight, out_cotangent):
    params = tuple((member.astype(jnp.float32) for member in (norm_gain, in_weight, conv_weight, conv_bias, x_weight, dt_weight, dt_bias, skip_gain, out_weight)))
    total_seqs = hidden_in.shape[0]
    group_size = math.gcd(total_seqs, max(1, 4096 // SEQ_LEN))
    group_count = total_seqs // group_size

    def one_group(summed, batch_in):
        x_part, lengths, cot_part = batch_in

        def forward(x_in, *weights):
            return layer(x_in, *weights, lengths)
        result, pullback = jax.vjp(forward, x_part.astype(jnp.float32), *params)
        gradients = pullback(cot_part.astype(jnp.float32))
        summed = tuple((running_sum + new_term for running_sum, new_term in zip(summed, gradients[1:])))
        return (summed, (result.astype(jnp.bfloat16), gradients[0].astype(jnp.bfloat16)))
    batches = (hidden_in.reshape(group_count, group_size, SEQ_LEN, D), doc_lengths.reshape(group_count, group_size, DOCS), out_cotangent.reshape(group_count, group_size, SEQ_LEN, D))
    initial = tuple((jnp.zeros_like(member) for member in params))
    totals, (outputs, input_grads) = lax.scan(one_group, initial, batches)
    return (outputs.reshape(total_seqs, SEQ_LEN, D), input_grads.reshape(total_seqs, SEQ_LEN, D), totals[0], totals[1], totals[2], totals[3], totals[4], totals[5], totals[6], totals[7], totals[8])
```

```python
import functools
import math

import jax
import jax.numpy as jnp
from jax import lax
from jax.experimental import pallas as pl
from jax.experimental.pallas import tpu as pltpu
from jax.sharding import PartitionSpec as P

N = 16
R = 128
KCONV = 4
CHUNK = 16
LANES = 128

norm_eps = 1e-05
BF = jnp.bfloat16
F32 = jnp.float32


def silu_slope(pre_value):
    sigmoid_of = jax.nn.sigmoid(pre_value)
    return sigmoid_of * (1.0 + pre_value * (1.0 - sigmoid_of))


def token_begins(lengths, position_count):
    doc_ends = jnp.cumsum(lengths, axis=1)
    doc_starts = doc_ends - lengths
    places = jnp.arange(position_count, dtype=jnp.int32)
    inside = doc_starts[:, None, :] <= places[None, :, None]
    return (jnp.max(jnp.where(inside, doc_starts[:, None, :], 0), axis=2), places)


def mm(left, right, dims):
    return lax.dot_general(left, right, (dims, ((), ())), preferred_element_type=F32)


NN = ((1,), (0,))
NT = ((1,), (1,))
TN = ((0,), (0,))


def row(ref, i, lane):
    return jnp.broadcast_to(ref[i : i + 1, pl.ds(lane, LANES)], (8, LANES))


def lane_groups(channels):
    group = math.gcd(channels, 512)
    return [(g, group) for g in range(0, channels, group)]


def scan_forward(step_ref, inj_ref, key_ref, ksq_ref, keep_ref, wq_ref, s_ref, y_ref, carry):
    @pl.when(pl.program_id(1) == 0)
    def _():
        carry[...] = jnp.zeros_like(carry)

    tokens, channels = step_ref.shape
    for first, group in lane_groups(channels):
        tiles = list(range(first, first + group, LANES))

        def chunk(k, state):
            base = pl.multiple_of(k * CHUNK, CHUNK)
            state = list(state)
            steps, injs, keeps = (r.at[pl.ds(base, CHUNK)] for r in (step_ref, inj_ref, keep_ref))
            for i in range(CHUNK):
                at = base + i
                keep = row(keeps, i, 0)
                key = [key_ref[at, 0:8, :], key_ref[at, 8:16, :]]
                ksq = [ksq_ref[at, 0:8, :], ksq_ref[at, 8:16, :]]
                for j, lane in enumerate(tiles):
                    step = row(steps, i, lane)
                    inj = row(injs, i, lane)
                    for h in range(2):
                        state[2 * j + h] = (keep - step * ksq[h]) * state[2 * j + h] + inj * key[h]
                    both = jnp.concatenate([state[2 * j], state[2 * j + 1]], axis=0)
                    s_ref[pl.ds(pl.multiple_of(at * N, N), N), pl.ds(lane, LANES)] = both.astype(BF)
            rows = pl.ds(pl.multiple_of(k * CHUNK * N, CHUNK * N), CHUNK * N)
            y_ref[pl.ds(base, CHUNK), pl.ds(first, group)] = mm(
                wq_ref[pl.ds(base, CHUNK), :], s_ref[rows, pl.ds(first, group)], NN
            )
            return tuple(state)

        start = []
        for lane in tiles:
            start += [carry[0:8, pl.ds(lane, LANES)], carry[8:16, pl.ds(lane, LANES)]]
        end = lax.fori_loop(0, tokens // CHUNK, chunk, tuple(start))
        for j, lane in enumerate(tiles):
            carry[0:8, pl.ds(lane, LANES)] = end[2 * j]
            carry[8:16, pl.ds(lane, LANES)] = end[2 * j + 1]


def scan_backward(
    step_ref, inj_ref, dy_ref, ksq_ref, query_ref, keep_ref, wk_ref, wk2_ref, s_ref, before_ref,
    dinj_ref, pull_ref, dq_ref, dk1_ref, dk2_ref, carry, g_buf, sg_buf,
):
    @pl.when(pl.program_id(1) == 0)
    def _():
        carry[...] = jnp.zeros_like(carry)

    tokens, channels = step_ref.shape
    chunks = tokens // CHUNK
    span = CHUNK * N
    pick = lax.broadcasted_iota(jnp.int32, (CHUNK, span), 0) == (
        lax.broadcasted_iota(jnp.int32, (CHUNK, span), 1) // N
    )

    def diagonal(left, right):
        return jnp.sum(jnp.where(pick, mm(left.astype(BF), right, NT), 0.0), axis=0, keepdims=True)

    for first, group in lane_groups(channels):
        tiles = list(range(first, first + group, LANES))
        cols = pl.ds(first, group)

        def chunk(turn, pulled):
            k = chunks - 1 - turn
            base = pl.multiple_of(k * CHUNK, CHUNK)
            pulled = list(pulled)
            steps, dys, keeps = (r.at[pl.ds(base, CHUNK)] for r in (step_ref, dy_ref, keep_ref))
            for i in reversed(range(CHUNK)):
                at = base + i
                keep = row(keeps, i, 0)
                ksq = [ksq_ref[at, 0:8, :], ksq_ref[at, 8:16, :]]
                query = [query_ref[at, 0:8, :], query_ref[at, 8:16, :]]
                for j, lane in enumerate(tiles):
                    step = row(steps, i, lane)
                    dy = row(dys, i, lane)
                    here = []
                    for h in range(2):
                        grad = pulled[2 * j + h] + dy * query[h]
                        pulled[2 * j + h] = (keep - step * ksq[h]) * grad
                        here.append(grad)
                    g_buf[i * N : (i + 1) * N, pl.ds(lane, LANES)] = jnp.concatenate(here, axis=0).astype(BF)
            low = pl.multiple_of(k * span, span)
            now = s_ref[pl.ds(low, span), cols]
            grads = g_buf[:, cols]
            sg_buf[N:span, cols] = g_buf[N:span, cols] * s_ref[pl.ds(low, span - N), cols]

            @pl.when(k == 0)
            def _():
                sg_buf[0:N, cols] = g_buf[0:N, cols] * before_ref[:, cols]

            @pl.when(k > 0)
            def _():
                prior = s_ref[pl.ds(pl.multiple_of(jnp.maximum(low - N, 0), N), N), cols]
                sg_buf[0:N, cols] = g_buf[0:N, cols] * prior

            prods = sg_buf[:, cols]
            here = pl.ds(base, CHUNK)
            dinj_ref[here, cols] = mm(wk_ref[here, :], grads, NN)
            pull_ref[here, cols] = mm(wk2_ref[here, :], prods, NN)
            dq = diagonal(dy_ref[here, cols], now)
            dk1 = diagonal(inj_ref[here, cols], grads)
            dk2 = diagonal(step_ref[here, cols], prods)
            one = pl.ds(k, 1)
            if first == 0:
                dq_ref[one, :] = dq
                dk1_ref[one, :] = dk1
                dk2_ref[one, :] = dk2
            else:
                dq_ref[one, :] += dq
                dk1_ref[one, :] += dk1
                dk2_ref[one, :] += dk2
            return tuple(pulled)

        start = []
        for lane in tiles:
            start += [carry[0:8, pl.ds(lane, LANES)], carry[8:16, pl.ds(lane, LANES)]]
        end = lax.fori_loop(0, chunks, chunk, tuple(start))
        for j, lane in enumerate(tiles):
            carry[0:8, pl.ds(lane, LANES)] = end[2 * j]
            carry[8:16, pl.ds(lane, LANES)] = end[2 * j + 1]


def run_forward(seqs, length, step, inj, key_lanes, ksq_lanes, keep_lanes, wq):
    channels = step.shape[1]
    block = math.gcd(length, 128)
    blocks = length // block

    def at(b, t):
        return (b * blocks + t, 0)

    def at3(b, t):
        return (b * blocks + t, 0, 0)

    tokens = seqs * length
    return pl.pallas_call(
        scan_forward,
        grid=(seqs, blocks),
        in_specs=[
            pl.BlockSpec((block, channels), at),
            pl.BlockSpec((block, channels), at),
            pl.BlockSpec((block, N, LANES), at3),
            pl.BlockSpec((block, N, LANES), at3),
            pl.BlockSpec((block, LANES), at),
            pl.BlockSpec((block, CHUNK * N), at),
        ],
        out_specs=[
            pl.BlockSpec((block * N, channels), at),
            pl.BlockSpec((block, channels), at),
        ],
        out_shape=[
            jax.ShapeDtypeStruct((tokens * N, channels), BF),
            jax.ShapeDtypeStruct((tokens, channels), F32),
        ],
        scratch_shapes=[pltpu.VMEM((N, channels), F32)],
        cost_estimate=pl.CostEstimate(
            flops=tokens * channels * N * 40, bytes_accessed=tokens * channels * 44, transcendentals=0
        ),
        compiler_params=pltpu.CompilerParams(vmem_limit_bytes=48 << 20),
        name="scan_forward",
    )(step, inj, key_lanes, ksq_lanes, keep_lanes, wq)


def run_backward(seqs, length, step, inj, dy, ksq_lanes, query_lanes, keep_lanes, wk, wk2, states):
    channels = step.shape[1]
    block = math.gcd(length, 128)
    blocks = length // block

    def at(b, t):
        return (b * blocks + blocks - 1 - t, 0)

    def at3(b, t):
        return (b * blocks + blocks - 1 - t, 0, 0)

    def prior(b, t):
        return (jnp.maximum((b * blocks + blocks - 1 - t) * block - 1, 0), 0)

    tokens = seqs * length
    span = CHUNK * N
    rows = pl.BlockSpec((block, channels), at)
    lanes = pl.BlockSpec((block, N, LANES), at3)
    weights = pl.BlockSpec((block, span), at)
    small = pl.BlockSpec((block // CHUNK, span), at)
    return pl.pallas_call(
        scan_backward,
        grid=(seqs, blocks),
        in_specs=[
            rows, rows, rows, lanes, lanes, pl.BlockSpec((block, LANES), at), weights, weights,
            pl.BlockSpec((block * N, channels), at), pl.BlockSpec((N, channels), prior),
        ],
        out_specs=[rows, rows, small, small, small],
        out_shape=[jax.ShapeDtypeStruct((tokens, channels), F32)] * 2
        + [jax.ShapeDtypeStruct((tokens // CHUNK, span), F32)] * 3,
        scratch_shapes=[
            pltpu.VMEM((N, channels), F32),
            pltpu.VMEM((span, channels), BF),
            pltpu.VMEM((span, channels), BF),
        ],
        cost_estimate=pl.CostEstimate(
            flops=tokens * channels * N * 100, bytes_accessed=tokens * channels * 56, transcendentals=0
        ),
        compiler_params=pltpu.CompilerParams(vmem_limit_bytes=56 << 20),
        name="scan_backward",
    )(step, inj, dy, ksq_lanes, query_lanes, keep_lanes, wk, wk2, states, states)


def regroup(dp, seq):
    half = seq // 2
    forth = [
        (d * seq + s, (2 * (d // 2) + s % 2) * seq + half * (d % 2) + s // 2)
        for d in range(dp)
        for s in range(seq)
    ]
    return forth, [(b, a) for a, b in forth]


def local(
    hidden_in,
    doc_lengths,
    norm_gain,
    in_weight,
    conv_weight,
    conv_bias,
    x_weight,
    dt_weight,
    dt_bias,
    skip_gain,
    out_weight,
    out_cotangent,
):
    seqs, part_len, width = hidden_in.shape
    both = ("dp", "seq")
    dp, seq = lax.axis_size("dp"), lax.axis_size("seq")
    length = part_len * seq
    tokens = seqs * length
    forth, back = regroup(dp, seq)
    rows = out_weight.shape[0]
    channels = rows * dp
    lag_max = KCONV - 1

    small = jnp.concatenate(
        [x_weight, dt_weight, conv_weight.T, conv_bias[:, None], dt_bias[:, None], skip_gain[:, None]], axis=1
    )
    used = small.shape[1]
    padded_cols = -(-used // LANES) * LANES
    packed = jnp.concatenate([out_weight, jnp.pad(small, ((0, 0), (0, padded_cols - used)))], axis=1)

    hidden = lax.all_gather(hidden_in, "seq", axis=1, tiled=True).reshape(tokens, width)
    w_in = lax.all_gather(in_weight, "dp", axis=0, tiled=True)
    packed = lax.all_gather(lax.ppermute(packed, both, forth), "dp", axis=0, tiled=True)
    cot = lax.all_gather(out_cotangent, "seq", axis=1, tiled=True).reshape(tokens, width)

    w_out = packed[:, :width]
    tail = packed[:, width:]
    w_x = tail[:, : R + 2 * N]
    w_dt = tail[:, R + 2 * N : 2 * R + 2 * N]
    vectors = tail[:, 2 * R + 2 * N : used].astype(F32).T
    taps, conv_shift, rate_shift, skip = vectors[:KCONV], vectors[KCONV], vectors[KCONV + 1], vectors[KCONV + 2]

    begins, places = token_begins(doc_lengths, length)
    keep = (places[None, :] != begins).astype(F32).reshape(tokens, 1)
    valid = [(places[None, :] - (lag_max - w) >= begins)[:, :, None] for w in range(KCONV)]

    gain = norm_gain.astype(F32)
    x_full = hidden.astype(F32)
    inv_rms = lax.rsqrt(jnp.mean(x_full * x_full, axis=1, keepdims=True) + norm_eps)
    normed = (x_full * inv_rms * gain).astype(BF)
    pre = mm(normed, w_in, NT).astype(BF)
    x_inner = pre[:, :channels].reshape(seqs, length, channels)
    z_inner = pre[:, channels:].astype(F32)

    padded = jnp.pad(x_inner, ((0, 0), (lag_max, 0), (0, 0)))
    conv_sum = jnp.broadcast_to(conv_shift, (seqs, length, channels))
    for w in range(KCONV):
        window = padded[:, w : w + length, :].astype(F32)
        conv_sum = conv_sum + jnp.where(valid[w], window * taps[w], 0.0)
    conv_flat = conv_sum.reshape(tokens, channels)
    xc_low = jax.nn.silu(conv_flat).astype(BF)
    xc = xc_low.astype(F32)
    proj = lax.psum(mm(xc_low, w_x, NN), "seq")
    rate = proj[:, :R].astype(BF)
    key = proj[:, R : R + N]
    query = proj[:, R + N :]
    beta = jax.nn.sigmoid(mm(rate, w_dt, NT) + rate_shift)
    den = 1.0 + beta * jnp.sum(key * key, axis=1, keepdims=True)
    step = beta / den
    inj = step * xc

    def lanes(values):
        return jnp.broadcast_to(values[:, :, None], (tokens, N, LANES))

    ksq = keep * key * key
    key_lanes, ksq_lanes, query_lanes = lanes(key), lanes(ksq), lanes(query)
    keep_lanes = jnp.broadcast_to(keep, (tokens, LANES))
    eye = (jnp.arange(tokens)[:, None] % CHUNK == jnp.arange(CHUNK)[None, :]).astype(F32)

    def spread(values):
        return (values[:, None, :] * eye[:, :, None]).reshape(tokens, CHUNK * N).astype(BF)

    states, mixed = run_forward(seqs, length, step, inj, key_lanes, ksq_lanes, keep_lanes, spread(query))
    y_full = mixed + skip * xc

    d_gated = mm(cot, w_out, NT)
    z_gate = jax.nn.silu(z_inner)
    dy = d_gated * z_gate
    gated = (y_full * z_gate).astype(BF)
    branch = mm(gated, w_out, NN).astype(BF).reshape(seqs, length, width)
    branch = lax.psum_scatter(branch, "seq", scatter_dimension=1, tiled=True)
    output = (hidden_in.astype(F32) + branch.astype(F32)).astype(BF)

    d_inj, pull, dq, dk1, dk2 = run_backward(
        seqs, length, step, inj, dy, ksq_lanes, query_lanes, keep_lanes, spread(key), spread(ksq), states
    )
    dq, dk1, dk2 = dq.reshape(tokens, N), dk1.reshape(tokens, N), dk2.reshape(tokens, N)
    d_z = d_gated * y_full * silu_slope(z_inner)
    d_step = d_inj * xc - pull
    den_square = den * den
    d_norm = -jnp.sum(d_step * beta * beta / den_square, axis=1, keepdims=True)
    d_keys = dk1 - 2.0 * keep * key * dk2 + 2.0 * key * d_norm
    d_rate = (d_step / den_square * beta * (1.0 - beta)).astype(BF)
    d_proj = jnp.concatenate([mm(d_rate, w_dt, NN), d_keys, dq], axis=1)
    d_proj = lax.psum(d_proj, "seq").astype(BF)
    d_conv_out = mm(d_proj, w_x, NT) + step * d_inj + skip * dy
    d_conv = (d_conv_out * silu_slope(conv_flat)).reshape(seqs, length, channels)

    tap_grads = []
    d_x_inner = jnp.zeros((seqs, length, channels), F32)
    for w in range(KCONV):
        lag = lag_max - w
        window = padded[:, w : w + length, :].astype(F32)
        masked = jnp.where(valid[w], d_conv, 0.0)
        tap_grads.append(jnp.sum(masked * window, axis=(0, 1)))
        d_x_inner = d_x_inner + jnp.pad(masked, ((0, 0), (0, lag), (0, 0)))[:, lag:, :] * taps[w]
    d_pre = jnp.concatenate([d_x_inner.reshape(tokens, channels), d_z], axis=1).astype(BF)

    grad_w_out = mm(gated, cot, TN)
    vector_grads = jnp.stack(
        tap_grads
        + [
            jnp.sum(d_conv, axis=(0, 1)),
            jnp.sum(d_rate.astype(F32), axis=0),
            jnp.sum(dy * xc, axis=0),
        ],
        axis=1,
    )
    small_grads = jnp.concatenate([mm(xc_low, d_proj, TN), mm(d_rate, rate, TN), vector_grads], axis=1)
    packed_grads = jnp.concatenate([grad_w_out, jnp.pad(small_grads, ((0, 0), (0, padded_cols - used)))], axis=1)
    packed_grads = lax.psum_scatter(packed_grads.astype(BF), "dp", scatter_dimension=0, tiled=True)
    packed_grads = lax.ppermute(packed_grads, both, back).astype(F32)
    grad_out_weight = packed_grads[:, :width]
    tail = packed_grads[:, width:]

    grad_in_weight = lax.psum_scatter(mm(d_pre, normed, TN).astype(BF), "dp", scatter_dimension=0, tiled=True)
    grad_in_weight = grad_in_weight.astype(F32)
    d_normed = mm(d_pre, w_in, NN)
    gain_local = jnp.sum(d_normed * x_full * inv_rms, axis=0)
    grad_norm_gain = lax.psum(gain_local, both)
    d_normed = d_normed.astype(BF).reshape(seqs, length, width)
    d_normed = lax.psum_scatter(d_normed, "seq", scatter_dimension=1, tiled=True).astype(F32)
    own = hidden_in.astype(F32)
    own_rms = lax.rsqrt(jnp.mean(own * own, axis=2, keepdims=True) + norm_eps)
    scaled = d_normed * gain
    grad_in = (
        out_cotangent.astype(F32)
        + own_rms * scaled
        - own * (own_rms * own_rms * own_rms) * jnp.mean(own * scaled, axis=2, keepdims=True)
    ).astype(BF)

    base = 2 * R + 2 * N
    return (
        output,
        grad_in,
        grad_norm_gain,
        grad_in_weight,
        tail[:, base : base + KCONV].T,
        tail[:, base + KCONV],
        tail[:, : R + 2 * N],
        tail[:, R + 2 * N : base],
        tail[:, base + KCONV + 1],
        tail[:, base + KCONV + 2],
        grad_out_weight,
    )


def solution(mesh):
    both = ("dp", "seq")
    tokens = P("dp", "seq", None)
    matrix, vector = P(both, None), P(both)
    return jax.shard_map(
        local,
        mesh=mesh,
        in_specs=(
            tokens, P("dp", None), P(), matrix, P(None, both), vector,
            matrix, matrix, vector, vector, matrix, tokens,
        ),
        out_specs=(
            tokens, tokens, P(), matrix, P(None, both), vector,
            matrix, matrix, vector, vector, matrix,
        ),
        check_vma=False,
    )
```

```python
import functools
import math

import jax
import jax.numpy as jnp
from jax import lax
from jax.experimental import pallas as pl
from jax.experimental.pallas import tpu as pltpu
from jax.sharding import PartitionSpec as P

N = 16
R = 128
KCONV = 4
CHUNK = 16
LANES = 128

norm_eps = 1e-05
BF = jnp.bfloat16
F32 = jnp.float32


def silu_slope(pre_value):
    sigmoid_of = jax.nn.sigmoid(pre_value)
    return sigmoid_of * (1.0 + pre_value * (1.0 - sigmoid_of))


def token_begins(lengths, position_count):
    doc_ends = jnp.cumsum(lengths, axis=1)
    doc_starts = doc_ends - lengths
    places = jnp.arange(position_count, dtype=jnp.int32)
    inside = doc_starts[:, None, :] <= places[None, :, None]
    return (jnp.max(jnp.where(inside, doc_starts[:, None, :], 0), axis=2), places)


def mm(left, right, dims):
    return lax.dot_general(left, right, (dims, ((), ())), preferred_element_type=F32)


NN = ((1,), (0,))
NT = ((1,), (1,))
TN = ((0,), (0,))


def row(ref, i, lane):
    return jnp.broadcast_to(ref[i : i + 1, pl.ds(lane, LANES)], (8, LANES))


def lane_groups(channels):
    group = math.gcd(channels, 512)
    return [(g, group) for g in range(0, channels, group)]


def scan_forward(step_ref, inj_ref, key_ref, ksq_ref, keep_ref, wq_ref, s_ref, y_ref, carry):
    @pl.when(pl.program_id(1) == 0)
    def _():
        carry[...] = jnp.zeros_like(carry)

    tokens, channels = step_ref.shape
    for first, group in lane_groups(channels):
        tiles = list(range(first, first + group, LANES))

        def chunk(k, state):
            base = pl.multiple_of(k * CHUNK, CHUNK)
            state = list(state)
            steps, injs, keeps = (r.at[pl.ds(base, CHUNK)] for r in (step_ref, inj_ref, keep_ref))
            for i in range(CHUNK):
                at = base + i
                keep = row(keeps, i, 0)
                key = [key_ref[at, 0:8, :], key_ref[at, 8:16, :]]
                ksq = [ksq_ref[at, 0:8, :], ksq_ref[at, 8:16, :]]
                for j, lane in enumerate(tiles):
                    step = row(steps, i, lane)
                    inj = row(injs, i, lane)
                    for h in range(2):
                        state[2 * j + h] = (keep - step * ksq[h]) * state[2 * j + h] + inj * key[h]
                    both = jnp.concatenate([state[2 * j], state[2 * j + 1]], axis=0)
                    s_ref[pl.ds(pl.multiple_of(at * N, N), N), pl.ds(lane, LANES)] = both.astype(BF)
            rows = pl.ds(pl.multiple_of(k * CHUNK * N, CHUNK * N), CHUNK * N)
            y_ref[pl.ds(base, CHUNK), pl.ds(first, group)] = mm(
                wq_ref[pl.ds(base, CHUNK), :], s_ref[rows, pl.ds(first, group)], NN
            )
            return tuple(state)

        start = []
        for lane in tiles:
            start += [carry[0:8, pl.ds(lane, LANES)], carry[8:16, pl.ds(lane, LANES)]]
        end = lax.fori_loop(0, tokens // CHUNK, chunk, tuple(start))
        for j, lane in enumerate(tiles):
            carry[0:8, pl.ds(lane, LANES)] = end[2 * j]
            carry[8:16, pl.ds(lane, LANES)] = end[2 * j + 1]


def scan_backward(
    step_ref, inj_ref, dy_ref, ksq_ref, query_ref, keep_ref, wk_ref, wk2_ref, s_ref, before_ref,
    dinj_ref, pull_ref, dq_ref, dk1_ref, dk2_ref, carry, g_buf, sg_buf,
):
    @pl.when(pl.program_id(1) == 0)
    def _():
        carry[...] = jnp.zeros_like(carry)

    tokens, channels = step_ref.shape
    chunks = tokens // CHUNK
    span = CHUNK * N
    pick = lax.broadcasted_iota(jnp.int32, (CHUNK, span), 0) == (
        lax.broadcasted_iota(jnp.int32, (CHUNK, span), 1) // N
    )

    def diagonal(left, right):
        return jnp.sum(jnp.where(pick, mm(left.astype(BF), right, NT), 0.0), axis=0, keepdims=True)

    for first, group in lane_groups(channels):
        tiles = list(range(first, first + group, LANES))
        cols = pl.ds(first, group)

        def chunk(turn, pulled):
            k = chunks - 1 - turn
            base = pl.multiple_of(k * CHUNK, CHUNK)
            pulled = list(pulled)
            steps, dys, keeps = (r.at[pl.ds(base, CHUNK)] for r in (step_ref, dy_ref, keep_ref))
            for i in reversed(range(CHUNK)):
                at = base + i
                keep = row(keeps, i, 0)
                ksq = [ksq_ref[at, 0:8, :], ksq_ref[at, 8:16, :]]
                query = [query_ref[at, 0:8, :], query_ref[at, 8:16, :]]
                for j, lane in enumerate(tiles):
                    step = row(steps, i, lane)
                    dy = row(dys, i, lane)
                    here = []
                    for h in range(2):
                        grad = pulled[2 * j + h] + dy * query[h]
                        pulled[2 * j + h] = (keep - step * ksq[h]) * grad
                        here.append(grad)
                    g_buf[i * N : (i + 1) * N, pl.ds(lane, LANES)] = jnp.concatenate(here, axis=0).astype(BF)
            low = pl.multiple_of(k * span, span)
            now = s_ref[pl.ds(low, span), cols]
            grads = g_buf[:, cols]
            sg_buf[N:span, cols] = g_buf[N:span, cols] * s_ref[pl.ds(low, span - N), cols]

            @pl.when(k == 0)
            def _():
                sg_buf[0:N, cols] = g_buf[0:N, cols] * before_ref[:, cols]

            @pl.when(k > 0)
            def _():
                prior = s_ref[pl.ds(pl.multiple_of(jnp.maximum(low - N, 0), N), N), cols]
                sg_buf[0:N, cols] = g_buf[0:N, cols] * prior

            prods = sg_buf[:, cols]
            here = pl.ds(base, CHUNK)
            dinj_ref[here, cols] = mm(wk_ref[here, :], grads, NN)
            pull_ref[here, cols] = mm(wk2_ref[here, :], prods, NN)
            dq = diagonal(dy_ref[here, cols], now)
            dk1 = diagonal(inj_ref[here, cols], grads)
            dk2 = diagonal(step_ref[here, cols], prods)
            one = pl.ds(k, 1)
            if first == 0:
                dq_ref[one, :] = dq
                dk1_ref[one, :] = dk1
                dk2_ref[one, :] = dk2
            else:
                dq_ref[one, :] += dq
                dk1_ref[one, :] += dk1
                dk2_ref[one, :] += dk2
            return tuple(pulled)

        start = []
        for lane in tiles:
            start += [carry[0:8, pl.ds(lane, LANES)], carry[8:16, pl.ds(lane, LANES)]]
        end = lax.fori_loop(0, chunks, chunk, tuple(start))
        for j, lane in enumerate(tiles):
            carry[0:8, pl.ds(lane, LANES)] = end[2 * j]
            carry[8:16, pl.ds(lane, LANES)] = end[2 * j + 1]


def run_forward(seqs, length, step, inj, key_lanes, ksq_lanes, keep_lanes, wq):
    channels = step.shape[1]
    block = math.gcd(length, 128)
    blocks = length // block

    def at(b, t):
        return (b * blocks + t, 0)

    def at3(b, t):
        return (b * blocks + t, 0, 0)

    tokens = seqs * length
    return pl.pallas_call(
        scan_forward,
        grid=(seqs, blocks),
        in_specs=[
            pl.BlockSpec((block, channels), at),
            pl.BlockSpec((block, channels), at),
            pl.BlockSpec((block, N, LANES), at3),
            pl.BlockSpec((block, N, LANES), at3),
            pl.BlockSpec((block, LANES), at),
            pl.BlockSpec((block, CHUNK * N), at),
        ],
        out_specs=[
            pl.BlockSpec((block * N, channels), at),
            pl.BlockSpec((block, channels), at),
        ],
        out_shape=[
            jax.ShapeDtypeStruct((tokens * N, channels), BF),
            jax.ShapeDtypeStruct((tokens, channels), F32),
        ],
        scratch_shapes=[pltpu.VMEM((N, channels), F32)],
        cost_estimate=pl.CostEstimate(
            flops=tokens * channels * N * 40, bytes_accessed=tokens * channels * 44, transcendentals=0
        ),
        compiler_params=pltpu.CompilerParams(vmem_limit_bytes=48 << 20),
        name="scan_forward",
    )(step, inj, key_lanes, ksq_lanes, keep_lanes, wq)


def run_backward(seqs, length, step, inj, dy, ksq_lanes, query_lanes, keep_lanes, wk, wk2, states):
    channels = step.shape[1]
    block = math.gcd(length, 128)
    blocks = length // block

    def at(b, t):
        return (b * blocks + blocks - 1 - t, 0)

    def at3(b, t):
        return (b * blocks + blocks - 1 - t, 0, 0)

    def prior(b, t):
        return (jnp.maximum((b * blocks + blocks - 1 - t) * block - 1, 0), 0)

    tokens = seqs * length
    span = CHUNK * N
    rows = pl.BlockSpec((block, channels), at)
    lanes = pl.BlockSpec((block, N, LANES), at3)
    weights = pl.BlockSpec((block, span), at)
    small = pl.BlockSpec((block // CHUNK, span), at)
    return pl.pallas_call(
        scan_backward,
        grid=(seqs, blocks),
        in_specs=[
            rows, rows, rows, lanes, lanes, pl.BlockSpec((block, LANES), at), weights, weights,
            pl.BlockSpec((block * N, channels), at), pl.BlockSpec((N, channels), prior),
        ],
        out_specs=[rows, rows, small, small, small],
        out_shape=[jax.ShapeDtypeStruct((tokens, channels), F32)] * 2
        + [jax.ShapeDtypeStruct((tokens // CHUNK, span), F32)] * 3,
        scratch_shapes=[
            pltpu.VMEM((N, channels), F32),
            pltpu.VMEM((span, channels), BF),
            pltpu.VMEM((span, channels), BF),
        ],
        cost_estimate=pl.CostEstimate(
            flops=tokens * channels * N * 100, bytes_accessed=tokens * channels * 56, transcendentals=0
        ),
        compiler_params=pltpu.CompilerParams(vmem_limit_bytes=56 << 20),
        name="scan_backward",
    )(step, inj, dy, ksq_lanes, query_lanes, keep_lanes, wk, wk2, states, states)


MESH = pl.DeviceIdType.MESH


def any_specs(count):
    return [pl.BlockSpec(memory_space=pl.ANY)] * count


def place():
    return lax.axis_index("dp"), lax.axis_index("seq")


def mate(d):
    return d + 1 - 2 * lax.rem(d, 2)


def remote(src, dst, send, recv, device):
    return pltpu.make_async_remote_copy(
        src_ref=src, dst_ref=dst, send_sem=send, recv_sem=recv, device_id=device, device_id_type=MESH
    )


def greet(device, here=True):
    barrier = pltpu.get_barrier_semaphore()

    def tell():
        pl.semaphore_signal(barrier, inc=1, device_id=device, device_id_type=MESH)

    if here is True:
        tell()
    else:
        pl.when(here)(tell)


def gather_kernel(
    dp, seq, hid_ref, w_ref, pk_ref, hid_out, w_out, pk_out,
    z_send, z_recv, w_send, w_recv, f_send, f_recv, p_send, p_recv, q_send, q_recv, t_sem, own_sem,
):
    d, s = place()
    part = hid_ref.shape[1]
    w_rows, p_rows = w_ref.shape[0], pk_ref.shape[0]
    pieces = z_send.shape[2]
    piece = part // pieces
    half = seq // 2
    pairs = dp // 2
    to_d, to_s = 2 * (d // 2) + lax.rem(s, 2), half * lax.rem(d, 2) + s // 2
    from_d, from_s = 2 * (d // 2) + s // half, 2 * lax.rem(s, half) + lax.rem(d, 2)
    moves = jnp.logical_or(to_d != d, to_s != s)

    greet((d, s - 1), s > 0)
    greet((d, s + 1), s < seq - 1)
    for k in range(1, pairs):
        greet((lax.rem(d + 2 * k, dp), s))
    greet((mate(d), s))
    greet((to_d, to_s), moves)
    greet((from_d, from_s), moves)
    count = pairs + jnp.where(s > 0, 1, 0) + jnp.where(s < seq - 1, 1, 0) + jnp.where(moves, 2, 0)
    pl.semaphore_wait(pltpu.get_barrier_semaphore(), count)

    def shard(which, q):
        return hid_out.at[:, pl.ds(which * part + q * piece, piece), :]

    def hop(way, k, q):
        which = s - k if way == 0 else s + k
        src = hid_ref.at[:, pl.ds(q * piece, piece), :] if k == 0 else shard(which, q)
        near = s + 1 if way == 0 else s - 1
        return remote(src, shard(which, q), z_send.at[way, k, q], z_recv.at[way, k, q], (d, near))

    def can_send(way, k):
        if way == 0:
            return jnp.logical_and(s - k >= 0, s < seq - 1)
        return jnp.logical_and(s + k < seq, s > 0)

    def w_slot(which):
        return w_out.at[pl.ds(which * w_rows, w_rows)]

    def p_slot(which):
        return pk_out.at[pl.ds(which * p_rows, p_rows)]

    def spread(slot, own, send, recv, k):
        return remote(own, slot(d), send.at[k], recv.at[k], (lax.rem(d + 2 * k, dp), s))

    def source(k):
        return lax.rem(d - 2 * k + dp, dp)

    def across(slot, send, recv, k, own=None):
        return remote(own if k == 0 else slot(source(k)), slot(source(k)), send.at[k], recv.at[k], (mate(d), s))

    for q in range(pieces):
        for way in range(2):
            pl.when(can_send(way, 0))(hop(way, 0, q).start)
    transfer = remote(pk_ref, p_slot(to_d), t_sem.at[0], t_sem.at[1], (to_d, to_s))
    stay = pltpu.make_async_copy(pk_ref, p_slot(d), own_sem.at[2])
    pl.when(moves)(transfer.start)
    pl.when(jnp.logical_not(moves))(stay.start)
    for k in range(1, pairs):
        spread(w_slot, w_ref, w_send, w_recv, k).start()
    across(w_slot, f_send, f_recv, 0, w_ref).start()
    own_w = pltpu.make_async_copy(w_ref, w_slot(d), own_sem.at[0])
    own_h = pltpu.make_async_copy(hid_ref, hid_out.at[:, pl.ds(s * part, part), :], own_sem.at[1])
    own_w.start()
    own_h.start()

    pl.when(moves)(remote(pk_ref, p_slot(d), t_sem.at[0], t_sem.at[1], (to_d, to_s)).wait_recv)
    pl.when(jnp.logical_not(moves))(stay.wait)
    for k in range(1, pairs):
        spread(p_slot, p_slot(d), p_send, p_recv, k).start()
    across(p_slot, q_send, q_recv, 0, p_slot(d)).start()

    def arrive(k):
        for q in range(pieces):
            for way in range(2):
                got = s - k >= 0 if way == 0 else s + k < seq

                @pl.when(got)
                def _():
                    which = s - k if way == 0 else s + k
                    remote(
                        shard(which, q), shard(which, q), z_send.at[way, k - 1, q], z_recv.at[way, k - 1, q], (d, s)
                    ).wait_recv()

                if k < seq - 1:
                    pl.when(can_send(way, k))(hop(way, k, q).start)

    for k in range(1, seq - 1):
        arrive(k)
    for slot, own, send, recv, over_send, over_recv in (
        (w_slot, w_ref, w_send, w_recv, f_send, f_recv),
        (p_slot, None, p_send, p_recv, q_send, q_recv),
    ):
        for k in range(1, pairs):
            remote(slot(source(k)), slot(source(k)), send.at[k], recv.at[k], (d, s)).wait_recv()
            across(slot, over_send, over_recv, k).start()
    arrive(seq - 1)

    def other(k):
        return lax.rem(mate(d) - 2 * k + dp, dp)

    for slot, own, over_send, over_recv in ((w_slot, w_ref, f_send, f_recv), (p_slot, p_slot(d), q_send, q_recv)):
        for k in range(pairs):
            remote(slot(other(k)), slot(other(k)), over_send.at[k], over_recv.at[k], (d, s)).wait_recv()
            across(slot, over_send, over_recv, k, own).wait_send()
    for k in range(1, pairs):
        spread(w_slot, w_ref, w_send, w_recv, k).wait_send()
        spread(p_slot, p_slot(d), p_send, p_recv, k).wait_send()
    for k in range(seq - 1):
        for q in range(pieces):
            for way in range(2):
                pl.when(can_send(way, k))(hop(way, k, q).wait_send)
    pl.when(moves)(transfer.wait_send)
    own_w.wait()
    own_h.wait()


def gather(hidden, weight, packed, collective_id=0):
    dp, seq = lax.axis_size("dp"), lax.axis_size("seq")
    seqs, part, width = hidden.shape
    pieces = 4 if part % 64 == 0 else 1
    dma = pltpu.SemaphoreType.DMA
    return pl.pallas_call(
        functools.partial(gather_kernel, dp, seq),
        in_specs=any_specs(3),
        out_specs=any_specs(3),
        out_shape=[
            jax.ShapeDtypeStruct((seqs, part * seq, width), hidden.dtype),
            jax.ShapeDtypeStruct((weight.shape[0] * dp, weight.shape[1]), weight.dtype),
            jax.ShapeDtypeStruct((packed.shape[0] * dp, packed.shape[1]), packed.dtype),
        ],
        scratch_shapes=[
            dma((2, seq, pieces)), dma((2, seq, pieces)),
            dma((dp // 2,)), dma((dp // 2,)), dma((dp // 2,)), dma((dp // 2,)),
            dma((dp // 2,)), dma((dp // 2,)), dma((dp // 2,)), dma((dp // 2,)),
            dma((2,)), dma((3,)),
        ],
        compiler_params=pltpu.CompilerParams(collective_id=collective_id, has_side_effects=True),
        name="gather_in",
    )(hidden, weight, packed)


def regroup(dp, seq):
    half = seq // 2
    forth = [
        (d * seq + s, (2 * (d // 2) + s % 2) * seq + half * (d % 2) + s // 2)
        for d in range(dp)
        for s in range(seq)
    ]
    return forth, [(b, a) for a, b in forth]


def local(
    hidden_in,
    doc_lengths,
    norm_gain,
    in_weight,
    conv_weight,
    conv_bias,
    x_weight,
    dt_weight,
    dt_bias,
    skip_gain,
    out_weight,
    out_cotangent,
):
    seqs, part_len, width = hidden_in.shape
    both = ("dp", "seq")
    dp, seq = lax.axis_size("dp"), lax.axis_size("seq")
    length = part_len * seq
    tokens = seqs * length
    forth, back = regroup(dp, seq)
    rows = out_weight.shape[0]
    channels = rows * dp
    lag_max = KCONV - 1

    small = jnp.concatenate(
        [x_weight, dt_weight, conv_weight.T, conv_bias[:, None], dt_bias[:, None], skip_gain[:, None]], axis=1
    )
    used = small.shape[1]
    padded_cols = -(-used // LANES) * LANES
    packed = jnp.concatenate([out_weight, jnp.pad(small, ((0, 0), (0, padded_cols - used)))], axis=1)

    hidden, w_in, packed = gather(hidden_in, in_weight, packed)
    hidden = hidden.reshape(tokens, width)
    cot = lax.all_gather(out_cotangent, "seq", axis=1, tiled=True).reshape(tokens, width)

    w_out = packed[:, :width]
    tail = packed[:, width:]
    w_x = tail[:, : R + 2 * N]
    w_dt = tail[:, R + 2 * N : 2 * R + 2 * N]
    vectors = tail[:, 2 * R + 2 * N : used].astype(F32).T
    taps, conv_shift, rate_shift, skip = vectors[:KCONV], vectors[KCONV], vectors[KCONV + 1], vectors[KCONV + 2]

    begins, places = token_begins(doc_lengths, length)
    keep = (places[None, :] != begins).astype(F32).reshape(tokens, 1)
    valid = [(places[None, :] - (lag_max - w) >= begins)[:, :, None] for w in range(KCONV)]

    gain = norm_gain.astype(F32)
    x_full = hidden.astype(F32)
    inv_rms = lax.rsqrt(jnp.mean(x_full * x_full, axis=1, keepdims=True) + norm_eps)
    normed = (x_full * inv_rms * gain).astype(BF)
    pre = mm(normed, w_in, NT).astype(BF)
    x_inner = pre[:, :channels].reshape(seqs, length, channels)
    z_inner = pre[:, channels:].astype(F32)

    padded = jnp.pad(x_inner, ((0, 0), (lag_max, 0), (0, 0)))
    conv_sum = jnp.broadcast_to(conv_shift, (seqs, length, channels))
    for w in range(KCONV):
        window = padded[:, w : w + length, :].astype(F32)
        conv_sum = conv_sum + jnp.where(valid[w], window * taps[w], 0.0)
    conv_flat = conv_sum.reshape(tokens, channels)
    xc_low = jax.nn.silu(conv_flat).astype(BF)
    xc = xc_low.astype(F32)
    proj = lax.psum(mm(xc_low, w_x, NN), "seq")
    rate = proj[:, :R].astype(BF)
    key = proj[:, R : R + N]
    query = proj[:, R + N :]
    beta = jax.nn.sigmoid(mm(rate, w_dt, NT) + rate_shift)
    den = 1.0 + beta * jnp.sum(key * key, axis=1, keepdims=True)
    step = beta / den
    inj = step * xc

    def lanes(values):
        return jnp.broadcast_to(values[:, :, None], (tokens, N, LANES))

    ksq = keep * key * key
    key_lanes, ksq_lanes, query_lanes = lanes(key), lanes(ksq), lanes(query)
    keep_lanes = jnp.broadcast_to(keep, (tokens, LANES))
    eye = (jnp.arange(tokens)[:, None] % CHUNK == jnp.arange(CHUNK)[None, :]).astype(F32)

    def spread(values):
        return (values[:, None, :] * eye[:, :, None]).reshape(tokens, CHUNK * N).astype(BF)

    states, mixed = run_forward(seqs, length, step, inj, key_lanes, ksq_lanes, keep_lanes, spread(query))
    y_full = mixed + skip * xc

    d_gated = mm(cot, w_out, NT)
    z_gate = jax.nn.silu(z_inner)
    dy = d_gated * z_gate
    gated = (y_full * z_gate).astype(BF)
    branch = mm(gated, w_out, NN).astype(BF).reshape(seqs, length, width)
    branch = lax.psum_scatter(branch, "seq", scatter_dimension=1, tiled=True)
    output = (hidden_in.astype(F32) + branch.astype(F32)).astype(BF)

    d_inj, pull, dq, dk1, dk2 = run_backward(
        seqs, length, step, inj, dy, ksq_lanes, query_lanes, keep_lanes, spread(key), spread(ksq), states
    )
    dq, dk1, dk2 = dq.reshape(tokens, N), dk1.reshape(tokens, N), dk2.reshape(tokens, N)
    d_z = d_gated * y_full * silu_slope(z_inner)
    d_step = d_inj * xc - pull
    den_square = den * den
    d_norm = -jnp.sum(d_step * beta * beta / den_square, axis=1, keepdims=True)
    d_keys = dk1 - 2.0 * keep * key * dk2 + 2.0 * key * d_norm
    d_rate = (d_step / den_square * beta * (1.0 - beta)).astype(BF)
    d_proj = jnp.concatenate([mm(d_rate, w_dt, NN), d_keys, dq], axis=1)
    d_proj = lax.psum(d_proj, "seq").astype(BF)
    d_conv_out = mm(d_proj, w_x, NT) + step * d_inj + skip * dy
    d_conv = (d_conv_out * silu_slope(conv_flat)).reshape(seqs, length, channels)

    tap_grads = []
    d_x_inner = jnp.zeros((seqs, length, channels), F32)
    for w in range(KCONV):
        lag = lag_max - w
        window = padded[:, w : w + length, :].astype(F32)
        masked = jnp.where(valid[w], d_conv, 0.0)
        tap_grads.append(jnp.sum(masked * window, axis=(0, 1)))
        d_x_inner = d_x_inner + jnp.pad(masked, ((0, 0), (0, lag), (0, 0)))[:, lag:, :] * taps[w]
    d_pre = jnp.concatenate([d_x_inner.reshape(tokens, channels), d_z], axis=1).astype(BF)

    grad_w_out = mm(gated, cot, TN)
    vector_grads = jnp.stack(
        tap_grads
        + [
            jnp.sum(d_conv, axis=(0, 1)),
            jnp.sum(d_rate.astype(F32), axis=0),
            jnp.sum(dy * xc, axis=0),
        ],
        axis=1,
    )
    small_grads = jnp.concatenate([mm(xc_low, d_proj, TN), mm(d_rate, rate, TN), vector_grads], axis=1)
    packed_grads = jnp.concatenate([grad_w_out, jnp.pad(small_grads, ((0, 0), (0, padded_cols - used)))], axis=1)
    packed_grads = lax.psum_scatter(packed_grads.astype(BF), "dp", scatter_dimension=0, tiled=True)
    packed_grads = lax.ppermute(packed_grads, both, back).astype(F32)
    grad_out_weight = packed_grads[:, :width]
    tail = packed_grads[:, width:]

    grad_in_weight = lax.psum_scatter(mm(d_pre, normed, TN).astype(BF), "dp", scatter_dimension=0, tiled=True)
    grad_in_weight = grad_in_weight.astype(F32)
    d_normed = mm(d_pre, w_in, NN)
    gain_local = jnp.sum(d_normed * x_full * inv_rms, axis=0)
    grad_norm_gain = lax.psum(gain_local, both)
    d_normed = d_normed.astype(BF).reshape(seqs, length, width)
    d_normed = lax.psum_scatter(d_normed, "seq", scatter_dimension=1, tiled=True).astype(F32)
    own = hidden_in.astype(F32)
    own_rms = lax.rsqrt(jnp.mean(own * own, axis=2, keepdims=True) + norm_eps)
    scaled = d_normed * gain
    grad_in = (
        out_cotangent.astype(F32)
        + own_rms * scaled
        - own * (own_rms * own_rms * own_rms) * jnp.mean(own * scaled, axis=2, keepdims=True)
    ).astype(BF)

    base = 2 * R + 2 * N
    return (
        output,
        grad_in,
        grad_norm_gain,
        grad_in_weight,
        tail[:, base : base + KCONV].T,
        tail[:, base + KCONV],
        tail[:, : R + 2 * N],
        tail[:, R + 2 * N : base],
        tail[:, base + KCONV + 1],
        tail[:, base + KCONV + 2],
        grad_out_weight,
    )


def solution(mesh):
    both = ("dp", "seq")
    tokens = P("dp", "seq", None)
    matrix, vector = P(both, None), P(both)
    return jax.shard_map(
        local,
        mesh=mesh,
        in_specs=(
            tokens, P("dp", None), P(), matrix, P(None, both), vector,
            matrix, matrix, vector, vector, matrix, tokens,
        ),
        out_specs=(
            tokens, tokens, P(), matrix, P(None, both), vector,
            matrix, matrix, vector, vector, matrix,
        ),
        check_vma=False,
    )
```

```python
import functools
import math

import jax
import jax.numpy as jnp
from jax import lax
from jax.experimental import pallas as pl
from jax.experimental.pallas import tpu as pltpu
from jax.sharding import PartitionSpec as P

N = 16
R = 128
KCONV = 4
CHUNK = 16
LANES = 128

norm_eps = 1e-05
BF = jnp.bfloat16
F32 = jnp.float32


def silu_slope(pre_value):
    sigmoid_of = jax.nn.sigmoid(pre_value)
    return sigmoid_of * (1.0 + pre_value * (1.0 - sigmoid_of))


def token_begins(lengths, position_count):
    doc_ends = jnp.cumsum(lengths, axis=1)
    doc_starts = doc_ends - lengths
    places = jnp.arange(position_count, dtype=jnp.int32)
    inside = doc_starts[:, None, :] <= places[None, :, None]
    return (jnp.max(jnp.where(inside, doc_starts[:, None, :], 0), axis=2), places)


def mm(left, right, dims):
    return lax.dot_general(left, right, (dims, ((), ())), preferred_element_type=F32)


NN = ((1,), (0,))
NT = ((1,), (1,))
TN = ((0,), (0,))


def row(ref, i, lane):
    return jnp.broadcast_to(ref[i : i + 1, pl.ds(lane, LANES)], (8, LANES))


def lane_groups(channels):
    group = math.gcd(channels, 512)
    return [(g, group) for g in range(0, channels, group)]


def scan_forward(step_ref, inj_ref, key_ref, ksq_ref, keep_ref, wq_ref, s_ref, y_ref, carry):
    @pl.when(pl.program_id(1) == 0)
    def _():
        carry[...] = jnp.zeros_like(carry)

    tokens, channels = step_ref.shape
    for first, group in lane_groups(channels):
        tiles = list(range(first, first + group, LANES))

        def chunk(k, state):
            base = pl.multiple_of(k * CHUNK, CHUNK)
            state = list(state)
            steps, injs, keeps = (r.at[pl.ds(base, CHUNK)] for r in (step_ref, inj_ref, keep_ref))
            for i in range(CHUNK):
                at = base + i
                keep = row(keeps, i, 0)
                key = [key_ref[at, 0:8, :], key_ref[at, 8:16, :]]
                ksq = [ksq_ref[at, 0:8, :], ksq_ref[at, 8:16, :]]
                for j, lane in enumerate(tiles):
                    step = row(steps, i, lane)
                    inj = row(injs, i, lane)
                    for h in range(2):
                        state[2 * j + h] = (keep - step * ksq[h]) * state[2 * j + h] + inj * key[h]
                    both = jnp.concatenate([state[2 * j], state[2 * j + 1]], axis=0)
                    s_ref[pl.ds(pl.multiple_of(at * N, N), N), pl.ds(lane, LANES)] = both.astype(BF)
            rows = pl.ds(pl.multiple_of(k * CHUNK * N, CHUNK * N), CHUNK * N)
            y_ref[pl.ds(base, CHUNK), pl.ds(first, group)] = mm(
                wq_ref[pl.ds(base, CHUNK), :], s_ref[rows, pl.ds(first, group)], NN
            )
            return tuple(state)

        start = []
        for lane in tiles:
            start += [carry[0:8, pl.ds(lane, LANES)], carry[8:16, pl.ds(lane, LANES)]]
        end = lax.fori_loop(0, tokens // CHUNK, chunk, tuple(start))
        for j, lane in enumerate(tiles):
            carry[0:8, pl.ds(lane, LANES)] = end[2 * j]
            carry[8:16, pl.ds(lane, LANES)] = end[2 * j + 1]


def scan_backward(
    step_ref, inj_ref, dy_ref, ksq_ref, query_ref, keep_ref, wk_ref, wk2_ref, s_ref, before_ref,
    dinj_ref, pull_ref, dq_ref, dk1_ref, dk2_ref, carry, g_buf, sg_buf,
):
    @pl.when(pl.program_id(1) == 0)
    def _():
        carry[...] = jnp.zeros_like(carry)

    tokens, channels = step_ref.shape
    chunks = tokens // CHUNK
    span = CHUNK * N
    pick = lax.broadcasted_iota(jnp.int32, (CHUNK, span), 0) == (
        lax.broadcasted_iota(jnp.int32, (CHUNK, span), 1) // N
    )

    def diagonal(left, right):
        return jnp.sum(jnp.where(pick, mm(left.astype(BF), right, NT), 0.0), axis=0, keepdims=True)

    for first, group in lane_groups(channels):
        tiles = list(range(first, first + group, LANES))
        cols = pl.ds(first, group)

        def chunk(turn, pulled):
            k = chunks - 1 - turn
            base = pl.multiple_of(k * CHUNK, CHUNK)
            pulled = list(pulled)
            steps, dys, keeps = (r.at[pl.ds(base, CHUNK)] for r in (step_ref, dy_ref, keep_ref))
            for i in reversed(range(CHUNK)):
                at = base + i
                keep = row(keeps, i, 0)
                ksq = [ksq_ref[at, 0:8, :], ksq_ref[at, 8:16, :]]
                query = [query_ref[at, 0:8, :], query_ref[at, 8:16, :]]
                for j, lane in enumerate(tiles):
                    step = row(steps, i, lane)
                    dy = row(dys, i, lane)
                    here = []
                    for h in range(2):
                        grad = pulled[2 * j + h] + dy * query[h]
                        pulled[2 * j + h] = (keep - step * ksq[h]) * grad
                        here.append(grad)
                    g_buf[i * N : (i + 1) * N, pl.ds(lane, LANES)] = jnp.concatenate(here, axis=0).astype(BF)
            low = pl.multiple_of(k * span, span)
            now = s_ref[pl.ds(low, span), cols]
            grads = g_buf[:, cols]
            sg_buf[N:span, cols] = g_buf[N:span, cols] * s_ref[pl.ds(low, span - N), cols]

            @pl.when(k == 0)
            def _():
                sg_buf[0:N, cols] = g_buf[0:N, cols] * before_ref[:, cols]

            @pl.when(k > 0)
            def _():
                prior = s_ref[pl.ds(pl.multiple_of(jnp.maximum(low - N, 0), N), N), cols]
                sg_buf[0:N, cols] = g_buf[0:N, cols] * prior

            prods = sg_buf[:, cols]
            here = pl.ds(base, CHUNK)
            dinj_ref[here, cols] = mm(wk_ref[here, :], grads, NN)
            pull_ref[here, cols] = mm(wk2_ref[here, :], prods, NN)
            dq = diagonal(dy_ref[here, cols], now)
            dk1 = diagonal(inj_ref[here, cols], grads)
            dk2 = diagonal(step_ref[here, cols], prods)
            one = pl.ds(k, 1)
            if first == 0:
                dq_ref[one, :] = dq
                dk1_ref[one, :] = dk1
                dk2_ref[one, :] = dk2
            else:
                dq_ref[one, :] += dq
                dk1_ref[one, :] += dk1
                dk2_ref[one, :] += dk2
            return tuple(pulled)

        start = []
        for lane in tiles:
            start += [carry[0:8, pl.ds(lane, LANES)], carry[8:16, pl.ds(lane, LANES)]]
        end = lax.fori_loop(0, chunks, chunk, tuple(start))
        for j, lane in enumerate(tiles):
            carry[0:8, pl.ds(lane, LANES)] = end[2 * j]
            carry[8:16, pl.ds(lane, LANES)] = end[2 * j + 1]


def run_forward(seqs, length, step, inj, key_lanes, ksq_lanes, keep_lanes, wq):
    channels = step.shape[1]
    block = math.gcd(length, 128)
    blocks = length // block

    def at(b, t):
        return (b * blocks + t, 0)

    def at3(b, t):
        return (b * blocks + t, 0, 0)

    tokens = seqs * length
    return pl.pallas_call(
        scan_forward,
        grid=(seqs, blocks),
        in_specs=[
            pl.BlockSpec((block, channels), at),
            pl.BlockSpec((block, channels), at),
            pl.BlockSpec((block, N, LANES), at3),
            pl.BlockSpec((block, N, LANES), at3),
            pl.BlockSpec((block, LANES), at),
            pl.BlockSpec((block, CHUNK * N), at),
        ],
        out_specs=[
            pl.BlockSpec((block * N, channels), at),
            pl.BlockSpec((block, channels), at),
        ],
        out_shape=[
            jax.ShapeDtypeStruct((tokens * N, channels), BF),
            jax.ShapeDtypeStruct((tokens, channels), F32),
        ],
        scratch_shapes=[pltpu.VMEM((N, channels), F32)],
        cost_estimate=pl.CostEstimate(
            flops=tokens * channels * N * 40, bytes_accessed=tokens * channels * 44, transcendentals=0
        ),
        compiler_params=pltpu.CompilerParams(vmem_limit_bytes=48 << 20),
        name="scan_forward",
    )(step, inj, key_lanes, ksq_lanes, keep_lanes, wq)


def run_backward(seqs, length, step, inj, dy, ksq_lanes, query_lanes, keep_lanes, wk, wk2, states):
    channels = step.shape[1]
    block = math.gcd(length, 128)
    blocks = length // block

    def at(b, t):
        return (b * blocks + blocks - 1 - t, 0)

    def at3(b, t):
        return (b * blocks + blocks - 1 - t, 0, 0)

    def prior(b, t):
        return (jnp.maximum((b * blocks + blocks - 1 - t) * block - 1, 0), 0)

    tokens = seqs * length
    span = CHUNK * N
    rows = pl.BlockSpec((block, channels), at)
    lanes = pl.BlockSpec((block, N, LANES), at3)
    weights = pl.BlockSpec((block, span), at)
    small = pl.BlockSpec((block // CHUNK, span), at)
    return pl.pallas_call(
        scan_backward,
        grid=(seqs, blocks),
        in_specs=[
            rows, rows, rows, lanes, lanes, pl.BlockSpec((block, LANES), at), weights, weights,
            pl.BlockSpec((block * N, channels), at), pl.BlockSpec((N, channels), prior),
        ],
        out_specs=[rows, rows, small, small, small],
        out_shape=[jax.ShapeDtypeStruct((tokens, channels), F32)] * 2
        + [jax.ShapeDtypeStruct((tokens // CHUNK, span), F32)] * 3,
        scratch_shapes=[
            pltpu.VMEM((N, channels), F32),
            pltpu.VMEM((span, channels), BF),
            pltpu.VMEM((span, channels), BF),
        ],
        cost_estimate=pl.CostEstimate(
            flops=tokens * channels * N * 100, bytes_accessed=tokens * channels * 56, transcendentals=0
        ),
        compiler_params=pltpu.CompilerParams(vmem_limit_bytes=56 << 20),
        name="scan_backward",
    )(step, inj, dy, ksq_lanes, query_lanes, keep_lanes, wk, wk2, states, states)


MESH = pl.DeviceIdType.MESH


def any_specs(count):
    return [pl.BlockSpec(memory_space=pl.ANY)] * count


def place():
    return lax.axis_index("dp"), lax.axis_index("seq")


def mate(d):
    return d + 1 - 2 * lax.rem(d, 2)


def remote(src, dst, send, recv, device):
    return pltpu.make_async_remote_copy(
        src_ref=src, dst_ref=dst, send_sem=send, recv_sem=recv, device_id=device, device_id_type=MESH
    )


def greet(device, here=True):
    barrier = pltpu.get_barrier_semaphore()

    def tell():
        pl.semaphore_signal(barrier, inc=1, device_id=device, device_id_type=MESH)

    if here is True:
        tell()
    else:
        pl.when(here)(tell)


def gather_kernel(
    dp, seq, hid_ref, w_ref, pk_ref, hid_out, w_out, pk_out,
    z_send, z_recv, w_send, w_recv, f_send, f_recv, p_send, p_recv, q_send, q_recv, t_sem, own_sem,
):
    d, s = place()
    part = hid_ref.shape[1]
    w_rows, p_rows = w_ref.shape[0], pk_ref.shape[0]
    pieces = z_send.shape[2]
    piece = part // pieces
    half = seq // 2
    pairs = dp // 2
    to_d, to_s = 2 * (d // 2) + lax.rem(s, 2), half * lax.rem(d, 2) + s // 2
    from_d, from_s = 2 * (d // 2) + s // half, 2 * lax.rem(s, half) + lax.rem(d, 2)
    moves = jnp.logical_or(to_d != d, to_s != s)

    greet((d, s - 1), s > 0)
    greet((d, s + 1), s < seq - 1)
    for k in range(1, pairs):
        greet((lax.rem(d + 2 * k, dp), s))
    greet((mate(d), s))
    greet((to_d, to_s), moves)
    greet((from_d, from_s), moves)
    count = pairs + jnp.where(s > 0, 1, 0) + jnp.where(s < seq - 1, 1, 0) + jnp.where(moves, 2, 0)
    pl.semaphore_wait(pltpu.get_barrier_semaphore(), count)

    def shard(which, q):
        return hid_out.at[:, pl.ds(which * part + q * piece, piece), :]

    def hop(way, k, q):
        which = s - k if way == 0 else s + k
        src = hid_ref.at[:, pl.ds(q * piece, piece), :] if k == 0 else shard(which, q)
        near = s + 1 if way == 0 else s - 1
        return remote(src, shard(which, q), z_send.at[way, k, q], z_recv.at[way, k, q], (d, near))

    def can_send(way, k):
        if way == 0:
            return jnp.logical_and(s - k >= 0, s < seq - 1)
        return jnp.logical_and(s + k < seq, s > 0)

    def w_slot(which):
        return w_out.at[pl.ds(which * w_rows, w_rows)]

    def p_slot(which):
        return pk_out.at[pl.ds(which * p_rows, p_rows)]

    def spread(slot, own, send, recv, k):
        return remote(own, slot(d), send.at[k], recv.at[k], (lax.rem(d + 2 * k, dp), s))

    def source(k):
        return lax.rem(d - 2 * k + dp, dp)

    def across(slot, send, recv, k, own=None):
        return remote(own if k == 0 else slot(source(k)), slot(source(k)), send.at[k], recv.at[k], (mate(d), s))

    for q in range(pieces):
        for way in range(2):
            pl.when(can_send(way, 0))(hop(way, 0, q).start)
    transfer = remote(pk_ref, p_slot(to_d), t_sem.at[0], t_sem.at[1], (to_d, to_s))
    stay = pltpu.make_async_copy(pk_ref, p_slot(d), own_sem.at[2])
    pl.when(moves)(transfer.start)
    pl.when(jnp.logical_not(moves))(stay.start)
    for k in range(1, pairs):
        spread(w_slot, w_ref, w_send, w_recv, k).start()
    across(w_slot, f_send, f_recv, 0, w_ref).start()
    own_w = pltpu.make_async_copy(w_ref, w_slot(d), own_sem.at[0])
    own_h = pltpu.make_async_copy(hid_ref, hid_out.at[:, pl.ds(s * part, part), :], own_sem.at[1])
    own_w.start()
    own_h.start()

    pl.when(moves)(remote(pk_ref, p_slot(d), t_sem.at[0], t_sem.at[1], (to_d, to_s)).wait_recv)
    pl.when(jnp.logical_not(moves))(stay.wait)
    for k in range(1, pairs):
        spread(p_slot, p_slot(d), p_send, p_recv, k).start()
    across(p_slot, q_send, q_recv, 0, p_slot(d)).start()

    def arrive(k):
        for q in range(pieces):
            for way in range(2):
                got = s - k >= 0 if way == 0 else s + k < seq

                @pl.when(got)
                def _():
                    which = s - k if way == 0 else s + k
                    remote(
                        shard(which, q), shard(which, q), z_send.at[way, k - 1, q], z_recv.at[way, k - 1, q], (d, s)
                    ).wait_recv()

                if k < seq - 1:
                    pl.when(can_send(way, k))(hop(way, k, q).start)

    for k in range(1, seq - 1):
        arrive(k)
    for slot, own, send, recv, over_send, over_recv in (
        (w_slot, w_ref, w_send, w_recv, f_send, f_recv),
        (p_slot, None, p_send, p_recv, q_send, q_recv),
    ):
        for k in range(1, pairs):
            remote(slot(source(k)), slot(source(k)), send.at[k], recv.at[k], (d, s)).wait_recv()
            across(slot, over_send, over_recv, k).start()
    arrive(seq - 1)

    def other(k):
        return lax.rem(mate(d) - 2 * k + dp, dp)

    for slot, own, over_send, over_recv in ((w_slot, w_ref, f_send, f_recv), (p_slot, p_slot(d), q_send, q_recv)):
        for k in range(pairs):
            remote(slot(other(k)), slot(other(k)), over_send.at[k], over_recv.at[k], (d, s)).wait_recv()
            across(slot, over_send, over_recv, k, own).wait_send()
    for k in range(1, pairs):
        spread(w_slot, w_ref, w_send, w_recv, k).wait_send()
        spread(p_slot, p_slot(d), p_send, p_recv, k).wait_send()
    for k in range(seq - 1):
        for q in range(pieces):
            for way in range(2):
                pl.when(can_send(way, k))(hop(way, k, q).wait_send)
    pl.when(moves)(transfer.wait_send)
    own_w.wait()
    own_h.wait()


def gather(hidden, weight, packed, collective_id=0):
    dp, seq = lax.axis_size("dp"), lax.axis_size("seq")
    seqs, part, width = hidden.shape
    pieces = 4 if part % 64 == 0 else 1
    dma = pltpu.SemaphoreType.DMA
    return pl.pallas_call(
        functools.partial(gather_kernel, dp, seq),
        in_specs=any_specs(3),
        out_specs=any_specs(3),
        out_shape=[
            jax.ShapeDtypeStruct((seqs, part * seq, width), hidden.dtype),
            jax.ShapeDtypeStruct((weight.shape[0] * dp, weight.shape[1]), weight.dtype),
            jax.ShapeDtypeStruct((packed.shape[0] * dp, packed.shape[1]), packed.dtype),
        ],
        scratch_shapes=[
            dma((2, seq, pieces)), dma((2, seq, pieces)),
            dma((dp // 2,)), dma((dp // 2,)), dma((dp // 2,)), dma((dp // 2,)),
            dma((dp // 2,)), dma((dp // 2,)), dma((dp // 2,)), dma((dp // 2,)),
            dma((2,)), dma((3,)),
        ],
        compiler_params=pltpu.CompilerParams(collective_id=collective_id, has_side_effects=True),
        name="gather_in",
    )(hidden, weight, packed)


def added(ref, *others):
    total = ref[...].astype(F32)
    for other in others:
        total = total + other[...].astype(F32)
    return total


def scatter_kernel(
    dp, seq, dn_ref, gw_ref, pk_ref, gain_ref, hid_ref, cot_ref, scale_ref,
    out_ref, gw_out, pk_out, gain_out,
    own, come, gw_own, gw_x, gw_r, pk_own, pk_x, pk_r, pk_fin, g_x, g_r, g_z, g_a, g_b,
    load, z_send, z_recv, w_load, wx_send, wx_recv, w_send, w_recv,
    p_load, px_send, px_recv, p_send, p_recv, t_sem, gx_sem, g_send, g_recv, gz_send, gz_recv,
):
    d, s = place()
    seqs, part, width = out_ref.shape
    pieces = z_send.shape[1]
    piece = part // pieces
    half = seq // 2
    pairs = dp // 2
    mine, odd = d // 2, lax.rem(d, 2)
    to_d, to_s = 2 * (d // 2) + s // half, 2 * lax.rem(s, half) + lax.rem(d, 2)
    from_d, from_s = 2 * (d // 2) + lax.rem(s, 2), half * lax.rem(d, 2) + s // 2
    moves = jnp.logical_or(to_d != d, to_s != s)

    for k in range(1, seq):
        greet((d, lax.rem(s + k, seq)))
    for k in range(1, pairs):
        greet((lax.rem(d + 2 * k, dp), s))
    greet((mate(d), s))
    greet((to_d, to_s), moves)
    greet((from_d, from_s), moves)
    pl.semaphore_wait(pltpu.get_barrier_semaphore(), seq - 1 + pairs + jnp.where(moves, 2, 0))

    def swap(src_ref, dst, send, recv, j):
        rows = dst.shape[1]
        other = 2 * j + 1 - odd
        return remote(src_ref.at[pl.ds(other * rows, rows)], dst.at[j], send.at[j], recv.at[j], (mate(d), s))

    def fetch(src_ref, dst, sem, j):
        rows = dst.shape[1]
        return pltpu.make_async_copy(src_ref.at[pl.ds((2 * j + odd) * rows, rows)], dst.at[j], sem.at[j])

    def chunk(r):
        return pltpu.make_async_copy(dn_ref.at[:, pl.ds(r * part, part), :], own.at[r], load.at[r])

    gain_swap = remote(gain_ref, g_x, gx_sem.at[0], gx_sem.at[1], (mate(d), s))
    gain_swap.start()
    for j in range(pairs):
        swap(pk_ref, pk_x, px_send, px_recv, j).start()
    ends = []
    for i in range(seq):
        ends.append(seq - 1 - i // 2 if i % 2 == 0 else i // 2)
    for r in ends:
        chunk(r).start()
    for j in range(pairs):
        fetch(pk_ref, pk_own, p_load, j).start()
    for j in range(pairs):
        swap(gw_ref, gw_x, wx_send, wx_recv, j).start()
        fetch(gw_ref, gw_own, w_load, j).start()
    for r in ends:
        chunk(r).wait()

    def give(way, r, q):
        rows = pl.ds(q * piece, piece)
        slot = r if way == 0 else jnp.where(s - 1 == r, seq, r)
        near = s + 1 if way == 0 else s - 1
        return remote(own.at[r, :, rows, :], come.at[slot, :, rows, :], z_send.at[r, q], z_recv.at[slot, q], (d, near))

    def landed(slot, q):
        rows = pl.ds(q * piece, piece)
        here = come.at[slot, :, rows, :]
        remote(here, here, z_send.at[0, q], z_recv.at[slot, q], (d, s)).wait_recv()

    def pass_on(way, r):
        first = s == 0 if way == 0 else s == seq - 1
        sends = s < r if way == 0 else s > r
        for q in range(pieces):
            @pl.when(jnp.logical_and(sends, jnp.logical_not(first)))
            def _():
                rows = pl.ds(q * piece, piece)
                landed(r, q)
                own[r, :, rows, :] = added(own.at[r, :, rows, :], come.at[r, :, rows, :]).astype(BF)

            pl.when(sends)(give(way, r, q).start)

    def round_of(i):
        pass_on(0, seq - 1 - i)
        pass_on(1, i)

    def onward(part_own, part_r, send, recv, k):
        j = lax.rem(mine + k, pairs)
        return remote(part_own.at[j], part_r.at[k - 1], send.at[k], recv.at[k], (lax.rem(d + 2 * k, dp), s))

    def join(src_ref, part_own, part_x, part_r, sem, xs, xr, send, recv):
        for k in range(1, pairs + 1):
            j = lax.rem(mine + k, pairs)
            fetch(src_ref, part_own, sem, j).wait()
            swap(src_ref, part_x, xs, xr, j).wait_recv()
            if k < pairs:
                part_own[j] = added(part_own.at[j], part_x.at[j]).astype(BF)
                onward(part_own, part_r, send, recv, k).start()

    def finish(part_own, part_x, part_r, send, recv):
        for k in range(1, pairs):
            onward(part_own, part_r, send, recv, k).wait_recv()
        return added(part_own.at[mine], part_x.at[mine], *[part_r.at[k] for k in range(pairs - 1)])

    round_of(0) if seq == 2 else None
    gain_swap.wait_recv()
    g_a[...] = gain_ref[...] + g_x[...]

    def gain_near(k):
        return remote(g_a, g_r.at[k - 1], g_send.at[k], g_recv.at[k], (lax.rem(d + 2 * k, dp), s))

    def gain_far(k):
        return remote(g_b, g_z.at[k - 1], gz_send.at[k], gz_recv.at[k], (d, lax.rem(s + k, seq)))

    for k in range(1, pairs):
        gain_near(k).start()
    join(pk_ref, pk_own, pk_x, pk_r, p_load, px_send, px_recv, p_send, p_recv)
    if seq > 2:
        round_of(0)
    join(gw_ref, gw_own, gw_x, gw_r, w_load, wx_send, wx_recv, w_send, w_recv)
    for k in range(1, pairs):
        gain_near(k).wait_recv()
    g_b[...] = added(g_a, *[g_r.at[k] for k in range(pairs - 1)])
    for k in range(1, seq):
        gain_far(k).start()
    for i in range(1, seq - 2):
        round_of(i)
    pk_fin[...] = finish(pk_own, pk_x, pk_r, p_send, p_recv).astype(BF)
    back = remote(pk_fin, pk_out, t_sem.at[0], t_sem.at[1], (to_d, to_s))
    stay = pltpu.make_async_copy(pk_fin, pk_out, t_sem.at[2])
    pl.when(moves)(back.start)
    pl.when(jnp.logical_not(moves))(stay.start)
    if seq > 2:
        round_of(seq - 2)
    gw_out[...] = finish(gw_own, gw_x, gw_r, w_send, w_recv)
    for k in range(1, seq):
        gain_far(k).wait_recv()
    gain_out[...] = added(g_b, *[g_z.at[k] for k in range(seq - 1)])

    for q in range(pieces):
        pl.when(s > 0)(functools.partial(landed, s, q))
        pl.when(s < seq - 1)(functools.partial(landed, seq, q))
        rows = pl.ds(q * piece, piece)
        from_left = jnp.where(s > 0, come[s, :, rows, :].astype(F32), 0.0)
        from_right = jnp.where(s < seq - 1, come[seq, :, rows, :].astype(F32), 0.0)
        total = own[s, :, rows, :].astype(F32) + from_left + from_right
        x = hid_ref[:, rows, :].astype(F32)
        inv = lax.rsqrt(jnp.mean(x * x, axis=2, keepdims=True) + norm_eps)
        scaled = total * scale_ref[...].astype(F32)[None]
        out_ref[:, rows, :] = (
            cot_ref[:, rows, :].astype(F32)
            + inv * scaled
            - x * (inv * inv * inv) * jnp.mean(x * scaled, axis=2, keepdims=True)
        ).astype(BF)

    for q in range(pieces):
        for r in range(1, seq):
            pl.when(s < r)(give(0, r, q).wait_send)
        for r in range(seq - 1):
            pl.when(s > r)(give(1, r, q).wait_send)
    gain_swap.wait_send()
    for j in range(pairs):
        swap(pk_ref, pk_x, px_send, px_recv, j).wait_send()
        swap(gw_ref, gw_x, wx_send, wx_recv, j).wait_send()
    for k in range(1, pairs):
        onward(pk_own, pk_r, p_send, p_recv, k).wait_send()
        onward(gw_own, gw_r, w_send, w_recv, k).wait_send()
        gain_near(k).wait_send()
    for k in range(1, seq):
        gain_far(k).wait_send()
    pl.when(moves)(back.wait_send)
    pl.when(moves)(remote(pk_fin, pk_out, t_sem.at[0], t_sem.at[1], (to_d, to_s)).wait_recv)
    pl.when(jnp.logical_not(moves))(stay.wait)


def scatter(d_normed, grad_in_w, packed_grads, gain, hidden_in, cotangent, norm_gain, collective_id=1):
    dp, seq = lax.axis_size("dp"), lax.axis_size("seq")
    seqs, part, width = hidden_in.shape
    w_rows, p_rows = grad_in_w.shape[0] // dp, packed_grads.shape[0] // dp
    cols = packed_grads.shape[1]
    pieces = 4 if part % 64 == 0 else 1
    pairs = dp // 2
    dma, vmem = pltpu.SemaphoreType.DMA, pltpu.VMEM
    here = pl.BlockSpec(memory_space=pltpu.VMEM)
    return pl.pallas_call(
        functools.partial(scatter_kernel, dp, seq),
        in_specs=any_specs(3) + [here] * 4,
        out_specs=[here] * 4,
        out_shape=[
            jax.ShapeDtypeStruct((seqs, part, width), BF),
            jax.ShapeDtypeStruct((w_rows, width), F32),
            jax.ShapeDtypeStruct((p_rows, cols), BF),
            jax.ShapeDtypeStruct(gain.shape, F32),
        ],
        scratch_shapes=[
            vmem((seq, seqs, part, width), BF), vmem((seq + 1, seqs, part, width), BF),
            vmem((pairs, w_rows, width), BF), vmem((pairs, w_rows, width), BF), vmem((pairs - 1, w_rows, width), BF),
            vmem((pairs, p_rows, cols), BF), vmem((pairs, p_rows, cols), BF), vmem((pairs - 1, p_rows, cols), BF),
            vmem((p_rows, cols), BF),
            vmem(gain.shape, F32), vmem((pairs - 1,) + gain.shape, F32), vmem((seq - 1,) + gain.shape, F32),
            vmem(gain.shape, F32), vmem(gain.shape, F32),
            dma((seq,)), dma((seq, pieces)), dma((seq + 1, pieces)),
            dma((pairs,)), dma((pairs,)), dma((pairs,)), dma((pairs,)), dma((pairs,)),
            dma((pairs,)), dma((pairs,)), dma((pairs,)), dma((pairs,)), dma((pairs,)),
            dma((3,)), dma((2,)), dma((pairs,)), dma((pairs,)), dma((seq,)), dma((seq,)),
        ],
        compiler_params=pltpu.CompilerParams(
            collective_id=collective_id, has_side_effects=True, vmem_limit_bytes=60 << 20
        ),
        name="scatter_out",
    )(d_normed, grad_in_w, packed_grads, gain, hidden_in, cotangent, norm_gain)


def local(
    hidden_in,
    doc_lengths,
    norm_gain,
    in_weight,
    conv_weight,
    conv_bias,
    x_weight,
    dt_weight,
    dt_bias,
    skip_gain,
    out_weight,
    out_cotangent,
):
    seqs, part_len, width = hidden_in.shape
    dp, seq = lax.axis_size("dp"), lax.axis_size("seq")
    length = part_len * seq
    tokens = seqs * length
    rows = out_weight.shape[0]
    channels = rows * dp
    lag_max = KCONV - 1

    small = jnp.concatenate(
        [x_weight, dt_weight, conv_weight.T, conv_bias[:, None], dt_bias[:, None], skip_gain[:, None]], axis=1
    )
    used = small.shape[1]
    padded_cols = -(-used // LANES) * LANES
    packed = jnp.concatenate([out_weight, jnp.pad(small, ((0, 0), (0, padded_cols - used)))], axis=1)

    hidden, w_in, packed = gather(hidden_in, in_weight, packed)
    hidden = hidden.reshape(tokens, width)
    cot = lax.all_gather(out_cotangent, "seq", axis=1, tiled=True).reshape(tokens, width)

    w_out = packed[:, :width]
    tail = packed[:, width:]
    w_x = tail[:, : R + 2 * N]
    w_dt = tail[:, R + 2 * N : 2 * R + 2 * N]
    vectors = tail[:, 2 * R + 2 * N : used].astype(F32).T
    taps, conv_shift, rate_shift, skip = vectors[:KCONV], vectors[KCONV], vectors[KCONV + 1], vectors[KCONV + 2]

    begins, places = token_begins(doc_lengths, length)
    keep = (places[None, :] != begins).astype(F32).reshape(tokens, 1)
    valid = [(places[None, :] - (lag_max - w) >= begins)[:, :, None] for w in range(KCONV)]

    gain = norm_gain.astype(F32)
    x_full = hidden.astype(F32)
    inv_rms = lax.rsqrt(jnp.mean(x_full * x_full, axis=1, keepdims=True) + norm_eps)
    normed = (x_full * inv_rms * gain).astype(BF)
    pre = mm(normed, w_in, NT).astype(BF)
    x_inner = pre[:, :channels].reshape(seqs, length, channels)
    z_inner = pre[:, channels:].astype(F32)

    padded = jnp.pad(x_inner, ((0, 0), (lag_max, 0), (0, 0)))
    conv_sum = jnp.broadcast_to(conv_shift, (seqs, length, channels))
    for w in range(KCONV):
        window = padded[:, w : w + length, :].astype(F32)
        conv_sum = conv_sum + jnp.where(valid[w], window * taps[w], 0.0)
    conv_flat = conv_sum.reshape(tokens, channels)
    xc_low = jax.nn.silu(conv_flat).astype(BF)
    xc = xc_low.astype(F32)
    proj = lax.psum(mm(xc_low, w_x, NN), "seq")
    rate = proj[:, :R].astype(BF)
    key = proj[:, R : R + N]
    query = proj[:, R + N :]
    beta = jax.nn.sigmoid(mm(rate, w_dt, NT) + rate_shift)
    den = 1.0 + beta * jnp.sum(key * key, axis=1, keepdims=True)
    step = beta / den
    inj = step * xc

    def lanes(values):
        return jnp.broadcast_to(values[:, :, None], (tokens, N, LANES))

    ksq = keep * key * key
    key_lanes, ksq_lanes, query_lanes = lanes(key), lanes(ksq), lanes(query)
    keep_lanes = jnp.broadcast_to(keep, (tokens, LANES))
    eye = (jnp.arange(tokens)[:, None] % CHUNK == jnp.arange(CHUNK)[None, :]).astype(F32)

    def spread(values):
        return (values[:, None, :] * eye[:, :, None]).reshape(tokens, CHUNK * N).astype(BF)

    states, mixed = run_forward(seqs, length, step, inj, key_lanes, ksq_lanes, keep_lanes, spread(query))
    y_full = mixed + skip * xc

    d_gated = mm(cot, w_out, NT)
    z_gate = jax.nn.silu(z_inner)
    dy = d_gated * z_gate
    gated = (y_full * z_gate).astype(BF)
    branch = mm(gated, w_out, NN).astype(BF).reshape(seqs, length, width)
    branch = lax.psum_scatter(branch, "seq", scatter_dimension=1, tiled=True)
    output = (hidden_in.astype(F32) + branch.astype(F32)).astype(BF)

    d_inj, pull, dq, dk1, dk2 = run_backward(
        seqs, length, step, inj, dy, ksq_lanes, query_lanes, keep_lanes, spread(key), spread(ksq), states
    )
    dq, dk1, dk2 = dq.reshape(tokens, N), dk1.reshape(tokens, N), dk2.reshape(tokens, N)
    d_z = d_gated * y_full * silu_slope(z_inner)
    d_step = d_inj * xc - pull
    den_square = den * den
    d_norm = -jnp.sum(d_step * beta * beta / den_square, axis=1, keepdims=True)
    d_keys = dk1 - 2.0 * keep * key * dk2 + 2.0 * key * d_norm
    d_rate = (d_step / den_square * beta * (1.0 - beta)).astype(BF)
    d_proj = jnp.concatenate([mm(d_rate, w_dt, NN), d_keys, dq], axis=1)
    d_proj = lax.psum(d_proj, "seq").astype(BF)
    d_conv_out = mm(d_proj, w_x, NT) + step * d_inj + skip * dy
    d_conv = (d_conv_out * silu_slope(conv_flat)).reshape(seqs, length, channels)

    tap_grads = []
    d_x_inner = jnp.zeros((seqs, length, channels), F32)
    for w in range(KCONV):
        lag = lag_max - w
        window = padded[:, w : w + length, :].astype(F32)
        masked = jnp.where(valid[w], d_conv, 0.0)
        tap_grads.append(jnp.sum(masked * window, axis=(0, 1)))
        d_x_inner = d_x_inner + jnp.pad(masked, ((0, 0), (0, lag), (0, 0)))[:, lag:, :] * taps[w]
    d_pre = jnp.concatenate([d_x_inner.reshape(tokens, channels), d_z], axis=1).astype(BF)

    grad_w_out = mm(gated, cot, TN)
    vector_grads = jnp.stack(
        tap_grads
        + [
            jnp.sum(d_conv, axis=(0, 1)),
            jnp.sum(d_rate.astype(F32), axis=0),
            jnp.sum(dy * xc, axis=0),
        ],
        axis=1,
    )
    small_grads = jnp.concatenate([mm(xc_low, d_proj, TN), mm(d_rate, rate, TN), vector_grads], axis=1)
    packed_grads = jnp.concatenate([grad_w_out, jnp.pad(small_grads, ((0, 0), (0, padded_cols - used)))], axis=1)
    d_normed = mm(d_pre, w_in, NN)
    gain_local = jnp.sum(d_normed * x_full * inv_rms, axis=0)
    grad_in, grad_in_weight, packed_grads, grad_norm_gain = scatter(
        d_normed.astype(BF).reshape(seqs, length, width),
        mm(d_pre, normed, TN).astype(BF),
        packed_grads.astype(BF),
        gain_local.reshape(8, width // 8),
        hidden_in,
        out_cotangent,
        norm_gain.reshape(1, width),
    )
    grad_norm_gain = grad_norm_gain.reshape(width)
    packed_grads = packed_grads.astype(F32)
    grad_out_weight = packed_grads[:, :width]
    tail = packed_grads[:, width:]

    base = 2 * R + 2 * N
    return (
        output,
        grad_in,
        grad_norm_gain,
        grad_in_weight,
        tail[:, base : base + KCONV].T,
        tail[:, base + KCONV],
        tail[:, : R + 2 * N],
        tail[:, R + 2 * N : base],
        tail[:, base + KCONV + 1],
        tail[:, base + KCONV + 2],
        grad_out_weight,
    )


def solution(mesh):
    both = ("dp", "seq")
    tokens = P("dp", "seq", None)
    matrix, vector = P(both, None), P(both)
    return jax.shard_map(
        local,
        mesh=mesh,
        in_specs=(
            tokens, P("dp", None), P(), matrix, P(None, both), vector,
            matrix, matrix, vector, vector, matrix, tokens,
        ),
        out_specs=(
            tokens, tokens, P(), matrix, P(None, both), vector,
            matrix, matrix, vector, vector, matrix,
        ),
        check_vma=False,
    )
```

```python
import functools
import math

import jax
import jax.numpy as jnp
from jax import lax
from jax.experimental import pallas as pl
from jax.experimental.pallas import tpu as pltpu
from jax.sharding import PartitionSpec as P

N = 16
R = 128
KCONV = 4
CHUNK = 16
LANES = 128
GROUP = 1024
BLOCK = 128

norm_eps = 1e-05
BF = jnp.bfloat16
F32 = jnp.float32


def silu_slope(pre_value):
    sigmoid_of = jax.nn.sigmoid(pre_value)
    return sigmoid_of * (1.0 + pre_value * (1.0 - sigmoid_of))


def token_begins(lengths, position_count):
    doc_ends = jnp.cumsum(lengths, axis=1)
    doc_starts = doc_ends - lengths
    places = jnp.arange(position_count, dtype=jnp.int32)
    inside = doc_starts[:, None, :] <= places[None, :, None]
    return (jnp.max(jnp.where(inside, doc_starts[:, None, :], 0), axis=2), places)


def mm(left, right, dims):
    return lax.dot_general(left, right, (dims, ((), ())), preferred_element_type=F32)


NN = ((1,), (0,))
NT = ((1,), (1,))
TN = ((0,), (0,))


def row(ref, i, lane):
    return jnp.broadcast_to(ref[i : i + 1, pl.ds(lane, LANES)], (8, LANES))


def wide(ref, rows, count):
    value = ref[rows, :]
    return jnp.concatenate([value] * (count // LANES), axis=1)


def merge(even, odd, stride):
    low = lax.broadcasted_iota(jnp.int32, (8, LANES), 0) % (2 * stride) < stride
    if stride == 4:
        return jnp.where(low, even, odd) + pltpu.roll(jnp.where(low, odd, even), 4, 0)
    return jnp.where(low, even + pltpu.roll(even, 8 - stride, 0), odd + pltpu.roll(odd, stride, 0))


def collect(stack, value, descending):
    level = 0
    while stack and stack[-1][0] == level:
        other = stack.pop()[1]
        value = merge(value, other, 1 << level) if descending else merge(other, value, 1 << level)
        level += 1
    stack.append((level, value))


def each_chunk(tokens, channels, body):
    group = math.gcd(channels, 512)

    def run(k, carried):
        rows = pl.ds(pl.multiple_of(k * CHUNK, CHUNK), CHUNK)
        for first in range(0, channels, group):
            body(rows, pl.ds(first, group), first)
        return carried

    lax.fori_loop(0, tokens // CHUNK, run, 0)


def load_carry(carry, tiles):
    out = []
    for lane in tiles:
        out += [carry[0:8, pl.ds(lane, LANES)], carry[8:16, pl.ds(lane, LANES)]]
    return tuple(out)


def store_carry(carry, tiles, values):
    for j, lane in enumerate(tiles):
        carry[0:8, pl.ds(lane, LANES)] = values[2 * j]
        carry[8:16, pl.ds(lane, LANES)] = values[2 * j + 1]


def halves(value):
    return [value[0:8], value[8:16]]


def token(keys, queries, keeps, i):
    return row(keeps, i, 0), halves(keys[i].astype(F32)), halves(queries[i].astype(F32))


def lane_groups(channels):
    group = math.gcd(channels, GROUP)
    return [list(range(first, first + group, LANES)) for first in range(0, channels, group)]


def forward_kernel(
    xc_ref, z_ref, rate_ref, key_ref, query_ref, keep_ref, ksum_ref, wdt_ref, vec_ref,
    s_ref, y_ref, gated_ref, step, inj, carry,
):
    @pl.when(pl.program_id(1) == 0)
    def _():
        carry[...] = jnp.zeros_like(carry)

    tokens, channels = xc_ref.shape
    step[...] = mm(rate_ref[...], wdt_ref[...], NT)

    def prepare(rows, cols, first):
        beta = jax.nn.sigmoid(step[rows, cols] + vec_ref[0:1, cols])
        eps = beta / (1.0 + beta * wide(ksum_ref, rows, cols.size))
        step[rows, cols] = eps
        inj[rows, cols] = eps * xc_ref[rows, cols].astype(F32)

    each_chunk(tokens, channels, prepare)
    for tiles in lane_groups(channels):

        def chunk(k, state):
            state = list(state)
            base = pl.multiple_of(k * CHUNK, CHUNK)
            steps, injs, keeps, keys, queries = (
                r.at[pl.ds(base, CHUNK)] for r in (step, inj, keep_ref, key_ref, query_ref)
            )
            saved = s_ref.at[pl.ds(pl.multiple_of(k * CHUNK * N, CHUNK * N), CHUNK * N)]
            stacks = [[] for _ in tiles]
            for i in range(CHUNK):
                keep, key, query = token(keys, queries, keeps, i)
                ksq = [keep * key[h] * key[h] for h in range(2)]
                for j, lane in enumerate(tiles):
                    eps, push = row(steps, i, lane), row(injs, i, lane)
                    for h in range(2):
                        state[2 * j + h] = (keep - eps * ksq[h]) * state[2 * j + h] + push * key[h]
                    both = jnp.concatenate([state[2 * j], state[2 * j + 1]], axis=0)
                    saved[i * N : (i + 1) * N, pl.ds(lane, LANES)] = both.astype(BF)
                    collect(stacks[j], state[2 * j] * query[0] + state[2 * j + 1] * query[1], False)
                    if i % 8 == 7:
                        y_ref[pl.ds(pl.multiple_of(base + i - 7, 8), 8), pl.ds(lane, LANES)] = stacks[j].pop()[1]
            return tuple(state)

        store_carry(carry, tiles, lax.fori_loop(0, tokens // CHUNK, chunk, load_carry(carry, tiles)))

    def emit(rows, cols, first):
        y_full = y_ref[rows, cols] + vec_ref[1:2, cols] * xc_ref[rows, cols].astype(F32)
        y_ref[rows, cols] = y_full
        z = z_ref[rows, cols].astype(F32)
        gated_ref[rows, cols] = (y_full * (z * jax.nn.sigmoid(z))).astype(BF)

    each_chunk(tokens, channels, emit)


def backward_kernel(
    dg_ref, y_ref, xc_ref, z_ref, rate_ref, key_ref, query_ref, keep_ref, ksum_ref, wdt_ref, vec_ref, s_ref, before_ref,
    dz_ref, rest_ref, dq_ref, dk_ref, dnorm_ref, drow_ref, gdt_ref, sums_ref,
    step, inj, dy, mix, pull, beta, drate, carry, acc_q, acc_k,
):
    turn = pl.program_id(1)
    tokens, channels = xc_ref.shape
    chunks = tokens // CHUNK

    @pl.when(jnp.logical_and(pl.program_id(0) == 0, turn == 0))
    def _():
        gdt_ref[...] = jnp.zeros_like(gdt_ref)
        sums_ref[...] = jnp.zeros_like(sums_ref)

    @pl.when(turn == 0)
    def _():
        carry[...] = jnp.zeros_like(carry)

    beta[...] = mm(rate_ref[...], wdt_ref[...], NT)

    def prepare(rows, cols, first):
        rate_beta = jax.nn.sigmoid(beta[rows, cols] + vec_ref[0:1, cols])
        eps = rate_beta / (1.0 + rate_beta * wide(ksum_ref, rows, cols.size))
        beta[rows, cols] = rate_beta
        step[rows, cols] = eps
        xc = xc_ref[rows, cols].astype(F32)
        inj[rows, cols] = eps * xc
        z = z_ref[rows, cols].astype(F32)
        sig = jax.nn.sigmoid(z)
        d_gated = dg_ref[rows, cols]
        d_y = d_gated * (z * sig)
        dy[rows, cols] = d_y
        dz_ref[rows, cols] = (d_gated * y_ref[rows, cols] * (sig * (1.0 + z * (1.0 - sig)))).astype(BF)
        weighted = d_y * xc
        sums_ref[8:16, cols] += weighted[0:8] + weighted[8:16]

    each_chunk(tokens, channels, prepare)
    for tiles in lane_groups(channels):
        start = tiles[0] == 0

        def chunk(back, carried):
            k = chunks - 1 - back
            pulled, now = list(carried[0]), list(carried[1])
            base = pl.multiple_of(k * CHUNK, CHUNK)
            steps, injs, dys, keeps, keys, queries = (
                r.at[pl.ds(base, CHUNK)] for r in (step, inj, dy, keep_ref, key_ref, query_ref)
            )
            stacks = [([], []) for _ in tiles]
            for i in reversed(range(CHUNK)):
                keep, key, query = token(keys, queries, keeps, i)
                kept = [keep * key[h] for h in range(2)]
                ksq = [kept[h] * key[h] for h in range(2)]
                if i > 0:
                    before = pl.ds(pl.multiple_of((base + i) * N - N, N), N)
                else:
                    before = pl.ds(pl.multiple_of(jnp.maximum(base * N - N, 0), N), N)
                seen, plain, scaled = [0.0, 0.0], [0.0, 0.0], [0.0, 0.0]
                for j, lane in enumerate(tiles):
                    eps, push, d_y = row(steps, i, lane), row(injs, i, lane), row(dys, i, lane)
                    prior = s_ref[before, pl.ds(lane, LANES)]
                    if i == 0:
                        prior = jnp.where(k > 0, prior, before_ref[:, pl.ds(lane, LANES)])
                    prior = halves(prior.astype(F32))
                    by_key, by_square = [], []
                    for h in range(2):
                        at = 2 * j + h
                        grad = pulled[at] + d_y * query[h]
                        pulled[at] = (keep - eps * ksq[h]) * grad
                        keyed = eps * (grad * key[h])
                        prod = keyed * prior[h]
                        seen[h] += now[at] * d_y
                        plain[h] += grad * push
                        scaled[h] += prod
                        by_key.append(keyed)
                        by_square.append(prod * kept[h])
                        now[at] = prior[h]
                    collect(stacks[j][0], by_key[0] + by_key[1], True)
                    collect(stacks[j][1], by_square[0] + by_square[1], True)
                    if i % 8 == 0:
                        rows = pl.ds(pl.multiple_of(base + i, 8), 8)
                        mix[rows, pl.ds(lane, LANES)] = stacks[j][0].pop()[1]
                        pull[rows, pl.ds(lane, LANES)] = stacks[j][1].pop()[1]
                for ref, parts in ((acc_q, seen), (acc_k, [plain[h] - 2.0 * keep * scaled[h] for h in range(2)])):
                    for h in range(2):
                        rows = pl.ds(pl.multiple_of((base + i) * N + 8 * h, 8), 8)
                        if start:
                            ref[rows, :] = parts[h]
                        else:
                            ref[rows, :] += parts[h]
            return (tuple(pulled), tuple(now))

        now = []
        for lane in tiles:
            now += halves(s_ref[tokens * N - N : tokens * N, pl.ds(lane, LANES)].astype(F32))
        pulled, now = lax.fori_loop(0, chunks, chunk, (load_carry(carry, tiles), tuple(now)))
        store_carry(carry, tiles, pulled)

    ones = jnp.ones((LANES, LANES), BF)
    diagonal = lax.broadcasted_iota(jnp.int32, (LANES, LANES), 0) == (
        lax.broadcasted_iota(jnp.int32, (LANES, LANES), 1)
    )
    for out, ref in ((dq_ref, acc_q), (dk_ref, acc_k)):
        for first in range(0, tokens * N, LANES):
            sums = mm(ref[first : first + LANES, :].astype(BF), ones, NN)
            at = first // LANES
            out[at : at + 1, :] = jnp.sum(jnp.where(diagonal, sums, 0.0), axis=0, keepdims=True)

    def settle(rows, cols, first):
        rate_beta, eps = beta[rows, cols], step[rows, cols]
        through = mix[rows, cols]
        change = through * xc_ref[rows, cols].astype(F32) - pull[rows, cols]
        inverse = 1.0 / (1.0 + rate_beta * wide(ksum_ref, rows, cols.size))
        low = (change * inverse * (1.0 - rate_beta)).astype(BF)
        drate[rows, cols] = low
        lowered = low.astype(F32)
        sums_ref[0:8, cols] += lowered[0:8] + lowered[8:16]
        rest_ref[rows, cols] = through + vec_ref[1:2, cols] * dy[rows, cols]
        square = change * eps
        total = square[:, 0:LANES]
        for lane in range(LANES, cols.size, LANES):
            total = total + square[:, lane : lane + LANES]
        if first == 0:
            dnorm_ref[rows, :] = total
        else:
            dnorm_ref[rows, :] += total

    each_chunk(tokens, channels, settle)
    drow_ref[...] = mm(drate[...], wdt_ref[...], NN)
    gdt_ref[...] += mm(drate[...], rate_ref[...], TN)


def scan_blocks(length):
    block = math.gcd(length, BLOCK)
    return block, length // block


def row_spec(rows, cols, when, col=0):
    return pl.BlockSpec((rows, cols), lambda b, t: (when(b, t), col))


def spread_spec(block, when):
    return pl.BlockSpec((block, N, LANES), lambda b, t: (when(b, t), 0, 0))


def whole(array):
    return pl.BlockSpec(array.shape, lambda b, t: (0, 0), pipeline_mode=pl.Buffered(1))


def scan_forward(seqs, length, xc, pre, rate, key_lanes, query_lanes, keep_lanes, ksum_lanes, w_dt, vectors):
    tokens, channels = xc.shape
    block, blocks = scan_blocks(length)

    def at(b, t):
        return b * blocks + t

    rows = row_spec(block, channels, at)
    lanes = row_spec(block, LANES, at)
    vmem = pltpu.VMEM
    return pl.pallas_call(
        forward_kernel,
        grid=(seqs, blocks),
        in_specs=[
            rows, row_spec(block, channels, at, 1), row_spec(block, R, at),
            spread_spec(block, at), spread_spec(block, at), lanes, lanes, whole(w_dt), whole(vectors),
        ],
        out_specs=[row_spec(block * N, channels, at), rows, rows],
        out_shape=[
            jax.ShapeDtypeStruct((tokens * N, channels), BF),
            jax.ShapeDtypeStruct((tokens, channels), F32),
            jax.ShapeDtypeStruct((tokens, channels), BF),
        ],
        scratch_shapes=[vmem((block, channels), F32), vmem((block, channels), F32), vmem((N, channels), F32)],
        cost_estimate=pl.CostEstimate(
            flops=tokens * channels * N * 60, bytes_accessed=tokens * channels * 44, transcendentals=0
        ),
        compiler_params=pltpu.CompilerParams(vmem_limit_bytes=40 << 20),
        name="scan_forward",
    )(xc, pre, rate, key_lanes, query_lanes, keep_lanes, ksum_lanes, w_dt, vectors)


def scan_backward(seqs, length, d_gated, y, xc, pre, rate, key_lanes, query_lanes, keep_lanes, ksum_lanes, w_dt, vectors, states):
    tokens, channels = xc.shape
    block, blocks = scan_blocks(length)

    def at(b, t):
        return b * blocks + blocks - 1 - t

    def prior(b, t):
        return (jnp.maximum(at(b, t) * block - 1, 0), 0)

    rows = row_spec(block, channels, at)
    lanes = row_spec(block, LANES, at)
    flat = row_spec(block * N // LANES, LANES, at)
    vmem = pltpu.VMEM
    wide_f32 = vmem((block, channels), F32)
    return pl.pallas_call(
        backward_kernel,
        grid=(seqs, blocks),
        in_specs=[
            rows, rows, rows, row_spec(block, channels, at, 1), row_spec(block, R, at),
            spread_spec(block, at), spread_spec(block, at), lanes, lanes, whole(w_dt), whole(vectors),
            row_spec(block * N, channels, at), pl.BlockSpec((N, channels), prior),
        ],
        out_specs=[
            rows, rows, flat, flat, lanes, row_spec(block, R, at),
            pl.BlockSpec((channels, R), lambda b, t: (0, 0)), pl.BlockSpec((16, channels), lambda b, t: (0, 0)),
        ],
        out_shape=[
            jax.ShapeDtypeStruct((tokens, channels), BF),
            jax.ShapeDtypeStruct((tokens, channels), F32),
            jax.ShapeDtypeStruct((tokens * N // LANES, LANES), F32),
            jax.ShapeDtypeStruct((tokens * N // LANES, LANES), F32),
            jax.ShapeDtypeStruct((tokens, LANES), F32),
            jax.ShapeDtypeStruct((tokens, R), F32),
            jax.ShapeDtypeStruct((channels, R), F32),
            jax.ShapeDtypeStruct((16, channels), F32),
        ],
        scratch_shapes=[
            wide_f32, wide_f32, wide_f32, wide_f32, wide_f32, wide_f32, vmem((block, channels), BF),
            vmem((N, channels), F32), vmem((block * N, LANES), F32), vmem((block * N, LANES), F32),
        ],
        cost_estimate=pl.CostEstimate(
            flops=tokens * channels * N * 100, bytes_accessed=tokens * channels * 56, transcendentals=0
        ),
        compiler_params=pltpu.CompilerParams(vmem_limit_bytes=48 << 20),
        name="scan_backward",
    )(d_gated, y, xc, pre, rate, key_lanes, query_lanes, keep_lanes, ksum_lanes, w_dt, vectors, states, states)


MESH = pl.DeviceIdType.MESH


def any_specs(count):
    return [pl.BlockSpec(memory_space=pl.ANY)] * count


def place():
    return lax.axis_index("dp"), lax.axis_index("seq")


def mate(d):
    return d + 1 - 2 * lax.rem(d, 2)


def remote(src, dst, send, recv, device):
    return pltpu.make_async_remote_copy(
        src_ref=src, dst_ref=dst, send_sem=send, recv_sem=recv, device_id=device, device_id_type=MESH
    )


def greet(device, here=True):
    barrier = pltpu.get_barrier_semaphore()

    def tell():
        pl.semaphore_signal(barrier, inc=1, device_id=device, device_id_type=MESH)

    if here is True:
        tell()
    else:
        pl.when(here)(tell)


def gather_kernel(
    dp, seq, hid_ref, w_ref, pk_ref, hid_out, w_out, pk_out,
    z_send, z_recv, w_send, w_recv, f_send, f_recv, p_send, p_recv, q_send, q_recv, t_sem, own_sem,
):
    d, s = place()
    part = hid_ref.shape[1]
    w_rows, p_rows = w_ref.shape[0], pk_ref.shape[0]
    pieces = z_send.shape[2]
    piece = part // pieces
    half = seq // 2
    pairs = dp // 2
    to_d, to_s = 2 * (d // 2) + lax.rem(s, 2), half * lax.rem(d, 2) + s // 2
    from_d, from_s = 2 * (d // 2) + s // half, 2 * lax.rem(s, half) + lax.rem(d, 2)
    moves = jnp.logical_or(to_d != d, to_s != s)

    greet((d, s - 1), s > 0)
    greet((d, s + 1), s < seq - 1)
    for k in range(1, pairs):
        greet((lax.rem(d + 2 * k, dp), s))
    greet((mate(d), s))
    greet((to_d, to_s), moves)
    greet((from_d, from_s), moves)
    count = pairs + jnp.where(s > 0, 1, 0) + jnp.where(s < seq - 1, 1, 0) + jnp.where(moves, 2, 0)
    pl.semaphore_wait(pltpu.get_barrier_semaphore(), count)

    def shard(which, q):
        return hid_out.at[:, pl.ds(which * part + q * piece, piece), :]

    def hop(way, k, q):
        which = s - k if way == 0 else s + k
        src = hid_ref.at[:, pl.ds(q * piece, piece), :] if k == 0 else shard(which, q)
        near = s + 1 if way == 0 else s - 1
        return remote(src, shard(which, q), z_send.at[way, k, q], z_recv.at[way, k, q], (d, near))

    def can_send(way, k):
        if way == 0:
            return jnp.logical_and(s - k >= 0, s < seq - 1)
        return jnp.logical_and(s + k < seq, s > 0)

    def w_slot(which):
        return w_out.at[pl.ds(which * w_rows, w_rows)]

    def p_slot(which):
        return pk_out.at[pl.ds(which * p_rows, p_rows)]

    def spread(slot, own, send, recv, k):
        return remote(own, slot(d), send.at[k], recv.at[k], (lax.rem(d + 2 * k, dp), s))

    def source(k):
        return lax.rem(d - 2 * k + dp, dp)

    def across(slot, send, recv, k, own=None):
        return remote(own if k == 0 else slot(source(k)), slot(source(k)), send.at[k], recv.at[k], (mate(d), s))

    for q in range(pieces):
        for way in range(2):
            pl.when(can_send(way, 0))(hop(way, 0, q).start)
    transfer = remote(pk_ref, p_slot(to_d), t_sem.at[0], t_sem.at[1], (to_d, to_s))
    stay = pltpu.make_async_copy(pk_ref, p_slot(d), own_sem.at[2])
    pl.when(moves)(transfer.start)
    pl.when(jnp.logical_not(moves))(stay.start)
    for k in range(1, pairs):
        spread(w_slot, w_ref, w_send, w_recv, k).start()
    across(w_slot, f_send, f_recv, 0, w_ref).start()
    own_w = pltpu.make_async_copy(w_ref, w_slot(d), own_sem.at[0])
    own_h = pltpu.make_async_copy(hid_ref, hid_out.at[:, pl.ds(s * part, part), :], own_sem.at[1])
    own_w.start()
    own_h.start()

    pl.when(moves)(remote(pk_ref, p_slot(d), t_sem.at[0], t_sem.at[1], (to_d, to_s)).wait_recv)
    pl.when(jnp.logical_not(moves))(stay.wait)
    for k in range(1, pairs):
        spread(p_slot, p_slot(d), p_send, p_recv, k).start()
    across(p_slot, q_send, q_recv, 0, p_slot(d)).start()

    def arrive(k):
        for q in range(pieces):
            for way in range(2):
                got = s - k >= 0 if way == 0 else s + k < seq

                @pl.when(got)
                def _():
                    which = s - k if way == 0 else s + k
                    remote(
                        shard(which, q), shard(which, q), z_send.at[way, k - 1, q], z_recv.at[way, k - 1, q], (d, s)
                    ).wait_recv()

                if k < seq - 1:
                    pl.when(can_send(way, k))(hop(way, k, q).start)

    for k in range(1, seq - 1):
        arrive(k)
    for slot, own, send, recv, over_send, over_recv in (
        (w_slot, w_ref, w_send, w_recv, f_send, f_recv),
        (p_slot, None, p_send, p_recv, q_send, q_recv),
    ):
        for k in range(1, pairs):
            remote(slot(source(k)), slot(source(k)), send.at[k], recv.at[k], (d, s)).wait_recv()
            across(slot, over_send, over_recv, k).start()
    arrive(seq - 1)

    def other(k):
        return lax.rem(mate(d) - 2 * k + dp, dp)

    for slot, own, over_send, over_recv in ((w_slot, w_ref, f_send, f_recv), (p_slot, p_slot(d), q_send, q_recv)):
        for k in range(pairs):
            remote(slot(other(k)), slot(other(k)), over_send.at[k], over_recv.at[k], (d, s)).wait_recv()
            across(slot, over_send, over_recv, k, own).wait_send()
    for k in range(1, pairs):
        spread(w_slot, w_ref, w_send, w_recv, k).wait_send()
        spread(p_slot, p_slot(d), p_send, p_recv, k).wait_send()
    for k in range(seq - 1):
        for q in range(pieces):
            for way in range(2):
                pl.when(can_send(way, k))(hop(way, k, q).wait_send)
    pl.when(moves)(transfer.wait_send)
    own_w.wait()
    own_h.wait()


def gather(hidden, weight, packed, collective_id=0):
    dp, seq = lax.axis_size("dp"), lax.axis_size("seq")
    seqs, part, width = hidden.shape
    pieces = 4 if part % 64 == 0 else 1
    dma = pltpu.SemaphoreType.DMA
    return pl.pallas_call(
        functools.partial(gather_kernel, dp, seq),
        in_specs=any_specs(3),
        out_specs=any_specs(3),
        out_shape=[
            jax.ShapeDtypeStruct((seqs, part * seq, width), hidden.dtype),
            jax.ShapeDtypeStruct((weight.shape[0] * dp, weight.shape[1]), weight.dtype),
            jax.ShapeDtypeStruct((packed.shape[0] * dp, packed.shape[1]), packed.dtype),
        ],
        scratch_shapes=[
            dma((2, seq, pieces)), dma((2, seq, pieces)),
            dma((dp // 2,)), dma((dp // 2,)), dma((dp // 2,)), dma((dp // 2,)),
            dma((dp // 2,)), dma((dp // 2,)), dma((dp // 2,)), dma((dp // 2,)),
            dma((2,)), dma((3,)),
        ],
        compiler_params=pltpu.CompilerParams(collective_id=collective_id, has_side_effects=True),
        name="gather_in",
    )(hidden, weight, packed)


def added(ref, *others):
    total = ref[...].astype(F32)
    for other in others:
        total = total + other[...].astype(F32)
    return total


def scatter_kernel(
    dp, seq, dn_ref, gw_ref, pk_ref, gain_ref, hid_ref, cot_ref, scale_ref,
    out_ref, gw_out, pk_out, gain_out,
    own, come, gw_own, gw_x, gw_r, pk_own, pk_x, pk_r, pk_fin, g_x, g_r, g_z, g_a, g_b,
    load, z_send, z_recv, w_load, wx_send, wx_recv, w_send, w_recv,
    p_load, px_send, px_recv, p_send, p_recv, t_sem, gx_sem, g_send, g_recv, gz_send, gz_recv,
):
    d, s = place()
    seqs, part, width = out_ref.shape
    pieces = z_send.shape[1]
    piece = part // pieces
    half = seq // 2
    pairs = dp // 2
    mine, odd = d // 2, lax.rem(d, 2)
    to_d, to_s = 2 * (d // 2) + s // half, 2 * lax.rem(s, half) + lax.rem(d, 2)
    from_d, from_s = 2 * (d // 2) + lax.rem(s, 2), half * lax.rem(d, 2) + s // 2
    moves = jnp.logical_or(to_d != d, to_s != s)

    for k in range(1, seq):
        greet((d, lax.rem(s + k, seq)))
    for k in range(1, pairs):
        greet((lax.rem(d + 2 * k, dp), s))
    greet((mate(d), s))
    greet((to_d, to_s), moves)
    greet((from_d, from_s), moves)
    pl.semaphore_wait(pltpu.get_barrier_semaphore(), seq - 1 + pairs + jnp.where(moves, 2, 0))

    def swap(src_ref, dst, send, recv, j):
        rows = dst.shape[1]
        other = 2 * j + 1 - odd
        return remote(src_ref.at[pl.ds(other * rows, rows)], dst.at[j], send.at[j], recv.at[j], (mate(d), s))

    def fetch(src_ref, dst, sem, j):
        rows = dst.shape[1]
        return pltpu.make_async_copy(src_ref.at[pl.ds((2 * j + odd) * rows, rows)], dst.at[j], sem.at[j])

    def chunk(r):
        return pltpu.make_async_copy(dn_ref.at[:, pl.ds(r * part, part), :], own.at[r], load.at[r])

    gain_swap = remote(gain_ref, g_x, gx_sem.at[0], gx_sem.at[1], (mate(d), s))
    gain_swap.start()
    for j in range(pairs):
        swap(pk_ref, pk_x, px_send, px_recv, j).start()
    ends = []
    for i in range(seq):
        ends.append(seq - 1 - i // 2 if i % 2 == 0 else i // 2)
    for r in ends:
        chunk(r).start()
    for j in range(pairs):
        fetch(pk_ref, pk_own, p_load, j).start()
    for j in range(pairs):
        swap(gw_ref, gw_x, wx_send, wx_recv, j).start()
        fetch(gw_ref, gw_own, w_load, j).start()
    for r in ends:
        chunk(r).wait()

    def give(way, r, q):
        rows = pl.ds(q * piece, piece)
        slot = r if way == 0 else jnp.where(s - 1 == r, seq, r)
        near = s + 1 if way == 0 else s - 1
        return remote(own.at[r, :, rows, :], come.at[slot, :, rows, :], z_send.at[r, q], z_recv.at[slot, q], (d, near))

    def landed(slot, q):
        rows = pl.ds(q * piece, piece)
        here = come.at[slot, :, rows, :]
        remote(here, here, z_send.at[0, q], z_recv.at[slot, q], (d, s)).wait_recv()

    def pass_on(way, r):
        first = s == 0 if way == 0 else s == seq - 1
        sends = s < r if way == 0 else s > r
        for q in range(pieces):
            @pl.when(jnp.logical_and(sends, jnp.logical_not(first)))
            def _():
                rows = pl.ds(q * piece, piece)
                landed(r, q)
                own[r, :, rows, :] = added(own.at[r, :, rows, :], come.at[r, :, rows, :]).astype(BF)

            pl.when(sends)(give(way, r, q).start)

    def round_of(i):
        pass_on(0, seq - 1 - i)
        pass_on(1, i)

    def onward(part_own, part_r, send, recv, k):
        j = lax.rem(mine + k, pairs)
        return remote(part_own.at[j], part_r.at[k - 1], send.at[k], recv.at[k], (lax.rem(d + 2 * k, dp), s))

    def join(src_ref, part_own, part_x, part_r, sem, xs, xr, send, recv):
        for k in range(1, pairs + 1):
            j = lax.rem(mine + k, pairs)
            fetch(src_ref, part_own, sem, j).wait()
            swap(src_ref, part_x, xs, xr, j).wait_recv()
            if k < pairs:
                part_own[j] = added(part_own.at[j], part_x.at[j]).astype(BF)
                onward(part_own, part_r, send, recv, k).start()

    def finish(part_own, part_x, part_r, send, recv):
        for k in range(1, pairs):
            onward(part_own, part_r, send, recv, k).wait_recv()
        return added(part_own.at[mine], part_x.at[mine], *[part_r.at[k] for k in range(pairs - 1)])

    round_of(0) if seq == 2 else None
    gain_swap.wait_recv()
    g_a[...] = gain_ref[...] + g_x[...]

    def gain_near(k):
        return remote(g_a, g_r.at[k - 1], g_send.at[k], g_recv.at[k], (lax.rem(d + 2 * k, dp), s))

    def gain_far(k):
        return remote(g_b, g_z.at[k - 1], gz_send.at[k], gz_recv.at[k], (d, lax.rem(s + k, seq)))

    for k in range(1, pairs):
        gain_near(k).start()
    join(pk_ref, pk_own, pk_x, pk_r, p_load, px_send, px_recv, p_send, p_recv)
    if seq > 2:
        round_of(0)
    join(gw_ref, gw_own, gw_x, gw_r, w_load, wx_send, wx_recv, w_send, w_recv)
    for k in range(1, pairs):
        gain_near(k).wait_recv()
    g_b[...] = added(g_a, *[g_r.at[k] for k in range(pairs - 1)])
    for k in range(1, seq):
        gain_far(k).start()
    for i in range(1, seq - 2):
        round_of(i)
    pk_fin[...] = finish(pk_own, pk_x, pk_r, p_send, p_recv).astype(BF)
    back = remote(pk_fin, pk_out, t_sem.at[0], t_sem.at[1], (to_d, to_s))
    stay = pltpu.make_async_copy(pk_fin, pk_out, t_sem.at[2])
    pl.when(moves)(back.start)
    pl.when(jnp.logical_not(moves))(stay.start)
    if seq > 2:
        round_of(seq - 2)
    gw_out[...] = finish(gw_own, gw_x, gw_r, w_send, w_recv)
    for k in range(1, seq):
        gain_far(k).wait_recv()
    gain_out[...] = added(g_b, *[g_z.at[k] for k in range(seq - 1)])

    for q in range(pieces):
        pl.when(s > 0)(functools.partial(landed, s, q))
        pl.when(s < seq - 1)(functools.partial(landed, seq, q))
        rows = pl.ds(q * piece, piece)
        from_left = jnp.where(s > 0, come[s, :, rows, :].astype(F32), 0.0)
        from_right = jnp.where(s < seq - 1, come[seq, :, rows, :].astype(F32), 0.0)
        total = own[s, :, rows, :].astype(F32) + from_left + from_right
        x = hid_ref[:, rows, :].astype(F32)
        inv = lax.rsqrt(jnp.mean(x * x, axis=2, keepdims=True) + norm_eps)
        scaled = total * scale_ref[...].astype(F32)[None]
        out_ref[:, rows, :] = (
            cot_ref[:, rows, :].astype(F32)
            + inv * scaled
            - x * (inv * inv * inv) * jnp.mean(x * scaled, axis=2, keepdims=True)
        ).astype(BF)

    for q in range(pieces):
        for r in range(1, seq):
            pl.when(s < r)(give(0, r, q).wait_send)
        for r in range(seq - 1):
            pl.when(s > r)(give(1, r, q).wait_send)
    gain_swap.wait_send()
    for j in range(pairs):
        swap(pk_ref, pk_x, px_send, px_recv, j).wait_send()
        swap(gw_ref, gw_x, wx_send, wx_recv, j).wait_send()
    for k in range(1, pairs):
        onward(pk_own, pk_r, p_send, p_recv, k).wait_send()
        onward(gw_own, gw_r, w_send, w_recv, k).wait_send()
        gain_near(k).wait_send()
    for k in range(1, seq):
        gain_far(k).wait_send()
    pl.when(moves)(back.wait_send)
    pl.when(moves)(remote(pk_fin, pk_out, t_sem.at[0], t_sem.at[1], (to_d, to_s)).wait_recv)
    pl.when(jnp.logical_not(moves))(stay.wait)


def scatter(d_normed, grad_in_w, packed_grads, gain, hidden_in, cotangent, norm_gain, collective_id=1):
    dp, seq = lax.axis_size("dp"), lax.axis_size("seq")
    seqs, part, width = hidden_in.shape
    w_rows, p_rows = grad_in_w.shape[0] // dp, packed_grads.shape[0] // dp
    cols = packed_grads.shape[1]
    pieces = 4 if part % 64 == 0 else 1
    pairs = dp // 2
    dma, vmem = pltpu.SemaphoreType.DMA, pltpu.VMEM
    here = pl.BlockSpec(memory_space=pltpu.VMEM)
    return pl.pallas_call(
        functools.partial(scatter_kernel, dp, seq),
        in_specs=any_specs(3) + [here] * 4,
        out_specs=[here] * 4,
        out_shape=[
            jax.ShapeDtypeStruct((seqs, part, width), BF),
            jax.ShapeDtypeStruct((w_rows, width), F32),
            jax.ShapeDtypeStruct((p_rows, cols), BF),
            jax.ShapeDtypeStruct(gain.shape, F32),
        ],
        scratch_shapes=[
            vmem((seq, seqs, part, width), BF), vmem((seq + 1, seqs, part, width), BF),
            vmem((pairs, w_rows, width), BF), vmem((pairs, w_rows, width), BF), vmem((pairs - 1, w_rows, width), BF),
            vmem((pairs, p_rows, cols), BF), vmem((pairs, p_rows, cols), BF), vmem((pairs - 1, p_rows, cols), BF),
            vmem((p_rows, cols), BF),
            vmem(gain.shape, F32), vmem((pairs - 1,) + gain.shape, F32), vmem((seq - 1,) + gain.shape, F32),
            vmem(gain.shape, F32), vmem(gain.shape, F32),
            dma((seq,)), dma((seq, pieces)), dma((seq + 1, pieces)),
            dma((pairs,)), dma((pairs,)), dma((pairs,)), dma((pairs,)), dma((pairs,)),
            dma((pairs,)), dma((pairs,)), dma((pairs,)), dma((pairs,)), dma((pairs,)),
            dma((3,)), dma((2,)), dma((pairs,)), dma((pairs,)), dma((seq,)), dma((seq,)),
        ],
        compiler_params=pltpu.CompilerParams(
            collective_id=collective_id, has_side_effects=True, vmem_limit_bytes=60 << 20
        ),
        name="scatter_out",
    )(d_normed, grad_in_w, packed_grads, gain, hidden_in, cotangent, norm_gain)


def reduce_kernel(
    seq, wide_ref, thin_ref, wide_out, thin_out, wide_x, thin_x, wide_s, thin_s,
    xw_send, xw_recv, xt_send, xt_recv, sw_send, sw_recv, st_send, st_recv,
):
    d, s = place()
    rows = wide_ref.shape[0] // seq
    for k in range(1, seq):
        greet((d, lax.rem(s + k, seq)))
    pl.semaphore_wait(pltpu.get_barrier_semaphore(), seq - 1)

    def piece(ref, which):
        return ref.at[pl.ds(pl.multiple_of(which * rows, rows), rows)]

    def ask(k):
        to = lax.rem(s + k, seq)
        return (
            remote(piece(wide_ref, to), wide_x.at[k - 1], xw_send.at[k - 1], xw_recv.at[k - 1], (d, to)),
            remote(thin_ref.at[to], thin_x.at[k - 1], xt_send.at[k - 1], xt_recv.at[k - 1], (d, to)),
        )

    def tell(k):
        to = lax.rem(s + k, seq)
        return (
            remote(wide_s, piece(wide_out, s), sw_send.at[k - 1], sw_recv.at[k - 1], (d, to)),
            remote(thin_s, thin_out.at[s], st_send.at[k - 1], st_recv.at[k - 1], (d, to)),
        )

    def told(k):
        source = lax.rem(s - k + seq, seq)
        return (
            remote(wide_s, piece(wide_out, source), sw_send.at[k - 1], sw_recv.at[k - 1], (d, s)),
            remote(thin_s, thin_out.at[source], st_send.at[k - 1], st_recv.at[k - 1], (d, s)),
        )

    order = sorted(range(1, seq), key=lambda k: -min(k, seq - k))
    for k in order:
        for copy in ask(k):
            copy.start()
    for k in order:
        for copy in ask(k):
            copy.wait_recv()
    start = pl.ds(pl.multiple_of(s * rows, rows), rows)
    total = wide_ref[start, :].astype(F32)
    thin = thin_ref[s]
    for k in range(seq - 1):
        total = total + wide_x[k].astype(F32)
        thin = thin + thin_x[k]
    wide_s[...] = total.astype(BF)
    thin_s[...] = thin
    for k in order:
        for copy in tell(k):
            copy.start()
    wide_out[start, :] = total.astype(BF)
    thin_out[s] = thin
    for k in order:
        for copy in told(k):
            copy.wait_recv()
    for k in order:
        for copy in ask(k) + tell(k):
            copy.wait_send()


def reduce_over_seq(wide_part, thin_part, collective_id):
    seq = lax.axis_size("seq")
    tokens, cols = wide_part.shape
    thin_part = jnp.swapaxes(thin_part.reshape(-1, seq, tokens // seq), 0, 1)
    dma, vmem = pltpu.SemaphoreType.DMA, pltpu.VMEM
    here = pl.BlockSpec(memory_space=pltpu.VMEM)
    rows, few = tokens // seq, thin_part.shape[1:]
    wide_sum, thin_sum = pl.pallas_call(
        functools.partial(reduce_kernel, seq),
        in_specs=[here] * 2,
        out_specs=[here] * 2,
        out_shape=[
            jax.ShapeDtypeStruct((tokens, cols), BF),
            jax.ShapeDtypeStruct(thin_part.shape, F32),
        ],
        scratch_shapes=[
            vmem((seq - 1, rows, cols), BF), vmem((seq - 1,) + few, F32), vmem((rows, cols), BF), vmem(few, F32),
        ] + [dma((seq - 1,))] * 8,
        compiler_params=pltpu.CompilerParams(collective_id=collective_id, has_side_effects=True),
        name="reduce_seq",
    )(wide_part.astype(BF), thin_part)
    return wide_sum, jnp.swapaxes(thin_sum, 0, 1).reshape(-1, tokens)


def local(
    hidden_in,
    doc_lengths,
    norm_gain,
    in_weight,
    conv_weight,
    conv_bias,
    x_weight,
    dt_weight,
    dt_bias,
    skip_gain,
    out_weight,
    out_cotangent,
):
    seqs, part_len, width = hidden_in.shape
    dp, seq = lax.axis_size("dp"), lax.axis_size("seq")
    length = part_len * seq
    tokens = seqs * length
    rows = out_weight.shape[0]
    channels = rows * dp
    lag_max = KCONV - 1

    small = jnp.concatenate(
        [x_weight, dt_weight, conv_weight.T, conv_bias[:, None], dt_bias[:, None], skip_gain[:, None]], axis=1
    )
    used = small.shape[1]
    padded_cols = -(-used // LANES) * LANES
    packed = jnp.concatenate([out_weight, jnp.pad(small, ((0, 0), (0, padded_cols - used)))], axis=1)

    hidden, w_in, packed = gather(hidden_in, in_weight, packed)
    hidden = hidden.reshape(tokens, width)
    cot, hidden = lax.optimization_barrier((out_cotangent, hidden))
    cot = lax.all_gather(cot, "seq", axis=1, tiled=True).reshape(tokens, width)

    w_out = packed[:, :width]
    tail = packed[:, width:]
    w_x = tail[:, : R + 2 * N]
    w_dt = tail[:, R + 2 * N : 2 * R + 2 * N]
    vectors = tail[:, 2 * R + 2 * N : used].astype(F32).T
    taps, conv_shift, rate_shift, skip = vectors[:KCONV], vectors[KCONV], vectors[KCONV + 1], vectors[KCONV + 2]

    begins, places = token_begins(doc_lengths, length)
    keep = (places[None, :] != begins).astype(F32).reshape(tokens, 1)
    valid = [(places[None, :] - (lag_max - w) >= begins)[:, :, None] for w in range(KCONV)]

    gain = norm_gain.astype(F32)
    x_full = hidden.astype(F32)
    inv_rms = lax.rsqrt(jnp.mean(x_full * x_full, axis=1, keepdims=True) + norm_eps)
    normed = (x_full * inv_rms * gain).astype(BF)
    pre = mm(normed, w_in, NT).astype(BF)
    x_inner = pre[:, :channels].reshape(seqs, length, channels)

    padded = jnp.pad(x_inner, ((0, 0), (lag_max, 0), (0, 0)))
    conv_sum = jnp.broadcast_to(conv_shift, (seqs, length, channels))
    for w in range(KCONV):
        window = padded[:, w : w + length, :].astype(F32)
        conv_sum = conv_sum + jnp.where(valid[w], window * taps[w], 0.0)
    conv_flat = conv_sum.reshape(tokens, channels)
    xc_low = jax.nn.silu(conv_flat).astype(BF)
    rate, thin = reduce_over_seq(mm(xc_low, w_x[:, :R], NN), mm(w_x[:, R:], xc_low, ((0,), (1,))), 2)
    key, query = thin[:N].T, thin[N:].T
    key_lanes, query_lanes = (
        jnp.broadcast_to(part.astype(BF)[:, :, None], (tokens, N, LANES)) for part in (key, query)
    )
    ksum = jnp.sum(key * key, axis=1, keepdims=True)
    keep_lanes = jnp.broadcast_to(keep, (tokens, LANES))
    ksum_lanes = jnp.broadcast_to(ksum, (tokens, LANES))
    vectors = jnp.pad(jnp.stack([rate_shift, skip]), ((0, 6), (0, 0)))
    states, y_full, gated = scan_forward(
        seqs, length, xc_low, pre, rate, key_lanes, query_lanes, keep_lanes, ksum_lanes, w_dt, vectors
    )
    branch = mm(gated, w_out, NN).astype(BF).reshape(seqs, length, width)
    branch = lax.psum_scatter(branch, "seq", scatter_dimension=1, tiled=True)
    output = (hidden_in.astype(F32) + branch.astype(F32)).astype(BF)

    d_z, rest, dq, dk, d_norm, d_row, grad_dt, sums = scan_backward(
        seqs, length, mm(cot, w_out, NT), y_full, xc_low, pre, rate, key_lanes, query_lanes, keep_lanes, ksum_lanes, w_dt, vectors, states
    )
    dq, dk = dq.reshape(tokens, N), dk.reshape(tokens, N)
    d_norm = -jnp.sum(d_norm, axis=1, keepdims=True)
    d_keys = dk + 2.0 * key * d_norm
    d_row, thin = reduce_over_seq(d_row, jnp.concatenate([d_keys.T, dq.T], axis=0), 3)
    d_proj = jnp.concatenate([d_row, thin.T.astype(BF)], axis=1)
    d_conv_out = mm(d_proj, w_x, NT) + rest
    d_conv = (d_conv_out * silu_slope(conv_flat)).reshape(seqs, length, channels)

    tap_grads = []
    d_x_inner = jnp.zeros((seqs, length, channels), F32)
    for w in range(KCONV):
        lag = lag_max - w
        window = padded[:, w : w + length, :].astype(F32)
        masked = jnp.where(valid[w], d_conv, 0.0)
        tap_grads.append(jnp.sum(masked * window, axis=(0, 1)))
        d_x_inner = d_x_inner + jnp.pad(masked, ((0, 0), (0, lag), (0, 0)))[:, lag:, :] * taps[w]
    d_pre = jnp.concatenate([d_x_inner.reshape(tokens, channels).astype(BF), d_z], axis=1)

    grad_w_out = mm(gated, cot, TN)
    vector_grads = jnp.stack(
        tap_grads
        + [
            jnp.sum(d_conv, axis=(0, 1)),
            jnp.sum(sums[:8], axis=0),
            jnp.sum(sums[8:], axis=0),
        ],
        axis=1,
    )
    small_grads = jnp.concatenate([mm(xc_low, d_proj, TN), grad_dt, vector_grads], axis=1)
    packed_grads = jnp.concatenate([grad_w_out, jnp.pad(small_grads, ((0, 0), (0, padded_cols - used)))], axis=1)
    d_normed = mm(d_pre, w_in, NN)
    gain_local = jnp.sum(d_normed * x_full * inv_rms, axis=0)
    grad_in, grad_in_weight, packed_grads, grad_norm_gain = scatter(
        d_normed.astype(BF).reshape(seqs, length, width),
        mm(d_pre, normed, TN).astype(BF),
        packed_grads.astype(BF),
        gain_local.reshape(8, width // 8),
        hidden_in,
        out_cotangent,
        norm_gain.reshape(1, width),
    )
    grad_norm_gain = grad_norm_gain.reshape(width)
    packed_grads = packed_grads.astype(F32)
    grad_out_weight = packed_grads[:, :width]
    tail = packed_grads[:, width:]

    base = 2 * R + 2 * N
    return (
        output,
        grad_in,
        grad_norm_gain,
        grad_in_weight,
        tail[:, base : base + KCONV].T,
        tail[:, base + KCONV],
        tail[:, : R + 2 * N],
        tail[:, R + 2 * N : base],
        tail[:, base + KCONV + 1],
        tail[:, base + KCONV + 2],
        grad_out_weight,
    )


def solution(mesh):
    both = ("dp", "seq")
    tokens = P("dp", "seq", None)
    matrix, vector = P(both, None), P(both)
    return jax.shard_map(
        local,
        mesh=mesh,
        in_specs=(
            tokens, P("dp", None), P(), matrix, P(None, both), vector,
            matrix, matrix, vector, vector, matrix, tokens,
        ),
        out_specs=(
            tokens, tokens, P(), matrix, P(None, both), vector,
            matrix, matrix, vector, vector, matrix,
        ),
        check_vma=False,
    )
```

```python
import functools
import math

import jax
import jax.numpy as jnp
from jax import lax
from jax.experimental import pallas as pl
from jax.experimental.pallas import tpu as pltpu
from jax.sharding import PartitionSpec as P

N = 16
R = 128
KCONV = 4
CHUNK = 16
LANES = 128
GROUP = 1024
BLOCK = 128

norm_eps = 1e-05
BF = jnp.bfloat16
F32 = jnp.float32


def silu_slope(pre_value):
    sigmoid_of = jax.nn.sigmoid(pre_value)
    return sigmoid_of * (1.0 + pre_value * (1.0 - sigmoid_of))


def token_begins(lengths, position_count):
    doc_ends = jnp.cumsum(lengths, axis=1)
    doc_starts = doc_ends - lengths
    places = jnp.arange(position_count, dtype=jnp.int32)
    inside = doc_starts[:, None, :] <= places[None, :, None]
    return (jnp.max(jnp.where(inside, doc_starts[:, None, :], 0), axis=2), places)


def mm(left, right, dims):
    return lax.dot_general(left, right, (dims, ((), ())), preferred_element_type=F32)


NN = ((1,), (0,))
NT = ((1,), (1,))
TN = ((0,), (0,))


def row(ref, i, lane):
    return jnp.broadcast_to(ref[i : i + 1, pl.ds(lane, LANES)], (8, LANES))


def wide(ref, rows, count):
    value = ref[rows, :]
    return jnp.concatenate([value] * (count // LANES), axis=1)


def merge(even, odd, stride):
    low = lax.broadcasted_iota(jnp.int32, (8, LANES), 0) % (2 * stride) < stride
    if stride == 4:
        return jnp.where(low, even, odd) + pltpu.roll(jnp.where(low, odd, even), 4, 0)
    return jnp.where(low, even + pltpu.roll(even, 8 - stride, 0), odd + pltpu.roll(odd, stride, 0))


def collect(stack, value, descending):
    level = 0
    while stack and stack[-1][0] == level:
        other = stack.pop()[1]
        value = merge(value, other, 1 << level) if descending else merge(other, value, 1 << level)
        level += 1
    stack.append((level, value))


def each_chunk(tokens, channels, body):
    group = math.gcd(channels, 512)

    def run(k, carried):
        rows = pl.ds(pl.multiple_of(k * CHUNK, CHUNK), CHUNK)
        for first in range(0, channels, group):
            body(rows, pl.ds(first, group), first)
        return carried

    lax.fori_loop(0, tokens // CHUNK, run, 0)


def load_carry(carry, tiles):
    out = []
    for lane in tiles:
        out += [carry[0:8, pl.ds(lane, LANES)], carry[8:16, pl.ds(lane, LANES)]]
    return tuple(out)


def store_carry(carry, tiles, values):
    for j, lane in enumerate(tiles):
        carry[0:8, pl.ds(lane, LANES)] = values[2 * j]
        carry[8:16, pl.ds(lane, LANES)] = values[2 * j + 1]


def halves(value):
    return [value[0:8], value[8:16]]


def token(keys, queries, keeps, i):
    return row(keeps, i, 0), halves(keys[i].astype(F32)), halves(queries[i].astype(F32))


def lane_groups(channels):
    group = math.gcd(channels, GROUP)
    return [list(range(first, first + group, LANES)) for first in range(0, channels, group)]


def forward_kernel(
    xc_ref, z_ref, rate_ref, key_ref, query_ref, keep_ref, ksum_ref, wdt_ref, vec_ref,
    s_ref, y_ref, gated_ref, step, inj, carry,
):
    @pl.when(pl.program_id(1) == 0)
    def _():
        carry[...] = jnp.zeros_like(carry)

    tokens, channels = xc_ref.shape
    step[...] = mm(rate_ref[...], wdt_ref[...], NT)

    def prepare(rows, cols, first):
        beta = jax.nn.sigmoid(step[rows, cols] + vec_ref[0:1, cols])
        eps = beta / (1.0 + beta * wide(ksum_ref, rows, cols.size))
        step[rows, cols] = eps
        inj[rows, cols] = eps * xc_ref[rows, cols].astype(F32)

    each_chunk(tokens, channels, prepare)
    for tiles in lane_groups(channels):

        def chunk(k, state):
            state = list(state)
            base = pl.multiple_of(k * CHUNK, CHUNK)
            steps, injs, keeps, keys, queries = (
                r.at[pl.ds(base, CHUNK)] for r in (step, inj, keep_ref, key_ref, query_ref)
            )
            saved = s_ref.at[pl.ds(pl.multiple_of(k * CHUNK * N, CHUNK * N), CHUNK * N)]
            stacks = [[] for _ in tiles]
            for i in range(CHUNK):
                keep, key, query = token(keys, queries, keeps, i)
                ksq = [keep * key[h] * key[h] for h in range(2)]
                for j, lane in enumerate(tiles):
                    eps, push = row(steps, i, lane), row(injs, i, lane)
                    for h in range(2):
                        state[2 * j + h] = (keep - eps * ksq[h]) * state[2 * j + h] + push * key[h]
                    both = jnp.concatenate([state[2 * j], state[2 * j + 1]], axis=0)
                    saved[i * N : (i + 1) * N, pl.ds(lane, LANES)] = both.astype(BF)
                    collect(stacks[j], state[2 * j] * query[0] + state[2 * j + 1] * query[1], False)
                    if i % 8 == 7:
                        y_ref[pl.ds(pl.multiple_of(base + i - 7, 8), 8), pl.ds(lane, LANES)] = stacks[j].pop()[1]
            return tuple(state)

        store_carry(carry, tiles, lax.fori_loop(0, tokens // CHUNK, chunk, load_carry(carry, tiles)))

    def emit(rows, cols, first):
        y_full = y_ref[rows, cols] + vec_ref[1:2, cols] * xc_ref[rows, cols].astype(F32)
        y_ref[rows, cols] = y_full
        z = z_ref[rows, cols].astype(F32)
        gated_ref[rows, cols] = (y_full * (z * jax.nn.sigmoid(z))).astype(BF)

    each_chunk(tokens, channels, emit)


def backward_kernel(
    dg_ref, y_ref, xc_ref, z_ref, rate_ref, key_ref, query_ref, keep_ref, ksum_ref, wdt_ref, vec_ref, s_ref, before_ref,
    dz_ref, rest_ref, dq_ref, dk_ref, dnorm_ref, drow_ref, gdt_ref, sums_ref,
    step, inj, dy, mix, pull, beta, drate, carry, acc_q, acc_k,
):
    turn = pl.program_id(1)
    tokens, channels = xc_ref.shape
    chunks = tokens // CHUNK

    @pl.when(jnp.logical_and(pl.program_id(0) == 0, turn == 0))
    def _():
        gdt_ref[...] = jnp.zeros_like(gdt_ref)
        sums_ref[...] = jnp.zeros_like(sums_ref)

    @pl.when(turn == 0)
    def _():
        carry[...] = jnp.zeros_like(carry)

    beta[...] = mm(rate_ref[...], wdt_ref[...], NT)

    def prepare(rows, cols, first):
        rate_beta = jax.nn.sigmoid(beta[rows, cols] + vec_ref[0:1, cols])
        eps = rate_beta / (1.0 + rate_beta * wide(ksum_ref, rows, cols.size))
        beta[rows, cols] = rate_beta
        step[rows, cols] = eps
        xc = xc_ref[rows, cols].astype(F32)
        inj[rows, cols] = eps * xc
        z = z_ref[rows, cols].astype(F32)
        sig = jax.nn.sigmoid(z)
        d_gated = dg_ref[rows, cols]
        d_y = d_gated * (z * sig)
        dy[rows, cols] = d_y
        dz_ref[rows, cols] = (d_gated * y_ref[rows, cols] * (sig * (1.0 + z * (1.0 - sig)))).astype(BF)
        weighted = d_y * xc
        sums_ref[8:16, cols] += weighted[0:8] + weighted[8:16]

    each_chunk(tokens, channels, prepare)
    for tiles in lane_groups(channels):
        start = tiles[0] == 0

        def chunk(back, carried):
            k = chunks - 1 - back
            pulled, now = list(carried[0]), list(carried[1])
            base = pl.multiple_of(k * CHUNK, CHUNK)
            steps, injs, dys, keeps, keys, queries = (
                r.at[pl.ds(base, CHUNK)] for r in (step, inj, dy, keep_ref, key_ref, query_ref)
            )
            stacks = [([], []) for _ in tiles]
            for i in reversed(range(CHUNK)):
                keep, key, query = token(keys, queries, keeps, i)
                kept = [keep * key[h] for h in range(2)]
                ksq = [kept[h] * key[h] for h in range(2)]
                if i > 0:
                    before = pl.ds(pl.multiple_of((base + i) * N - N, N), N)
                else:
                    before = pl.ds(pl.multiple_of(jnp.maximum(base * N - N, 0), N), N)
                seen, plain, scaled = [0.0, 0.0], [0.0, 0.0], [0.0, 0.0]
                for j, lane in enumerate(tiles):
                    eps, push, d_y = row(steps, i, lane), row(injs, i, lane), row(dys, i, lane)
                    prior = s_ref[before, pl.ds(lane, LANES)]
                    if i == 0:
                        prior = jnp.where(k > 0, prior, before_ref[:, pl.ds(lane, LANES)])
                    prior = halves(prior.astype(F32))
                    by_key, by_square = [], []
                    for h in range(2):
                        at = 2 * j + h
                        grad = pulled[at] + d_y * query[h]
                        pulled[at] = (keep - eps * ksq[h]) * grad
                        keyed = eps * (grad * key[h])
                        prod = keyed * prior[h]
                        seen[h] += now[at] * d_y
                        plain[h] += grad * push
                        scaled[h] += prod
                        by_key.append(keyed)
                        by_square.append(prod * kept[h])
                        now[at] = prior[h]
                    collect(stacks[j][0], by_key[0] + by_key[1], True)
                    collect(stacks[j][1], by_square[0] + by_square[1], True)
                    if i % 8 == 0:
                        rows = pl.ds(pl.multiple_of(base + i, 8), 8)
                        mix[rows, pl.ds(lane, LANES)] = stacks[j][0].pop()[1]
                        pull[rows, pl.ds(lane, LANES)] = stacks[j][1].pop()[1]
                for ref, parts in ((acc_q, seen), (acc_k, [plain[h] - 2.0 * keep * scaled[h] for h in range(2)])):
                    for h in range(2):
                        rows = pl.ds(pl.multiple_of((base + i) * N + 8 * h, 8), 8)
                        if start:
                            ref[rows, :] = parts[h]
                        else:
                            ref[rows, :] += parts[h]
            return (tuple(pulled), tuple(now))

        now = []
        for lane in tiles:
            now += halves(s_ref[tokens * N - N : tokens * N, pl.ds(lane, LANES)].astype(F32))
        pulled, now = lax.fori_loop(0, chunks, chunk, (load_carry(carry, tiles), tuple(now)))
        store_carry(carry, tiles, pulled)

    ones = jnp.ones((LANES, LANES), BF)
    diagonal = lax.broadcasted_iota(jnp.int32, (LANES, LANES), 0) == (
        lax.broadcasted_iota(jnp.int32, (LANES, LANES), 1)
    )
    for out, ref in ((dq_ref, acc_q), (dk_ref, acc_k)):
        for first in range(0, tokens * N, LANES):
            sums = mm(ref[first : first + LANES, :].astype(BF), ones, NN)
            at = first // LANES
            out[at : at + 1, :] = jnp.sum(jnp.where(diagonal, sums, 0.0), axis=0, keepdims=True)

    def settle(rows, cols, first):
        rate_beta, eps = beta[rows, cols], step[rows, cols]
        through = mix[rows, cols]
        change = through * xc_ref[rows, cols].astype(F32) - pull[rows, cols]
        inverse = 1.0 / (1.0 + rate_beta * wide(ksum_ref, rows, cols.size))
        low = (change * inverse * (1.0 - rate_beta)).astype(BF)
        drate[rows, cols] = low
        lowered = low.astype(F32)
        sums_ref[0:8, cols] += lowered[0:8] + lowered[8:16]
        rest_ref[rows, cols] = through + vec_ref[1:2, cols] * dy[rows, cols]
        square = change * eps
        total = square[:, 0:LANES]
        for lane in range(LANES, cols.size, LANES):
            total = total + square[:, lane : lane + LANES]
        if first == 0:
            dnorm_ref[rows, :] = total
        else:
            dnorm_ref[rows, :] += total

    each_chunk(tokens, channels, settle)
    drow_ref[...] = mm(drate[...], wdt_ref[...], NN)
    gdt_ref[...] += mm(drate[...], rate_ref[...], TN)


def scan_blocks(length):
    block = math.gcd(length, BLOCK)
    return block, length // block


def row_spec(rows, cols, when, col=0):
    return pl.BlockSpec((rows, cols), lambda b, t: (when(b, t), col))


def spread_spec(block, when):
    return pl.BlockSpec((block, N, LANES), lambda b, t: (when(b, t), 0, 0))


def whole(array):
    return pl.BlockSpec(array.shape, lambda b, t: (0, 0), pipeline_mode=pl.Buffered(1))


def scan_forward(seqs, length, xc, pre, rate, key_lanes, query_lanes, keep_lanes, ksum_lanes, w_dt, vectors):
    tokens, channels = xc.shape
    block, blocks = scan_blocks(length)

    def at(b, t):
        return b * blocks + t

    rows = row_spec(block, channels, at)
    lanes = row_spec(block, LANES, at)
    vmem = pltpu.VMEM
    return pl.pallas_call(
        forward_kernel,
        grid=(seqs, blocks),
        in_specs=[
            rows, row_spec(block, channels, at, 1), row_spec(block, R, at),
            spread_spec(block, at), spread_spec(block, at), lanes, lanes, whole(w_dt), whole(vectors),
        ],
        out_specs=[row_spec(block * N, channels, at), rows, rows],
        out_shape=[
            jax.ShapeDtypeStruct((tokens * N, channels), BF),
            jax.ShapeDtypeStruct((tokens, channels), F32),
            jax.ShapeDtypeStruct((tokens, channels), BF),
        ],
        scratch_shapes=[vmem((block, channels), F32), vmem((block, channels), F32), vmem((N, channels), F32)],
        cost_estimate=pl.CostEstimate(
            flops=tokens * channels * N * 60, bytes_accessed=tokens * channels * 44, transcendentals=0
        ),
        compiler_params=pltpu.CompilerParams(vmem_limit_bytes=40 << 20),
        name="scan_forward",
    )(xc, pre, rate, key_lanes, query_lanes, keep_lanes, ksum_lanes, w_dt, vectors)


def scan_backward(seqs, length, d_gated, y, xc, pre, rate, key_lanes, query_lanes, keep_lanes, ksum_lanes, w_dt, vectors, states):
    tokens, channels = xc.shape
    block, blocks = scan_blocks(length)

    def at(b, t):
        return b * blocks + blocks - 1 - t

    def prior(b, t):
        return (jnp.maximum(at(b, t) * block - 1, 0), 0)

    rows = row_spec(block, channels, at)
    lanes = row_spec(block, LANES, at)
    flat = row_spec(block * N // LANES, LANES, at)
    vmem = pltpu.VMEM
    wide_f32 = vmem((block, channels), F32)
    return pl.pallas_call(
        backward_kernel,
        grid=(seqs, blocks),
        in_specs=[
            rows, rows, rows, row_spec(block, channels, at, 1), row_spec(block, R, at),
            spread_spec(block, at), spread_spec(block, at), lanes, lanes, whole(w_dt), whole(vectors),
            row_spec(block * N, channels, at), pl.BlockSpec((N, channels), prior),
        ],
        out_specs=[
            rows, rows, flat, flat, lanes, row_spec(block, R, at),
            pl.BlockSpec((channels, R), lambda b, t: (0, 0)), pl.BlockSpec((16, channels), lambda b, t: (0, 0)),
        ],
        out_shape=[
            jax.ShapeDtypeStruct((tokens, channels), BF),
            jax.ShapeDtypeStruct((tokens, channels), F32),
            jax.ShapeDtypeStruct((tokens * N // LANES, LANES), F32),
            jax.ShapeDtypeStruct((tokens * N // LANES, LANES), F32),
            jax.ShapeDtypeStruct((tokens, LANES), F32),
            jax.ShapeDtypeStruct((tokens, R), F32),
            jax.ShapeDtypeStruct((channels, R), F32),
            jax.ShapeDtypeStruct((16, channels), F32),
        ],
        scratch_shapes=[
            wide_f32, wide_f32, wide_f32, wide_f32, wide_f32, wide_f32, vmem((block, channels), BF),
            vmem((N, channels), F32), vmem((block * N, LANES), F32), vmem((block * N, LANES), F32),
        ],
        cost_estimate=pl.CostEstimate(
            flops=tokens * channels * N * 100, bytes_accessed=tokens * channels * 56, transcendentals=0
        ),
        compiler_params=pltpu.CompilerParams(vmem_limit_bytes=48 << 20),
        name="scan_backward",
    )(d_gated, y, xc, pre, rate, key_lanes, query_lanes, keep_lanes, ksum_lanes, w_dt, vectors, states, states)


MESH = pl.DeviceIdType.MESH


def any_specs(count):
    return [pl.BlockSpec(memory_space=pl.ANY)] * count


def place():
    return lax.axis_index("dp"), lax.axis_index("seq")


def mate(d):
    return d + 1 - 2 * lax.rem(d, 2)


def forward_home(d, s, seq):
    return 2 * (d // 2) + lax.rem(s, 2), (seq // 2) * lax.rem(d, 2) + s // 2


def backward_home(d, s, seq):
    return 2 * (d // 2) + s // (seq // 2), 2 * lax.rem(s, seq // 2) + lax.rem(d, 2)


def remote(src, dst, send, recv, device):
    return pltpu.make_async_remote_copy(
        src_ref=src, dst_ref=dst, send_sem=send, recv_sem=recv, device_id=device, device_id_type=MESH
    )


def greet(device, here=True):
    barrier = pltpu.get_barrier_semaphore()

    def tell():
        pl.semaphore_signal(barrier, inc=1, device_id=device, device_id_type=MESH)

    if here is True:
        tell()
    else:
        pl.when(here)(tell)


PARTS = 4


def gather_kernel(dp, seq, fused, *refs):
    refs = list(refs)

    def take(count):
        out = refs[:count]
        del refs[:count]
        return out

    hid_ref, w_ref = take(2)
    parts = take(PARTS)
    gain_ref = take(1)[0] if fused else None
    hid_out, w_out = take(2)
    slots = take(PARTS)
    normed_out, pre_out = take(2) if fused else (None, None)
    z_send, z_recv, w_send, w_recv, f_send, f_recv, p_send, p_recv, q_send, q_recv, t_send, t_recv, own_sem = take(13)
    d, s = place()
    part = hid_ref.shape[1]
    pieces = z_send.shape[2]
    piece = part // pieces
    pairs = dp // 2
    to_d, to_s = forward_home(d, s, seq)
    from_d, from_s = backward_home(d, s, seq)
    moves = jnp.logical_or(to_d != d, to_s != s)

    greet((d, s - 1), s > 0)
    greet((d, s + 1), s < seq - 1)
    for k in range(1, pairs):
        greet((lax.rem(d + 2 * k, dp), s))
    greet((mate(d), s))
    greet((to_d, to_s), moves)
    greet((from_d, from_s), moves)
    count = pairs + jnp.where(s > 0, 1, 0) + jnp.where(s < seq - 1, 1, 0) + jnp.where(moves, 2, 0)
    pl.semaphore_wait(pltpu.get_barrier_semaphore(), count)

    def shard(which, q):
        return hid_out.at[:, pl.ds(which * part + q * piece, piece), :]

    def hop(way, k, q):
        which = s - k if way == 0 else s + k
        src = hid_ref.at[:, pl.ds(q * piece, piece), :] if k == 0 else shard(which, q)
        near = s + 1 if way == 0 else s - 1
        return remote(src, shard(which, q), z_send.at[way, k, q], z_recv.at[way, k, q], (d, near))

    def can_send(way, k):
        if way == 0:
            return jnp.logical_and(s - k >= 0, s < seq - 1)
        return jnp.logical_and(s + k < seq, s > 0)

    def landed(way, k, q):
        which = jnp.where(way == 0, s - k, s + k)
        here = shard(which, q)
        remote(here, here, z_send.at[way, k - 1, q], z_recv.at[way, k - 1, q], (d, s)).wait_recv()

    def spread(out, own, send, recv, k):
        return remote(own, out.at[d], send.at[k], recv.at[k], (lax.rem(d + 2 * k, dp), s))

    def source(k):
        return lax.rem(d - 2 * k + dp, dp)

    def across(out, send, recv, k, own=None):
        return remote(own if k == 0 else out.at[source(k)], out.at[source(k)], send.at[k], recv.at[k], (mate(d), s))

    for q in range(pieces):
        for way in range(2):
            pl.when(can_send(way, 0))(hop(way, 0, q).start)
    transfers = [remote(parts[m], slots[m].at[to_d], t_send.at[m], t_recv.at[m], (to_d, to_s)) for m in range(PARTS)]
    stays = [pltpu.make_async_copy(parts[m], slots[m].at[d], own_sem.at[2 + m]) for m in range(PARTS)]
    for m in range(PARTS):
        pl.when(moves)(transfers[m].start)
        pl.when(jnp.logical_not(moves))(stays[m].start)
    for k in range(1, pairs):
        spread(w_out, w_ref, w_send, w_recv, k).start()
    across(w_out, f_send, f_recv, 0, w_ref).start()
    own_w = pltpu.make_async_copy(w_ref, w_out.at[d], own_sem.at[0])
    own_h = pltpu.make_async_copy(hid_ref, hid_out.at[:, pl.ds(s * part, part), :], own_sem.at[1])
    own_w.start()
    own_h.start()

    for m in range(PARTS):
        slot = slots[m].at[d]
        pl.when(moves)(remote(parts[m], slot, t_send.at[m], t_recv.at[m], (to_d, to_s)).wait_recv)
        pl.when(jnp.logical_not(moves))(stays[m].wait)
        for k in range(1, pairs):
            spread(slots[m], slot, p_send.at[m], p_recv.at[m], k).start()
        across(slots[m], q_send.at[m], q_recv.at[m], 0, slot).start()

    for k in range(1, seq - 1):
        for q in range(pieces):
            for way in range(2):
                pl.when(s - k >= 0 if way == 0 else s + k < seq)(functools.partial(landed, way, k, q))
                pl.when(can_send(way, k))(hop(way, k, q).start)
    own_w.wait()
    own_h.wait()
    flows = [(w_out, w_ref, w_send, w_recv, f_send, f_recv)]
    flows += [
        (slots[m], slots[m].at[d], p_send.at[m], p_recv.at[m], q_send.at[m], q_recv.at[m]) for m in range(PARTS)
    ]
    for out, own, send, recv, over_send, over_recv in flows:
        for k in range(1, pairs):
            here = out.at[source(k)]
            remote(here, here, send.at[k], recv.at[k], (d, s)).wait_recv()
            across(out, over_send, over_recv, k).start()
    for out, own, send, recv, over_send, over_recv in flows:
        for k in range(pairs):
            here = out.at[lax.rem(mate(d) - 2 * k + dp, dp)]
            remote(here, here, over_send.at[k], over_recv.at[k], (d, s)).wait_recv()

    last = seq - 1
    if fused:
        w_all, x_buf, w_sem, x_sem = take(4)
        width, columns = x_buf.shape[1], pre_out.shape[1]
        cut = math.gcd(columns, 512)
        fetch_w = pltpu.make_async_copy(w_out, w_all, w_sem)
        fetch_w.start()
        fetch_w.wait()

        def project(which, k, way):
            here = pl.multiple_of(which * part, part)
            for q in range(pieces):
                pl.when(k == last)(functools.partial(landed, way, last, q))
                fetch = pltpu.make_async_copy(
                    hid_out.at[0, pl.ds(which * part + q * piece, piece)], x_buf.at[pl.ds(q * piece, piece)], x_sem
                )
                fetch.start()
                fetch.wait()
                x = x_buf[pl.ds(q * piece, piece), :].astype(F32)
                inv = lax.rsqrt(jnp.mean(x * x, axis=1, keepdims=True) + norm_eps)
                rows = pl.ds(pl.multiple_of(here + q * piece, piece), piece)
                normed_out[rows, :] = (x * inv * gain_ref[...].astype(F32)).astype(BF)

            def matmul(at, carried):
                cols = pl.ds(pl.multiple_of(at * cut, cut), cut)
                w_rows = w_all.shape[1]
                block = w_all[pl.ds(at * (cut // w_rows), cut // w_rows)].reshape(cut, width)
                pre_out[pl.ds(here, part), cols] = mm(normed_out[pl.ds(here, part), :], block, NT).astype(BF)
                return carried

            lax.fori_loop(0, columns // cut, matmul, 0)

        def visit(m, carried):
            k = (m + 1) // 2
            way = lax.rem(m, 2)
            which = jnp.where(way == 0, s - k, s + k)

            @pl.when(jnp.logical_and(which >= 0, which < seq))
            def _():
                project(which, k, way)

            return carried

        lax.fori_loop(0, 2 * seq - 1, visit, 0)
    else:
        for q in range(pieces):
            for way in range(2):
                pl.when(s - last >= 0 if way == 0 else s + last < seq)(functools.partial(landed, way, last, q))

    for out, own, send, recv, over_send, over_recv in flows:
        for k in range(pairs):
            across(out, over_send, over_recv, k, own).wait_send()
        for k in range(1, pairs):
            spread(out, own, send, recv, k).wait_send()
    for k in range(seq - 1):
        for q in range(pieces):
            for way in range(2):
                pl.when(can_send(way, k))(hop(way, k, q).wait_send)
    for m in range(PARTS):
        pl.when(moves)(transfers[m].wait_send)


def fits_whole(seqs, length, width, channels):
    return seqs == 1 and length % 256 == 0 and length * (width + channels) + channels * width <= 6 << 20


def gather(hidden, weight, parts, norm_gain, collective_id=0):
    dp, seq = lax.axis_size("dp"), lax.axis_size("seq")
    seqs, part, width = hidden.shape
    columns = weight.shape[0] * dp
    fused = fits_whole(seqs, part * seq, width, columns // 2)
    pieces = 4 if part % 64 == 0 else 1
    dma, vmem, pairs = pltpu.SemaphoreType.DMA, pltpu.VMEM, dp // 2
    shape = jax.ShapeDtypeStruct
    outs = [shape((seqs, part * seq, width), BF), shape((dp,) + weight.shape, BF)]
    outs += [shape((dp,) + member.shape, BF) for member in parts]
    scratch = [dma((2, seq, pieces)), dma((2, seq, pieces))] + [dma((pairs,))] * 4
    scratch += [dma((PARTS, pairs))] * 4 + [dma((PARTS,)), dma((PARTS,)), dma((2 + PARTS,))]
    ins, in_specs = [hidden, weight, *parts], any_specs(2 + PARTS)
    out_specs = any_specs(2 + PARTS)
    if fused:
        ins.append(norm_gain.reshape(1, width))
        in_specs = in_specs + [pl.BlockSpec(memory_space=pltpu.VMEM)]
        outs += [shape((part * seq, width), BF), shape((part * seq, columns), BF)]
        scratch += [
            vmem((dp,) + weight.shape, BF), vmem((part, width), BF), dma, dma,
        ]
        out_specs = out_specs + [pl.BlockSpec(memory_space=pltpu.VMEM)] * 2
    out = pl.pallas_call(
        functools.partial(gather_kernel, dp, seq, fused),
        in_specs=in_specs,
        out_specs=out_specs,
        out_shape=outs,
        scratch_shapes=scratch,
        compiler_params=pltpu.CompilerParams(
            collective_id=collective_id, has_side_effects=True, vmem_limit_bytes=32 << 20
        ),
        name="gather_in",
    )(*ins)
    hidden = out[0].reshape(-1, width)
    w_in = out[1].reshape(columns, width)
    if fused:
        return hidden, w_in, out[2 : 2 + PARTS], out[-2], out[-1]
    x = hidden.astype(F32)
    inv = lax.rsqrt(jnp.mean(x * x, axis=1, keepdims=True) + norm_eps)
    normed = (x * inv * norm_gain.astype(F32)).astype(BF)
    return hidden, w_in, out[2:], normed, mm(normed, w_in, NT).astype(BF)


def added(ref, *others):
    total = ref[...].astype(F32)
    for other in others:
        total = total + other[...].astype(F32)
    return total


def scatter_kernel(dp, seq, count, fused, *refs):
    refs = list(refs)

    def take(count):
        out = refs[:count]
        del refs[:count]
        return out

    if fused:
        dx_ref, dz_ref, normed_ref, w_ref, full_ref = take(5)
        dn_ref = gw_ref = None
    else:
        dn_ref, gw_ref, gain_ref = take(3)
    parts = take(count)
    hid_ref, cot_ref, scale_ref = take(3)
    out_ref, gw_out = take(2)
    part_outs = take(count)
    gain_out = take(1)[0]
    own, come, gw_own, gw_x, gw_r = take(5)
    p_own, p_x, p_r, p_fin = take(count), take(count), take(count), take(count)
    g_in, g_x, g_r, g_z, g_a, g_b = take(6)
    z_load, z_send, z_recv, w_load, wx_send, wx_recv, w_send, w_recv = take(8)
    p_load, px_send, px_recv, p_send, p_recv, t_send, t_recv, gx_sem, g_send, g_recv, gz_send, gz_recv = take(12)

    d, s = place()
    seqs, part, width = out_ref.shape
    pieces = z_send.shape[1]
    piece = part // pieces
    pairs = dp // 2
    mine, odd = d // 2, lax.rem(d, 2)
    to_d, to_s = backward_home(d, s, seq)
    from_d, from_s = forward_home(d, s, seq)
    moves = jnp.logical_or(to_d != d, to_s != s)

    for k in range(1, seq):
        greet((d, lax.rem(s + k, seq)))
    for k in range(1, pairs):
        greet((lax.rem(d + 2 * k, dp), s))
    greet((mate(d), s))
    greet((to_d, to_s), moves)
    greet((from_d, from_s), moves)
    pl.semaphore_wait(pltpu.get_barrier_semaphore(), seq - 1 + pairs + jnp.where(moves, 2, 0))

    def swap(src, dst, send, recv, j):
        return remote(src, dst.at[j], send.at[j], recv.at[j], (mate(d), s))

    def part_swap(m, j):
        return swap(parts[m].at[2 * j + 1 - odd], p_x[m], px_send.at[m], px_recv.at[m], j)

    def part_fetch(m, j):
        return pltpu.make_async_copy(parts[m].at[2 * j + odd], p_own[m].at[j], p_load.at[m, j])

    for m in range(count):
        for j in range(pairs):
            part_swap(m, j).start()
            part_fetch(m, j).start()

    if fused:
        d_pre, normed, w_all, x_buf, gw_give, f_sem, x_sem = take(7)
        channels = dx_ref.shape[1]
        loads = [
            pltpu.make_async_copy(dx_ref, d_pre.at[:, pl.ds(0, channels)], f_sem.at[0]),
            pltpu.make_async_copy(dz_ref, d_pre.at[:, pl.ds(channels, channels)], f_sem.at[1]),
            pltpu.make_async_copy(w_ref, w_all, f_sem.at[2]),
            pltpu.make_async_copy(normed_ref, normed, f_sem.at[3]),
        ]
        for copy in loads:
            copy.start()
        for copy in loads[:3]:
            copy.wait()
        g_in[...] = jnp.zeros_like(g_in)
        w_rows = gw_own.shape[1]
        half_width = width // 2

        def dn_tasks(first, last):
            def run(i, carried):
                r = jnp.where(lax.rem(i, 2) == 0, seq - 1 - i // 2, i // 2)
                rows = pl.ds(pl.multiple_of(r * part, part), part)
                fetch = pltpu.make_async_copy(full_ref.at[rows], x_buf, x_sem)
                fetch.start()
                for at in range(2):
                    cols = pl.ds(at * half_width, half_width)
                    own[r, 0, :, cols] = mm(d_pre[rows, :], w_all[:, cols], NN).astype(BF)
                fetch.wait()

                def fold(at, carried):
                    some = pl.ds(pl.multiple_of(at * 64, 64), 64)
                    x = x_buf[some, :].astype(F32)
                    inv = lax.rsqrt(jnp.mean(x * x, axis=1, keepdims=True) + norm_eps)
                    weighted = own[r, 0, some, :].astype(F32) * (x * inv)
                    g_in[...] += jnp.sum(weighted.reshape(8, 8, width), axis=0)
                    return carried

                return lax.fori_loop(0, part // 64, fold, carried)

            lax.fori_loop(first, last, run, 0)

        def gw_task(dest, out, j):
            cols = pl.ds(pl.multiple_of(dest * w_rows, w_rows), w_rows)
            for at in range(2):
                some = pl.ds(at * half_width, half_width)
                out[j, :, some] = mm(d_pre[:, cols], normed[:, some], TN).astype(BF)

        def gw_swap(j):
            return swap(gw_give.at[j], gw_x, wx_send, wx_recv, j)

        def gw_away():
            def run(j, carried):
                gw_task(2 * j + 1 - odd, gw_give, j)
                gw_swap(j).start()
                return carried

            lax.fori_loop(0, pairs, run, 0)

        def gw_home():
            def run(k, carried):
                j = lax.rem(mine + 1 + k, pairs)
                gw_task(2 * j + odd, gw_own, j)
                return carried

            lax.fori_loop(0, pairs, run, 0)

        def gw_ready(j):
            pass
    else:
        def gw_swap(j):
            return swap(gw_ref.at[2 * j + 1 - odd], gw_x, wx_send, wx_recv, j)

        def gw_fetch(j):
            return pltpu.make_async_copy(gw_ref.at[2 * j + odd], gw_own.at[j], w_load.at[j])

        def chunk(r):
            return pltpu.make_async_copy(dn_ref.at[:, pl.ds(r * part, part), :], own.at[r], z_load.at[r])

        for r in range(seq):
            chunk(r).start()
        for j in range(pairs):
            gw_swap(j).start()
            gw_fetch(j).start()
        for r in range(seq):
            chunk(r).wait()
        g_in[...] = gain_ref[...]

        def gw_ready(j):
            gw_fetch(j).wait()

    def give(way, r, q):
        rows = pl.ds(q * piece, piece)
        slot = r if way == 0 else jnp.where(s - 1 == r, seq, r)
        near = s + 1 if way == 0 else s - 1
        return remote(own.at[r, :, rows, :], come.at[slot, :, rows, :], z_send.at[r, q], z_recv.at[slot, q], (d, near))

    def landed(slot, q):
        rows = pl.ds(q * piece, piece)
        here = come.at[slot, :, rows, :]
        remote(here, here, z_send.at[0, q], z_recv.at[slot, q], (d, s)).wait_recv()

    def send(way, r, q):
        before = r + 1 if way == 0 else r - 1
        if 0 <= before < seq:
            give(way, before, q).wait_send()
        give(way, r, q).start()

    def begin():
        for q in range(pieces):
            pl.when(s == 0)(give(0, seq - 1, q).start)
            pl.when(s == seq - 1)(give(1, 0, q).start)

    def pass_on(way, r, q):
        first = s == 0 if way == 0 else s == seq - 1
        sends = s < r if way == 0 else s > r
        begun = r == (seq - 1 if way == 0 else 0)

        @pl.when(jnp.logical_and(sends, jnp.logical_not(first)))
        def _():
            rows = pl.ds(q * piece, piece)
            landed(r, q)
            own[r, :, rows, :] = added(own.at[r, :, rows, :], come.at[r, :, rows, :]).astype(BF)
            send(way, r, q)

        if not begun:
            pl.when(jnp.logical_and(sends, first))(functools.partial(send, way, r, q))

    def hop(i, q):
        pass_on(0, seq - 1 - i, q)
        pass_on(1, i, q)

    def onward(part_own, part_r, send, recv, k):
        j = lax.rem(mine + k, pairs)
        return remote(part_own.at[j], part_r.at[k - 1], send.at[k], recv.at[k], (lax.rem(d + 2 * k, dp), s))

    def part_onward(m, k):
        return onward(p_own[m], p_r[m], p_send.at[m], p_recv.at[m], k)

    def gw_onward(k):
        return onward(gw_own, gw_r, w_send, w_recv, k)

    def part_join():
        for m in range(count):
            for k in range(1, pairs + 1):
                j = lax.rem(mine + k, pairs)
                part_fetch(m, j).wait()
                part_swap(m, j).wait_recv()
                if k < pairs:
                    p_own[m][j] = added(p_own[m].at[j], p_x[m].at[j]).astype(BF)
                    part_onward(m, k).start()

    def gw_join():
        for k in range(1, pairs + 1):
            j = lax.rem(mine + k, pairs)
            gw_ready(j)
            gw_swap(j).wait_recv()
            if k < pairs:
                gw_own[j] = added(gw_own.at[j], gw_x.at[j]).astype(BF)
                gw_onward(k).start()

    gain_swap = remote(g_in, g_x, gx_sem.at[0], gx_sem.at[1], (mate(d), s))

    def gain_near(k):
        return remote(g_a, g_r.at[k - 1], g_send.at[k], g_recv.at[k], (lax.rem(d + 2 * k, dp), s))

    def gain_far(k):
        return remote(g_b, g_z.at[k - 1], gz_send.at[k], gz_recv.at[k], (d, lax.rem(s + k, seq)))

    def gain_middle():
        gain_swap.wait_recv()
        g_a[...] = g_in[...] + g_x[...]
        for k in range(1, pairs):
            gain_near(k).start()

    def gain_last():
        for k in range(1, pairs):
            gain_near(k).wait_recv()
        g_b[...] = added(g_a, *[g_r.at[k] for k in range(pairs - 1)])
        for k in range(1, seq):
            gain_far(k).start()

    backs = [remote(p_fin[m], part_outs[m], t_send.at[m], t_recv.at[m], (to_d, to_s)) for m in range(count)]
    stays = [pltpu.make_async_copy(p_fin[m], part_outs[m], t_send.at[count + m]) for m in range(count)]

    def part_finish():
        for m in range(count):
            for k in range(1, pairs):
                part_onward(m, k).wait_recv()
            rest = [p_r[m].at[k] for k in range(pairs - 1)]
            p_fin[m][...] = added(p_own[m].at[mine], p_x[m].at[mine], *rest).astype(BF)
            pl.when(moves)(backs[m].start)
            pl.when(jnp.logical_not(moves))(stays[m].start)

    if fused:
        dn_tasks(0, 2)
        begin()
        part_join()
        loads[3].wait()
        gw_away()
        dn_tasks(2, seq)
        gain_swap.start()
        gw_home()
    else:
        begin()
        part_join()
        gain_swap.start()
    gw_join()
    later = [gain_middle, gain_last, part_finish]
    for i in range(seq - 1):
        for q in range(pieces):
            hop(i, q)
            if later and q == pieces - 1:
                later.pop(0)()
    for task in later:
        task()

    for k in range(1, pairs):
        gw_onward(k).wait_recv()
    gw_out[...] = added(gw_own.at[mine], gw_x.at[mine], *[gw_r.at[k] for k in range(pairs - 1)])
    for k in range(1, seq):
        gain_far(k).wait_recv()
    gain_out[...] = added(g_b, *[g_z.at[k] for k in range(seq - 1)])

    some = math.gcd(piece, 64)
    for q in range(pieces):
        pl.when(s > 0)(functools.partial(landed, s, q))
        pl.when(s < seq - 1)(functools.partial(landed, seq, q))

        def settle(at, carried):
            rows = pl.ds(pl.multiple_of(q * piece + at * some, some), some)
            from_left = jnp.where(s > 0, come[s, :, rows, :].astype(F32), 0.0)
            from_right = jnp.where(s < seq - 1, come[seq, :, rows, :].astype(F32), 0.0)
            total = own[s, :, rows, :].astype(F32) + from_left + from_right
            x = hid_ref[:, rows, :].astype(F32)
            inv = lax.rsqrt(jnp.mean(x * x, axis=2, keepdims=True) + norm_eps)
            scaled = total * scale_ref[...].astype(F32)[None]
            out_ref[:, rows, :] = (
                cot_ref[:, rows, :].astype(F32)
                + inv * scaled
                - x * (inv * inv * inv) * jnp.mean(x * scaled, axis=2, keepdims=True)
            ).astype(BF)
            return carried

        lax.fori_loop(0, piece // some, settle, 0)

    for q in range(pieces):
        pl.when(s < seq - 1)(give(0, s + 1, q).wait_send)
        pl.when(s > 0)(give(1, s - 1, q).wait_send)
    gain_swap.wait_send()
    for j in range(pairs):
        gw_swap(j).wait_send()
        for m in range(count):
            part_swap(m, j).wait_send()
    for k in range(1, pairs):
        gw_onward(k).wait_send()
        gain_near(k).wait_send()
        for m in range(count):
            part_onward(m, k).wait_send()
    for k in range(1, seq):
        gain_far(k).wait_send()
    for m in range(count):
        pl.when(moves)(backs[m].wait_send)
        pl.when(moves)(remote(p_fin[m], part_outs[m], t_send.at[m], t_recv.at[m], (to_d, to_s)).wait_recv)
        pl.when(jnp.logical_not(moves))(stays[m].wait)


def scatter(d_x, d_z, normed, w_in, hidden, parts, hidden_in, cotangent, norm_gain, collective_id=1):
    dp, seq = lax.axis_size("dp"), lax.axis_size("seq")
    seqs, part, width = hidden_in.shape
    tokens, channels = d_x.shape
    w_rows = 2 * channels // dp
    fused = fits_whole(seqs, part * seq, width, channels)
    pieces = 4 if part % 64 == 0 else 1
    pairs, count = dp // 2, len(parts)
    dma, vmem, shape = pltpu.SemaphoreType.DMA, pltpu.VMEM, jax.ShapeDtypeStruct
    here = pl.BlockSpec(memory_space=pltpu.VMEM)
    if fused:
        ins, in_specs = [d_x, d_z, normed, w_in, hidden], any_specs(5)
        extra = [
            vmem((tokens, 2 * channels), BF), vmem((tokens, width), BF), vmem((2 * channels, width), BF),
            vmem((part, width), BF), vmem((pairs, w_rows, width), BF), dma((4,)), dma,
        ]
        gain_shape = (8, width)
    else:
        d_pre = jnp.concatenate([d_x, d_z], axis=1)
        x = hidden.astype(F32)
        d_normed = mm(d_pre, w_in, NN)
        inv = lax.rsqrt(jnp.mean(x * x, axis=1, keepdims=True) + norm_eps)
        gain = jnp.sum(d_normed * x * inv, axis=0).reshape(8, -1)
        ins = [
            d_normed.astype(BF).reshape(seqs, -1, width),
            mm(d_pre, normed, TN).astype(BF).reshape(dp, w_rows, width), gain,
        ]
        in_specs, extra = any_specs(2) + [here], []
        gain_shape = gain.shape
    part_shapes = [member.shape[1:] for member in parts]
    token_shape = (seqs, part, width)

    def each(count):
        return [vmem((count,) + member, BF) for member in part_shapes]

    out = pl.pallas_call(
        functools.partial(scatter_kernel, dp, seq, len(parts), fused),
        in_specs=in_specs + any_specs(count) + [here] * 3,
        out_specs=[here] * (3 + count),
        out_shape=[shape(token_shape, BF), shape((w_rows, width), F32)]
        + [shape(member, BF) for member in part_shapes]
        + [shape(gain_shape, F32)],
        scratch_shapes=[
            vmem((seq,) + token_shape, BF), vmem((seq + 1,) + token_shape, BF),
            vmem((pairs, w_rows, width), BF), vmem((pairs, w_rows, width), BF), vmem((pairs - 1, w_rows, width), BF),
            *each(pairs), *each(pairs), *each(pairs - 1), *[vmem(member, BF) for member in part_shapes],
            vmem(gain_shape, F32), vmem(gain_shape, F32), vmem((pairs - 1,) + gain_shape, F32),
            vmem((seq - 1,) + gain_shape, F32), vmem(gain_shape, F32), vmem(gain_shape, F32),
            dma((seq,)), dma((seq, pieces)), dma((seq + 1, pieces)),
            dma((pairs,)), dma((pairs,)), dma((pairs,)), dma((pairs,)), dma((pairs,)),
            *[dma((count, pairs))] * 5, dma((2 * count,)), dma((count,)),
            dma((2,)), dma((pairs,)), dma((pairs,)), dma((seq,)), dma((seq,)),
            *extra,
        ],
        compiler_params=pltpu.CompilerParams(
            collective_id=collective_id, has_side_effects=True, vmem_limit_bytes=63 << 20
        ),
        name="scatter_out",
    )(*ins, *parts, hidden_in, cotangent, norm_gain.reshape(1, width))
    gain = jnp.sum(out[-1], axis=0) if fused else out[-1].reshape(width)
    return out[0], out[1], out[2 : 2 + count], gain


def reduce_kernel(dp, seq, grads, *refs):
    refs = list(refs)

    def take(count):
        out = refs[:count]
        del refs[:count]
        return out

    wide_ref, thin_ref = take(2)
    g_ref = take(1)[0] if grads else None
    wide_out, thin_out = take(2)
    g_out = take(1)[0] if grads else None
    wide_x, thin_x, wide_s, thin_s = take(4)
    xw_send, xw_recv, xt_send, xt_recv, sw_send, sw_recv, st_send, st_recv = take(8)
    d, s = place()
    rows = wide_ref.shape[0] // seq
    pairs = dp // 2
    mine, odd = d // 2, lax.rem(d, 2)
    for k in range(1, seq):
        greet((d, lax.rem(s + k, seq)))
    if grads:
        for k in range(1, pairs):
            greet((lax.rem(d + 2 * k, dp), s))
        greet((mate(d), s))
    pl.semaphore_wait(pltpu.get_barrier_semaphore(), seq - 1 + (pairs if grads else 0))

    def piece(ref, which):
        return ref.at[pl.ds(pl.multiple_of(which * rows, rows), rows)]

    def ask(k):
        to = lax.rem(s + k, seq)
        return (
            remote(piece(wide_ref, to), wide_x.at[k - 1], xw_send.at[k - 1], xw_recv.at[k - 1], (d, to)),
            remote(thin_ref.at[to], thin_x.at[k - 1], xt_send.at[k - 1], xt_recv.at[k - 1], (d, to)),
        )

    def tell(k):
        to = lax.rem(s + k, seq)
        return (
            remote(wide_s, piece(wide_out, s), sw_send.at[k - 1], sw_recv.at[k - 1], (d, to)),
            remote(thin_s, thin_out.at[s], st_send.at[k - 1], st_recv.at[k - 1], (d, to)),
        )

    def told(k):
        source = lax.rem(s - k + seq, seq)
        return (
            remote(wide_s, piece(wide_out, source), sw_send.at[k - 1], sw_recv.at[k - 1], (d, s)),
            remote(thin_s, thin_out.at[source], st_send.at[k - 1], st_recv.at[k - 1], (d, s)),
        )

    order = sorted(range(1, seq), key=lambda k: -min(k, seq - k))
    for k in order:
        for copy in ask(k):
            copy.start()
    if grads:
        g_own, g_x, g_r, g_load, gx_send, gx_recv, g_send, g_recv = take(8)

        def swap(j):
            return remote(g_ref.at[2 * j + 1 - odd], g_x.at[j], gx_send.at[j], gx_recv.at[j], (mate(d), s))

        def fetch(j):
            return pltpu.make_async_copy(g_ref.at[2 * j + odd], g_own.at[j], g_load.at[j])

        def onward(k):
            to = lax.rem(d + 2 * k, dp)
            return remote(g_own.at[to // 2], g_r.at[k - 1], g_send.at[k], g_recv.at[k], (to, s))

        for j in range(pairs):
            swap(j).start()
            fetch(j).start()
        for k in range(1, pairs + 1):
            j = lax.rem(mine + k, pairs)
            fetch(j).wait()
            swap(j).wait_recv()
            if k < pairs:
                g_own[j] = added(g_own.at[j], g_x.at[j]).astype(BF)
                onward(k).start()
    for k in order:
        for copy in ask(k):
            copy.wait_recv()
    start = pl.ds(pl.multiple_of(s * rows, rows), rows)
    total = wide_ref[start, :].astype(F32)
    thin = thin_ref[s]
    for k in range(seq - 1):
        total = total + wide_x[k].astype(F32)
        thin = thin + thin_x[k]
    wide_s[...] = total.astype(BF)
    thin_s[...] = thin
    for k in order:
        for copy in tell(k):
            copy.start()
    wide_out[start, :] = total.astype(BF)
    thin_out[s] = thin
    if grads:
        for k in range(1, pairs):
            onward(k).wait_recv()
        g_out[...] = added(g_own.at[mine], g_x.at[mine], *[g_r.at[k] for k in range(pairs - 1)]).astype(BF)
        for j in range(pairs):
            swap(j).wait_send()
        for k in range(1, pairs):
            onward(k).wait_send()
    for k in order:
        for copy in told(k):
            copy.wait_recv()
    for k in order:
        for copy in ask(k) + tell(k):
            copy.wait_send()


def reduce_over_seq(wide_part, thin_part, collective_id, grads=None):
    dp, seq = lax.axis_size("dp"), lax.axis_size("seq")
    tokens, cols = wide_part.shape
    thin_part = jnp.swapaxes(thin_part.reshape(-1, seq, tokens // seq), 0, 1)
    dma, vmem, shape = pltpu.SemaphoreType.DMA, pltpu.VMEM, jax.ShapeDtypeStruct
    here = pl.BlockSpec(memory_space=pltpu.VMEM)
    rows, few, pairs = tokens // seq, thin_part.shape[1:], dp // 2
    ins, in_specs = [wide_part.astype(BF), thin_part], [here] * 2
    outs = [shape((tokens, cols), BF), shape(thin_part.shape, F32)]
    scratch = [
        vmem((seq - 1, rows, cols), BF), vmem((seq - 1,) + few, F32), vmem((rows, cols), BF), vmem(few, F32),
    ] + [dma((seq - 1,))] * 8
    if grads is not None:
        ins, in_specs = ins + [grads], in_specs + any_specs(1)
        outs.append(shape(grads.shape[1:], BF))
        scratch += [vmem((pairs,) + grads.shape[1:], BF)] * 2 + [vmem((pairs - 1,) + grads.shape[1:], BF)]
        scratch += [dma((pairs,))] * 5
    out = pl.pallas_call(
        functools.partial(reduce_kernel, dp, seq, grads is not None),
        in_specs=in_specs,
        out_specs=[here] * len(outs),
        out_shape=outs,
        scratch_shapes=scratch,
        compiler_params=pltpu.CompilerParams(
            collective_id=collective_id, has_side_effects=True, vmem_limit_bytes=24 << 20
        ),
        name="reduce_seq",
    )(*ins)
    return (out[0], jnp.swapaxes(out[1], 0, 1).reshape(-1, tokens)) + tuple(out[2:])


def homes_back(dp, seq):
    pairs = []
    for d in range(dp):
        for s in range(seq):
            home_d, home_s = 2 * (d // 2) + s % 2, (seq // 2) * (d % 2) + s // 2
            pairs.append((home_d * seq + home_s, d * seq + s))
    return pairs


def local(
    hidden_in,
    doc_lengths,
    norm_gain,
    in_weight,
    conv_weight,
    conv_bias,
    x_weight,
    dt_weight,
    dt_bias,
    skip_gain,
    out_weight,
    out_cotangent,
):
    seqs, part_len, width = hidden_in.shape
    dp, seq = lax.axis_size("dp"), lax.axis_size("seq")
    length = part_len * seq
    tokens = seqs * length
    rows = out_weight.shape[0]
    channels = rows * dp
    lag_max = KCONV - 1

    vectors = [conv_weight, conv_bias[None], dt_bias[None], skip_gain[None]]
    vectors = jnp.pad(jnp.concatenate(vectors, axis=0), ((0, 16 - KCONV - 3), (0, 0)))
    parts = [out_weight, x_weight, dt_weight, vectors]
    hidden, w_in, parts, normed, pre = gather(hidden_in, in_weight, parts, norm_gain)
    cot, pre = lax.optimization_barrier((out_cotangent, pre))
    cot = lax.all_gather(cot, "seq", axis=1, tiled=True).reshape(tokens, width)

    w_out, w_x, w_dt = (part.reshape(channels, part.shape[2]) for part in parts[:3])
    vectors = jnp.swapaxes(parts[3], 0, 1).reshape(16, channels).astype(F32)
    taps, conv_shift, rate_shift, skip = vectors[:KCONV], vectors[KCONV], vectors[KCONV + 1], vectors[KCONV + 2]

    begins, places = token_begins(doc_lengths, length)
    keep = (places[None, :] != begins).astype(F32).reshape(tokens, 1)
    valid = [(places[None, :] - (lag_max - w) >= begins)[:, :, None] for w in range(KCONV)]

    x_inner = pre[:, :channels].reshape(seqs, length, channels)

    padded = jnp.pad(x_inner, ((0, 0), (lag_max, 0), (0, 0)))
    conv_sum = jnp.broadcast_to(conv_shift, (seqs, length, channels))
    for w in range(KCONV):
        window = padded[:, w : w + length, :].astype(F32)
        conv_sum = conv_sum + jnp.where(valid[w], window * taps[w], 0.0)
    conv_flat = conv_sum.reshape(tokens, channels)
    xc_low = jax.nn.silu(conv_flat).astype(BF)
    rate, thin = reduce_over_seq(mm(xc_low, w_x[:, :R], NN), mm(w_x[:, R:], xc_low, ((0,), (1,))), 2)
    key, query = thin[:N].T, thin[N:].T
    key_lanes, query_lanes = (
        jnp.broadcast_to(part.astype(BF)[:, :, None], (tokens, N, LANES)) for part in (key, query)
    )
    ksum = jnp.sum(key * key, axis=1, keepdims=True)
    keep_lanes = jnp.broadcast_to(keep, (tokens, LANES))
    ksum_lanes = jnp.broadcast_to(ksum, (tokens, LANES))
    vectors = jnp.pad(jnp.stack([rate_shift, skip]), ((0, 6), (0, 0)))
    states, y_full, gated = scan_forward(
        seqs, length, xc_low, pre, rate, key_lanes, query_lanes, keep_lanes, ksum_lanes, w_dt, vectors
    )
    branch = mm(gated, w_out, NN).astype(BF).reshape(seqs, length, width)
    branch = lax.psum_scatter(branch, "seq", scatter_dimension=1, tiled=True)
    output = (hidden_in.astype(F32) + branch.astype(F32)).astype(BF)

    d_z, rest, dq, dk, d_norm, d_row, grad_dt, sums = scan_backward(
        seqs, length, mm(cot, w_out, NT), y_full, xc_low, pre, rate, key_lanes, query_lanes, keep_lanes, ksum_lanes, w_dt, vectors, states
    )
    dq, dk = dq.reshape(tokens, N), dk.reshape(tokens, N)
    d_norm = -jnp.sum(d_norm, axis=1, keepdims=True)
    d_keys = dk + 2.0 * key * d_norm
    grad_out = mm(gated, cot, TN).astype(BF).reshape(dp, rows, width)
    d_row, thin, grad_out = reduce_over_seq(d_row, jnp.concatenate([d_keys.T, dq.T], axis=0), 3, grad_out)
    grad_out = lax.ppermute(grad_out, ("dp", "seq"), homes_back(dp, seq))
    d_proj = jnp.concatenate([d_row, thin.T.astype(BF)], axis=1)
    d_conv_out = mm(d_proj, w_x, NT) + rest
    d_conv = (d_conv_out * silu_slope(conv_flat)).reshape(seqs, length, channels)

    tap_grads = []
    d_x_inner = jnp.zeros((seqs, length, channels), F32)
    for w in range(KCONV):
        lag = lag_max - w
        window = padded[:, w : w + length, :].astype(F32)
        masked = jnp.where(valid[w], d_conv, 0.0)
        tap_grads.append(jnp.sum(masked * window, axis=(0, 1)))
        d_x_inner = d_x_inner + jnp.pad(masked, ((0, 0), (0, lag), (0, 0)))[:, lag:, :] * taps[w]
    vector_grads = jnp.stack(
        tap_grads + [jnp.sum(d_conv, axis=(0, 1)), jnp.sum(sums[:8], axis=0), jnp.sum(sums[8:], axis=0)], axis=0
    )
    vector_grads = jnp.pad(vector_grads, ((0, 16 - KCONV - 3), (0, 0))).reshape(16, dp, rows)
    grads = [part.astype(BF).reshape(dp, rows, -1) for part in (mm(xc_low, d_proj, TN), grad_dt)]
    grads.append(jnp.swapaxes(vector_grads, 0, 1).astype(BF))
    grad_in, grad_in_weight, grads, grad_norm_gain = scatter(
        d_x_inner.reshape(tokens, channels).astype(BF), d_z, normed, w_in, hidden, grads,
        hidden_in, out_cotangent, norm_gain,
    )
    grad_x, grad_dt, grad_vectors = (part.astype(F32) for part in grads)
    grad_out_weight = grad_out.astype(F32)
    return (
        output,
        grad_in,
        grad_norm_gain,
        grad_in_weight,
        grad_vectors[:KCONV],
        grad_vectors[KCONV],
        grad_x,
        grad_dt,
        grad_vectors[KCONV + 1],
        grad_vectors[KCONV + 2],
        grad_out_weight,
    )


def solution(mesh):
    both = ("dp", "seq")
    tokens = P("dp", "seq", None)
    matrix, vector = P(both, None), P(both)
    return jax.shard_map(
        local,
        mesh=mesh,
        in_specs=(
            tokens, P("dp", None), P(), matrix, P(None, both), vector,
            matrix, matrix, vector, vector, matrix, tokens,
        ),
        out_specs=(
            tokens, tokens, P(), matrix, P(None, both), vector,
            matrix, matrix, vector, vector, matrix,
        ),
        check_vma=False,
    )
```

```python
import functools
import math

import jax
import jax.numpy as jnp
from jax import lax
from jax.experimental import pallas as pl
from jax.experimental.pallas import tpu as pltpu
from jax.sharding import PartitionSpec as P

N = 16
R = 128
KCONV = 4
CHUNK = 16
LANES = 128
GROUP = 1024
BLOCK = 128

norm_eps = 1e-05
BF = jnp.bfloat16
F32 = jnp.float32


def silu_slope(pre_value):
    sigmoid_of = jax.nn.sigmoid(pre_value)
    return sigmoid_of * (1.0 + pre_value * (1.0 - sigmoid_of))


def token_begins(lengths, position_count):
    doc_ends = jnp.cumsum(lengths, axis=1)
    doc_starts = doc_ends - lengths
    places = jnp.arange(position_count, dtype=jnp.int32)
    inside = doc_starts[:, None, :] <= places[None, :, None]
    return (jnp.max(jnp.where(inside, doc_starts[:, None, :], 0), axis=2), places)


def mm(left, right, dims):
    return lax.dot_general(left, right, (dims, ((), ())), preferred_element_type=F32)


NN = ((1,), (0,))
NT = ((1,), (1,))
TN = ((0,), (0,))


def row(ref, i, lane):
    return jnp.broadcast_to(ref[i : i + 1, pl.ds(lane, LANES)], (8, LANES))


def wide(ref, rows, count):
    value = ref[rows, :]
    return jnp.concatenate([value] * (count // LANES), axis=1)


def merge(even, odd, stride):
    low = lax.broadcasted_iota(jnp.int32, (8, LANES), 0) % (2 * stride) < stride
    if stride == 4:
        return jnp.where(low, even, odd) + pltpu.roll(jnp.where(low, odd, even), 4, 0)
    return jnp.where(low, even + pltpu.roll(even, 8 - stride, 0), odd + pltpu.roll(odd, stride, 0))


def collect(stack, value, descending):
    level = 0
    while stack and stack[-1][0] == level:
        other = stack.pop()[1]
        value = merge(value, other, 1 << level) if descending else merge(other, value, 1 << level)
        level += 1
    stack.append((level, value))


def each_chunk(tokens, channels, body):
    group = math.gcd(channels, 512)

    def run(k, carried):
        rows = pl.ds(pl.multiple_of(k * CHUNK, CHUNK), CHUNK)
        for first in range(0, channels, group):
            body(rows, pl.ds(first, group), first)
        return carried

    lax.fori_loop(0, tokens // CHUNK, run, 0)


def load_carry(carry, tiles):
    out = []
    for lane in tiles:
        out += [carry[0:8, pl.ds(lane, LANES)], carry[8:16, pl.ds(lane, LANES)]]
    return tuple(out)


def store_carry(carry, tiles, values):
    for j, lane in enumerate(tiles):
        carry[0:8, pl.ds(lane, LANES)] = values[2 * j]
        carry[8:16, pl.ds(lane, LANES)] = values[2 * j + 1]


def halves(value):
    return [value[0:8], value[8:16]]


def token(keys, queries, keeps, i):
    return row(keeps, i, 0), halves(keys[i].astype(F32)), halves(queries[i].astype(F32))


def lane_groups(channels):
    group = math.gcd(channels, GROUP)
    return [list(range(first, first + group, LANES)) for first in range(0, channels, group)]


def forward_kernel(
    xc_ref, z_ref, rate_ref, key_ref, query_ref, keep_ref, ksum_ref, wdt_ref, vec_ref,
    s_ref, y_ref, gated_ref, step, inj, carry,
):
    @pl.when(pl.program_id(1) == 0)
    def _():
        carry[...] = jnp.zeros_like(carry)

    tokens, channels = xc_ref.shape
    step[...] = mm(rate_ref[...], wdt_ref[...], NT)

    def prepare(rows, cols, first):
        beta = jax.nn.sigmoid(step[rows, cols] + vec_ref[0:1, cols])
        eps = beta / (1.0 + beta * wide(ksum_ref, rows, cols.size))
        step[rows, cols] = eps
        inj[rows, cols] = eps * xc_ref[rows, cols].astype(F32)

    each_chunk(tokens, channels, prepare)
    for tiles in lane_groups(channels):

        def chunk(k, state):
            state = list(state)
            base = pl.multiple_of(k * CHUNK, CHUNK)
            steps, injs, keeps, keys, queries = (
                r.at[pl.ds(base, CHUNK)] for r in (step, inj, keep_ref, key_ref, query_ref)
            )
            saved = s_ref.at[pl.ds(pl.multiple_of(k * CHUNK * N, CHUNK * N), CHUNK * N)]
            stacks = [[] for _ in tiles]
            for i in range(CHUNK):
                keep, key, query = token(keys, queries, keeps, i)
                ksq = [keep * key[h] * key[h] for h in range(2)]
                for j, lane in enumerate(tiles):
                    eps, push = row(steps, i, lane), row(injs, i, lane)
                    for h in range(2):
                        state[2 * j + h] = (keep - eps * ksq[h]) * state[2 * j + h] + push * key[h]
                    both = jnp.concatenate([state[2 * j], state[2 * j + 1]], axis=0)
                    saved[i * N : (i + 1) * N, pl.ds(lane, LANES)] = both.astype(BF)
                    collect(stacks[j], state[2 * j] * query[0] + state[2 * j + 1] * query[1], False)
                    if i % 8 == 7:
                        y_ref[pl.ds(pl.multiple_of(base + i - 7, 8), 8), pl.ds(lane, LANES)] = stacks[j].pop()[1]
            return tuple(state)

        store_carry(carry, tiles, lax.fori_loop(0, tokens // CHUNK, chunk, load_carry(carry, tiles)))

    def emit(rows, cols, first):
        y_full = y_ref[rows, cols] + vec_ref[1:2, cols] * xc_ref[rows, cols].astype(F32)
        y_ref[rows, cols] = y_full
        z = z_ref[rows, cols].astype(F32)
        gated_ref[rows, cols] = (y_full * (z * jax.nn.sigmoid(z))).astype(BF)

    each_chunk(tokens, channels, emit)


def backward_kernel(
    dg_ref, y_ref, xc_ref, z_ref, rate_ref, key_ref, query_ref, keep_ref, ksum_ref, wdt_ref, vec_ref, s_ref, before_ref,
    dz_ref, rest_ref, dq_ref, dk_ref, dnorm_ref, drow_ref, gdt_ref, sums_ref,
    step, inj, dy, mix, pull, beta, drate, carry, acc_q, acc_k,
):
    turn = pl.program_id(1)
    tokens, channels = xc_ref.shape
    chunks = tokens // CHUNK

    @pl.when(jnp.logical_and(pl.program_id(0) == 0, turn == 0))
    def _():
        gdt_ref[...] = jnp.zeros_like(gdt_ref)
        sums_ref[...] = jnp.zeros_like(sums_ref)

    @pl.when(turn == 0)
    def _():
        carry[...] = jnp.zeros_like(carry)

    beta[...] = mm(rate_ref[...], wdt_ref[...], NT)

    def prepare(rows, cols, first):
        rate_beta = jax.nn.sigmoid(beta[rows, cols] + vec_ref[0:1, cols])
        eps = rate_beta / (1.0 + rate_beta * wide(ksum_ref, rows, cols.size))
        beta[rows, cols] = rate_beta
        step[rows, cols] = eps
        xc = xc_ref[rows, cols].astype(F32)
        inj[rows, cols] = eps * xc
        z = z_ref[rows, cols].astype(F32)
        sig = jax.nn.sigmoid(z)
        d_gated = dg_ref[rows, cols]
        d_y = d_gated * (z * sig)
        dy[rows, cols] = d_y
        dz_ref[rows, cols] = (d_gated * y_ref[rows, cols] * (sig * (1.0 + z * (1.0 - sig)))).astype(BF)
        weighted = d_y * xc
        sums_ref[8:16, cols] += weighted[0:8] + weighted[8:16]

    each_chunk(tokens, channels, prepare)
    for tiles in lane_groups(channels):
        start = tiles[0] == 0

        def chunk(back, carried):
            k = chunks - 1 - back
            pulled, now = list(carried[0]), list(carried[1])
            base = pl.multiple_of(k * CHUNK, CHUNK)
            steps, injs, dys, keeps, keys, queries = (
                r.at[pl.ds(base, CHUNK)] for r in (step, inj, dy, keep_ref, key_ref, query_ref)
            )
            stacks = [([], []) for _ in tiles]
            for i in reversed(range(CHUNK)):
                keep, key, query = token(keys, queries, keeps, i)
                kept = [keep * key[h] for h in range(2)]
                ksq = [kept[h] * key[h] for h in range(2)]
                if i > 0:
                    before = pl.ds(pl.multiple_of((base + i) * N - N, N), N)
                else:
                    before = pl.ds(pl.multiple_of(jnp.maximum(base * N - N, 0), N), N)
                seen, plain, scaled = [0.0, 0.0], [0.0, 0.0], [0.0, 0.0]
                for j, lane in enumerate(tiles):
                    eps, push, d_y = row(steps, i, lane), row(injs, i, lane), row(dys, i, lane)
                    prior = s_ref[before, pl.ds(lane, LANES)]
                    if i == 0:
                        prior = jnp.where(k > 0, prior, before_ref[:, pl.ds(lane, LANES)])
                    prior = halves(prior.astype(F32))
                    by_key, by_square = [], []
                    for h in range(2):
                        at = 2 * j + h
                        grad = pulled[at] + d_y * query[h]
                        pulled[at] = (keep - eps * ksq[h]) * grad
                        keyed = eps * (grad * key[h])
                        prod = keyed * prior[h]
                        seen[h] += now[at] * d_y
                        plain[h] += grad * push
                        scaled[h] += prod
                        by_key.append(keyed)
                        by_square.append(prod * kept[h])
                        now[at] = prior[h]
                    collect(stacks[j][0], by_key[0] + by_key[1], True)
                    collect(stacks[j][1], by_square[0] + by_square[1], True)
                    if i % 8 == 0:
                        rows = pl.ds(pl.multiple_of(base + i, 8), 8)
                        mix[rows, pl.ds(lane, LANES)] = stacks[j][0].pop()[1]
                        pull[rows, pl.ds(lane, LANES)] = stacks[j][1].pop()[1]
                for ref, parts in ((acc_q, seen), (acc_k, [plain[h] - 2.0 * keep * scaled[h] for h in range(2)])):
                    for h in range(2):
                        rows = pl.ds(pl.multiple_of((base + i) * N + 8 * h, 8), 8)
                        if start:
                            ref[rows, :] = parts[h]
                        else:
                            ref[rows, :] += parts[h]
            return (tuple(pulled), tuple(now))

        now = []
        for lane in tiles:
            now += halves(s_ref[tokens * N - N : tokens * N, pl.ds(lane, LANES)].astype(F32))
        pulled, now = lax.fori_loop(0, chunks, chunk, (load_carry(carry, tiles), tuple(now)))
        store_carry(carry, tiles, pulled)

    ones = jnp.ones((LANES, LANES), BF)
    diagonal = lax.broadcasted_iota(jnp.int32, (LANES, LANES), 0) == (
        lax.broadcasted_iota(jnp.int32, (LANES, LANES), 1)
    )
    for out, ref in ((dq_ref, acc_q), (dk_ref, acc_k)):
        for first in range(0, tokens * N, LANES):
            sums = mm(ref[first : first + LANES, :].astype(BF), ones, NN)
            at = first // LANES
            out[at : at + 1, :] = jnp.sum(jnp.where(diagonal, sums, 0.0), axis=0, keepdims=True)

    def settle(rows, cols, first):
        rate_beta, eps = beta[rows, cols], step[rows, cols]
        through = mix[rows, cols]
        change = through * xc_ref[rows, cols].astype(F32) - pull[rows, cols]
        inverse = 1.0 / (1.0 + rate_beta * wide(ksum_ref, rows, cols.size))
        low = (change * inverse * (1.0 - rate_beta)).astype(BF)
        drate[rows, cols] = low
        lowered = low.astype(F32)
        sums_ref[0:8, cols] += lowered[0:8] + lowered[8:16]
        rest_ref[rows, cols] = through + vec_ref[1:2, cols] * dy[rows, cols]
        square = change * eps
        total = square[:, 0:LANES]
        for lane in range(LANES, cols.size, LANES):
            total = total + square[:, lane : lane + LANES]
        if first == 0:
            dnorm_ref[rows, :] = total
        else:
            dnorm_ref[rows, :] += total

    each_chunk(tokens, channels, settle)
    drow_ref[...] = mm(drate[...], wdt_ref[...], NN)
    gdt_ref[...] += mm(drate[...], rate_ref[...], TN)


def scan_blocks(length):
    block = math.gcd(length, BLOCK)
    return block, length // block


def row_spec(rows, cols, when, col=0):
    return pl.BlockSpec((rows, cols), lambda b, t: (when(b, t), col))


def spread_spec(block, when):
    return pl.BlockSpec((block, N, LANES), lambda b, t: (when(b, t), 0, 0))


def whole(array):
    return pl.BlockSpec(array.shape, lambda b, t: (0, 0), pipeline_mode=pl.Buffered(1))


def scan_forward(seqs, length, xc, pre, rate, key_lanes, query_lanes, keep_lanes, ksum_lanes, w_dt, vectors):
    tokens, channels = xc.shape
    block, blocks = scan_blocks(length)

    def at(b, t):
        return b * blocks + t

    rows = row_spec(block, channels, at)
    lanes = row_spec(block, LANES, at)
    vmem = pltpu.VMEM
    return pl.pallas_call(
        forward_kernel,
        grid=(seqs, blocks),
        in_specs=[
            rows, row_spec(block, channels, at, 1), row_spec(block, R, at),
            spread_spec(block, at), spread_spec(block, at), lanes, lanes, whole(w_dt), whole(vectors),
        ],
        out_specs=[row_spec(block * N, channels, at), rows, rows],
        out_shape=[
            jax.ShapeDtypeStruct((tokens * N, channels), BF),
            jax.ShapeDtypeStruct((tokens, channels), F32),
            jax.ShapeDtypeStruct((tokens, channels), BF),
        ],
        scratch_shapes=[vmem((block, channels), F32), vmem((block, channels), F32), vmem((N, channels), F32)],
        cost_estimate=pl.CostEstimate(
            flops=tokens * channels * N * 60, bytes_accessed=tokens * channels * 44, transcendentals=0
        ),
        compiler_params=pltpu.CompilerParams(vmem_limit_bytes=40 << 20),
        name="scan_forward",
    )(xc, pre, rate, key_lanes, query_lanes, keep_lanes, ksum_lanes, w_dt, vectors)


def scan_backward(seqs, length, d_gated, y, xc, pre, rate, key_lanes, query_lanes, keep_lanes, ksum_lanes, w_dt, vectors, states):
    tokens, channels = xc.shape
    block, blocks = scan_blocks(length)

    def at(b, t):
        return b * blocks + blocks - 1 - t

    def prior(b, t):
        return (jnp.maximum(at(b, t) * block - 1, 0), 0)

    rows = row_spec(block, channels, at)
    lanes = row_spec(block, LANES, at)
    flat = row_spec(block * N // LANES, LANES, at)
    vmem = pltpu.VMEM
    wide_f32 = vmem((block, channels), F32)
    return pl.pallas_call(
        backward_kernel,
        grid=(seqs, blocks),
        in_specs=[
            rows, rows, rows, row_spec(block, channels, at, 1), row_spec(block, R, at),
            spread_spec(block, at), spread_spec(block, at), lanes, lanes, whole(w_dt), whole(vectors),
            row_spec(block * N, channels, at), pl.BlockSpec((N, channels), prior),
        ],
        out_specs=[
            rows, rows, flat, flat, lanes, row_spec(block, R, at),
            pl.BlockSpec((channels, R), lambda b, t: (0, 0)), pl.BlockSpec((16, channels), lambda b, t: (0, 0)),
        ],
        out_shape=[
            jax.ShapeDtypeStruct((tokens, channels), BF),
            jax.ShapeDtypeStruct((tokens, channels), F32),
            jax.ShapeDtypeStruct((tokens * N // LANES, LANES), F32),
            jax.ShapeDtypeStruct((tokens * N // LANES, LANES), F32),
            jax.ShapeDtypeStruct((tokens, LANES), F32),
            jax.ShapeDtypeStruct((tokens, R), F32),
            jax.ShapeDtypeStruct((channels, R), F32),
            jax.ShapeDtypeStruct((16, channels), F32),
        ],
        scratch_shapes=[
            wide_f32, wide_f32, wide_f32, wide_f32, wide_f32, wide_f32, vmem((block, channels), BF),
            vmem((N, channels), F32), vmem((block * N, LANES), F32), vmem((block * N, LANES), F32),
        ],
        cost_estimate=pl.CostEstimate(
            flops=tokens * channels * N * 100, bytes_accessed=tokens * channels * 56, transcendentals=0
        ),
        compiler_params=pltpu.CompilerParams(vmem_limit_bytes=48 << 20),
        name="scan_backward",
    )(d_gated, y, xc, pre, rate, key_lanes, query_lanes, keep_lanes, ksum_lanes, w_dt, vectors, states, states)


MESH = pl.DeviceIdType.MESH


def any_specs(count):
    return [pl.BlockSpec(memory_space=pl.ANY)] * count


def place():
    return lax.axis_index("dp"), lax.axis_index("seq")


def mate(d):
    return d + 1 - 2 * lax.rem(d, 2)


def forward_home(d, s, seq):
    return 2 * (d // 2) + lax.rem(s, 2), (seq // 2) * lax.rem(d, 2) + s // 2


def backward_home(d, s, seq):
    return 2 * (d // 2) + s // (seq // 2), 2 * lax.rem(s, seq // 2) + lax.rem(d, 2)


def remote(src, dst, send, recv, device):
    return pltpu.make_async_remote_copy(
        src_ref=src, dst_ref=dst, send_sem=send, recv_sem=recv, device_id=device, device_id_type=MESH
    )


def greet(device, here=True):
    barrier = pltpu.get_barrier_semaphore()

    def tell():
        pl.semaphore_signal(barrier, inc=1, device_id=device, device_id_type=MESH)

    if here is True:
        tell()
    else:
        pl.when(here)(tell)


PARTS = 4


def gather_kernel(dp, seq, fused, *refs):
    refs = list(refs)

    def take(count):
        out = refs[:count]
        del refs[:count]
        return out

    hid_ref, w_ref = take(2)
    parts = take(PARTS)
    gain_ref = take(1)[0] if fused else None
    hid_out, w_out = take(2)
    slots = take(PARTS)
    normed_out, pre_out = take(2) if fused else (None, None)
    z_send, z_recv, w_send, w_recv, f_send, f_recv, p_send, p_recv, q_send, q_recv, t_send, t_recv, own_sem = take(13)
    d, s = place()
    part = hid_ref.shape[1]
    pieces = z_send.shape[2]
    piece = part // pieces
    pairs = dp // 2
    to_d, to_s = forward_home(d, s, seq)
    from_d, from_s = backward_home(d, s, seq)
    moves = jnp.logical_or(to_d != d, to_s != s)

    greet((d, s - 1), s > 0)
    greet((d, s + 1), s < seq - 1)
    for k in range(1, pairs):
        greet((lax.rem(d + 2 * k, dp), s))
    greet((mate(d), s))
    greet((to_d, to_s), moves)
    greet((from_d, from_s), moves)
    count = pairs + jnp.where(s > 0, 1, 0) + jnp.where(s < seq - 1, 1, 0) + jnp.where(moves, 2, 0)
    pl.semaphore_wait(pltpu.get_barrier_semaphore(), count)

    def shard(which, q):
        return hid_out.at[:, pl.ds(which * part + q * piece, piece), :]

    def hop(way, k, q):
        which = s - k if way == 0 else s + k
        src = hid_ref.at[:, pl.ds(q * piece, piece), :] if k == 0 else shard(which, q)
        near = s + 1 if way == 0 else s - 1
        return remote(src, shard(which, q), z_send.at[way, k, q], z_recv.at[way, k, q], (d, near))

    def can_send(way, k):
        if way == 0:
            return jnp.logical_and(s - k >= 0, s < seq - 1)
        return jnp.logical_and(s + k < seq, s > 0)

    def landed(way, k, q):
        which = jnp.where(way == 0, s - k, s + k)
        here = shard(which, q)
        remote(here, here, z_send.at[way, k - 1, q], z_recv.at[way, k - 1, q], (d, s)).wait_recv()

    def spread(out, own, send, recv, k):
        return remote(own, out.at[d], send.at[k], recv.at[k], (lax.rem(d + 2 * k, dp), s))

    def source(k):
        return lax.rem(d - 2 * k + dp, dp)

    def across(out, send, recv, k, own=None):
        return remote(own if k == 0 else out.at[source(k)], out.at[source(k)], send.at[k], recv.at[k], (mate(d), s))

    for q in range(pieces):
        for way in range(2):
            pl.when(can_send(way, 0))(hop(way, 0, q).start)
    transfers = [remote(parts[m], slots[m].at[to_d], t_send.at[m], t_recv.at[m], (to_d, to_s)) for m in range(PARTS)]
    stays = [pltpu.make_async_copy(parts[m], slots[m].at[d], own_sem.at[2 + m]) for m in range(PARTS)]
    for m in range(PARTS):
        pl.when(moves)(transfers[m].start)
        pl.when(jnp.logical_not(moves))(stays[m].start)
    for k in range(1, pairs):
        spread(w_out, w_ref, w_send, w_recv, k).start()
    across(w_out, f_send, f_recv, 0, w_ref).start()
    own_w = pltpu.make_async_copy(w_ref, w_out.at[d], own_sem.at[0])
    own_h = pltpu.make_async_copy(hid_ref, hid_out.at[:, pl.ds(s * part, part), :], own_sem.at[1])
    own_w.start()
    own_h.start()

    for m in range(PARTS):
        slot = slots[m].at[d]
        pl.when(moves)(remote(parts[m], slot, t_send.at[m], t_recv.at[m], (to_d, to_s)).wait_recv)
        pl.when(jnp.logical_not(moves))(stays[m].wait)
        for k in range(1, pairs):
            spread(slots[m], slot, p_send.at[m], p_recv.at[m], k).start()
        across(slots[m], q_send.at[m], q_recv.at[m], 0, slot).start()

    for k in range(1, seq - 1):
        for q in range(pieces):
            for way in range(2):
                pl.when(s - k >= 0 if way == 0 else s + k < seq)(functools.partial(landed, way, k, q))
                pl.when(can_send(way, k))(hop(way, k, q).start)
    own_w.wait()
    own_h.wait()
    flows = [(w_out, w_ref, w_send, w_recv, f_send, f_recv)]
    flows += [
        (slots[m], slots[m].at[d], p_send.at[m], p_recv.at[m], q_send.at[m], q_recv.at[m]) for m in range(PARTS)
    ]
    for out, own, send, recv, over_send, over_recv in flows:
        for k in range(1, pairs):
            here = out.at[source(k)]
            remote(here, here, send.at[k], recv.at[k], (d, s)).wait_recv()
            across(out, over_send, over_recv, k).start()
    for out, own, send, recv, over_send, over_recv in flows:
        for k in range(pairs):
            here = out.at[lax.rem(mate(d) - 2 * k + dp, dp)]
            remote(here, here, over_send.at[k], over_recv.at[k], (d, s)).wait_recv()

    last = seq - 1
    if fused:
        w_all, x_buf, w_sem, x_sem = take(4)
        width, columns = x_buf.shape[1], pre_out.shape[1]
        cut = math.gcd(columns, 512)
        fetch_w = pltpu.make_async_copy(w_out, w_all, w_sem)
        fetch_w.start()
        fetch_w.wait()

        def project(which, k, way):
            here = pl.multiple_of(which * part, part)
            for q in range(pieces):
                pl.when(k == last)(functools.partial(landed, way, last, q))
                fetch = pltpu.make_async_copy(
                    hid_out.at[0, pl.ds(which * part + q * piece, piece)], x_buf.at[pl.ds(q * piece, piece)], x_sem
                )
                fetch.start()
                fetch.wait()
                x = x_buf[pl.ds(q * piece, piece), :].astype(F32)
                inv = lax.rsqrt(jnp.mean(x * x, axis=1, keepdims=True) + norm_eps)
                rows = pl.ds(pl.multiple_of(here + q * piece, piece), piece)
                normed_out[rows, :] = (x * inv * gain_ref[...].astype(F32)).astype(BF)

            def matmul(at, carried):
                cols = pl.ds(pl.multiple_of(at * cut, cut), cut)
                w_rows = w_all.shape[1]
                block = w_all[pl.ds(at * (cut // w_rows), cut // w_rows)].reshape(cut, width)
                pre_out[pl.ds(here, part), cols] = mm(normed_out[pl.ds(here, part), :], block, NT).astype(BF)
                return carried

            lax.fori_loop(0, columns // cut, matmul, 0)

        def visit(m, carried):
            k = (m + 1) // 2
            way = lax.rem(m, 2)
            which = jnp.where(way == 0, s - k, s + k)

            @pl.when(jnp.logical_and(which >= 0, which < seq))
            def _():
                project(which, k, way)

            return carried

        lax.fori_loop(0, 2 * seq - 1, visit, 0)
    else:
        for q in range(pieces):
            for way in range(2):
                pl.when(s - last >= 0 if way == 0 else s + last < seq)(functools.partial(landed, way, last, q))

    for out, own, send, recv, over_send, over_recv in flows:
        for k in range(pairs):
            across(out, over_send, over_recv, k, own).wait_send()
        for k in range(1, pairs):
            spread(out, own, send, recv, k).wait_send()
    for k in range(seq - 1):
        for q in range(pieces):
            for way in range(2):
                pl.when(can_send(way, k))(hop(way, k, q).wait_send)
    for m in range(PARTS):
        pl.when(moves)(transfers[m].wait_send)


def fits_whole(seqs, length, width, channels):
    return seqs == 1 and length % 256 == 0 and length * (width + channels) + channels * width <= 6 << 20


def gather(hidden, weight, parts, norm_gain, collective_id=0):
    dp, seq = lax.axis_size("dp"), lax.axis_size("seq")
    seqs, part, width = hidden.shape
    columns = weight.shape[0] * dp
    fused = fits_whole(seqs, part * seq, width, columns // 2)
    pieces = 4 if part % 64 == 0 else 1
    dma, vmem, pairs = pltpu.SemaphoreType.DMA, pltpu.VMEM, dp // 2
    shape = jax.ShapeDtypeStruct
    outs = [shape((seqs, part * seq, width), BF), shape((dp,) + weight.shape, BF)]
    outs += [shape((dp,) + member.shape, BF) for member in parts]
    scratch = [dma((2, seq, pieces)), dma((2, seq, pieces))] + [dma((pairs,))] * 4
    scratch += [dma((PARTS, pairs))] * 4 + [dma((PARTS,)), dma((PARTS,)), dma((2 + PARTS,))]
    ins, in_specs = [hidden, weight, *parts], any_specs(2 + PARTS)
    out_specs = any_specs(2 + PARTS)
    if fused:
        ins.append(norm_gain.reshape(1, width))
        in_specs = in_specs + [pl.BlockSpec(memory_space=pltpu.VMEM)]
        outs += [shape((part * seq, width), BF), shape((part * seq, columns), BF)]
        scratch += [
            vmem((dp,) + weight.shape, BF), vmem((part, width), BF), dma, dma,
        ]
        out_specs = out_specs + [pl.BlockSpec(memory_space=pltpu.VMEM)] * 2
    out = pl.pallas_call(
        functools.partial(gather_kernel, dp, seq, fused),
        in_specs=in_specs,
        out_specs=out_specs,
        out_shape=outs,
        scratch_shapes=scratch,
        compiler_params=pltpu.CompilerParams(
            collective_id=collective_id, has_side_effects=True, vmem_limit_bytes=32 << 20
        ),
        name="gather_in",
    )(*ins)
    hidden = out[0].reshape(-1, width)
    w_in = out[1].reshape(columns, width)
    if fused:
        return hidden, w_in, out[2 : 2 + PARTS], out[-2], out[-1]
    x = hidden.astype(F32)
    inv = lax.rsqrt(jnp.mean(x * x, axis=1, keepdims=True) + norm_eps)
    normed = (x * inv * norm_gain.astype(F32)).astype(BF)
    return hidden, w_in, out[2:], normed, mm(normed, w_in, NT).astype(BF)


def added(ref, *others):
    total = ref[...].astype(F32)
    for other in others:
        total = total + other[...].astype(F32)
    return total


def scatter_kernel(dp, seq, count, fused, *refs):
    refs = list(refs)

    def take(count):
        out = refs[:count]
        del refs[:count]
        return out

    if fused:
        dx_ref, dz_ref, normed_ref, w_ref, full_ref = take(5)
        dn_ref = gw_ref = None
    else:
        dn_ref, gw_ref, gain_ref = take(3)
    parts = take(count)
    hid_ref, cot_ref, scale_ref = take(3)
    out_ref, gw_out = take(2)
    part_outs = take(count)
    gain_out = take(1)[0]
    own, come, gw_own, gw_x, gw_r = take(5)
    p_own, p_x, p_r, p_fin = take(count), take(count), take(count), take(count)
    g_in, g_one, g_x, g_r, g_z, g_a, g_b = take(7)
    z_load, z_send, z_recv, w_load, wx_send, wx_recv, w_send, w_recv = take(8)
    p_load, px_send, px_recv, p_send, p_recv, t_send, t_recv, gx_sem, g_send, g_recv, gz_send, gz_recv = take(12)

    d, s = place()
    seqs, part, width = out_ref.shape
    pieces = z_send.shape[1]
    piece = part // pieces
    pairs = dp // 2
    mine, odd = d // 2, lax.rem(d, 2)
    to_d, to_s = backward_home(d, s, seq)
    from_d, from_s = forward_home(d, s, seq)
    moves = jnp.logical_or(to_d != d, to_s != s)

    for k in range(1, seq):
        greet((d, lax.rem(s + k, seq)))
    for k in range(1, pairs):
        greet((lax.rem(d + 2 * k, dp), s))
    greet((mate(d), s))
    greet((to_d, to_s), moves)
    greet((from_d, from_s), moves)
    pl.semaphore_wait(pltpu.get_barrier_semaphore(), seq - 1 + pairs + jnp.where(moves, 2, 0))

    def swap(src, dst, send, recv, j):
        return remote(src, dst.at[j], send.at[j], recv.at[j], (mate(d), s))

    def part_swap(m, j):
        return swap(parts[m].at[2 * j + 1 - odd], p_x[m], px_send.at[m], px_recv.at[m], j)

    def part_fetch(m, j):
        return pltpu.make_async_copy(parts[m].at[2 * j + odd], p_own[m].at[j], p_load.at[m, j])

    for m in range(count):
        for j in range(pairs):
            part_swap(m, j).start()
            part_fetch(m, j).start()

    if fused:
        d_pre, normed, w_all, x_buf, gw_give, f_sem, x_sem = take(7)
        channels = dx_ref.shape[1]
        loads = [
            pltpu.make_async_copy(dx_ref, d_pre.at[:, pl.ds(0, channels)], f_sem.at[0]),
            pltpu.make_async_copy(dz_ref, d_pre.at[:, pl.ds(channels, channels)], f_sem.at[1]),
            pltpu.make_async_copy(w_ref, w_all, f_sem.at[2]),
            pltpu.make_async_copy(normed_ref, normed, f_sem.at[3]),
        ]
        for copy in loads:
            copy.start()
        for copy in loads[:3]:
            copy.wait()
        g_in[...] = jnp.zeros_like(g_in)
        w_rows = gw_own.shape[1]
        half_width = width // 2

        def dn_tasks(first, last):
            def run(i, carried):
                r = jnp.where(lax.rem(i, 2) == 0, seq - 1 - i // 2, i // 2)
                rows = pl.ds(pl.multiple_of(r * part, part), part)
                fetch = pltpu.make_async_copy(full_ref.at[rows], x_buf, x_sem)
                fetch.start()
                for at in range(2):
                    cols = pl.ds(at * half_width, half_width)
                    own[r, 0, :, cols] = mm(d_pre[rows, :], w_all[:, cols], NN).astype(BF)
                fetch.wait()

                def fold(at, carried):
                    some = pl.ds(pl.multiple_of(at * 64, 64), 64)
                    x = x_buf[some, :].astype(F32)
                    inv = lax.rsqrt(jnp.mean(x * x, axis=1, keepdims=True) + norm_eps)
                    weighted = own[r, 0, some, :].astype(F32) * (x * inv)
                    g_in[...] += jnp.sum(weighted.reshape(8, 8, width), axis=0)
                    return carried

                return lax.fori_loop(0, part // 64, fold, carried)

            lax.fori_loop(first, last, run, 0)

        def gw_task(dest, out, j):
            cols = pl.ds(pl.multiple_of(dest * w_rows, w_rows), w_rows)
            for at in range(2):
                some = pl.ds(at * half_width, half_width)
                out[j, :, some] = mm(d_pre[:, cols], normed[:, some], TN).astype(BF)

        def gw_swap(j):
            return swap(gw_give.at[j], gw_x, wx_send, wx_recv, j)

        def gw_away():
            def run(j, carried):
                gw_task(2 * j + 1 - odd, gw_give, j)
                gw_swap(j).start()
                return carried

            lax.fori_loop(0, pairs, run, 0)

        def gw_home():
            def run(k, carried):
                j = lax.rem(mine + 1 + k, pairs)
                gw_task(2 * j + odd, gw_own, j)
                return carried

            lax.fori_loop(0, pairs, run, 0)

        def gw_ready(j):
            pass
    else:
        def gw_swap(j):
            return swap(gw_ref.at[2 * j + 1 - odd], gw_x, wx_send, wx_recv, j)

        def gw_fetch(j):
            return pltpu.make_async_copy(gw_ref.at[2 * j + odd], gw_own.at[j], w_load.at[j])

        def chunk(r):
            return pltpu.make_async_copy(dn_ref.at[:, pl.ds(r * part, part), :], own.at[r], z_load.at[r])

        for r in range(seq):
            chunk(r).start()
        for j in range(pairs):
            gw_swap(j).start()
            gw_fetch(j).start()
        for r in range(seq):
            chunk(r).wait()
        g_in[...] = gain_ref[...]

        def gw_ready(j):
            gw_fetch(j).wait()

    def give(way, r, q):
        rows = pl.ds(q * piece, piece)
        slot = r if way == 0 else jnp.where(s - 1 == r, seq, r)
        near = s + 1 if way == 0 else s - 1
        return remote(own.at[r, :, rows, :], come.at[slot, :, rows, :], z_send.at[r, q], z_recv.at[slot, q], (d, near))

    def landed(slot, q):
        rows = pl.ds(q * piece, piece)
        here = come.at[slot, :, rows, :]
        remote(here, here, z_send.at[0, q], z_recv.at[slot, q], (d, s)).wait_recv()

    def begin():
        for q in range(pieces):
            pl.when(s == 0)(give(0, seq - 1, q).start)
            pl.when(s == seq - 1)(give(1, 0, q).start)

    def hop(turn, q):
        rows = pl.ds(q * piece, piece)
        for way in range(2):
            far = s if way == 0 else seq - 1 - s
            i = turn - far
            r = seq - 1 - i if way == 0 else i
            before = r + 1 if way == 0 else r - 1
            sends = jnp.logical_and(i >= 0, s < r if way == 0 else s > r)

            @pl.when(jnp.logical_and(sends, far > 0))
            def _():
                landed(r, q)
                own[r, :, rows, :] = added(own.at[r, :, rows, :], come.at[r, :, rows, :]).astype(BF)

            pl.when(jnp.logical_and(sends, i > 0))(give(way, before, q).wait_send)
            pl.when(jnp.logical_and(sends, far + i > 0))(give(way, r, q).start)

    def onward(part_own, part_r, send, recv, k):
        j = lax.rem(mine + k, pairs)
        return remote(part_own.at[j], part_r.at[k - 1], send.at[k], recv.at[k], (lax.rem(d + 2 * k, dp), s))

    def part_onward(m, k):
        return onward(p_own[m], p_r[m], p_send.at[m], p_recv.at[m], k)

    def gw_onward(k):
        return onward(gw_own, gw_r, w_send, w_recv, k)

    def part_join():
        for m in range(count):
            for k in range(1, pairs + 1):
                j = lax.rem(mine + k, pairs)
                part_fetch(m, j).wait()
                part_swap(m, j).wait_recv()
                if k < pairs:
                    p_own[m][j] = added(p_own[m].at[j], p_x[m].at[j]).astype(BF)
                    part_onward(m, k).start()

    def gw_join():
        for k in range(1, pairs + 1):
            j = lax.rem(mine + k, pairs)
            gw_ready(j)
            gw_swap(j).wait_recv()
            if k < pairs:
                gw_own[j] = added(gw_own.at[j], gw_x.at[j]).astype(BF)
                gw_onward(k).start()

    gain_swap = remote(g_one, g_x, gx_sem.at[0], gx_sem.at[1], (mate(d), s))

    def gain_near(k):
        return remote(g_a, g_r.at[k - 1], g_send.at[k], g_recv.at[k], (lax.rem(d + 2 * k, dp), s))

    def gain_far(k):
        return remote(g_b, g_z.at[k - 1], gz_send.at[k], gz_recv.at[k], (d, lax.rem(s + k, seq)))

    def gain_middle():
        gain_swap.wait_recv()
        g_a[...] = g_one[...] + g_x[...]
        for k in range(1, pairs):
            gain_near(k).start()

    def gain_last():
        for k in range(1, pairs):
            gain_near(k).wait_recv()
        g_b[...] = added(g_a, *[g_r.at[k] for k in range(pairs - 1)])
        for k in range(1, seq):
            gain_far(k).start()

    backs = [remote(p_fin[m], part_outs[m], t_send.at[m], t_recv.at[m], (to_d, to_s)) for m in range(count)]
    stays = [pltpu.make_async_copy(p_fin[m], part_outs[m], t_send.at[count + m]) for m in range(count)]

    def part_finish():
        for m in range(count):
            for k in range(1, pairs):
                part_onward(m, k).wait_recv()
            rest = [p_r[m].at[k] for k in range(pairs - 1)]
            p_fin[m][...] = added(p_own[m].at[mine], p_x[m].at[mine], *rest).astype(BF)
            pl.when(moves)(backs[m].start)
            pl.when(jnp.logical_not(moves))(stays[m].start)

    if fused:
        dn_tasks(0, 2)
        begin()
        part_join()
        loads[3].wait()
        gw_away()
        gw_home()
        gw_join()
        dn_tasks(2, seq)
    else:
        begin()
        part_join()
        gw_join()
    g_one[...] = jnp.sum(g_in[...], axis=0, keepdims=True)
    gain_swap.start()
    later = [gain_middle, gain_last, part_finish]
    for i in range(seq - 1):
        for q in range(pieces):
            hop(i, q)
            if later and q == pieces - 1:
                later.pop(0)()
    for task in later:
        task()

    for k in range(1, pairs):
        gw_onward(k).wait_recv()
    gw_out[...] = added(gw_own.at[mine], gw_x.at[mine], *[gw_r.at[k] for k in range(pairs - 1)])
    for k in range(1, seq):
        gain_far(k).wait_recv()
    gain_out[...] = added(g_b, *[g_z.at[k] for k in range(seq - 1)])

    some = math.gcd(piece, 64)
    for q in range(pieces):
        pl.when(s > 0)(functools.partial(landed, s, q))
        pl.when(s < seq - 1)(functools.partial(landed, seq, q))

        def settle(at, carried):
            rows = pl.ds(pl.multiple_of(q * piece + at * some, some), some)
            from_left = jnp.where(s > 0, come[s, :, rows, :].astype(F32), 0.0)
            from_right = jnp.where(s < seq - 1, come[seq, :, rows, :].astype(F32), 0.0)
            total = own[s, :, rows, :].astype(F32) + from_left + from_right
            x = hid_ref[:, rows, :].astype(F32)
            inv = lax.rsqrt(jnp.mean(x * x, axis=2, keepdims=True) + norm_eps)
            scaled = total * scale_ref[...].astype(F32)[None]
            out_ref[:, rows, :] = (
                cot_ref[:, rows, :].astype(F32)
                + inv * scaled
                - x * (inv * inv * inv) * jnp.mean(x * scaled, axis=2, keepdims=True)
            ).astype(BF)
            return carried

        lax.fori_loop(0, piece // some, settle, 0)

    for q in range(pieces):
        pl.when(s < seq - 1)(give(0, s + 1, q).wait_send)
        pl.when(s > 0)(give(1, s - 1, q).wait_send)
    gain_swap.wait_send()
    for j in range(pairs):
        gw_swap(j).wait_send()
        for m in range(count):
            part_swap(m, j).wait_send()
    for k in range(1, pairs):
        gw_onward(k).wait_send()
        gain_near(k).wait_send()
        for m in range(count):
            part_onward(m, k).wait_send()
    for k in range(1, seq):
        gain_far(k).wait_send()
    for m in range(count):
        pl.when(moves)(backs[m].wait_send)
        pl.when(moves)(remote(p_fin[m], part_outs[m], t_send.at[m], t_recv.at[m], (to_d, to_s)).wait_recv)
        pl.when(jnp.logical_not(moves))(stays[m].wait)


def scatter(d_x, d_z, normed, w_in, hidden, parts, hidden_in, cotangent, norm_gain, collective_id=1):
    dp, seq = lax.axis_size("dp"), lax.axis_size("seq")
    seqs, part, width = hidden_in.shape
    tokens, channels = d_x.shape
    w_rows = 2 * channels // dp
    fused = fits_whole(seqs, part * seq, width, channels)
    pieces = 4 if part % 64 == 0 else 1
    pairs, count = dp // 2, len(parts)
    dma, vmem, shape = pltpu.SemaphoreType.DMA, pltpu.VMEM, jax.ShapeDtypeStruct
    here = pl.BlockSpec(memory_space=pltpu.VMEM)
    if fused:
        ins, in_specs = [d_x, d_z, normed, w_in, hidden], any_specs(5)
        extra = [
            vmem((tokens, 2 * channels), BF), vmem((tokens, width), BF), vmem((2 * channels, width), BF),
            vmem((part, width), BF), vmem((pairs, w_rows, width), BF), dma((4,)), dma,
        ]
    else:
        d_pre = jnp.concatenate([d_x, d_z], axis=1)
        x = hidden.astype(F32)
        d_normed = mm(d_pre, w_in, NN)
        inv = lax.rsqrt(jnp.mean(x * x, axis=1, keepdims=True) + norm_eps)
        gain = jnp.pad(jnp.sum(d_normed * x * inv, axis=0)[None], ((0, 7), (0, 0)))
        ins = [
            d_normed.astype(BF).reshape(seqs, -1, width),
            mm(d_pre, normed, TN).astype(BF).reshape(dp, w_rows, width), gain,
        ]
        in_specs, extra = any_specs(2) + [here], []
    part_shapes = [member.shape[1:] for member in parts]
    token_shape, one = (seqs, part, width), (1, width)

    def each(count):
        return [vmem((count,) + member, BF) for member in part_shapes]

    out = pl.pallas_call(
        functools.partial(scatter_kernel, dp, seq, len(parts), fused),
        in_specs=in_specs + any_specs(count) + [here] * 3,
        out_specs=[here] * (3 + count),
        out_shape=[shape(token_shape, BF), shape((w_rows, width), F32)]
        + [shape(member, BF) for member in part_shapes]
        + [shape(one, F32)],
        scratch_shapes=[
            vmem((seq,) + token_shape, BF), vmem((seq + 1,) + token_shape, BF),
            vmem((pairs, w_rows, width), BF), vmem((pairs, w_rows, width), BF), vmem((pairs - 1, w_rows, width), BF),
            *each(pairs), *each(pairs), *each(pairs - 1), *[vmem(member, BF) for member in part_shapes],
            vmem((8, width), F32), vmem(one, F32), vmem(one, F32), vmem((pairs - 1,) + one, F32),
            vmem((seq - 1,) + one, F32), vmem(one, F32), vmem(one, F32),
            dma((seq,)), dma((seq, pieces)), dma((seq + 1, pieces)),
            dma((pairs,)), dma((pairs,)), dma((pairs,)), dma((pairs,)), dma((pairs,)),
            *[dma((count, pairs))] * 5, dma((2 * count,)), dma((count,)),
            dma((2,)), dma((pairs,)), dma((pairs,)), dma((seq,)), dma((seq,)),
            *extra,
        ],
        compiler_params=pltpu.CompilerParams(
            collective_id=collective_id, has_side_effects=True, vmem_limit_bytes=63 << 20
        ),
        name="scatter_out",
    )(*ins, *parts, hidden_in, cotangent, norm_gain.reshape(1, width))
    return out[0], out[1], out[2 : 2 + count], out[-1].reshape(width)


def reduce_kernel(dp, seq, grads, *refs):
    refs = list(refs)

    def take(count):
        out = refs[:count]
        del refs[:count]
        return out

    wide_ref, thin_ref = take(2)
    g_ref = take(1)[0] if grads else None
    wide_out, thin_out = take(2)
    g_out = take(1)[0] if grads else None
    wide_x, thin_x, wide_s, thin_s = take(4)
    xw_send, xw_recv, xt_send, xt_recv, sw_send, sw_recv, st_send, st_recv = take(8)
    d, s = place()
    rows = wide_ref.shape[0] // seq
    pairs = dp // 2
    mine, odd = d // 2, lax.rem(d, 2)
    for k in range(1, seq):
        greet((d, lax.rem(s + k, seq)))
    if grads:
        for k in range(1, pairs):
            greet((lax.rem(d + 2 * k, dp), s))
        greet((mate(d), s))
    pl.semaphore_wait(pltpu.get_barrier_semaphore(), seq - 1 + (pairs if grads else 0))

    def piece(ref, which):
        return ref.at[pl.ds(pl.multiple_of(which * rows, rows), rows)]

    def ask(k):
        to = lax.rem(s + k, seq)
        return (
            remote(piece(wide_ref, to), wide_x.at[k - 1], xw_send.at[k - 1], xw_recv.at[k - 1], (d, to)),
            remote(thin_ref.at[to], thin_x.at[k - 1], xt_send.at[k - 1], xt_recv.at[k - 1], (d, to)),
        )

    def tell(k):
        to = lax.rem(s + k, seq)
        return (
            remote(wide_s, piece(wide_out, s), sw_send.at[k - 1], sw_recv.at[k - 1], (d, to)),
            remote(thin_s, thin_out.at[s], st_send.at[k - 1], st_recv.at[k - 1], (d, to)),
        )

    def told(k):
        source = lax.rem(s - k + seq, seq)
        return (
            remote(wide_s, piece(wide_out, source), sw_send.at[k - 1], sw_recv.at[k - 1], (d, s)),
            remote(thin_s, thin_out.at[source], st_send.at[k - 1], st_recv.at[k - 1], (d, s)),
        )

    order = sorted(range(1, seq), key=lambda k: -min(k, seq - k))
    for k in order:
        for copy in ask(k):
            copy.start()
    if grads:
        g_own, g_x, g_r, g_load, gx_send, gx_recv, g_send, g_recv = take(8)

        def swap(j):
            return remote(g_ref.at[2 * j + 1 - odd], g_x.at[j], gx_send.at[j], gx_recv.at[j], (mate(d), s))

        def fetch(j):
            return pltpu.make_async_copy(g_ref.at[2 * j + odd], g_own.at[j], g_load.at[j])

        def onward(k):
            to = lax.rem(d + 2 * k, dp)
            return remote(g_own.at[to // 2], g_r.at[k - 1], g_send.at[k], g_recv.at[k], (to, s))

        for j in range(pairs):
            swap(j).start()
            fetch(j).start()
        for k in range(1, pairs + 1):
            j = lax.rem(mine + k, pairs)
            fetch(j).wait()
            swap(j).wait_recv()
            if k < pairs:
                g_own[j] = added(g_own.at[j], g_x.at[j]).astype(BF)
                onward(k).start()
    for k in order:
        for copy in ask(k):
            copy.wait_recv()
    start = pl.ds(pl.multiple_of(s * rows, rows), rows)
    total = wide_ref[start, :].astype(F32)
    thin = thin_ref[s]
    for k in range(seq - 1):
        total = total + wide_x[k].astype(F32)
        thin = thin + thin_x[k]
    wide_s[...] = total.astype(BF)
    thin_s[...] = thin
    for k in order:
        for copy in tell(k):
            copy.start()
    wide_out[start, :] = total.astype(BF)
    thin_out[s] = thin
    if grads:
        for k in range(1, pairs):
            onward(k).wait_recv()
        g_out[...] = added(g_own.at[mine], g_x.at[mine], *[g_r.at[k] for k in range(pairs - 1)]).astype(BF)
        for j in range(pairs):
            swap(j).wait_send()
        for k in range(1, pairs):
            onward(k).wait_send()
    for k in order:
        for copy in told(k):
            copy.wait_recv()
    for k in order:
        for copy in ask(k) + tell(k):
            copy.wait_send()


def reduce_over_seq(wide_part, thin_part, collective_id, grads=None):
    dp, seq = lax.axis_size("dp"), lax.axis_size("seq")
    tokens, cols = wide_part.shape
    thin_part = jnp.swapaxes(thin_part.reshape(-1, seq, tokens // seq), 0, 1)
    dma, vmem, shape = pltpu.SemaphoreType.DMA, pltpu.VMEM, jax.ShapeDtypeStruct
    here = pl.BlockSpec(memory_space=pltpu.VMEM)
    rows, few, pairs = tokens // seq, thin_part.shape[1:], dp // 2
    ins, in_specs = [wide_part.astype(BF), thin_part], [here] * 2
    outs = [shape((tokens, cols), BF), shape(thin_part.shape, F32)]
    scratch = [
        vmem((seq - 1, rows, cols), BF), vmem((seq - 1,) + few, F32), vmem((rows, cols), BF), vmem(few, F32),
    ] + [dma((seq - 1,))] * 8
    if grads is not None:
        ins, in_specs = ins + [grads], in_specs + any_specs(1)
        outs.append(shape(grads.shape[1:], BF))
        scratch += [vmem((pairs,) + grads.shape[1:], BF)] * 2 + [vmem((pairs - 1,) + grads.shape[1:], BF)]
        scratch += [dma((pairs,))] * 5
    out = pl.pallas_call(
        functools.partial(reduce_kernel, dp, seq, grads is not None),
        in_specs=in_specs,
        out_specs=[here] * len(outs),
        out_shape=outs,
        scratch_shapes=scratch,
        compiler_params=pltpu.CompilerParams(
            collective_id=collective_id, has_side_effects=True, vmem_limit_bytes=24 << 20
        ),
        name="reduce_seq",
    )(*ins)
    return (out[0], jnp.swapaxes(out[1], 0, 1).reshape(-1, tokens)) + tuple(out[2:])


def homes_back(dp, seq):
    pairs = []
    for d in range(dp):
        for s in range(seq):
            home_d, home_s = 2 * (d // 2) + s % 2, (seq // 2) * (d % 2) + s // 2
            pairs.append((home_d * seq + home_s, d * seq + s))
    return pairs


def local(
    hidden_in,
    doc_lengths,
    norm_gain,
    in_weight,
    conv_weight,
    conv_bias,
    x_weight,
    dt_weight,
    dt_bias,
    skip_gain,
    out_weight,
    out_cotangent,
):
    seqs, part_len, width = hidden_in.shape
    dp, seq = lax.axis_size("dp"), lax.axis_size("seq")
    length = part_len * seq
    tokens = seqs * length
    rows = out_weight.shape[0]
    channels = rows * dp
    lag_max = KCONV - 1

    vectors = [conv_weight, conv_bias[None], dt_bias[None], skip_gain[None]]
    vectors = jnp.pad(jnp.concatenate(vectors, axis=0), ((0, 16 - KCONV - 3), (0, 0)))
    parts = [out_weight, x_weight, dt_weight, vectors]
    hidden, w_in, parts, normed, pre = gather(hidden_in, in_weight, parts, norm_gain)
    cot, pre = lax.optimization_barrier((out_cotangent, pre))
    cot = lax.all_gather(cot, "seq", axis=1, tiled=True).reshape(tokens, width)

    w_out, w_x, w_dt = (part.reshape(channels, part.shape[2]) for part in parts[:3])
    vectors = jnp.swapaxes(parts[3], 0, 1).reshape(16, channels).astype(F32)
    taps, conv_shift, rate_shift, skip = vectors[:KCONV], vectors[KCONV], vectors[KCONV + 1], vectors[KCONV + 2]

    begins, places = token_begins(doc_lengths, length)
    keep = (places[None, :] != begins).astype(F32).reshape(tokens, 1)
    valid = [(places[None, :] - (lag_max - w) >= begins)[:, :, None] for w in range(KCONV)]

    x_inner = pre[:, :channels].reshape(seqs, length, channels)

    padded = jnp.pad(x_inner, ((0, 0), (lag_max, 0), (0, 0)))
    conv_sum = jnp.broadcast_to(conv_shift, (seqs, length, channels))
    for w in range(KCONV):
        window = padded[:, w : w + length, :].astype(F32)
        conv_sum = conv_sum + jnp.where(valid[w], window * taps[w], 0.0)
    conv_flat = conv_sum.reshape(tokens, channels)
    xc_low = jax.nn.silu(conv_flat).astype(BF)
    rate, thin = reduce_over_seq(mm(xc_low, w_x[:, :R], NN), mm(w_x[:, R:], xc_low, ((0,), (1,))), 2)
    key, query = thin[:N].T, thin[N:].T
    key_lanes, query_lanes = (
        jnp.broadcast_to(part.astype(BF)[:, :, None], (tokens, N, LANES)) for part in (key, query)
    )
    ksum = jnp.sum(key * key, axis=1, keepdims=True)
    keep_lanes = jnp.broadcast_to(keep, (tokens, LANES))
    ksum_lanes = jnp.broadcast_to(ksum, (tokens, LANES))
    vectors = jnp.pad(jnp.stack([rate_shift, skip]), ((0, 6), (0, 0)))
    states, y_full, gated = scan_forward(
        seqs, length, xc_low, pre, rate, key_lanes, query_lanes, keep_lanes, ksum_lanes, w_dt, vectors
    )
    branch = mm(gated, w_out, NN).astype(BF).reshape(seqs, length, width)
    branch = lax.psum_scatter(branch, "seq", scatter_dimension=1, tiled=True)
    output = (hidden_in.astype(F32) + branch.astype(F32)).astype(BF)

    d_z, rest, dq, dk, d_norm, d_row, grad_dt, sums = scan_backward(
        seqs, length, mm(cot, w_out, NT), y_full, xc_low, pre, rate, key_lanes, query_lanes, keep_lanes, ksum_lanes, w_dt, vectors, states
    )
    dq, dk = dq.reshape(tokens, N), dk.reshape(tokens, N)
    d_norm = -jnp.sum(d_norm, axis=1, keepdims=True)
    d_keys = dk + 2.0 * key * d_norm
    grad_out = mm(gated, cot, TN).astype(BF).reshape(dp, rows, width)
    d_row, thin, grad_out = reduce_over_seq(d_row, jnp.concatenate([d_keys.T, dq.T], axis=0), 3, grad_out)
    grad_out = lax.ppermute(grad_out, ("dp", "seq"), homes_back(dp, seq))
    d_proj = jnp.concatenate([d_row, thin.T.astype(BF)], axis=1)
    d_conv_out = mm(d_proj, w_x, NT) + rest
    d_conv = (d_conv_out * silu_slope(conv_flat)).reshape(seqs, length, channels)

    tap_grads = []
    d_x_inner = jnp.zeros((seqs, length, channels), F32)
    for w in range(KCONV):
        lag = lag_max - w
        window = padded[:, w : w + length, :].astype(F32)
        masked = jnp.where(valid[w], d_conv, 0.0)
        tap_grads.append(jnp.sum(masked * window, axis=(0, 1)))
        d_x_inner = d_x_inner + jnp.pad(masked, ((0, 0), (0, lag), (0, 0)))[:, lag:, :] * taps[w]
    vector_grads = jnp.stack(
        tap_grads + [jnp.sum(d_conv, axis=(0, 1)), jnp.sum(sums[:8], axis=0), jnp.sum(sums[8:], axis=0)], axis=0
    )
    vector_grads = jnp.pad(vector_grads, ((0, 16 - KCONV - 3), (0, 0))).reshape(16, dp, rows)
    grads = [part.astype(BF).reshape(dp, rows, -1) for part in (mm(xc_low, d_proj, TN), grad_dt)]
    grads.append(jnp.swapaxes(vector_grads, 0, 1).astype(BF))
    grad_in, grad_in_weight, grads, grad_norm_gain = scatter(
        d_x_inner.reshape(tokens, channels).astype(BF), d_z, normed, w_in, hidden, grads,
        hidden_in, out_cotangent, norm_gain,
    )
    grad_x, grad_dt, grad_vectors = (part.astype(F32) for part in grads)
    grad_out_weight = grad_out.astype(F32)
    return (
        output,
        grad_in,
        grad_norm_gain,
        grad_in_weight,
        grad_vectors[:KCONV],
        grad_vectors[KCONV],
        grad_x,
        grad_dt,
        grad_vectors[KCONV + 1],
        grad_vectors[KCONV + 2],
        grad_out_weight,
    )


def solution(mesh):
    both = ("dp", "seq")
    tokens = P("dp", "seq", None)
    matrix, vector = P(both, None), P(both)
    return jax.shard_map(
        local,
        mesh=mesh,
        in_specs=(
            tokens, P("dp", None), P(), matrix, P(None, both), vector,
            matrix, matrix, vector, vector, matrix, tokens,
        ),
        out_specs=(
            tokens, tokens, P(), matrix, P(None, both), vector,
            matrix, matrix, vector, vector, matrix,
        ),
        check_vma=False,
    )
```

```python
import functools
import math

import jax
import jax.numpy as jnp
from jax import lax
from jax.experimental import pallas as pl
from jax.experimental.pallas import tpu as pltpu
from jax.sharding import PartitionSpec as P

N = 16
R = 128
KCONV = 4
CHUNK = 16
LANES = 128
GROUP = 1024
BLOCK = 128

norm_eps = 1e-05
BF = jnp.bfloat16
F32 = jnp.float32


def silu_slope(pre_value):
    sigmoid_of = jax.nn.sigmoid(pre_value)
    return sigmoid_of * (1.0 + pre_value * (1.0 - sigmoid_of))


def token_begins(lengths, position_count):
    doc_ends = jnp.cumsum(lengths, axis=1)
    doc_starts = doc_ends - lengths
    places = jnp.arange(position_count, dtype=jnp.int32)
    inside = doc_starts[:, None, :] <= places[None, :, None]
    return (jnp.max(jnp.where(inside, doc_starts[:, None, :], 0), axis=2), places)


def mm(left, right, dims):
    return lax.dot_general(left, right, (dims, ((), ())), preferred_element_type=F32)


NN = ((1,), (0,))
NT = ((1,), (1,))
TN = ((0,), (0,))


def row(ref, i, lane):
    return jnp.broadcast_to(ref[i : i + 1, pl.ds(lane, LANES)], (8, LANES))


def wide(ref, rows, count):
    value = ref[rows, :]
    return jnp.concatenate([value] * (count // LANES), axis=1)


def merge(even, odd, stride):
    low = lax.broadcasted_iota(jnp.int32, (8, LANES), 0) % (2 * stride) < stride
    if stride == 4:
        return jnp.where(low, even, odd) + pltpu.roll(jnp.where(low, odd, even), 4, 0)
    return jnp.where(low, even + pltpu.roll(even, 8 - stride, 0), odd + pltpu.roll(odd, stride, 0))


def collect(stack, value, descending):
    level = 0
    while stack and stack[-1][0] == level:
        other = stack.pop()[1]
        value = merge(value, other, 1 << level) if descending else merge(other, value, 1 << level)
        level += 1
    stack.append((level, value))


def each_chunk(tokens, channels, body):
    group = math.gcd(channels, 512)

    def run(k, carried):
        rows = pl.ds(pl.multiple_of(k * CHUNK, CHUNK), CHUNK)
        for first in range(0, channels, group):
            body(rows, pl.ds(first, group), first)
        return carried

    lax.fori_loop(0, tokens // CHUNK, run, 0)


def load_carry(carry, tiles):
    out = []
    for lane in tiles:
        out += [carry[0:8, pl.ds(lane, LANES)], carry[8:16, pl.ds(lane, LANES)]]
    return tuple(out)


def store_carry(carry, tiles, values):
    for j, lane in enumerate(tiles):
        carry[0:8, pl.ds(lane, LANES)] = values[2 * j]
        carry[8:16, pl.ds(lane, LANES)] = values[2 * j + 1]


def halves(value):
    return [value[0:8], value[8:16]]


def token(keys, queries, keeps, i):
    return row(keeps, i, 0), halves(keys[i].astype(F32)), halves(queries[i].astype(F32))


def lane_groups(channels):
    group = math.gcd(channels, GROUP)
    return [list(range(first, first + group, LANES)) for first in range(0, channels, group)]


def forward_kernel(
    xc_ref, z_ref, rate_ref, key_ref, query_ref, keep_ref, ksum_ref, wdt_ref, vec_ref,
    s_ref, y_ref, gated_ref, step, inj, carry,
):
    @pl.when(pl.program_id(1) == 0)
    def _():
        carry[...] = jnp.zeros_like(carry)

    tokens, channels = xc_ref.shape
    step[...] = mm(rate_ref[...], wdt_ref[...], NT)

    def prepare(rows, cols, first):
        beta = jax.nn.sigmoid(step[rows, cols] + vec_ref[0:1, cols])
        eps = beta / (1.0 + beta * wide(ksum_ref, rows, cols.size))
        step[rows, cols] = eps
        inj[rows, cols] = eps * xc_ref[rows, cols].astype(F32)

    each_chunk(tokens, channels, prepare)
    for tiles in lane_groups(channels):

        def chunk(k, state):
            state = list(state)
            base = pl.multiple_of(k * CHUNK, CHUNK)
            steps, injs, keeps, keys, queries = (
                r.at[pl.ds(base, CHUNK)] for r in (step, inj, keep_ref, key_ref, query_ref)
            )
            saved = s_ref.at[pl.ds(pl.multiple_of(k * CHUNK * N, CHUNK * N), CHUNK * N)]
            stacks = [[] for _ in tiles]
            for i in range(CHUNK):
                keep, key, query = token(keys, queries, keeps, i)
                ksq = [keep * key[h] * key[h] for h in range(2)]
                for j, lane in enumerate(tiles):
                    eps, push = row(steps, i, lane), row(injs, i, lane)
                    for h in range(2):
                        state[2 * j + h] = (keep - eps * ksq[h]) * state[2 * j + h] + push * key[h]
                    both = jnp.concatenate([state[2 * j], state[2 * j + 1]], axis=0)
                    saved[i * N : (i + 1) * N, pl.ds(lane, LANES)] = both.astype(BF)
                    collect(stacks[j], state[2 * j] * query[0] + state[2 * j + 1] * query[1], False)
                    if i % 8 == 7:
                        y_ref[pl.ds(pl.multiple_of(base + i - 7, 8), 8), pl.ds(lane, LANES)] = stacks[j].pop()[1]
            return tuple(state)

        store_carry(carry, tiles, lax.fori_loop(0, tokens // CHUNK, chunk, load_carry(carry, tiles)))

    def emit(rows, cols, first):
        y_full = y_ref[rows, cols] + vec_ref[1:2, cols] * xc_ref[rows, cols].astype(F32)
        y_ref[rows, cols] = y_full
        z = z_ref[rows, cols].astype(F32)
        gated_ref[rows, cols] = (y_full * (z * jax.nn.sigmoid(z))).astype(BF)

    each_chunk(tokens, channels, emit)


def backward_kernel(
    dg_ref, y_ref, xc_ref, z_ref, rate_ref, key_ref, query_ref, keep_ref, ksum_ref, wdt_ref, vec_ref, s_ref, before_ref,
    dz_ref, rest_ref, dq_ref, dk_ref, dnorm_ref, drow_ref, gdt_ref, sums_ref,
    step, inj, dy, mix, pull, beta, drate, carry, acc_q, acc_k,
):
    turn = pl.program_id(1)
    tokens, channels = xc_ref.shape
    chunks = tokens // CHUNK

    @pl.when(jnp.logical_and(pl.program_id(0) == 0, turn == 0))
    def _():
        gdt_ref[...] = jnp.zeros_like(gdt_ref)
        sums_ref[...] = jnp.zeros_like(sums_ref)

    @pl.when(turn == 0)
    def _():
        carry[...] = jnp.zeros_like(carry)

    beta[...] = mm(rate_ref[...], wdt_ref[...], NT)

    def prepare(rows, cols, first):
        rate_beta = jax.nn.sigmoid(beta[rows, cols] + vec_ref[0:1, cols])
        eps = rate_beta / (1.0 + rate_beta * wide(ksum_ref, rows, cols.size))
        beta[rows, cols] = rate_beta
        step[rows, cols] = eps
        xc = xc_ref[rows, cols].astype(F32)
        inj[rows, cols] = eps * xc
        z = z_ref[rows, cols].astype(F32)
        sig = jax.nn.sigmoid(z)
        d_gated = dg_ref[rows, cols]
        d_y = d_gated * (z * sig)
        dy[rows, cols] = d_y
        dz_ref[rows, cols] = (d_gated * y_ref[rows, cols] * (sig * (1.0 + z * (1.0 - sig)))).astype(BF)
        weighted = d_y * xc
        sums_ref[8:16, cols] += weighted[0:8] + weighted[8:16]

    each_chunk(tokens, channels, prepare)
    for tiles in lane_groups(channels):
        start = tiles[0] == 0

        def chunk(back, carried):
            k = chunks - 1 - back
            pulled, now = list(carried[0]), list(carried[1])
            base = pl.multiple_of(k * CHUNK, CHUNK)
            steps, injs, dys, keeps, keys, queries = (
                r.at[pl.ds(base, CHUNK)] for r in (step, inj, dy, keep_ref, key_ref, query_ref)
            )
            stacks = [([], []) for _ in tiles]
            for i in reversed(range(CHUNK)):
                keep, key, query = token(keys, queries, keeps, i)
                kept = [keep * key[h] for h in range(2)]
                ksq = [kept[h] * key[h] for h in range(2)]
                if i > 0:
                    before = pl.ds(pl.multiple_of((base + i) * N - N, N), N)
                else:
                    before = pl.ds(pl.multiple_of(jnp.maximum(base * N - N, 0), N), N)
                seen, plain, scaled = [0.0, 0.0], [0.0, 0.0], [0.0, 0.0]
                for j, lane in enumerate(tiles):
                    eps, push, d_y = row(steps, i, lane), row(injs, i, lane), row(dys, i, lane)
                    prior = s_ref[before, pl.ds(lane, LANES)]
                    if i == 0:
                        prior = jnp.where(k > 0, prior, before_ref[:, pl.ds(lane, LANES)])
                    prior = halves(prior.astype(F32))
                    by_key, by_square = [], []
                    for h in range(2):
                        at = 2 * j + h
                        grad = pulled[at] + d_y * query[h]
                        pulled[at] = (keep - eps * ksq[h]) * grad
                        keyed = eps * (grad * key[h])
                        prod = keyed * prior[h]
                        seen[h] += now[at] * d_y
                        plain[h] += grad * push
                        scaled[h] += prod
                        by_key.append(keyed)
                        by_square.append(prod * kept[h])
                        now[at] = prior[h]
                    collect(stacks[j][0], by_key[0] + by_key[1], True)
                    collect(stacks[j][1], by_square[0] + by_square[1], True)
                    if i % 8 == 0:
                        rows = pl.ds(pl.multiple_of(base + i, 8), 8)
                        mix[rows, pl.ds(lane, LANES)] = stacks[j][0].pop()[1]
                        pull[rows, pl.ds(lane, LANES)] = stacks[j][1].pop()[1]
                for ref, parts in ((acc_q, seen), (acc_k, [plain[h] - 2.0 * keep * scaled[h] for h in range(2)])):
                    for h in range(2):
                        rows = pl.ds(pl.multiple_of((base + i) * N + 8 * h, 8), 8)
                        if start:
                            ref[rows, :] = parts[h]
                        else:
                            ref[rows, :] += parts[h]
            return (tuple(pulled), tuple(now))

        now = []
        for lane in tiles:
            now += halves(s_ref[tokens * N - N : tokens * N, pl.ds(lane, LANES)].astype(F32))
        pulled, now = lax.fori_loop(0, chunks, chunk, (load_carry(carry, tiles), tuple(now)))
        store_carry(carry, tiles, pulled)

    ones = jnp.ones((LANES, LANES), BF)
    diagonal = lax.broadcasted_iota(jnp.int32, (LANES, LANES), 0) == (
        lax.broadcasted_iota(jnp.int32, (LANES, LANES), 1)
    )
    for out, ref in ((dq_ref, acc_q), (dk_ref, acc_k)):
        for first in range(0, tokens * N, LANES):
            sums = mm(ref[first : first + LANES, :].astype(BF), ones, NN)
            at = first // LANES
            out[at : at + 1, :] = jnp.sum(jnp.where(diagonal, sums, 0.0), axis=0, keepdims=True)

    def settle(rows, cols, first):
        rate_beta, eps = beta[rows, cols], step[rows, cols]
        through = mix[rows, cols]
        change = through * xc_ref[rows, cols].astype(F32) - pull[rows, cols]
        inverse = 1.0 / (1.0 + rate_beta * wide(ksum_ref, rows, cols.size))
        low = (change * inverse * (1.0 - rate_beta)).astype(BF)
        drate[rows, cols] = low
        lowered = low.astype(F32)
        sums_ref[0:8, cols] += lowered[0:8] + lowered[8:16]
        rest_ref[rows, cols] = through + vec_ref[1:2, cols] * dy[rows, cols]
        square = change * eps
        total = square[:, 0:LANES]
        for lane in range(LANES, cols.size, LANES):
            total = total + square[:, lane : lane + LANES]
        if first == 0:
            dnorm_ref[rows, :] = total
        else:
            dnorm_ref[rows, :] += total

    each_chunk(tokens, channels, settle)
    drow_ref[...] = mm(drate[...], wdt_ref[...], NN)
    gdt_ref[...] += mm(drate[...], rate_ref[...], TN)


def scan_blocks(length):
    block = math.gcd(length, BLOCK)
    return block, length // block


def row_spec(rows, cols, when, col=0):
    return pl.BlockSpec((rows, cols), lambda b, t: (when(b, t), col))


def spread_spec(block, when):
    return pl.BlockSpec((block, N, LANES), lambda b, t: (when(b, t), 0, 0))


def whole(array):
    return pl.BlockSpec(array.shape, lambda b, t: (0, 0), pipeline_mode=pl.Buffered(1))


def scan_forward(seqs, length, xc, pre, rate, key_lanes, query_lanes, keep_lanes, ksum_lanes, w_dt, vectors):
    tokens, channels = xc.shape
    block, blocks = scan_blocks(length)

    def at(b, t):
        return b * blocks + t

    rows = row_spec(block, channels, at)
    lanes = row_spec(block, LANES, at)
    vmem = pltpu.VMEM
    return pl.pallas_call(
        forward_kernel,
        grid=(seqs, blocks),
        in_specs=[
            rows, row_spec(block, channels, at, 1), row_spec(block, R, at),
            spread_spec(block, at), spread_spec(block, at), lanes, lanes, whole(w_dt), whole(vectors),
        ],
        out_specs=[row_spec(block * N, channels, at), rows, rows],
        out_shape=[
            jax.ShapeDtypeStruct((tokens * N, channels), BF),
            jax.ShapeDtypeStruct((tokens, channels), F32),
            jax.ShapeDtypeStruct((tokens, channels), BF),
        ],
        scratch_shapes=[vmem((block, channels), F32), vmem((block, channels), F32), vmem((N, channels), F32)],
        cost_estimate=pl.CostEstimate(
            flops=tokens * channels * N * 60, bytes_accessed=tokens * channels * 44, transcendentals=0
        ),
        compiler_params=pltpu.CompilerParams(vmem_limit_bytes=40 << 20),
        name="scan_forward",
    )(xc, pre, rate, key_lanes, query_lanes, keep_lanes, ksum_lanes, w_dt, vectors)


def scan_backward(seqs, length, d_gated, y, xc, pre, rate, key_lanes, query_lanes, keep_lanes, ksum_lanes, w_dt, vectors, states):
    tokens, channels = xc.shape
    block, blocks = scan_blocks(length)

    def at(b, t):
        return b * blocks + blocks - 1 - t

    def prior(b, t):
        return (jnp.maximum(at(b, t) * block - 1, 0), 0)

    rows = row_spec(block, channels, at)
    lanes = row_spec(block, LANES, at)
    flat = row_spec(block * N // LANES, LANES, at)
    vmem = pltpu.VMEM
    wide_f32 = vmem((block, channels), F32)
    return pl.pallas_call(
        backward_kernel,
        grid=(seqs, blocks),
        in_specs=[
            rows, rows, rows, row_spec(block, channels, at, 1), row_spec(block, R, at),
            spread_spec(block, at), spread_spec(block, at), lanes, lanes, whole(w_dt), whole(vectors),
            row_spec(block * N, channels, at), pl.BlockSpec((N, channels), prior),
        ],
        out_specs=[
            rows, rows, flat, flat, lanes, row_spec(block, R, at),
            pl.BlockSpec((channels, R), lambda b, t: (0, 0)), pl.BlockSpec((16, channels), lambda b, t: (0, 0)),
        ],
        out_shape=[
            jax.ShapeDtypeStruct((tokens, channels), BF),
            jax.ShapeDtypeStruct((tokens, channels), F32),
            jax.ShapeDtypeStruct((tokens * N // LANES, LANES), F32),
            jax.ShapeDtypeStruct((tokens * N // LANES, LANES), F32),
            jax.ShapeDtypeStruct((tokens, LANES), F32),
            jax.ShapeDtypeStruct((tokens, R), F32),
            jax.ShapeDtypeStruct((channels, R), F32),
            jax.ShapeDtypeStruct((16, channels), F32),
        ],
        scratch_shapes=[
            wide_f32, wide_f32, wide_f32, wide_f32, wide_f32, wide_f32, vmem((block, channels), BF),
            vmem((N, channels), F32), vmem((block * N, LANES), F32), vmem((block * N, LANES), F32),
        ],
        cost_estimate=pl.CostEstimate(
            flops=tokens * channels * N * 100, bytes_accessed=tokens * channels * 56, transcendentals=0
        ),
        compiler_params=pltpu.CompilerParams(vmem_limit_bytes=48 << 20),
        name="scan_backward",
    )(d_gated, y, xc, pre, rate, key_lanes, query_lanes, keep_lanes, ksum_lanes, w_dt, vectors, states, states)


MESH = pl.DeviceIdType.MESH


def any_specs(count):
    return [pl.BlockSpec(memory_space=pl.ANY)] * count


def place():
    return lax.axis_index("dp"), lax.axis_index("seq")


def mate(d):
    return d + 1 - 2 * lax.rem(d, 2)


def forward_home(d, s, seq):
    return 2 * (d // 2) + lax.rem(s, 2), (seq // 2) * lax.rem(d, 2) + s // 2


def backward_home(d, s, seq):
    return 2 * (d // 2) + s // (seq // 2), 2 * lax.rem(s, seq // 2) + lax.rem(d, 2)


def remote(src, dst, send, recv, device):
    return pltpu.make_async_remote_copy(
        src_ref=src, dst_ref=dst, send_sem=send, recv_sem=recv, device_id=device, device_id_type=MESH
    )


def greet(device, here=True):
    barrier = pltpu.get_barrier_semaphore()

    def tell():
        pl.semaphore_signal(barrier, inc=1, device_id=device, device_id_type=MESH)

    if here is True:
        tell()
    else:
        pl.when(here)(tell)


PARTS = 4


def gather_kernel(dp, seq, fused, *refs):
    refs = list(refs)

    def take(count):
        out = refs[:count]
        del refs[:count]
        return out

    hid_ref, w_ref = take(2)
    parts = take(PARTS)
    gain_ref = take(1)[0] if fused else None
    hid_out, w_out = take(2)
    slots = take(PARTS)
    normed_out, pre_out = take(2) if fused else (None, None)
    z_send, z_recv, w_send, w_recv, f_send, f_recv, p_send, p_recv, q_send, q_recv, t_send, t_recv, own_sem = take(13)
    d, s = place()
    part = hid_ref.shape[1]
    pieces = z_send.shape[2]
    piece = part // pieces
    pairs = dp // 2
    to_d, to_s = forward_home(d, s, seq)
    from_d, from_s = backward_home(d, s, seq)
    moves = jnp.logical_or(to_d != d, to_s != s)

    greet((d, s - 1), s > 0)
    greet((d, s + 1), s < seq - 1)
    for k in range(1, pairs):
        greet((lax.rem(d + 2 * k, dp), s))
    greet((mate(d), s))
    greet((to_d, to_s), moves)
    greet((from_d, from_s), moves)
    count = pairs + jnp.where(s > 0, 1, 0) + jnp.where(s < seq - 1, 1, 0) + jnp.where(moves, 2, 0)
    pl.semaphore_wait(pltpu.get_barrier_semaphore(), count)

    def shard(which, q):
        return hid_out.at[:, pl.ds(which * part + q * piece, piece), :]

    def hop(way, k, q):
        which = s - k if way == 0 else s + k
        src = hid_ref.at[:, pl.ds(q * piece, piece), :] if k == 0 else shard(which, q)
        near = s + 1 if way == 0 else s - 1
        return remote(src, shard(which, q), z_send.at[way, k, q], z_recv.at[way, k, q], (d, near))

    def can_send(way, k):
        if way == 0:
            return jnp.logical_and(s - k >= 0, s < seq - 1)
        return jnp.logical_and(s + k < seq, s > 0)

    def landed(way, k, q):
        which = jnp.where(way == 0, s - k, s + k)
        here = shard(which, q)
        remote(here, here, z_send.at[way, k - 1, q], z_recv.at[way, k - 1, q], (d, s)).wait_recv()

    def spread(out, own, send, recv, k):
        return remote(own, out.at[d], send.at[k], recv.at[k], (lax.rem(d + 2 * k, dp), s))

    def source(k):
        return lax.rem(d - 2 * k + dp, dp)

    def across(out, send, recv, k, own=None):
        return remote(own if k == 0 else out.at[source(k)], out.at[source(k)], send.at[k], recv.at[k], (mate(d), s))

    for q in range(pieces):
        for way in range(2):
            pl.when(can_send(way, 0))(hop(way, 0, q).start)
    transfers = [remote(parts[m], slots[m].at[to_d], t_send.at[m], t_recv.at[m], (to_d, to_s)) for m in range(PARTS)]
    stays = [pltpu.make_async_copy(parts[m], slots[m].at[d], own_sem.at[2 + m]) for m in range(PARTS)]
    for m in range(PARTS):
        pl.when(moves)(transfers[m].start)
        pl.when(jnp.logical_not(moves))(stays[m].start)
    for k in range(1, pairs):
        spread(w_out, w_ref, w_send, w_recv, k).start()
    across(w_out, f_send, f_recv, 0, w_ref).start()
    own_w = pltpu.make_async_copy(w_ref, w_out.at[d], own_sem.at[0])
    own_h = pltpu.make_async_copy(hid_ref, hid_out.at[:, pl.ds(s * part, part), :], own_sem.at[1])
    own_w.start()
    own_h.start()

    for k in range(1, seq - 1):
        for q in range(pieces):
            for way in range(2):
                pl.when(s - k >= 0 if way == 0 else s + k < seq)(functools.partial(landed, way, k, q))
                pl.when(can_send(way, k))(hop(way, k, q).start)
    own_w.wait()
    own_h.wait()
    w_flow = (w_out, w_ref, w_send, w_recv, f_send, f_recv)
    part_flows = [
        (slots[m], slots[m].at[d], p_send.at[m], p_recv.at[m], q_send.at[m], q_recv.at[m]) for m in range(PARTS)
    ]

    def relay(out, own, send, recv, over_send, over_recv):
        for k in range(1, pairs):
            here = out.at[source(k)]
            remote(here, here, send.at[k], recv.at[k], (d, s)).wait_recv()
            across(out, over_send, over_recv, k).start()

    def complete(out, own, send, recv, over_send, over_recv):
        for k in range(pairs):
            here = out.at[lax.rem(mate(d) - 2 * k + dp, dp)]
            remote(here, here, over_send.at[k], over_recv.at[k], (d, s)).wait_recv()

    relay(*w_flow)
    for m in range(PARTS):
        slot = slots[m].at[d]
        pl.when(moves)(remote(parts[m], slot, t_send.at[m], t_recv.at[m], (to_d, to_s)).wait_recv)
        pl.when(jnp.logical_not(moves))(stays[m].wait)
        for k in range(1, pairs):
            spread(slots[m], slot, p_send.at[m], p_recv.at[m], k).start()
        across(slots[m], q_send.at[m], q_recv.at[m], 0, slot).start()

    complete(*w_flow)

    def relay_parts():
        for flow in part_flows:
            relay(*flow)

    last = seq - 1
    if fused:
        w_all, x_buf, w_sem, x_sem = take(4)
        width, columns = x_buf.shape[1], pre_out.shape[1]
        cut = math.gcd(columns, 512)
        fetch_w = pltpu.make_async_copy(w_out, w_all, w_sem)
        fetch_w.start()
        fetch_w.wait()

        def project(which, k, way):
            here = pl.multiple_of(which * part, part)
            for q in range(pieces):
                pl.when(k == last)(functools.partial(landed, way, last, q))
                fetch = pltpu.make_async_copy(
                    hid_out.at[0, pl.ds(which * part + q * piece, piece)], x_buf.at[pl.ds(q * piece, piece)], x_sem
                )
                fetch.start()
                fetch.wait()
                x = x_buf[pl.ds(q * piece, piece), :].astype(F32)
                inv = lax.rsqrt(jnp.mean(x * x, axis=1, keepdims=True) + norm_eps)
                rows = pl.ds(pl.multiple_of(here + q * piece, piece), piece)
                normed_out[rows, :] = (x * inv * gain_ref[...].astype(F32)).astype(BF)

            def matmul(at, carried):
                cols = pl.ds(pl.multiple_of(at * cut, cut), cut)
                w_rows = w_all.shape[1]
                block = w_all[pl.ds(at * (cut // w_rows), cut // w_rows)].reshape(cut, width)
                pre_out[pl.ds(here, part), cols] = mm(normed_out[pl.ds(here, part), :], block, NT).astype(BF)
                return carried

            lax.fori_loop(0, columns // cut, matmul, 0)

        def visit(m, carried):
            k = (m + 1) // 2
            way = lax.rem(m, 2)
            which = jnp.where(way == 0, s - k, s + k)
            pl.when(m == 2 * seq - 3)(relay_parts)

            @pl.when(jnp.logical_and(which >= 0, which < seq))
            def _():
                project(which, k, way)

            return carried

        lax.fori_loop(0, 2 * seq - 1, visit, 0)
    else:
        for q in range(pieces):
            for way in range(2):
                pl.when(s - last >= 0 if way == 0 else s + last < seq)(functools.partial(landed, way, last, q))
        relay_parts()

    for flow in part_flows:
        complete(*flow)
    for out, own, send, recv, over_send, over_recv in [w_flow, *part_flows]:
        for k in range(pairs):
            across(out, over_send, over_recv, k, own).wait_send()
        for k in range(1, pairs):
            spread(out, own, send, recv, k).wait_send()
    for k in range(seq - 1):
        for q in range(pieces):
            for way in range(2):
                pl.when(can_send(way, k))(hop(way, k, q).wait_send)
    for m in range(PARTS):
        pl.when(moves)(transfers[m].wait_send)


def fits_whole(seqs, length, width, channels):
    return seqs == 1 and length % 256 == 0 and length * (width + channels) + channels * width <= 6 << 20


def gather(hidden, weight, parts, norm_gain, collective_id=0):
    dp, seq = lax.axis_size("dp"), lax.axis_size("seq")
    seqs, part, width = hidden.shape
    columns = weight.shape[0] * dp
    fused = fits_whole(seqs, part * seq, width, columns // 2)
    pieces = 4 if part % 64 == 0 else 1
    dma, vmem, pairs = pltpu.SemaphoreType.DMA, pltpu.VMEM, dp // 2
    shape = jax.ShapeDtypeStruct
    outs = [shape((seqs, part * seq, width), BF), shape((dp,) + weight.shape, BF)]
    outs += [shape((dp,) + member.shape, BF) for member in parts]
    scratch = [dma((2, seq, pieces)), dma((2, seq, pieces))] + [dma((pairs,))] * 4
    scratch += [dma((PARTS, pairs))] * 4 + [dma((PARTS,)), dma((PARTS,)), dma((2 + PARTS,))]
    ins, in_specs = [hidden, weight, *parts], any_specs(2 + PARTS)
    out_specs = any_specs(2 + PARTS)
    if fused:
        ins.append(norm_gain.reshape(1, width))
        in_specs = in_specs + [pl.BlockSpec(memory_space=pltpu.VMEM)]
        outs += [shape((part * seq, width), BF), shape((part * seq, columns), BF)]
        scratch += [
            vmem((dp,) + weight.shape, BF), vmem((part, width), BF), dma, dma,
        ]
        out_specs = out_specs + [pl.BlockSpec(memory_space=pltpu.VMEM)] * 2
    out = pl.pallas_call(
        functools.partial(gather_kernel, dp, seq, fused),
        in_specs=in_specs,
        out_specs=out_specs,
        out_shape=outs,
        scratch_shapes=scratch,
        compiler_params=pltpu.CompilerParams(
            collective_id=collective_id, has_side_effects=True, vmem_limit_bytes=44 << 20
        ),
        name="gather_in",
    )(*ins)
    hidden = out[0].reshape(-1, width)
    w_in = out[1].reshape(columns, width)
    if fused:
        return hidden, w_in, out[2 : 2 + PARTS], out[-2], out[-1]
    x = hidden.astype(F32)
    inv = lax.rsqrt(jnp.mean(x * x, axis=1, keepdims=True) + norm_eps)
    normed = (x * inv * norm_gain.astype(F32)).astype(BF)
    return hidden, w_in, out[2:], normed, mm(normed, w_in, NT).astype(BF)


def added(ref, *others):
    total = ref[...].astype(F32)
    for other in others:
        total = total + other[...].astype(F32)
    return total


def scatter_kernel(dp, seq, count, fused, *refs):
    refs = list(refs)

    def take(count):
        out = refs[:count]
        del refs[:count]
        return out

    if fused:
        dx_ref, dz_ref, normed_ref, w_ref, full_ref = take(5)
        dn_ref = gw_ref = None
    else:
        dn_ref, gw_ref, gain_ref = take(3)
    parts = take(count)
    hid_ref, cot_ref, scale_ref = take(3)
    out_ref, gw_out = take(2)
    part_outs = take(count)
    gain_out = take(1)[0]
    own, come, gw_own, gw_x, gw_r = take(5)
    p_own, p_x, p_r, p_fin = take(count), take(count), take(count), take(count)
    g_in, g_one, g_x, g_r, g_z, g_a, g_b = take(7)
    z_load, z_send, z_recv, w_load, wx_send, wx_recv, w_send, w_recv = take(8)
    p_load, px_send, px_recv, p_send, p_recv, t_send, t_recv, gx_sem, g_send, g_recv, gz_send, gz_recv = take(12)

    d, s = place()
    seqs, part, width = out_ref.shape
    pieces = z_send.shape[1]
    piece = part // pieces
    pairs = dp // 2
    mine, odd = d // 2, lax.rem(d, 2)
    to_d, to_s = backward_home(d, s, seq)
    from_d, from_s = forward_home(d, s, seq)
    moves = jnp.logical_or(to_d != d, to_s != s)

    for k in range(1, seq):
        greet((d, lax.rem(s + k, seq)))
    for k in range(1, pairs):
        greet((lax.rem(d + 2 * k, dp), s))
    greet((mate(d), s))
    greet((to_d, to_s), moves)
    greet((from_d, from_s), moves)
    pl.semaphore_wait(pltpu.get_barrier_semaphore(), seq - 1 + pairs + jnp.where(moves, 2, 0))

    def swap(src, dst, send, recv, j):
        return remote(src, dst.at[j], send.at[j], recv.at[j], (mate(d), s))

    def part_swap(m, j):
        return swap(parts[m].at[2 * j + 1 - odd], p_x[m], px_send.at[m], px_recv.at[m], j)

    def part_fetch(m, j):
        return pltpu.make_async_copy(parts[m].at[2 * j + odd], p_own[m].at[j], p_load.at[m, j])

    for m in range(count):
        for j in range(pairs):
            part_swap(m, j).start()
            part_fetch(m, j).start()

    if fused:
        d_pre, normed, w_all, x_buf, gw_give, f_sem, x_sem = take(7)
        channels = dx_ref.shape[1]
        loads = [
            pltpu.make_async_copy(dx_ref, d_pre.at[:, pl.ds(0, channels)], f_sem.at[0]),
            pltpu.make_async_copy(dz_ref, d_pre.at[:, pl.ds(channels, channels)], f_sem.at[1]),
            pltpu.make_async_copy(w_ref, w_all, f_sem.at[2]),
            pltpu.make_async_copy(normed_ref, normed, f_sem.at[3]),
        ]
        for copy in loads:
            copy.start()
        for copy in loads[:3]:
            copy.wait()
        g_in[...] = jnp.zeros_like(g_in)
        w_rows = gw_own.shape[1]
        half_width = width // 2

        def dn_tasks(first, last):
            def run(i, carried):
                r = jnp.where(lax.rem(i, 2) == 0, seq - 1 - i // 2, i // 2)
                rows = pl.ds(pl.multiple_of(r * part, part), part)
                fetch = pltpu.make_async_copy(full_ref.at[rows], x_buf, x_sem)
                fetch.start()
                for at in range(2):
                    cols = pl.ds(at * half_width, half_width)
                    own[r, 0, :, cols] = mm(d_pre[rows, :], w_all[:, cols], NN).astype(BF)
                fetch.wait()

                def fold(at, carried):
                    some = pl.ds(pl.multiple_of(at * 64, 64), 64)
                    x = x_buf[some, :].astype(F32)
                    inv = lax.rsqrt(jnp.mean(x * x, axis=1, keepdims=True) + norm_eps)
                    weighted = own[r, 0, some, :].astype(F32) * (x * inv)
                    g_in[...] += jnp.sum(weighted.reshape(8, 8, width), axis=0)
                    return carried

                return lax.fori_loop(0, part // 64, fold, carried)

            lax.fori_loop(first, last, run, 0)

        def gw_task(dest, out, j):
            cols = pl.ds(pl.multiple_of(dest * w_rows, w_rows), w_rows)
            for at in range(2):
                some = pl.ds(at * half_width, half_width)
                out[j, :, some] = mm(d_pre[:, cols], normed[:, some], TN).astype(BF)

        def gw_swap(j):
            return swap(gw_give.at[j], gw_x, wx_send, wx_recv, j)

        def gw_away():
            def run(j, carried):
                gw_task(2 * j + 1 - odd, gw_give, j)
                gw_swap(j).start()
                return carried

            lax.fori_loop(0, pairs, run, 0)

        def gw_home():
            def run(k, carried):
                j = lax.rem(mine + 1 + k, pairs)
                gw_task(2 * j + odd, gw_own, j)
                return carried

            lax.fori_loop(0, pairs, run, 0)

        def gw_ready(j):
            pass
    else:
        def gw_swap(j):
            return swap(gw_ref.at[2 * j + 1 - odd], gw_x, wx_send, wx_recv, j)

        def gw_fetch(j):
            return pltpu.make_async_copy(gw_ref.at[2 * j + odd], gw_own.at[j], w_load.at[j])

        def chunk(r):
            return pltpu.make_async_copy(dn_ref.at[:, pl.ds(r * part, part), :], own.at[r], z_load.at[r])

        for r in range(seq):
            chunk(r).start()
        for j in range(pairs):
            gw_swap(j).start()
            gw_fetch(j).start()
        for r in range(seq):
            chunk(r).wait()
        g_in[...] = gain_ref[...]

        def gw_ready(j):
            gw_fetch(j).wait()

    def give(way, r, q):
        rows = pl.ds(q * piece, piece)
        slot = r if way == 0 else jnp.where(s - 1 == r, seq, r)
        near = s + 1 if way == 0 else s - 1
        return remote(own.at[r, :, rows, :], come.at[slot, :, rows, :], z_send.at[r, q], z_recv.at[slot, q], (d, near))

    def landed(slot, q):
        rows = pl.ds(q * piece, piece)
        here = come.at[slot, :, rows, :]
        remote(here, here, z_send.at[0, q], z_recv.at[slot, q], (d, s)).wait_recv()

    def begin():
        for q in range(pieces):
            pl.when(s == 0)(give(0, seq - 1, q).start)
            pl.when(s == seq - 1)(give(1, 0, q).start)

    def hop(turn, q):
        rows = pl.ds(q * piece, piece)
        for way in range(2):
            far = s if way == 0 else seq - 1 - s
            i = turn - far
            r = seq - 1 - i if way == 0 else i
            before = r + 1 if way == 0 else r - 1
            sends = jnp.logical_and(i >= 0, s < r if way == 0 else s > r)

            @pl.when(jnp.logical_and(sends, far > 0))
            def _():
                landed(r, q)
                own[r, :, rows, :] = added(own.at[r, :, rows, :], come.at[r, :, rows, :]).astype(BF)

            pl.when(jnp.logical_and(sends, i > 0))(give(way, before, q).wait_send)
            pl.when(jnp.logical_and(sends, far + i > 0))(give(way, r, q).start)

    def onward(part_own, part_r, send, recv, k):
        j = lax.rem(mine + k, pairs)
        return remote(part_own.at[j], part_r.at[k - 1], send.at[k], recv.at[k], (lax.rem(d + 2 * k, dp), s))

    def part_onward(m, k):
        return onward(p_own[m], p_r[m], p_send.at[m], p_recv.at[m], k)

    def gw_onward(k):
        return onward(gw_own, gw_r, w_send, w_recv, k)

    def part_join():
        for m in range(count):
            for k in range(1, pairs + 1):
                j = lax.rem(mine + k, pairs)
                part_fetch(m, j).wait()
                part_swap(m, j).wait_recv()
                if k < pairs:
                    p_own[m][j] = added(p_own[m].at[j], p_x[m].at[j]).astype(BF)
                    part_onward(m, k).start()

    def gw_join():
        for k in range(1, pairs + 1):
            j = lax.rem(mine + k, pairs)
            gw_ready(j)
            gw_swap(j).wait_recv()
            if k < pairs:
                gw_own[j] = added(gw_own.at[j], gw_x.at[j]).astype(BF)
                gw_onward(k).start()

    gain_swap = remote(g_one, g_x, gx_sem.at[0], gx_sem.at[1], (mate(d), s))

    def gain_near(k):
        return remote(g_a, g_r.at[k - 1], g_send.at[k], g_recv.at[k], (lax.rem(d + 2 * k, dp), s))

    def gain_far(k):
        return remote(g_b, g_z.at[k - 1], gz_send.at[k], gz_recv.at[k], (d, lax.rem(s + k, seq)))

    def gain_middle():
        gain_swap.wait_recv()
        g_a[...] = g_one[...] + g_x[...]
        for k in range(1, pairs):
            gain_near(k).start()

    def gain_last():
        for k in range(1, pairs):
            gain_near(k).wait_recv()
        g_b[...] = added(g_a, *[g_r.at[k] for k in range(pairs - 1)])
        for k in range(1, seq):
            gain_far(k).start()

    backs = [remote(p_fin[m], part_outs[m], t_send.at[m], t_recv.at[m], (to_d, to_s)) for m in range(count)]
    stays = [pltpu.make_async_copy(p_fin[m], part_outs[m], t_send.at[count + m]) for m in range(count)]

    def part_finish():
        for m in range(count):
            for k in range(1, pairs):
                part_onward(m, k).wait_recv()
            rest = [p_r[m].at[k] for k in range(pairs - 1)]
            p_fin[m][...] = added(p_own[m].at[mine], p_x[m].at[mine], *rest).astype(BF)
            pl.when(moves)(backs[m].start)
            pl.when(jnp.logical_not(moves))(stays[m].start)

    if fused:
        dn_tasks(0, 2)
        begin()
        part_join()
        loads[3].wait()
        gw_away()
        gw_home()
        gw_join()
        dn_tasks(2, seq)
    else:
        begin()
        part_join()
        gw_join()
    g_one[...] = jnp.sum(g_in[...], axis=0, keepdims=True)
    gain_swap.start()
    later = [gain_middle, gain_last, part_finish]
    for i in range(seq - 1):
        for q in range(pieces):
            hop(i, q)
            if later and q == pieces - 1:
                later.pop(0)()
    for task in later:
        task()

    for k in range(1, pairs):
        gw_onward(k).wait_recv()
    gw_out[...] = added(gw_own.at[mine], gw_x.at[mine], *[gw_r.at[k] for k in range(pairs - 1)])
    for k in range(1, seq):
        gain_far(k).wait_recv()
    gain_out[...] = added(g_b, *[g_z.at[k] for k in range(seq - 1)])

    some = math.gcd(piece, 64)
    for q in range(pieces):
        pl.when(s > 0)(functools.partial(landed, s, q))
        pl.when(s < seq - 1)(functools.partial(landed, seq, q))

        def settle(at, carried):
            rows = pl.ds(pl.multiple_of(q * piece + at * some, some), some)
            from_left = jnp.where(s > 0, come[s, :, rows, :].astype(F32), 0.0)
            from_right = jnp.where(s < seq - 1, come[seq, :, rows, :].astype(F32), 0.0)
            total = own[s, :, rows, :].astype(F32) + from_left + from_right
            x = hid_ref[:, rows, :].astype(F32)
            inv = lax.rsqrt(jnp.mean(x * x, axis=2, keepdims=True) + norm_eps)
            scaled = total * scale_ref[...].astype(F32)[None]
            out_ref[:, rows, :] = (
                cot_ref[:, rows, :].astype(F32)
                + inv * scaled
                - x * (inv * inv * inv) * jnp.mean(x * scaled, axis=2, keepdims=True)
            ).astype(BF)
            return carried

        lax.fori_loop(0, piece // some, settle, 0)

    for q in range(pieces):
        pl.when(s < seq - 1)(give(0, s + 1, q).wait_send)
        pl.when(s > 0)(give(1, s - 1, q).wait_send)
    gain_swap.wait_send()
    for j in range(pairs):
        gw_swap(j).wait_send()
        for m in range(count):
            part_swap(m, j).wait_send()
    for k in range(1, pairs):
        gw_onward(k).wait_send()
        gain_near(k).wait_send()
        for m in range(count):
            part_onward(m, k).wait_send()
    for k in range(1, seq):
        gain_far(k).wait_send()
    for m in range(count):
        pl.when(moves)(backs[m].wait_send)
        pl.when(moves)(remote(p_fin[m], part_outs[m], t_send.at[m], t_recv.at[m], (to_d, to_s)).wait_recv)
        pl.when(jnp.logical_not(moves))(stays[m].wait)


def scatter(d_x, d_z, normed, w_in, hidden, parts, hidden_in, cotangent, norm_gain, collective_id=1):
    dp, seq = lax.axis_size("dp"), lax.axis_size("seq")
    seqs, part, width = hidden_in.shape
    tokens, channels = d_x.shape
    w_rows = 2 * channels // dp
    fused = fits_whole(seqs, part * seq, width, channels)
    pieces = 4 if part % 64 == 0 else 1
    pairs, count = dp // 2, len(parts)
    dma, vmem, shape = pltpu.SemaphoreType.DMA, pltpu.VMEM, jax.ShapeDtypeStruct
    here = pl.BlockSpec(memory_space=pltpu.VMEM)
    if fused:
        ins, in_specs = [d_x, d_z, normed, w_in, hidden], any_specs(5)
        extra = [
            vmem((tokens, 2 * channels), BF), vmem((tokens, width), BF), vmem((2 * channels, width), BF),
            vmem((part, width), BF), vmem((pairs, w_rows, width), BF), dma((4,)), dma,
        ]
    else:
        d_pre = jnp.concatenate([d_x, d_z], axis=1)
        x = hidden.astype(F32)
        d_normed = mm(d_pre, w_in, NN)
        inv = lax.rsqrt(jnp.mean(x * x, axis=1, keepdims=True) + norm_eps)
        gain = jnp.pad(jnp.sum(d_normed * x * inv, axis=0)[None], ((0, 7), (0, 0)))
        ins = [
            d_normed.astype(BF).reshape(seqs, -1, width),
            mm(d_pre, normed, TN).astype(BF).reshape(dp, w_rows, width), gain,
        ]
        in_specs, extra = any_specs(2) + [here], []
    part_shapes = [member.shape[1:] for member in parts]
    token_shape, one = (seqs, part, width), (1, width)

    def each(count):
        return [vmem((count,) + member, BF) for member in part_shapes]

    out = pl.pallas_call(
        functools.partial(scatter_kernel, dp, seq, len(parts), fused),
        in_specs=in_specs + any_specs(count) + [here] * 3,
        out_specs=[here] * (3 + count),
        out_shape=[shape(token_shape, BF), shape((w_rows, width), F32)]
        + [shape(member, BF) for member in part_shapes]
        + [shape(one, F32)],
        scratch_shapes=[
            vmem((seq,) + token_shape, BF), vmem((seq + 1,) + token_shape, BF),
            vmem((pairs, w_rows, width), BF), vmem((pairs, w_rows, width), BF), vmem((pairs - 1, w_rows, width), BF),
            *each(pairs), *each(pairs), *each(pairs - 1), *[vmem(member, BF) for member in part_shapes],
            vmem((8, width), F32), vmem(one, F32), vmem(one, F32), vmem((pairs - 1,) + one, F32),
            vmem((seq - 1,) + one, F32), vmem(one, F32), vmem(one, F32),
            dma((seq,)), dma((seq, pieces)), dma((seq + 1, pieces)),
            dma((pairs,)), dma((pairs,)), dma((pairs,)), dma((pairs,)), dma((pairs,)),
            *[dma((count, pairs))] * 5, dma((2 * count,)), dma((count,)),
            dma((2,)), dma((pairs,)), dma((pairs,)), dma((seq,)), dma((seq,)),
            *extra,
        ],
        compiler_params=pltpu.CompilerParams(
            collective_id=collective_id, has_side_effects=True, vmem_limit_bytes=63 << 20
        ),
        name="scatter_out",
    )(*ins, *parts, hidden_in, cotangent, norm_gain.reshape(1, width))
    return out[0], out[1], out[2 : 2 + count], out[-1].reshape(width)


def reduce_kernel(dp, seq, grads, *refs):
    refs = list(refs)

    def take(count):
        out = refs[:count]
        del refs[:count]
        return out

    wide_ref, thin_ref = take(2)
    g_ref = take(1)[0] if grads else None
    wide_out, thin_out = take(2)
    g_out = take(1)[0] if grads else None
    wide_x, thin_x, wide_s, thin_s = take(4)
    xw_send, xw_recv, xt_send, xt_recv, sw_send, sw_recv, st_send, st_recv = take(8)
    d, s = place()
    rows = wide_ref.shape[0] // seq
    pairs = dp // 2
    mine, odd = d // 2, lax.rem(d, 2)
    for k in range(1, seq):
        greet((d, lax.rem(s + k, seq)))
    if grads:
        for k in range(1, pairs):
            greet((lax.rem(d + 2 * k, dp), s))
        greet((mate(d), s))
    pl.semaphore_wait(pltpu.get_barrier_semaphore(), seq - 1 + (pairs if grads else 0))

    def piece(ref, which):
        return ref.at[pl.ds(pl.multiple_of(which * rows, rows), rows)]

    def ask(k):
        to = lax.rem(s + k, seq)
        return (
            remote(piece(wide_ref, to), wide_x.at[k - 1], xw_send.at[k - 1], xw_recv.at[k - 1], (d, to)),
            remote(thin_ref.at[to], thin_x.at[k - 1], xt_send.at[k - 1], xt_recv.at[k - 1], (d, to)),
        )

    def tell(k):
        to = lax.rem(s + k, seq)
        return (
            remote(wide_s, piece(wide_out, s), sw_send.at[k - 1], sw_recv.at[k - 1], (d, to)),
            remote(thin_s, thin_out.at[s], st_send.at[k - 1], st_recv.at[k - 1], (d, to)),
        )

    def told(k):
        source = lax.rem(s - k + seq, seq)
        return (
            remote(wide_s, piece(wide_out, source), sw_send.at[k - 1], sw_recv.at[k - 1], (d, s)),
            remote(thin_s, thin_out.at[source], st_send.at[k - 1], st_recv.at[k - 1], (d, s)),
        )

    order = sorted(range(1, seq), key=lambda k: -min(k, seq - k))
    for k in order:
        for copy in ask(k):
            copy.start()
    if grads:
        g_own, g_x, g_r, g_load, gx_send, gx_recv, g_send, g_recv = take(8)

        def swap(j):
            return remote(g_ref.at[2 * j + 1 - odd], g_x.at[j], gx_send.at[j], gx_recv.at[j], (mate(d), s))

        def fetch(j):
            return pltpu.make_async_copy(g_ref.at[2 * j + odd], g_own.at[j], g_load.at[j])

        def onward(k):
            to = lax.rem(d + 2 * k, dp)
            return remote(g_own.at[to // 2], g_r.at[k - 1], g_send.at[k], g_recv.at[k], (to, s))

        for j in range(pairs):
            swap(j).start()
            fetch(j).start()
        for k in range(1, pairs + 1):
            j = lax.rem(mine + k, pairs)
            fetch(j).wait()
            swap(j).wait_recv()
            if k < pairs:
                g_own[j] = added(g_own.at[j], g_x.at[j]).astype(BF)
                onward(k).start()
    for k in order:
        for copy in ask(k):
            copy.wait_recv()
    start = pl.ds(pl.multiple_of(s * rows, rows), rows)
    total = wide_ref[start, :].astype(F32)
    thin = thin_ref[s]
    for k in range(seq - 1):
        total = total + wide_x[k].astype(F32)
        thin = thin + thin_x[k]
    wide_s[...] = total.astype(BF)
    thin_s[...] = thin
    for k in order:
        for copy in tell(k):
            copy.start()
    wide_out[start, :] = total.astype(BF)
    thin_out[s] = thin
    if grads:
        for k in range(1, pairs):
            onward(k).wait_recv()
        g_out[...] = added(g_own.at[mine], g_x.at[mine], *[g_r.at[k] for k in range(pairs - 1)]).astype(BF)
        for j in range(pairs):
            swap(j).wait_send()
        for k in range(1, pairs):
            onward(k).wait_send()
    for k in order:
        for copy in told(k):
            copy.wait_recv()
    for k in order:
        for copy in ask(k) + tell(k):
            copy.wait_send()


def reduce_over_seq(wide_part, thin_part, collective_id, grads=None):
    dp, seq = lax.axis_size("dp"), lax.axis_size("seq")
    tokens, cols = wide_part.shape
    thin_part = jnp.swapaxes(thin_part.reshape(-1, seq, tokens // seq), 0, 1)
    dma, vmem, shape = pltpu.SemaphoreType.DMA, pltpu.VMEM, jax.ShapeDtypeStruct
    here = pl.BlockSpec(memory_space=pltpu.VMEM)
    rows, few, pairs = tokens // seq, thin_part.shape[1:], dp // 2
    ins, in_specs = [wide_part.astype(BF), thin_part], [here] * 2
    outs = [shape((tokens, cols), BF), shape(thin_part.shape, F32)]
    scratch = [
        vmem((seq - 1, rows, cols), BF), vmem((seq - 1,) + few, F32), vmem((rows, cols), BF), vmem(few, F32),
    ] + [dma((seq - 1,))] * 8
    if grads is not None:
        ins, in_specs = ins + [grads], in_specs + any_specs(1)
        outs.append(shape(grads.shape[1:], BF))
        scratch += [vmem((pairs,) + grads.shape[1:], BF)] * 2 + [vmem((pairs - 1,) + grads.shape[1:], BF)]
        scratch += [dma((pairs,))] * 5
    out = pl.pallas_call(
        functools.partial(reduce_kernel, dp, seq, grads is not None),
        in_specs=in_specs,
        out_specs=[here] * len(outs),
        out_shape=outs,
        scratch_shapes=scratch,
        compiler_params=pltpu.CompilerParams(
            collective_id=collective_id, has_side_effects=True, vmem_limit_bytes=24 << 20
        ),
        name="reduce_seq",
    )(*ins)
    return (out[0], jnp.swapaxes(out[1], 0, 1).reshape(-1, tokens)) + tuple(out[2:])


def homes_back(dp, seq):
    pairs = []
    for d in range(dp):
        for s in range(seq):
            home_d, home_s = 2 * (d // 2) + s % 2, (seq // 2) * (d % 2) + s // 2
            pairs.append((home_d * seq + home_s, d * seq + s))
    return pairs


def local(
    hidden_in,
    doc_lengths,
    norm_gain,
    in_weight,
    conv_weight,
    conv_bias,
    x_weight,
    dt_weight,
    dt_bias,
    skip_gain,
    out_weight,
    out_cotangent,
):
    seqs, part_len, width = hidden_in.shape
    dp, seq = lax.axis_size("dp"), lax.axis_size("seq")
    length = part_len * seq
    tokens = seqs * length
    rows = out_weight.shape[0]
    channels = rows * dp
    lag_max = KCONV - 1

    vectors = [conv_weight, conv_bias[None], dt_bias[None], skip_gain[None]]
    vectors = jnp.pad(jnp.concatenate(vectors, axis=0), ((0, 16 - KCONV - 3), (0, 0)))
    parts = [out_weight, x_weight, dt_weight, vectors]
    hidden, w_in, parts, normed, pre = gather(hidden_in, in_weight, parts, norm_gain)
    cot, pre = lax.optimization_barrier((out_cotangent, pre))
    cot = lax.all_gather(cot, "seq", axis=1, tiled=True).reshape(tokens, width)

    w_out, w_x, w_dt = (part.reshape(channels, part.shape[2]) for part in parts[:3])
    vectors = jnp.swapaxes(parts[3], 0, 1).reshape(16, channels).astype(F32)
    taps, conv_shift, rate_shift, skip = vectors[:KCONV], vectors[KCONV], vectors[KCONV + 1], vectors[KCONV + 2]

    begins, places = token_begins(doc_lengths, length)
    keep = (places[None, :] != begins).astype(F32).reshape(tokens, 1)
    valid = [(places[None, :] - (lag_max - w) >= begins)[:, :, None] for w in range(KCONV)]

    x_inner = pre[:, :channels].reshape(seqs, length, channels)

    padded = jnp.pad(x_inner, ((0, 0), (lag_max, 0), (0, 0)))
    conv_sum = jnp.broadcast_to(conv_shift, (seqs, length, channels))
    for w in range(KCONV):
        window = padded[:, w : w + length, :].astype(F32)
        conv_sum = conv_sum + jnp.where(valid[w], window * taps[w], 0.0)
    conv_flat = conv_sum.reshape(tokens, channels)
    xc_low = jax.nn.silu(conv_flat).astype(BF)
    rate, thin = reduce_over_seq(mm(xc_low, w_x[:, :R], NN), mm(w_x[:, R:], xc_low, ((0,), (1,))), 2)
    key, query = thin[:N].T, thin[N:].T
    key_lanes, query_lanes = (
        jnp.broadcast_to(part.astype(BF)[:, :, None], (tokens, N, LANES)) for part in (key, query)
    )
    ksum = jnp.sum(key * key, axis=1, keepdims=True)
    keep_lanes = jnp.broadcast_to(keep, (tokens, LANES))
    ksum_lanes = jnp.broadcast_to(ksum, (tokens, LANES))
    vectors = jnp.pad(jnp.stack([rate_shift, skip]), ((0, 6), (0, 0)))
    states, y_full, gated = scan_forward(
        seqs, length, xc_low, pre, rate, key_lanes, query_lanes, keep_lanes, ksum_lanes, w_dt, vectors
    )
    branch = mm(gated, w_out, NN).astype(BF).reshape(seqs, length, width)
    branch = lax.psum_scatter(branch, "seq", scatter_dimension=1, tiled=True)
    output = (hidden_in.astype(F32) + branch.astype(F32)).astype(BF)

    d_z, rest, dq, dk, d_norm, d_row, grad_dt, sums = scan_backward(
        seqs, length, mm(cot, w_out, NT), y_full, xc_low, pre, rate, key_lanes, query_lanes, keep_lanes, ksum_lanes, w_dt, vectors, states
    )
    dq, dk = dq.reshape(tokens, N), dk.reshape(tokens, N)
    d_norm = -jnp.sum(d_norm, axis=1, keepdims=True)
    d_keys = dk + 2.0 * key * d_norm
    grad_out = mm(gated, cot, TN).astype(BF).reshape(dp, rows, width)
    d_row, thin, grad_out = reduce_over_seq(d_row, jnp.concatenate([d_keys.T, dq.T], axis=0), 3, grad_out)
    grad_out = lax.ppermute(grad_out, ("dp", "seq"), homes_back(dp, seq))
    d_proj = jnp.concatenate([d_row, thin.T.astype(BF)], axis=1)
    d_conv_out = mm(d_proj, w_x, NT) + rest
    d_conv = (d_conv_out * silu_slope(conv_flat)).reshape(seqs, length, channels)

    tap_grads = []
    d_x_inner = jnp.zeros((seqs, length, channels), F32)
    for w in range(KCONV):
        lag = lag_max - w
        window = padded[:, w : w + length, :].astype(F32)
        masked = jnp.where(valid[w], d_conv, 0.0)
        tap_grads.append(jnp.sum(masked * window, axis=(0, 1)))
        d_x_inner = d_x_inner + jnp.pad(masked, ((0, 0), (0, lag), (0, 0)))[:, lag:, :] * taps[w]
    vector_grads = jnp.stack(
        tap_grads + [jnp.sum(d_conv, axis=(0, 1)), jnp.sum(sums[:8], axis=0), jnp.sum(sums[8:], axis=0)], axis=0
    )
    vector_grads = jnp.pad(vector_grads, ((0, 16 - KCONV - 3), (0, 0))).reshape(16, dp, rows)
    grads = [part.astype(BF).reshape(dp, rows, -1) for part in (mm(xc_low, d_proj, TN), grad_dt)]
    grads.append(jnp.swapaxes(vector_grads, 0, 1).astype(BF))
    grad_in, grad_in_weight, grads, grad_norm_gain = scatter(
        d_x_inner.reshape(tokens, channels).astype(BF), d_z, normed, w_in, hidden, grads,
        hidden_in, out_cotangent, norm_gain,
    )
    grad_x, grad_dt, grad_vectors = (part.astype(F32) for part in grads)
    grad_out_weight = grad_out.astype(F32)
    return (
        output,
        grad_in,
        grad_norm_gain,
        grad_in_weight,
        grad_vectors[:KCONV],
        grad_vectors[KCONV],
        grad_x,
        grad_dt,
        grad_vectors[KCONV + 1],
        grad_vectors[KCONV + 2],
        grad_out_weight,
    )


def solution(mesh):
    both = ("dp", "seq")
    tokens = P("dp", "seq", None)
    matrix, vector = P(both, None), P(both)
    return jax.shard_map(
        local,
        mesh=mesh,
        in_specs=(
            tokens, P("dp", None), P(), matrix, P(None, both), vector,
            matrix, matrix, vector, vector, matrix, tokens,
        ),
        out_specs=(
            tokens, tokens, P(), matrix, P(None, both), vector,
            matrix, matrix, vector, vector, matrix,
        ),
        check_vma=False,
    )
```

```python
import functools
import math

import jax
import jax.numpy as jnp
from jax import lax
from jax.experimental import pallas as pl
from jax.experimental.pallas import tpu as pltpu
from jax.sharding import PartitionSpec as P

N = 16
R = 128
KCONV = 4
CHUNK = 16
LANES = 128
GROUP = 1024
BLOCK = 128

norm_eps = 1e-05
BF = jnp.bfloat16
F32 = jnp.float32


def silu_slope(pre_value):
    sigmoid_of = jax.nn.sigmoid(pre_value)
    return sigmoid_of * (1.0 + pre_value * (1.0 - sigmoid_of))


def token_begins(lengths, position_count):
    doc_ends = jnp.cumsum(lengths, axis=1)
    doc_starts = doc_ends - lengths
    places = jnp.arange(position_count, dtype=jnp.int32)
    inside = doc_starts[:, None, :] <= places[None, :, None]
    return (jnp.max(jnp.where(inside, doc_starts[:, None, :], 0), axis=2), places)


def mm(left, right, dims):
    return lax.dot_general(left, right, (dims, ((), ())), preferred_element_type=F32)


NN = ((1,), (0,))
NT = ((1,), (1,))
TN = ((0,), (0,))


def row(ref, i, lane):
    return jnp.broadcast_to(ref[i : i + 1, pl.ds(lane, LANES)], (8, LANES))


def wide(ref, rows, count):
    value = ref[rows, :]
    return jnp.concatenate([value] * (count // LANES), axis=1)


def merge(even, odd, stride):
    low = lax.broadcasted_iota(jnp.int32, (8, LANES), 0) % (2 * stride) < stride
    if stride == 4:
        return jnp.where(low, even, odd) + pltpu.roll(jnp.where(low, odd, even), 4, 0)
    return jnp.where(low, even + pltpu.roll(even, 8 - stride, 0), odd + pltpu.roll(odd, stride, 0))


def collect(stack, value, descending):
    level = 0
    while stack and stack[-1][0] == level:
        other = stack.pop()[1]
        value = merge(value, other, 1 << level) if descending else merge(other, value, 1 << level)
        level += 1
    stack.append((level, value))


def each_chunk(tokens, channels, body):
    group = math.gcd(channels, 512)

    def run(k, carried):
        rows = pl.ds(pl.multiple_of(k * CHUNK, CHUNK), CHUNK)
        for first in range(0, channels, group):
            body(rows, pl.ds(first, group), first)
        return carried

    lax.fori_loop(0, tokens // CHUNK, run, 0)


def load_carry(carry, tiles):
    out = []
    for lane in tiles:
        out += [carry[0:8, pl.ds(lane, LANES)], carry[8:16, pl.ds(lane, LANES)]]
    return tuple(out)


def store_carry(carry, tiles, values):
    for j, lane in enumerate(tiles):
        carry[0:8, pl.ds(lane, LANES)] = values[2 * j]
        carry[8:16, pl.ds(lane, LANES)] = values[2 * j + 1]


def halves(value):
    return [value[0:8], value[8:16]]


def token(keys, queries, keeps, i):
    return row(keeps, i, 0), halves(keys[i].astype(F32)), halves(queries[i].astype(F32))


def lane_groups(channels):
    group = math.gcd(channels, GROUP)
    return [list(range(first, first + group, LANES)) for first in range(0, channels, group)]


def forward_kernel(
    xc_ref, z_ref, rate_ref, key_ref, query_ref, keep_ref, ksum_ref, wdt_ref, vec_ref,
    s_ref, y_ref, gated_ref, step, inj, carry,
):
    @pl.when(pl.program_id(1) == 0)
    def _():
        carry[...] = jnp.zeros_like(carry)

    tokens, channels = xc_ref.shape
    step[...] = mm(rate_ref[...], wdt_ref[...], NT)

    def prepare(rows, cols, first):
        beta = jax.nn.sigmoid(step[rows, cols] + vec_ref[0:1, cols])
        eps = beta / (1.0 + beta * wide(ksum_ref, rows, cols.size))
        step[rows, cols] = eps
        inj[rows, cols] = eps * xc_ref[rows, cols].astype(F32)

    each_chunk(tokens, channels, prepare)
    for tiles in lane_groups(channels):

        def chunk(k, state):
            state = list(state)
            base = pl.multiple_of(k * CHUNK, CHUNK)
            steps, injs, keeps, keys, queries = (
                r.at[pl.ds(base, CHUNK)] for r in (step, inj, keep_ref, key_ref, query_ref)
            )
            saved = s_ref.at[pl.ds(pl.multiple_of(k * CHUNK * N, CHUNK * N), CHUNK * N)]
            stacks = [[] for _ in tiles]
            for i in range(CHUNK):
                keep, key, query = token(keys, queries, keeps, i)
                ksq = [keep * key[h] * key[h] for h in range(2)]
                for j, lane in enumerate(tiles):
                    eps, push = row(steps, i, lane), row(injs, i, lane)
                    for h in range(2):
                        state[2 * j + h] = (keep - eps * ksq[h]) * state[2 * j + h] + push * key[h]
                    both = jnp.concatenate([state[2 * j], state[2 * j + 1]], axis=0)
                    saved[i * N : (i + 1) * N, pl.ds(lane, LANES)] = both.astype(BF)
                    collect(stacks[j], state[2 * j] * query[0] + state[2 * j + 1] * query[1], False)
                    if i % 8 == 7:
                        y_ref[pl.ds(pl.multiple_of(base + i - 7, 8), 8), pl.ds(lane, LANES)] = stacks[j].pop()[1]
            return tuple(state)

        store_carry(carry, tiles, lax.fori_loop(0, tokens // CHUNK, chunk, load_carry(carry, tiles)))

    def emit(rows, cols, first):
        y_full = y_ref[rows, cols] + vec_ref[1:2, cols] * xc_ref[rows, cols].astype(F32)
        y_ref[rows, cols] = y_full
        z = z_ref[rows, cols].astype(F32)
        gated_ref[rows, cols] = (y_full * (z * jax.nn.sigmoid(z))).astype(BF)

    each_chunk(tokens, channels, emit)


def backward_kernel(
    dg_ref, y_ref, xc_ref, z_ref, rate_ref, key_ref, query_ref, keep_ref, ksum_ref, wdt_ref, vec_ref, s_ref, before_ref,
    dz_ref, rest_ref, dq_ref, dk_ref, dnorm_ref, drow_ref, gdt_ref, sums_ref,
    step, inj, dy, mix, pull, beta, drate, carry, acc_q, acc_k,
):
    turn = pl.program_id(1)
    tokens, channels = xc_ref.shape
    chunks = tokens // CHUNK

    @pl.when(jnp.logical_and(pl.program_id(0) == 0, turn == 0))
    def _():
        gdt_ref[...] = jnp.zeros_like(gdt_ref)
        sums_ref[...] = jnp.zeros_like(sums_ref)

    @pl.when(turn == 0)
    def _():
        carry[...] = jnp.zeros_like(carry)

    beta[...] = mm(rate_ref[...], wdt_ref[...], NT)

    def prepare(rows, cols, first):
        rate_beta = jax.nn.sigmoid(beta[rows, cols] + vec_ref[0:1, cols])
        eps = rate_beta / (1.0 + rate_beta * wide(ksum_ref, rows, cols.size))
        beta[rows, cols] = rate_beta
        step[rows, cols] = eps
        xc = xc_ref[rows, cols].astype(F32)
        inj[rows, cols] = eps * xc
        z = z_ref[rows, cols].astype(F32)
        sig = jax.nn.sigmoid(z)
        d_gated = dg_ref[rows, cols]
        d_y = d_gated * (z * sig)
        dy[rows, cols] = d_y
        dz_ref[rows, cols] = (d_gated * y_ref[rows, cols] * (sig * (1.0 + z * (1.0 - sig)))).astype(BF)
        weighted = d_y * xc
        sums_ref[8:16, cols] += weighted[0:8] + weighted[8:16]

    each_chunk(tokens, channels, prepare)
    for tiles in lane_groups(channels):
        start = tiles[0] == 0

        def chunk(back, carried):
            k = chunks - 1 - back
            pulled, now = list(carried[0]), list(carried[1])
            base = pl.multiple_of(k * CHUNK, CHUNK)
            steps, injs, dys, keeps, keys, queries = (
                r.at[pl.ds(base, CHUNK)] for r in (step, inj, dy, keep_ref, key_ref, query_ref)
            )
            stacks = [([], []) for _ in tiles]
            for i in reversed(range(CHUNK)):
                keep, key, query = token(keys, queries, keeps, i)
                kept = [keep * key[h] for h in range(2)]
                ksq = [kept[h] * key[h] for h in range(2)]
                if i > 0:
                    before = pl.ds(pl.multiple_of((base + i) * N - N, N), N)
                else:
                    before = pl.ds(pl.multiple_of(jnp.maximum(base * N - N, 0), N), N)
                seen, plain, scaled = [0.0, 0.0], [0.0, 0.0], [0.0, 0.0]
                for j, lane in enumerate(tiles):
                    eps, push, d_y = row(steps, i, lane), row(injs, i, lane), row(dys, i, lane)
                    prior = s_ref[before, pl.ds(lane, LANES)]
                    if i == 0:
                        prior = jnp.where(k > 0, prior, before_ref[:, pl.ds(lane, LANES)])
                    prior = halves(prior.astype(F32))
                    by_key, by_square = [], []
                    for h in range(2):
                        at = 2 * j + h
                        grad = pulled[at] + d_y * query[h]
                        pulled[at] = (keep - eps * ksq[h]) * grad
                        keyed = eps * (grad * key[h])
                        prod = keyed * prior[h]
                        seen[h] += now[at] * d_y
                        plain[h] += grad * push
                        scaled[h] += prod
                        by_key.append(keyed)
                        by_square.append(prod * kept[h])
                        now[at] = prior[h]
                    collect(stacks[j][0], by_key[0] + by_key[1], True)
                    collect(stacks[j][1], by_square[0] + by_square[1], True)
                    if i % 8 == 0:
                        rows = pl.ds(pl.multiple_of(base + i, 8), 8)
                        mix[rows, pl.ds(lane, LANES)] = stacks[j][0].pop()[1]
                        pull[rows, pl.ds(lane, LANES)] = stacks[j][1].pop()[1]
                for ref, parts in ((acc_q, seen), (acc_k, [plain[h] - 2.0 * keep * scaled[h] for h in range(2)])):
                    for h in range(2):
                        rows = pl.ds(pl.multiple_of((base + i) * N + 8 * h, 8), 8)
                        if start:
                            ref[rows, :] = parts[h]
                        else:
                            ref[rows, :] += parts[h]
            return (tuple(pulled), tuple(now))

        now = []
        for lane in tiles:
            now += halves(s_ref[tokens * N - N : tokens * N, pl.ds(lane, LANES)].astype(F32))
        pulled, now = lax.fori_loop(0, chunks, chunk, (load_carry(carry, tiles), tuple(now)))
        store_carry(carry, tiles, pulled)

    ones = jnp.ones((LANES, LANES), BF)
    diagonal = lax.broadcasted_iota(jnp.int32, (LANES, LANES), 0) == (
        lax.broadcasted_iota(jnp.int32, (LANES, LANES), 1)
    )
    for out, ref in ((dq_ref, acc_q), (dk_ref, acc_k)):
        for first in range(0, tokens * N, LANES):
            sums = mm(ref[first : first + LANES, :].astype(BF), ones, NN)
            at = first // LANES
            out[at : at + 1, :] = jnp.sum(jnp.where(diagonal, sums, 0.0), axis=0, keepdims=True)

    def settle(rows, cols, first):
        rate_beta, eps = beta[rows, cols], step[rows, cols]
        through = mix[rows, cols]
        change = through * xc_ref[rows, cols].astype(F32) - pull[rows, cols]
        inverse = 1.0 / (1.0 + rate_beta * wide(ksum_ref, rows, cols.size))
        low = (change * inverse * (1.0 - rate_beta)).astype(BF)
        drate[rows, cols] = low
        lowered = low.astype(F32)
        sums_ref[0:8, cols] += lowered[0:8] + lowered[8:16]
        rest_ref[rows, cols] = through + vec_ref[1:2, cols] * dy[rows, cols]
        square = change * eps
        total = square[:, 0:LANES]
        for lane in range(LANES, cols.size, LANES):
            total = total + square[:, lane : lane + LANES]
        if first == 0:
            dnorm_ref[rows, :] = total
        else:
            dnorm_ref[rows, :] += total

    each_chunk(tokens, channels, settle)
    drow_ref[...] = mm(drate[...], wdt_ref[...], NN)
    gdt_ref[...] += mm(drate[...], rate_ref[...], TN)


def scan_blocks(length):
    block = math.gcd(length, BLOCK)
    return block, length // block


def row_spec(rows, cols, when, col=0):
    return pl.BlockSpec((rows, cols), lambda b, t: (when(b, t), col))


def spread_spec(block, when):
    return pl.BlockSpec((block, N, LANES), lambda b, t: (when(b, t), 0, 0))


def whole(array):
    return pl.BlockSpec(array.shape, lambda b, t: (0, 0), pipeline_mode=pl.Buffered(1))


def scan_forward(seqs, length, xc, pre, rate, key_lanes, query_lanes, keep_lanes, ksum_lanes, w_dt, vectors):
    tokens, channels = xc.shape
    block, blocks = scan_blocks(length)

    def at(b, t):
        return b * blocks + t

    rows = row_spec(block, channels, at)
    lanes = row_spec(block, LANES, at)
    vmem = pltpu.VMEM
    return pl.pallas_call(
        forward_kernel,
        grid=(seqs, blocks),
        in_specs=[
            rows, row_spec(block, channels, at, 1), row_spec(block, R, at),
            spread_spec(block, at), spread_spec(block, at), lanes, lanes, whole(w_dt), whole(vectors),
        ],
        out_specs=[row_spec(block * N, channels, at), rows, rows],
        out_shape=[
            jax.ShapeDtypeStruct((tokens * N, channels), BF),
            jax.ShapeDtypeStruct((tokens, channels), F32),
            jax.ShapeDtypeStruct((tokens, channels), BF),
        ],
        scratch_shapes=[vmem((block, channels), F32), vmem((block, channels), F32), vmem((N, channels), F32)],
        cost_estimate=pl.CostEstimate(
            flops=tokens * channels * N * 60, bytes_accessed=tokens * channels * 44, transcendentals=0
        ),
        compiler_params=pltpu.CompilerParams(vmem_limit_bytes=40 << 20),
        name="scan_forward",
    )(xc, pre, rate, key_lanes, query_lanes, keep_lanes, ksum_lanes, w_dt, vectors)


def scan_backward(seqs, length, d_gated, y, xc, pre, rate, key_lanes, query_lanes, keep_lanes, ksum_lanes, w_dt, vectors, states):
    tokens, channels = xc.shape
    block, blocks = scan_blocks(length)

    def at(b, t):
        return b * blocks + blocks - 1 - t

    def prior(b, t):
        return (jnp.maximum(at(b, t) * block - 1, 0), 0)

    rows = row_spec(block, channels, at)
    lanes = row_spec(block, LANES, at)
    flat = row_spec(block * N // LANES, LANES, at)
    vmem = pltpu.VMEM
    wide_f32 = vmem((block, channels), F32)
    return pl.pallas_call(
        backward_kernel,
        grid=(seqs, blocks),
        in_specs=[
            rows, rows, rows, row_spec(block, channels, at, 1), row_spec(block, R, at),
            spread_spec(block, at), spread_spec(block, at), lanes, lanes, whole(w_dt), whole(vectors),
            row_spec(block * N, channels, at), pl.BlockSpec((N, channels), prior),
        ],
        out_specs=[
            rows, rows, flat, flat, lanes, row_spec(block, R, at),
            pl.BlockSpec((channels, R), lambda b, t: (0, 0)), pl.BlockSpec((16, channels), lambda b, t: (0, 0)),
        ],
        out_shape=[
            jax.ShapeDtypeStruct((tokens, channels), BF),
            jax.ShapeDtypeStruct((tokens, channels), F32),
            jax.ShapeDtypeStruct((tokens * N // LANES, LANES), F32),
            jax.ShapeDtypeStruct((tokens * N // LANES, LANES), F32),
            jax.ShapeDtypeStruct((tokens, LANES), F32),
            jax.ShapeDtypeStruct((tokens, R), F32),
            jax.ShapeDtypeStruct((channels, R), F32),
            jax.ShapeDtypeStruct((16, channels), F32),
        ],
        scratch_shapes=[
            wide_f32, wide_f32, wide_f32, wide_f32, wide_f32, wide_f32, vmem((block, channels), BF),
            vmem((N, channels), F32), vmem((block * N, LANES), F32), vmem((block * N, LANES), F32),
        ],
        cost_estimate=pl.CostEstimate(
            flops=tokens * channels * N * 100, bytes_accessed=tokens * channels * 56, transcendentals=0
        ),
        compiler_params=pltpu.CompilerParams(vmem_limit_bytes=48 << 20),
        name="scan_backward",
    )(d_gated, y, xc, pre, rate, key_lanes, query_lanes, keep_lanes, ksum_lanes, w_dt, vectors, states, states)


MESH = pl.DeviceIdType.MESH


def any_specs(count):
    return [pl.BlockSpec(memory_space=pl.ANY)] * count


def place():
    return lax.axis_index("dp"), lax.axis_index("seq")


def mate(d):
    return d + 1 - 2 * lax.rem(d, 2)


def forward_home(d, s, seq):
    return 2 * (d // 2) + lax.rem(s, 2), (seq // 2) * lax.rem(d, 2) + s // 2


def backward_home(d, s, seq):
    return 2 * (d // 2) + s // (seq // 2), 2 * lax.rem(s, seq // 2) + lax.rem(d, 2)


def remote(src, dst, send, recv, device):
    return pltpu.make_async_remote_copy(
        src_ref=src, dst_ref=dst, send_sem=send, recv_sem=recv, device_id=device, device_id_type=MESH
    )


def greet(device, here=True):
    barrier = pltpu.get_barrier_semaphore()

    def tell():
        pl.semaphore_signal(barrier, inc=1, device_id=device, device_id_type=MESH)

    if here is True:
        tell()
    else:
        pl.when(here)(tell)


PARTS = 4


def gather_kernel(dp, seq, fused, *refs):
    refs = list(refs)

    def take(count):
        out = refs[:count]
        del refs[:count]
        return out

    hid_ref, w_ref = take(2)
    parts = take(PARTS)
    gain_ref = take(1)[0] if fused else None
    hid_out, w_out = take(2)
    slots = take(PARTS)
    normed_out, pre_out = take(2) if fused else (None, None)
    z_send, z_recv, w_send, w_recv, f_send, f_recv, p_send, p_recv, q_send, q_recv, t_send, t_recv, own_sem = take(13)
    d, s = place()
    part = hid_ref.shape[1]
    pieces = z_send.shape[2]
    piece = part // pieces
    pairs = dp // 2
    to_d, to_s = forward_home(d, s, seq)
    from_d, from_s = backward_home(d, s, seq)
    moves = jnp.logical_or(to_d != d, to_s != s)

    greet((d, s - 1), s > 0)
    greet((d, s + 1), s < seq - 1)
    for k in range(1, pairs):
        greet((lax.rem(d + 2 * k, dp), s))
    greet((mate(d), s))
    greet((to_d, to_s), moves)
    greet((from_d, from_s), moves)
    count = pairs + jnp.where(s > 0, 1, 0) + jnp.where(s < seq - 1, 1, 0) + jnp.where(moves, 2, 0)
    pl.semaphore_wait(pltpu.get_barrier_semaphore(), count)

    def shard(which, q):
        return hid_out.at[:, pl.ds(which * part + q * piece, piece), :]

    def hop(way, k, q):
        which = s - k if way == 0 else s + k
        src = hid_ref.at[:, pl.ds(q * piece, piece), :] if k == 0 else shard(which, q)
        near = s + 1 if way == 0 else s - 1
        return remote(src, shard(which, q), z_send.at[way, k, q], z_recv.at[way, k, q], (d, near))

    def can_send(way, k):
        if way == 0:
            return jnp.logical_and(s - k >= 0, s < seq - 1)
        return jnp.logical_and(s + k < seq, s > 0)

    def landed(way, k, q):
        which = jnp.where(way == 0, s - k, s + k)
        here = shard(which, q)
        remote(here, here, z_send.at[way, k - 1, q], z_recv.at[way, k - 1, q], (d, s)).wait_recv()

    def spread(out, own, send, recv, k):
        return remote(own, out.at[d], send.at[k], recv.at[k], (lax.rem(d + 2 * k, dp), s))

    def source(k):
        return lax.rem(d - 2 * k + dp, dp)

    def across(out, send, recv, k, own=None):
        return remote(own if k == 0 else out.at[source(k)], out.at[source(k)], send.at[k], recv.at[k], (mate(d), s))

    for q in range(pieces):
        for way in range(2):
            pl.when(can_send(way, 0))(hop(way, 0, q).start)
    transfers = [remote(parts[m], slots[m].at[to_d], t_send.at[m], t_recv.at[m], (to_d, to_s)) for m in range(PARTS)]
    stays = [pltpu.make_async_copy(parts[m], slots[m].at[d], own_sem.at[2 + m]) for m in range(PARTS)]
    for m in range(PARTS):
        pl.when(moves)(transfers[m].start)
        pl.when(jnp.logical_not(moves))(stays[m].start)
    for k in range(1, pairs):
        spread(w_out, w_ref, w_send, w_recv, k).start()
    across(w_out, f_send, f_recv, 0, w_ref).start()
    own_w = pltpu.make_async_copy(w_ref, w_out.at[d], own_sem.at[0])
    own_h = pltpu.make_async_copy(hid_ref, hid_out.at[:, pl.ds(s * part, part), :], own_sem.at[1])
    own_w.start()
    own_h.start()

    for k in range(1, seq - 1):
        for q in range(pieces):
            for way in range(2):
                pl.when(s - k >= 0 if way == 0 else s + k < seq)(functools.partial(landed, way, k, q))
                pl.when(can_send(way, k))(hop(way, k, q).start)
    own_w.wait()
    own_h.wait()
    w_flow = (w_out, w_ref, w_send, w_recv, f_send, f_recv)
    part_flows = [
        (slots[m], slots[m].at[d], p_send.at[m], p_recv.at[m], q_send.at[m], q_recv.at[m]) for m in range(PARTS)
    ]

    def relay(out, own, send, recv, over_send, over_recv):
        for k in range(1, pairs):
            here = out.at[source(k)]
            remote(here, here, send.at[k], recv.at[k], (d, s)).wait_recv()
            across(out, over_send, over_recv, k).start()

    def complete(out, own, send, recv, over_send, over_recv):
        for k in range(pairs):
            here = out.at[lax.rem(mate(d) - 2 * k + dp, dp)]
            remote(here, here, over_send.at[k], over_recv.at[k], (d, s)).wait_recv()

    relay(*w_flow)
    for m in range(PARTS):
        slot = slots[m].at[d]
        pl.when(moves)(remote(parts[m], slot, t_send.at[m], t_recv.at[m], (to_d, to_s)).wait_recv)
        pl.when(jnp.logical_not(moves))(stays[m].wait)
        for k in range(1, pairs):
            spread(slots[m], slot, p_send.at[m], p_recv.at[m], k).start()
        across(slots[m], q_send.at[m], q_recv.at[m], 0, slot).start()

    complete(*w_flow)

    def relay_parts():
        for flow in part_flows:
            relay(*flow)

    last = seq - 1
    if fused:
        w_all, x_buf, w_sem, x_sem = take(4)
        width, columns = x_buf.shape[1], pre_out.shape[1]
        cut = math.gcd(columns, 512)
        fetch_w = pltpu.make_async_copy(w_out, w_all, w_sem)
        fetch_w.start()
        fetch_w.wait()

        def project(which, k, way):
            here = pl.multiple_of(which * part, part)
            for q in range(pieces):
                pl.when(k == last)(functools.partial(landed, way, last, q))
                fetch = pltpu.make_async_copy(
                    hid_out.at[0, pl.ds(which * part + q * piece, piece)], x_buf.at[pl.ds(q * piece, piece)], x_sem
                )
                fetch.start()
                fetch.wait()
                x = x_buf[pl.ds(q * piece, piece), :].astype(F32)
                inv = lax.rsqrt(jnp.mean(x * x, axis=1, keepdims=True) + norm_eps)
                rows = pl.ds(pl.multiple_of(here + q * piece, piece), piece)
                normed_out[rows, :] = (x * inv * gain_ref[...].astype(F32)).astype(BF)

            def matmul(at, carried):
                cols = pl.ds(pl.multiple_of(at * cut, cut), cut)
                w_rows = w_all.shape[1]
                block = w_all[pl.ds(at * (cut // w_rows), cut // w_rows)].reshape(cut, width)
                pre_out[pl.ds(here, part), cols] = mm(normed_out[pl.ds(here, part), :], block, NT).astype(BF)
                return carried

            lax.fori_loop(0, columns // cut, matmul, 0)

        def visit(m, carried):
            k = (m + 1) // 2
            way = lax.rem(m, 2)
            which = jnp.where(way == 0, s - k, s + k)
            pl.when(m == 2 * seq - 3)(relay_parts)

            @pl.when(jnp.logical_and(which >= 0, which < seq))
            def _():
                project(which, k, way)

            return carried

        lax.fori_loop(0, 2 * seq - 1, visit, 0)
    else:
        for q in range(pieces):
            for way in range(2):
                pl.when(s - last >= 0 if way == 0 else s + last < seq)(functools.partial(landed, way, last, q))
        relay_parts()

    for flow in part_flows:
        complete(*flow)
    for out, own, send, recv, over_send, over_recv in [w_flow, *part_flows]:
        for k in range(pairs):
            across(out, over_send, over_recv, k, own).wait_send()
        for k in range(1, pairs):
            spread(out, own, send, recv, k).wait_send()
    for k in range(seq - 1):
        for q in range(pieces):
            for way in range(2):
                pl.when(can_send(way, k))(hop(way, k, q).wait_send)
    for m in range(PARTS):
        pl.when(moves)(transfers[m].wait_send)


def fits_whole(seqs, length, width, channels):
    return seqs == 1 and length % 256 == 0 and length * (width + channels) + channels * width <= 6 << 20


def gather(hidden, weight, parts, norm_gain, collective_id=0):
    dp, seq = lax.axis_size("dp"), lax.axis_size("seq")
    seqs, part, width = hidden.shape
    columns = weight.shape[0] * dp
    fused = fits_whole(seqs, part * seq, width, columns // 2)
    pieces = 4 if part % 64 == 0 else 1
    dma, vmem, pairs = pltpu.SemaphoreType.DMA, pltpu.VMEM, dp // 2
    shape = jax.ShapeDtypeStruct
    outs = [shape((seqs, part * seq, width), BF), shape((dp,) + weight.shape, BF)]
    outs += [shape((dp,) + member.shape, BF) for member in parts]
    scratch = [dma((2, seq, pieces)), dma((2, seq, pieces))] + [dma((pairs,))] * 4
    scratch += [dma((PARTS, pairs))] * 4 + [dma((PARTS,)), dma((PARTS,)), dma((2 + PARTS,))]
    ins, in_specs = [hidden, weight, *parts], any_specs(2 + PARTS)
    out_specs = any_specs(2 + PARTS)
    if fused:
        ins.append(norm_gain.reshape(1, width))
        in_specs = in_specs + [pl.BlockSpec(memory_space=pltpu.VMEM)]
        outs += [shape((part * seq, width), BF), shape((part * seq, columns), BF)]
        scratch += [
            vmem((dp,) + weight.shape, BF), vmem((part, width), BF), dma, dma,
        ]
        out_specs = out_specs + [pl.BlockSpec(memory_space=pltpu.VMEM)] * 2
    out = pl.pallas_call(
        functools.partial(gather_kernel, dp, seq, fused),
        in_specs=in_specs,
        out_specs=out_specs,
        out_shape=outs,
        scratch_shapes=scratch,
        compiler_params=pltpu.CompilerParams(
            collective_id=collective_id, has_side_effects=True, vmem_limit_bytes=44 << 20
        ),
        name="gather_in",
    )(*ins)
    hidden = out[0].reshape(-1, width)
    w_in = out[1].reshape(columns, width)
    if fused:
        return hidden, w_in, out[2 : 2 + PARTS], out[-2], out[-1]
    x = hidden.astype(F32)
    inv = lax.rsqrt(jnp.mean(x * x, axis=1, keepdims=True) + norm_eps)
    normed = (x * inv * norm_gain.astype(F32)).astype(BF)
    return hidden, w_in, out[2:], normed, mm(normed, w_in, NT).astype(BF)


def added(ref, *others):
    total = ref[...].astype(F32)
    for other in others:
        total = total + other[...].astype(F32)
    return total


def scatter_kernel(dp, seq, count, fused, *refs):
    refs = list(refs)

    def take(count):
        out = refs[:count]
        del refs[:count]
        return out

    if fused:
        dx_ref, dz_ref, normed_ref, w_ref, full_ref = take(5)
        dn_ref = gw_ref = None
    else:
        dn_ref, gw_ref, gain_ref = take(3)
    parts = take(count)
    hid_ref, cot_ref, scale_ref = take(3)
    out_ref, gw_out = take(2)
    part_outs = take(count)
    gain_out = take(1)[0]
    own, come, gw_own, gw_x, gw_r = take(5)
    p_own, p_x, p_r, p_fin = take(count), take(count), take(count), take(count)
    g_in, g_one, g_x, g_r, g_z, g_a, g_b = take(7)
    z_load, z_send, z_recv, w_load, wx_send, wx_recv, w_send, w_recv = take(8)
    p_load, px_send, px_recv, p_send, p_recv, t_send, t_recv, gx_sem, g_send, g_recv, gz_send, gz_recv = take(12)

    d, s = place()
    seqs, part, width = out_ref.shape
    pieces = z_send.shape[1]
    piece = part // pieces
    pairs = dp // 2
    mine, odd = d // 2, lax.rem(d, 2)
    to_d, to_s = backward_home(d, s, seq)
    from_d, from_s = forward_home(d, s, seq)
    moves = jnp.logical_or(to_d != d, to_s != s)

    if fused:
        d_pre, normed, w_all, x_buf, gw_give, f_sem, x_sem = take(7)
        channels = dx_ref.shape[1]
        loads = [
            pltpu.make_async_copy(dx_ref, d_pre.at[:, pl.ds(0, channels)], f_sem.at[0]),
            pltpu.make_async_copy(dz_ref, d_pre.at[:, pl.ds(channels, channels)], f_sem.at[1]),
            pltpu.make_async_copy(w_ref, w_all, f_sem.at[2]),
            pltpu.make_async_copy(normed_ref, normed, f_sem.at[3]),
        ]
        for copy in loads:
            copy.start()

    for k in range(1, seq):
        greet((d, lax.rem(s + k, seq)))
    for k in range(1, pairs):
        greet((lax.rem(d + 2 * k, dp), s))
    greet((mate(d), s))
    greet((to_d, to_s), moves)
    greet((from_d, from_s), moves)
    pl.semaphore_wait(pltpu.get_barrier_semaphore(), seq - 1 + pairs + jnp.where(moves, 2, 0))

    def swap(src, dst, send, recv, j):
        return remote(src, dst.at[j], send.at[j], recv.at[j], (mate(d), s))

    def part_swap(m, j):
        return swap(parts[m].at[2 * j + 1 - odd], p_x[m], px_send.at[m], px_recv.at[m], j)

    def part_fetch(m, j):
        return pltpu.make_async_copy(parts[m].at[2 * j + odd], p_own[m].at[j], p_load.at[m, j])

    for m in range(count):
        for j in range(pairs):
            part_swap(m, j).start()
            part_fetch(m, j).start()

    if fused:
        for copy in loads[:3]:
            copy.wait()
        g_in[...] = jnp.zeros_like(g_in)
        w_rows = gw_own.shape[1]
        half_width = width // 2

        def chunk_of(i):
            return jnp.where(lax.rem(i, 2) == 0, seq - 1 - i // 2, i // 2)

        def dn_tasks(first, last):
            def run(i, carried):
                r = chunk_of(i)
                rows = pl.ds(pl.multiple_of(r * part, part), part)
                for at in range(2):
                    cols = pl.ds(at * half_width, half_width)
                    own[r, 0, :, cols] = mm(d_pre[rows, :], w_all[:, cols], NN).astype(BF)
                return carried

            lax.fori_loop(first, last, run, 0)

        def gain_tasks(first, last):
            def run(i, carried):
                r = chunk_of(i)
                fetch = pltpu.make_async_copy(full_ref.at[pl.ds(pl.multiple_of(r * part, part), part)], x_buf, x_sem)
                fetch.start()
                fetch.wait()

                def fold(at, carried):
                    some = pl.ds(pl.multiple_of(at * 64, 64), 64)
                    x = x_buf[some, :].astype(F32)
                    inv = lax.rsqrt(jnp.mean(x * x, axis=1, keepdims=True) + norm_eps)
                    weighted = own[r, 0, some, :].astype(F32) * (x * inv)
                    g_in[...] += jnp.sum(weighted.reshape(8, 8, width), axis=0)
                    return carried

                return lax.fori_loop(0, part // 64, fold, carried)

            lax.fori_loop(first, last, run, 0)

        def gw_task(dest, out, j):
            cols = pl.ds(pl.multiple_of(dest * w_rows, w_rows), w_rows)
            for at in range(2):
                some = pl.ds(at * half_width, half_width)
                out[j, :, some] = mm(d_pre[:, cols], normed[:, some], TN).astype(BF)

        def gw_swap(j):
            return swap(gw_give.at[j], gw_x, wx_send, wx_recv, j)

        def gw_away():
            def run(j, carried):
                gw_task(2 * j + 1 - odd, gw_give, j)
                gw_swap(j).start()
                return carried

            lax.fori_loop(0, pairs, run, 0)

        def gw_home():
            def run(k, carried):
                j = lax.rem(mine + 1 + k, pairs)
                gw_task(2 * j + odd, gw_own, j)
                return carried

            lax.fori_loop(0, pairs, run, 0)

        def gw_ready(j):
            pass
    else:
        def gw_swap(j):
            return swap(gw_ref.at[2 * j + 1 - odd], gw_x, wx_send, wx_recv, j)

        def gw_fetch(j):
            return pltpu.make_async_copy(gw_ref.at[2 * j + odd], gw_own.at[j], w_load.at[j])

        def chunk(r):
            return pltpu.make_async_copy(dn_ref.at[:, pl.ds(r * part, part), :], own.at[r], z_load.at[r])

        for r in range(seq):
            chunk(r).start()
        for j in range(pairs):
            gw_swap(j).start()
            gw_fetch(j).start()
        for r in range(seq):
            chunk(r).wait()
        g_in[...] = gain_ref[...]

        def gw_ready(j):
            gw_fetch(j).wait()

    def give(way, r, q):
        rows = pl.ds(q * piece, piece)
        slot = r if way == 0 else jnp.where(s - 1 == r, seq, r)
        near = s + 1 if way == 0 else s - 1
        return remote(own.at[r, :, rows, :], come.at[slot, :, rows, :], z_send.at[r, q], z_recv.at[slot, q], (d, near))

    def landed(slot, q):
        rows = pl.ds(q * piece, piece)
        here = come.at[slot, :, rows, :]
        remote(here, here, z_send.at[0, q], z_recv.at[slot, q], (d, s)).wait_recv()

    def begin():
        for q in range(pieces):
            pl.when(s == 0)(give(0, seq - 1, q).start)
            pl.when(s == seq - 1)(give(1, 0, q).start)

    def hop(turn, q):
        rows = pl.ds(q * piece, piece)
        for way in range(2):
            far = s if way == 0 else seq - 1 - s
            i = turn - far
            r = seq - 1 - i if way == 0 else i
            before = r + 1 if way == 0 else r - 1
            sends = jnp.logical_and(i >= 0, s < r if way == 0 else s > r)

            @pl.when(jnp.logical_and(sends, far > 0))
            def _():
                landed(r, q)
                own[r, :, rows, :] = added(own.at[r, :, rows, :], come.at[r, :, rows, :]).astype(BF)

            pl.when(jnp.logical_and(sends, i > 0))(give(way, before, q).wait_send)
            pl.when(jnp.logical_and(sends, far + i > 0))(give(way, r, q).start)

    def onward(part_own, part_r, send, recv, k):
        j = lax.rem(mine + k, pairs)
        return remote(part_own.at[j], part_r.at[k - 1], send.at[k], recv.at[k], (lax.rem(d + 2 * k, dp), s))

    def part_onward(m, k):
        return onward(p_own[m], p_r[m], p_send.at[m], p_recv.at[m], k)

    def gw_onward(k):
        return onward(gw_own, gw_r, w_send, w_recv, k)

    def part_join():
        for m in range(count):
            for k in range(1, pairs + 1):
                j = lax.rem(mine + k, pairs)
                part_fetch(m, j).wait()
                part_swap(m, j).wait_recv()
                if k < pairs:
                    p_own[m][j] = added(p_own[m].at[j], p_x[m].at[j]).astype(BF)
                    part_onward(m, k).start()

    def gw_join():
        for k in range(1, pairs + 1):
            j = lax.rem(mine + k, pairs)
            gw_ready(j)
            gw_swap(j).wait_recv()
            if k < pairs:
                gw_own[j] = added(gw_own.at[j], gw_x.at[j]).astype(BF)
                gw_onward(k).start()

    gain_swap = remote(g_one, g_x, gx_sem.at[0], gx_sem.at[1], (mate(d), s))

    def gain_near(k):
        return remote(g_a, g_r.at[k - 1], g_send.at[k], g_recv.at[k], (lax.rem(d + 2 * k, dp), s))

    def gain_far(k):
        return remote(g_b, g_z.at[k - 1], gz_send.at[k], gz_recv.at[k], (d, lax.rem(s + k, seq)))

    def gain_middle():
        gain_swap.wait_recv()
        g_a[...] = g_one[...] + g_x[...]
        for k in range(1, pairs):
            gain_near(k).start()

    def gain_last():
        for k in range(1, pairs):
            gain_near(k).wait_recv()
        g_b[...] = added(g_a, *[g_r.at[k] for k in range(pairs - 1)])
        for k in range(1, seq):
            gain_far(k).start()

    backs = [remote(p_fin[m], part_outs[m], t_send.at[m], t_recv.at[m], (to_d, to_s)) for m in range(count)]
    stays = [pltpu.make_async_copy(p_fin[m], part_outs[m], t_send.at[count + m]) for m in range(count)]

    def part_finish():
        for m in range(count):
            for k in range(1, pairs):
                part_onward(m, k).wait_recv()
            rest = [p_r[m].at[k] for k in range(pairs - 1)]
            p_fin[m][...] = added(p_own[m].at[mine], p_x[m].at[mine], *rest).astype(BF)
            pl.when(moves)(backs[m].start)
            pl.when(jnp.logical_not(moves))(stays[m].start)

    if fused:
        dn_tasks(0, 2)
        begin()
        part_join()
        loads[3].wait()
        gw_away()
        gw_home()
        gw_join()
        gain_tasks(0, 2)
        dn_tasks(2, seq)
        gain_tasks(2, seq)
    else:
        begin()
        part_join()
        gw_join()
    g_one[...] = jnp.sum(g_in[...], axis=0, keepdims=True)
    gain_swap.start()
    later = [gain_middle, gain_last, part_finish]
    for i in range(seq - 1):
        for q in range(pieces):
            hop(i, q)
            if later and q == pieces - 1:
                later.pop(0)()
    for task in later:
        task()

    for k in range(1, pairs):
        gw_onward(k).wait_recv()
    gw_out[...] = added(gw_own.at[mine], gw_x.at[mine], *[gw_r.at[k] for k in range(pairs - 1)])
    for k in range(1, seq):
        gain_far(k).wait_recv()
    gain_out[...] = added(g_b, *[g_z.at[k] for k in range(seq - 1)])

    some = math.gcd(piece, 64)
    for q in range(pieces):
        pl.when(s > 0)(functools.partial(landed, s, q))
        pl.when(s < seq - 1)(functools.partial(landed, seq, q))

        def settle(at, carried):
            rows = pl.ds(pl.multiple_of(q * piece + at * some, some), some)
            from_left = jnp.where(s > 0, come[s, :, rows, :].astype(F32), 0.0)
            from_right = jnp.where(s < seq - 1, come[seq, :, rows, :].astype(F32), 0.0)
            total = own[s, :, rows, :].astype(F32) + from_left + from_right
            x = hid_ref[:, rows, :].astype(F32)
            inv = lax.rsqrt(jnp.mean(x * x, axis=2, keepdims=True) + norm_eps)
            scaled = total * scale_ref[...].astype(F32)[None]
            out_ref[:, rows, :] = (
                cot_ref[:, rows, :].astype(F32)
                + inv * scaled
                - x * (inv * inv * inv) * jnp.mean(x * scaled, axis=2, keepdims=True)
            ).astype(BF)
            return carried

        lax.fori_loop(0, piece // some, settle, 0)

    for q in range(pieces):
        pl.when(s < seq - 1)(give(0, s + 1, q).wait_send)
        pl.when(s > 0)(give(1, s - 1, q).wait_send)
    gain_swap.wait_send()
    for j in range(pairs):
        gw_swap(j).wait_send()
        for m in range(count):
            part_swap(m, j).wait_send()
    for k in range(1, pairs):
        gw_onward(k).wait_send()
        gain_near(k).wait_send()
        for m in range(count):
            part_onward(m, k).wait_send()
    for k in range(1, seq):
        gain_far(k).wait_send()
    for m in range(count):
        pl.when(moves)(backs[m].wait_send)
        pl.when(moves)(remote(p_fin[m], part_outs[m], t_send.at[m], t_recv.at[m], (to_d, to_s)).wait_recv)
        pl.when(jnp.logical_not(moves))(stays[m].wait)


def scatter(d_x, d_z, normed, w_in, hidden, parts, hidden_in, cotangent, norm_gain, collective_id=1):
    dp, seq = lax.axis_size("dp"), lax.axis_size("seq")
    seqs, part, width = hidden_in.shape
    tokens, channels = d_x.shape
    w_rows = 2 * channels // dp
    fused = fits_whole(seqs, part * seq, width, channels)
    pieces = 4 if part % 64 == 0 else 1
    pairs, count = dp // 2, len(parts)
    dma, vmem, shape = pltpu.SemaphoreType.DMA, pltpu.VMEM, jax.ShapeDtypeStruct
    here = pl.BlockSpec(memory_space=pltpu.VMEM)
    if fused:
        ins, in_specs = [d_x, d_z, normed, w_in, hidden], any_specs(5)
        extra = [
            vmem((tokens, 2 * channels), BF), vmem((tokens, width), BF), vmem((2 * channels, width), BF),
            vmem((part, width), BF), vmem((pairs, w_rows, width), BF), dma((4,)), dma,
        ]
    else:
        d_pre = jnp.concatenate([d_x, d_z], axis=1)
        x = hidden.astype(F32)
        d_normed = mm(d_pre, w_in, NN)
        inv = lax.rsqrt(jnp.mean(x * x, axis=1, keepdims=True) + norm_eps)
        gain = jnp.pad(jnp.sum(d_normed * x * inv, axis=0)[None], ((0, 7), (0, 0)))
        ins = [
            d_normed.astype(BF).reshape(seqs, -1, width),
            mm(d_pre, normed, TN).astype(BF).reshape(dp, w_rows, width), gain,
        ]
        in_specs, extra = any_specs(2) + [here], []
    part_shapes = [member.shape[1:] for member in parts]
    token_shape, one = (seqs, part, width), (1, width)

    def each(count):
        return [vmem((count,) + member, BF) for member in part_shapes]

    out = pl.pallas_call(
        functools.partial(scatter_kernel, dp, seq, len(parts), fused),
        in_specs=in_specs + any_specs(count) + [here] * 3,
        out_specs=[here] * (3 + count),
        out_shape=[shape(token_shape, BF), shape((w_rows, width), F32)]
        + [shape(member, BF) for member in part_shapes]
        + [shape(one, F32)],
        scratch_shapes=[
            vmem((seq,) + token_shape, BF), vmem((seq + 1,) + token_shape, BF),
            vmem((pairs, w_rows, width), BF), vmem((pairs, w_rows, width), BF), vmem((pairs - 1, w_rows, width), BF),
            *each(pairs), *each(pairs), *each(pairs - 1), *[vmem(member, BF) for member in part_shapes],
            vmem((8, width), F32), vmem(one, F32), vmem(one, F32), vmem((pairs - 1,) + one, F32),
            vmem((seq - 1,) + one, F32), vmem(one, F32), vmem(one, F32),
            dma((seq,)), dma((seq, pieces)), dma((seq + 1, pieces)),
            dma((pairs,)), dma((pairs,)), dma((pairs,)), dma((pairs,)), dma((pairs,)),
            *[dma((count, pairs))] * 5, dma((2 * count,)), dma((count,)),
            dma((2,)), dma((pairs,)), dma((pairs,)), dma((seq,)), dma((seq,)),
            *extra,
        ],
        compiler_params=pltpu.CompilerParams(
            collective_id=collective_id, has_side_effects=True, vmem_limit_bytes=63 << 20
        ),
        name="scatter_out",
    )(*ins, *parts, hidden_in, cotangent, norm_gain.reshape(1, width))
    return out[0], out[1], out[2 : 2 + count], out[-1].reshape(width)


def reduce_kernel(dp, seq, grads, *refs):
    refs = list(refs)

    def take(count):
        out = refs[:count]
        del refs[:count]
        return out

    wide_ref, thin_ref = take(2)
    g_ref = take(1)[0] if grads else None
    wide_out, thin_out = take(2)
    g_out = take(1)[0] if grads else None
    wide_x, thin_x, wide_s, thin_s = take(4)
    xw_send, xw_recv, xt_send, xt_recv, sw_send, sw_recv, st_send, st_recv = take(8)
    d, s = place()
    rows = wide_ref.shape[0] // seq
    pairs = dp // 2
    mine, odd = d // 2, lax.rem(d, 2)
    for k in range(1, seq):
        greet((d, lax.rem(s + k, seq)))
    if grads:
        for k in range(1, pairs):
            greet((lax.rem(d + 2 * k, dp), s))
        greet((mate(d), s))
    pl.semaphore_wait(pltpu.get_barrier_semaphore(), seq - 1 + (pairs if grads else 0))

    def piece(ref, which):
        return ref.at[pl.ds(pl.multiple_of(which * rows, rows), rows)]

    def ask(k):
        to = lax.rem(s + k, seq)
        return (
            remote(piece(wide_ref, to), wide_x.at[k - 1], xw_send.at[k - 1], xw_recv.at[k - 1], (d, to)),
            remote(thin_ref.at[to], thin_x.at[k - 1], xt_send.at[k - 1], xt_recv.at[k - 1], (d, to)),
        )

    def tell(k):
        to = lax.rem(s + k, seq)
        return (
            remote(wide_s, piece(wide_out, s), sw_send.at[k - 1], sw_recv.at[k - 1], (d, to)),
            remote(thin_s, thin_out.at[s], st_send.at[k - 1], st_recv.at[k - 1], (d, to)),
        )

    def told(k):
        source = lax.rem(s - k + seq, seq)
        return (
            remote(wide_s, piece(wide_out, source), sw_send.at[k - 1], sw_recv.at[k - 1], (d, s)),
            remote(thin_s, thin_out.at[source], st_send.at[k - 1], st_recv.at[k - 1], (d, s)),
        )

    order = sorted(range(1, seq), key=lambda k: -min(k, seq - k))
    for k in order:
        for copy in ask(k):
            copy.start()
    if grads:
        g_own, g_x, g_r, g_load, gx_send, gx_recv, g_send, g_recv = take(8)

        def swap(j):
            return remote(g_ref.at[2 * j + 1 - odd], g_x.at[j], gx_send.at[j], gx_recv.at[j], (mate(d), s))

        def fetch(j):
            return pltpu.make_async_copy(g_ref.at[2 * j + odd], g_own.at[j], g_load.at[j])

        def onward(k):
            to = lax.rem(d + 2 * k, dp)
            return remote(g_own.at[to // 2], g_r.at[k - 1], g_send.at[k], g_recv.at[k], (to, s))

        for j in range(pairs):
            swap(j).start()
            fetch(j).start()
        for k in range(1, pairs + 1):
            j = lax.rem(mine + k, pairs)
            fetch(j).wait()
            swap(j).wait_recv()
            if k < pairs:
                g_own[j] = added(g_own.at[j], g_x.at[j]).astype(BF)
                onward(k).start()
    for k in order:
        for copy in ask(k):
            copy.wait_recv()
    start = pl.ds(pl.multiple_of(s * rows, rows), rows)
    total = wide_ref[start, :].astype(F32)
    thin = thin_ref[s]
    for k in range(seq - 1):
        total = total + wide_x[k].astype(F32)
        thin = thin + thin_x[k]
    wide_s[...] = total.astype(BF)
    thin_s[...] = thin
    for k in order:
        for copy in tell(k):
            copy.start()
    wide_out[start, :] = total.astype(BF)
    thin_out[s] = thin
    if grads:
        for k in range(1, pairs):
            onward(k).wait_recv()
        g_out[...] = added(g_own.at[mine], g_x.at[mine], *[g_r.at[k] for k in range(pairs - 1)]).astype(BF)
        for j in range(pairs):
            swap(j).wait_send()
        for k in range(1, pairs):
            onward(k).wait_send()
    for k in order:
        for copy in told(k):
            copy.wait_recv()
    for k in order:
        for copy in ask(k) + tell(k):
            copy.wait_send()


def reduce_over_seq(wide_part, thin_part, collective_id, grads=None):
    dp, seq = lax.axis_size("dp"), lax.axis_size("seq")
    tokens, cols = wide_part.shape
    thin_part = jnp.swapaxes(thin_part.reshape(-1, seq, tokens // seq), 0, 1)
    dma, vmem, shape = pltpu.SemaphoreType.DMA, pltpu.VMEM, jax.ShapeDtypeStruct
    here = pl.BlockSpec(memory_space=pltpu.VMEM)
    rows, few, pairs = tokens // seq, thin_part.shape[1:], dp // 2
    ins, in_specs = [wide_part.astype(BF), thin_part], [here] * 2
    outs = [shape((tokens, cols), BF), shape(thin_part.shape, F32)]
    scratch = [
        vmem((seq - 1, rows, cols), BF), vmem((seq - 1,) + few, F32), vmem((rows, cols), BF), vmem(few, F32),
    ] + [dma((seq - 1,))] * 8
    if grads is not None:
        ins, in_specs = ins + [grads], in_specs + any_specs(1)
        outs.append(shape(grads.shape[1:], BF))
        scratch += [vmem((pairs,) + grads.shape[1:], BF)] * 2 + [vmem((pairs - 1,) + grads.shape[1:], BF)]
        scratch += [dma((pairs,))] * 5
    out = pl.pallas_call(
        functools.partial(reduce_kernel, dp, seq, grads is not None),
        in_specs=in_specs,
        out_specs=[here] * len(outs),
        out_shape=outs,
        scratch_shapes=scratch,
        compiler_params=pltpu.CompilerParams(
            collective_id=collective_id, has_side_effects=True, vmem_limit_bytes=24 << 20
        ),
        name="reduce_seq",
    )(*ins)
    return (out[0], jnp.swapaxes(out[1], 0, 1).reshape(-1, tokens)) + tuple(out[2:])


def homes_back(dp, seq):
    pairs = []
    for d in range(dp):
        for s in range(seq):
            home_d, home_s = 2 * (d // 2) + s % 2, (seq // 2) * (d % 2) + s // 2
            pairs.append((home_d * seq + home_s, d * seq + s))
    return pairs


def local(
    hidden_in,
    doc_lengths,
    norm_gain,
    in_weight,
    conv_weight,
    conv_bias,
    x_weight,
    dt_weight,
    dt_bias,
    skip_gain,
    out_weight,
    out_cotangent,
):
    seqs, part_len, width = hidden_in.shape
    dp, seq = lax.axis_size("dp"), lax.axis_size("seq")
    length = part_len * seq
    tokens = seqs * length
    rows = out_weight.shape[0]
    channels = rows * dp
    lag_max = KCONV - 1

    vectors = [conv_weight, conv_bias[None], dt_bias[None], skip_gain[None]]
    vectors = jnp.pad(jnp.concatenate(vectors, axis=0), ((0, 16 - KCONV - 3), (0, 0)))
    parts = [out_weight, x_weight, dt_weight, vectors]
    hidden, w_in, parts, normed, pre = gather(hidden_in, in_weight, parts, norm_gain)
    cot, pre = lax.optimization_barrier((out_cotangent, pre))
    cot = lax.all_gather(cot, "seq", axis=1, tiled=True).reshape(tokens, width)

    w_out, w_x, w_dt = (part.reshape(channels, part.shape[2]) for part in parts[:3])
    vectors = jnp.swapaxes(parts[3], 0, 1).reshape(16, channels).astype(F32)
    taps, conv_shift, rate_shift, skip = vectors[:KCONV], vectors[KCONV], vectors[KCONV + 1], vectors[KCONV + 2]

    begins, places = token_begins(doc_lengths, length)
    keep = (places[None, :] != begins).astype(F32).reshape(tokens, 1)
    valid = [(places[None, :] - (lag_max - w) >= begins)[:, :, None] for w in range(KCONV)]

    x_inner = pre[:, :channels].reshape(seqs, length, channels)

    padded = jnp.pad(x_inner, ((0, 0), (lag_max, 0), (0, 0)))
    conv_sum = jnp.broadcast_to(conv_shift, (seqs, length, channels))
    for w in range(KCONV):
        window = padded[:, w : w + length, :].astype(F32)
        conv_sum = conv_sum + jnp.where(valid[w], window * taps[w], 0.0)
    conv_flat = conv_sum.reshape(tokens, channels)
    xc_low = jax.nn.silu(conv_flat).astype(BF)
    rate, thin = reduce_over_seq(mm(xc_low, w_x[:, :R], NN), mm(w_x[:, R:], xc_low, ((0,), (1,))), 2)
    key, query = thin[:N].T, thin[N:].T
    key_lanes, query_lanes = (
        jnp.broadcast_to(part.astype(BF)[:, :, None], (tokens, N, LANES)) for part in (key, query)
    )
    ksum = jnp.sum(key * key, axis=1, keepdims=True)
    keep_lanes = jnp.broadcast_to(keep, (tokens, LANES))
    ksum_lanes = jnp.broadcast_to(ksum, (tokens, LANES))
    vectors = jnp.pad(jnp.stack([rate_shift, skip]), ((0, 6), (0, 0)))
    states, y_full, gated = scan_forward(
        seqs, length, xc_low, pre, rate, key_lanes, query_lanes, keep_lanes, ksum_lanes, w_dt, vectors
    )
    branch = mm(gated, w_out, NN).astype(BF).reshape(seqs, length, width)
    branch = lax.psum_scatter(branch, "seq", scatter_dimension=1, tiled=True)
    output = (hidden_in.astype(F32) + branch.astype(F32)).astype(BF)

    d_z, rest, dq, dk, d_norm, d_row, grad_dt, sums = scan_backward(
        seqs, length, mm(cot, w_out, NT), y_full, xc_low, pre, rate, key_lanes, query_lanes, keep_lanes, ksum_lanes, w_dt, vectors, states
    )
    dq, dk = dq.reshape(tokens, N), dk.reshape(tokens, N)
    d_norm = -jnp.sum(d_norm, axis=1, keepdims=True)
    d_keys = dk + 2.0 * key * d_norm
    grad_out = mm(gated, cot, TN).astype(BF).reshape(dp, rows, width)
    d_row, thin, grad_out = reduce_over_seq(d_row, jnp.concatenate([d_keys.T, dq.T], axis=0), 3, grad_out)
    grad_out = lax.ppermute(grad_out, ("dp", "seq"), homes_back(dp, seq))
    d_proj = jnp.concatenate([d_row, thin.T.astype(BF)], axis=1)
    d_conv_out = mm(d_proj, w_x, NT) + rest
    d_conv = (d_conv_out * silu_slope(conv_flat)).reshape(seqs, length, channels)

    tap_grads = []
    d_x_inner = jnp.zeros((seqs, length, channels), F32)
    for w in range(KCONV):
        lag = lag_max - w
        window = padded[:, w : w + length, :].astype(F32)
        masked = jnp.where(valid[w], d_conv, 0.0)
        tap_grads.append(jnp.sum(masked * window, axis=(0, 1)))
        d_x_inner = d_x_inner + jnp.pad(masked, ((0, 0), (0, lag), (0, 0)))[:, lag:, :] * taps[w]
    vector_grads = jnp.stack(
        tap_grads + [jnp.sum(d_conv, axis=(0, 1)), jnp.sum(sums[:8], axis=0), jnp.sum(sums[8:], axis=0)], axis=0
    )
    vector_grads = jnp.pad(vector_grads, ((0, 16 - KCONV - 3), (0, 0))).reshape(16, dp, rows)
    grads = [part.astype(BF).reshape(dp, rows, -1) for part in (mm(xc_low, d_proj, TN), grad_dt)]
    grads.append(jnp.swapaxes(vector_grads, 0, 1).astype(BF))
    grad_in, grad_in_weight, grads, grad_norm_gain = scatter(
        d_x_inner.reshape(tokens, channels).astype(BF), d_z, normed, w_in, hidden, grads,
        hidden_in, out_cotangent, norm_gain,
    )
    grad_x, grad_dt, grad_vectors = (part.astype(F32) for part in grads)
    grad_out_weight = grad_out.astype(F32)
    return (
        output,
        grad_in,
        grad_norm_gain,
        grad_in_weight,
        grad_vectors[:KCONV],
        grad_vectors[KCONV],
        grad_x,
        grad_dt,
        grad_vectors[KCONV + 1],
        grad_vectors[KCONV + 2],
        grad_out_weight,
    )


def solution(mesh):
    both = ("dp", "seq")
    tokens = P("dp", "seq", None)
    matrix, vector = P(both, None), P(both)
    return jax.shard_map(
        local,
        mesh=mesh,
        in_specs=(
            tokens, P("dp", None), P(), matrix, P(None, both), vector,
            matrix, matrix, vector, vector, matrix, tokens,
        ),
        out_specs=(
            tokens, tokens, P(), matrix, P(None, both), vector,
            matrix, matrix, vector, vector, matrix,
        ),
        check_vma=False,
    )
```

```python
import functools
import math

import jax
import jax.numpy as jnp
from jax import lax
from jax.experimental import pallas as pl
from jax.experimental.pallas import tpu as pltpu
from jax.sharding import PartitionSpec as P

N = 16
R = 128
KCONV = 4
CHUNK = 16
LANES = 128
GROUP = 1024
BLOCK = 128

norm_eps = 1e-05
BF = jnp.bfloat16
F32 = jnp.float32


def silu_slope(pre_value):
    sigmoid_of = jax.nn.sigmoid(pre_value)
    return sigmoid_of * (1.0 + pre_value * (1.0 - sigmoid_of))


def token_begins(lengths, position_count):
    doc_ends = jnp.cumsum(lengths, axis=1)
    doc_starts = doc_ends - lengths
    places = jnp.arange(position_count, dtype=jnp.int32)
    inside = doc_starts[:, None, :] <= places[None, :, None]
    return (jnp.max(jnp.where(inside, doc_starts[:, None, :], 0), axis=2), places)


def mm(left, right, dims):
    return lax.dot_general(left, right, (dims, ((), ())), preferred_element_type=F32)


NN = ((1,), (0,))
NT = ((1,), (1,))
TN = ((0,), (0,))


def row(ref, i, lane):
    return jnp.broadcast_to(ref[i : i + 1, pl.ds(lane, LANES)], (8, LANES))


def wide(ref, rows, count):
    value = ref[rows, :]
    return jnp.concatenate([value] * (count // LANES), axis=1)


def merge(even, odd, stride):
    low = lax.broadcasted_iota(jnp.int32, (8, LANES), 0) % (2 * stride) < stride
    if stride == 4:
        return jnp.where(low, even, odd) + pltpu.roll(jnp.where(low, odd, even), 4, 0)
    return jnp.where(low, even + pltpu.roll(even, 8 - stride, 0), odd + pltpu.roll(odd, stride, 0))


def collect(stack, value, descending):
    level = 0
    while stack and stack[-1][0] == level:
        other = stack.pop()[1]
        value = merge(value, other, 1 << level) if descending else merge(other, value, 1 << level)
        level += 1
    stack.append((level, value))


def each_chunk(tokens, channels, body):
    group = math.gcd(channels, 512)

    def run(k, carried):
        rows = pl.ds(pl.multiple_of(k * CHUNK, CHUNK), CHUNK)
        for first in range(0, channels, group):
            body(rows, pl.ds(first, group), first)
        return carried

    lax.fori_loop(0, tokens // CHUNK, run, 0)


def load_carry(carry, tiles):
    out = []
    for lane in tiles:
        out += [carry[0:8, pl.ds(lane, LANES)], carry[8:16, pl.ds(lane, LANES)]]
    return tuple(out)


def store_carry(carry, tiles, values):
    for j, lane in enumerate(tiles):
        carry[0:8, pl.ds(lane, LANES)] = values[2 * j]
        carry[8:16, pl.ds(lane, LANES)] = values[2 * j + 1]


def halves(value):
    return [value[0:8], value[8:16]]


def token(keys, queries, keeps, i):
    return row(keeps, i, 0), halves(keys[i].astype(F32)), halves(queries[i].astype(F32))


def lane_groups(channels):
    group = math.gcd(channels, GROUP)
    return [list(range(first, first + group, LANES)) for first in range(0, channels, group)]


def forward_kernel(
    xc_ref, z_ref, rate_ref, key_ref, query_ref, keep_ref, ksum_ref, wdt_ref, vec_ref,
    s_ref, y_ref, gated_ref, step, inj, carry,
):
    @pl.when(pl.program_id(1) == 0)
    def _():
        carry[...] = jnp.zeros_like(carry)

    tokens, channels = xc_ref.shape
    step[...] = mm(rate_ref[...], wdt_ref[...], NT)

    def prepare(rows, cols, first):
        beta = jax.nn.sigmoid(step[rows, cols] + vec_ref[0:1, cols])
        eps = beta / (1.0 + beta * wide(ksum_ref, rows, cols.size))
        step[rows, cols] = eps
        inj[rows, cols] = eps * xc_ref[rows, cols].astype(F32)

    each_chunk(tokens, channels, prepare)
    for tiles in lane_groups(channels):

        def chunk(k, state):
            state = list(state)
            base = pl.multiple_of(k * CHUNK, CHUNK)
            steps, injs, keeps, keys, queries = (
                r.at[pl.ds(base, CHUNK)] for r in (step, inj, keep_ref, key_ref, query_ref)
            )
            saved = s_ref.at[pl.ds(pl.multiple_of(k * CHUNK * N, CHUNK * N), CHUNK * N)]
            stacks = [[] for _ in tiles]
            for i in range(CHUNK):
                keep, key, query = token(keys, queries, keeps, i)
                ksq = [keep * key[h] * key[h] for h in range(2)]
                for j, lane in enumerate(tiles):
                    eps, push = row(steps, i, lane), row(injs, i, lane)
                    for h in range(2):
                        state[2 * j + h] = (keep - eps * ksq[h]) * state[2 * j + h] + push * key[h]
                    both = jnp.concatenate([state[2 * j], state[2 * j + 1]], axis=0)
                    saved[i * N : (i + 1) * N, pl.ds(lane, LANES)] = both.astype(BF)
                    collect(stacks[j], state[2 * j] * query[0] + state[2 * j + 1] * query[1], False)
                    if i % 8 == 7:
                        y_ref[pl.ds(pl.multiple_of(base + i - 7, 8), 8), pl.ds(lane, LANES)] = stacks[j].pop()[1]
            return tuple(state)

        store_carry(carry, tiles, lax.fori_loop(0, tokens // CHUNK, chunk, load_carry(carry, tiles)))

    def emit(rows, cols, first):
        y_full = y_ref[rows, cols] + vec_ref[1:2, cols] * xc_ref[rows, cols].astype(F32)
        y_ref[rows, cols] = y_full
        z = z_ref[rows, cols].astype(F32)
        gated_ref[rows, cols] = (y_full * (z * jax.nn.sigmoid(z))).astype(BF)

    each_chunk(tokens, channels, emit)


def backward_kernel(
    dg_ref, y_ref, xc_ref, z_ref, rate_ref, key_ref, query_ref, keep_ref, ksum_ref, wdt_ref, vec_ref, s_ref, before_ref,
    dz_ref, rest_ref, dq_ref, dk_ref, dnorm_ref, drow_ref, gdt_ref, sums_ref,
    step, inj, dy, mix, pull, beta, drate, carry, acc_q, acc_k,
):
    turn = pl.program_id(1)
    tokens, channels = xc_ref.shape
    chunks = tokens // CHUNK

    @pl.when(jnp.logical_and(pl.program_id(0) == 0, turn == 0))
    def _():
        gdt_ref[...] = jnp.zeros_like(gdt_ref)
        sums_ref[...] = jnp.zeros_like(sums_ref)

    @pl.when(turn == 0)
    def _():
        carry[...] = jnp.zeros_like(carry)

    beta[...] = mm(rate_ref[...], wdt_ref[...], NT)

    def prepare(rows, cols, first):
        rate_beta = jax.nn.sigmoid(beta[rows, cols] + vec_ref[0:1, cols])
        eps = rate_beta / (1.0 + rate_beta * wide(ksum_ref, rows, cols.size))
        beta[rows, cols] = rate_beta
        step[rows, cols] = eps
        xc = xc_ref[rows, cols].astype(F32)
        inj[rows, cols] = eps * xc
        z = z_ref[rows, cols].astype(F32)
        sig = jax.nn.sigmoid(z)
        d_gated = dg_ref[rows, cols]
        d_y = d_gated * (z * sig)
        dy[rows, cols] = d_y
        dz_ref[rows, cols] = (d_gated * y_ref[rows, cols] * (sig * (1.0 + z * (1.0 - sig)))).astype(BF)
        weighted = d_y * xc
        sums_ref[8:16, cols] += weighted[0:8] + weighted[8:16]

    each_chunk(tokens, channels, prepare)
    for tiles in lane_groups(channels):
        start = tiles[0] == 0

        def chunk(back, carried):
            k = chunks - 1 - back
            pulled, now = list(carried[0]), list(carried[1])
            base = pl.multiple_of(k * CHUNK, CHUNK)
            steps, injs, dys, keeps, keys, queries = (
                r.at[pl.ds(base, CHUNK)] for r in (step, inj, dy, keep_ref, key_ref, query_ref)
            )
            stacks = [([], []) for _ in tiles]
            for i in reversed(range(CHUNK)):
                keep, key, query = token(keys, queries, keeps, i)
                kept = [keep * key[h] for h in range(2)]
                ksq = [kept[h] * key[h] for h in range(2)]
                if i > 0:
                    before = pl.ds(pl.multiple_of((base + i) * N - N, N), N)
                else:
                    before = pl.ds(pl.multiple_of(jnp.maximum(base * N - N, 0), N), N)
                seen, plain, scaled = [0.0, 0.0], [0.0, 0.0], [0.0, 0.0]
                for j, lane in enumerate(tiles):
                    eps, push, d_y = row(steps, i, lane), row(injs, i, lane), row(dys, i, lane)
                    prior = s_ref[before, pl.ds(lane, LANES)]
                    if i == 0:
                        prior = jnp.where(k > 0, prior, before_ref[:, pl.ds(lane, LANES)])
                    prior = halves(prior.astype(F32))
                    by_key, by_square = [], []
                    for h in range(2):
                        at = 2 * j + h
                        grad = pulled[at] + d_y * query[h]
                        pulled[at] = (keep - eps * ksq[h]) * grad
                        keyed = eps * (grad * key[h])
                        prod = keyed * prior[h]
                        seen[h] += now[at] * d_y
                        plain[h] += grad * push
                        scaled[h] += prod
                        by_key.append(keyed)
                        by_square.append(prod * kept[h])
                        now[at] = prior[h]
                    collect(stacks[j][0], by_key[0] + by_key[1], True)
                    collect(stacks[j][1], by_square[0] + by_square[1], True)
                    if i % 8 == 0:
                        rows = pl.ds(pl.multiple_of(base + i, 8), 8)
                        mix[rows, pl.ds(lane, LANES)] = stacks[j][0].pop()[1]
                        pull[rows, pl.ds(lane, LANES)] = stacks[j][1].pop()[1]
                for ref, parts in ((acc_q, seen), (acc_k, [plain[h] - 2.0 * keep * scaled[h] for h in range(2)])):
                    for h in range(2):
                        rows = pl.ds(pl.multiple_of((base + i) * N + 8 * h, 8), 8)
                        if start:
                            ref[rows, :] = parts[h]
                        else:
                            ref[rows, :] += parts[h]
            return (tuple(pulled), tuple(now))

        now = []
        for lane in tiles:
            now += halves(s_ref[tokens * N - N : tokens * N, pl.ds(lane, LANES)].astype(F32))
        pulled, now = lax.fori_loop(0, chunks, chunk, (load_carry(carry, tiles), tuple(now)))
        store_carry(carry, tiles, pulled)

    ones = jnp.ones((LANES, LANES), BF)
    diagonal = lax.broadcasted_iota(jnp.int32, (LANES, LANES), 0) == (
        lax.broadcasted_iota(jnp.int32, (LANES, LANES), 1)
    )
    for out, ref in ((dq_ref, acc_q), (dk_ref, acc_k)):
        for first in range(0, tokens * N, LANES):
            sums = mm(ref[first : first + LANES, :].astype(BF), ones, NN)
            at = first // LANES
            out[at : at + 1, :] = jnp.sum(jnp.where(diagonal, sums, 0.0), axis=0, keepdims=True)

    def settle(rows, cols, first):
        rate_beta, eps = beta[rows, cols], step[rows, cols]
        through = mix[rows, cols]
        change = through * xc_ref[rows, cols].astype(F32) - pull[rows, cols]
        inverse = 1.0 / (1.0 + rate_beta * wide(ksum_ref, rows, cols.size))
        low = (change * inverse * (1.0 - rate_beta)).astype(BF)
        drate[rows, cols] = low
        lowered = low.astype(F32)
        sums_ref[0:8, cols] += lowered[0:8] + lowered[8:16]
        rest_ref[rows, cols] = through + vec_ref[1:2, cols] * dy[rows, cols]
        square = change * eps
        total = square[:, 0:LANES]
        for lane in range(LANES, cols.size, LANES):
            total = total + square[:, lane : lane + LANES]
        if first == 0:
            dnorm_ref[rows, :] = total
        else:
            dnorm_ref[rows, :] += total

    each_chunk(tokens, channels, settle)
    drow_ref[...] = mm(drate[...], wdt_ref[...], NN)
    gdt_ref[...] += mm(drate[...], rate_ref[...], TN)


def scan_blocks(length):
    block = math.gcd(length, BLOCK)
    return block, length // block


def row_spec(rows, cols, when, col=0):
    return pl.BlockSpec((rows, cols), lambda b, t: (when(b, t), col))


def spread_spec(block, when):
    return pl.BlockSpec((block, N, LANES), lambda b, t: (when(b, t), 0, 0))


def whole(array):
    return pl.BlockSpec(array.shape, lambda b, t: (0, 0), pipeline_mode=pl.Buffered(1))


def scan_forward(seqs, length, xc, pre, rate, key_lanes, query_lanes, keep_lanes, ksum_lanes, w_dt, vectors):
    tokens, channels = xc.shape
    block, blocks = scan_blocks(length)

    def at(b, t):
        return b * blocks + t

    rows = row_spec(block, channels, at)
    lanes = row_spec(block, LANES, at)
    vmem = pltpu.VMEM
    return pl.pallas_call(
        forward_kernel,
        grid=(seqs, blocks),
        in_specs=[
            rows, row_spec(block, channels, at, 1), row_spec(block, R, at),
            spread_spec(block, at), spread_spec(block, at), lanes, lanes, whole(w_dt), whole(vectors),
        ],
        out_specs=[row_spec(block * N, channels, at), rows, rows],
        out_shape=[
            jax.ShapeDtypeStruct((tokens * N, channels), BF),
            jax.ShapeDtypeStruct((tokens, channels), F32),
            jax.ShapeDtypeStruct((tokens, channels), BF),
        ],
        scratch_shapes=[vmem((block, channels), F32), vmem((block, channels), F32), vmem((N, channels), F32)],
        cost_estimate=pl.CostEstimate(
            flops=tokens * channels * N * 60, bytes_accessed=tokens * channels * 44, transcendentals=0
        ),
        compiler_params=pltpu.CompilerParams(vmem_limit_bytes=28 << 20),
        name="scan_forward",
    )(xc, pre, rate, key_lanes, query_lanes, keep_lanes, ksum_lanes, w_dt, vectors)


def scan_backward(seqs, length, d_gated, y, xc, pre, rate, key_lanes, query_lanes, keep_lanes, ksum_lanes, w_dt, vectors, states):
    tokens, channels = xc.shape
    block, blocks = scan_blocks(length)

    def at(b, t):
        return b * blocks + blocks - 1 - t

    def prior(b, t):
        return (jnp.maximum(at(b, t) * block - 1, 0), 0)

    rows = row_spec(block, channels, at)
    lanes = row_spec(block, LANES, at)
    flat = row_spec(block * N // LANES, LANES, at)
    vmem = pltpu.VMEM
    wide_f32 = vmem((block, channels), F32)
    return pl.pallas_call(
        backward_kernel,
        grid=(seqs, blocks),
        in_specs=[
            rows, rows, rows, row_spec(block, channels, at, 1), row_spec(block, R, at),
            spread_spec(block, at), spread_spec(block, at), lanes, lanes, whole(w_dt), whole(vectors),
            row_spec(block * N, channels, at), pl.BlockSpec((N, channels), prior),
        ],
        out_specs=[
            rows, rows, flat, flat, lanes, row_spec(block, R, at),
            pl.BlockSpec((channels, R), lambda b, t: (0, 0)), pl.BlockSpec((16, channels), lambda b, t: (0, 0)),
        ],
        out_shape=[
            jax.ShapeDtypeStruct((tokens, channels), BF),
            jax.ShapeDtypeStruct((tokens, channels), F32),
            jax.ShapeDtypeStruct((tokens * N // LANES, LANES), F32),
            jax.ShapeDtypeStruct((tokens * N // LANES, LANES), F32),
            jax.ShapeDtypeStruct((tokens, LANES), F32),
            jax.ShapeDtypeStruct((tokens, R), F32),
            jax.ShapeDtypeStruct((channels, R), F32),
            jax.ShapeDtypeStruct((16, channels), F32),
        ],
        scratch_shapes=[
            wide_f32, wide_f32, wide_f32, wide_f32, wide_f32, wide_f32, vmem((block, channels), BF),
            vmem((N, channels), F32), vmem((block * N, LANES), F32), vmem((block * N, LANES), F32),
        ],
        cost_estimate=pl.CostEstimate(
            flops=tokens * channels * N * 100, bytes_accessed=tokens * channels * 56, transcendentals=0
        ),
        compiler_params=pltpu.CompilerParams(vmem_limit_bytes=36 << 20),
        name="scan_backward",
    )(d_gated, y, xc, pre, rate, key_lanes, query_lanes, keep_lanes, ksum_lanes, w_dt, vectors, states, states)


MESH = pl.DeviceIdType.MESH


def any_specs(count):
    return [pl.BlockSpec(memory_space=pl.ANY)] * count


def place():
    return lax.axis_index("dp"), lax.axis_index("seq")


def mate(d):
    return d + 1 - 2 * lax.rem(d, 2)


def forward_home(d, s, seq):
    return 2 * (d // 2) + lax.rem(s, 2), (seq // 2) * lax.rem(d, 2) + s // 2


def backward_home(d, s, seq):
    return 2 * (d // 2) + s // (seq // 2), 2 * lax.rem(s, seq // 2) + lax.rem(d, 2)


def remote(src, dst, send, recv, device):
    return pltpu.make_async_remote_copy(
        src_ref=src, dst_ref=dst, send_sem=send, recv_sem=recv, device_id=device, device_id_type=MESH
    )


def greet(device, here=True):
    barrier = pltpu.get_barrier_semaphore()

    def tell():
        pl.semaphore_signal(barrier, inc=1, device_id=device, device_id_type=MESH)

    if here is True:
        tell()
    else:
        pl.when(here)(tell)


PARTS = 4


def gather_kernel(dp, seq, fused, *refs):
    refs = list(refs)

    def take(count):
        out = refs[:count]
        del refs[:count]
        return out

    hid_ref, w_ref = take(2)
    parts = take(PARTS)
    gain_ref = take(1)[0] if fused else None
    hid_out, w_out = take(2)
    slots = take(PARTS)
    normed_out, pre_out = take(2) if fused else (None, None)
    z_send, z_recv, w_send, w_recv, f_send, f_recv, p_send, p_recv, q_send, q_recv, t_send, t_recv, own_sem = take(13)
    d, s = place()
    part = hid_ref.shape[1]
    pieces = z_send.shape[2]
    piece = part // pieces
    pairs = dp // 2
    to_d, to_s = forward_home(d, s, seq)
    from_d, from_s = backward_home(d, s, seq)
    moves = jnp.logical_or(to_d != d, to_s != s)

    greet((d, s - 1), s > 0)
    greet((d, s + 1), s < seq - 1)
    for k in range(1, pairs):
        greet((lax.rem(d + 2 * k, dp), s))
    greet((mate(d), s))
    greet((to_d, to_s), moves)
    greet((from_d, from_s), moves)
    count = pairs + jnp.where(s > 0, 1, 0) + jnp.where(s < seq - 1, 1, 0) + jnp.where(moves, 2, 0)
    pl.semaphore_wait(pltpu.get_barrier_semaphore(), count)

    def shard(which, q):
        return hid_out.at[:, pl.ds(which * part + q * piece, piece), :]

    def hop(way, k, q):
        which = s - k if way == 0 else s + k
        src = hid_ref.at[:, pl.ds(q * piece, piece), :] if k == 0 else shard(which, q)
        near = s + 1 if way == 0 else s - 1
        return remote(src, shard(which, q), z_send.at[way, k, q], z_recv.at[way, k, q], (d, near))

    def can_send(way, k):
        if way == 0:
            return jnp.logical_and(s - k >= 0, s < seq - 1)
        return jnp.logical_and(s + k < seq, s > 0)

    def landed(way, k, q):
        which = jnp.where(way == 0, s - k, s + k)
        here = shard(which, q)
        remote(here, here, z_send.at[way, k - 1, q], z_recv.at[way, k - 1, q], (d, s)).wait_recv()

    def spread(out, own, send, recv, k):
        return remote(own, out.at[d], send.at[k], recv.at[k], (lax.rem(d + 2 * k, dp), s))

    def source(k):
        return lax.rem(d - 2 * k + dp, dp)

    def across(out, send, recv, k, own=None):
        return remote(own if k == 0 else out.at[source(k)], out.at[source(k)], send.at[k], recv.at[k], (mate(d), s))

    for q in range(pieces):
        for way in range(2):
            pl.when(can_send(way, 0))(hop(way, 0, q).start)
    transfers = [remote(parts[m], slots[m].at[to_d], t_send.at[m], t_recv.at[m], (to_d, to_s)) for m in range(PARTS)]
    stays = [pltpu.make_async_copy(parts[m], slots[m].at[d], own_sem.at[2 + m]) for m in range(PARTS)]
    for m in range(PARTS):
        pl.when(moves)(transfers[m].start)
        pl.when(jnp.logical_not(moves))(stays[m].start)
    for k in range(1, pairs):
        spread(w_out, w_ref, w_send, w_recv, k).start()
    across(w_out, f_send, f_recv, 0, w_ref).start()
    own_w = pltpu.make_async_copy(w_ref, w_out.at[d], own_sem.at[0])
    own_h = pltpu.make_async_copy(hid_ref, hid_out.at[:, pl.ds(s * part, part), :], own_sem.at[1])
    own_w.start()
    own_h.start()

    for k in range(1, seq - 1):
        for q in range(pieces):
            for way in range(2):
                pl.when(s - k >= 0 if way == 0 else s + k < seq)(functools.partial(landed, way, k, q))
                pl.when(can_send(way, k))(hop(way, k, q).start)
    own_w.wait()
    own_h.wait()
    w_flow = (w_out, w_ref, w_send, w_recv, f_send, f_recv)
    part_flows = [
        (slots[m], slots[m].at[d], p_send.at[m], p_recv.at[m], q_send.at[m], q_recv.at[m]) for m in range(PARTS)
    ]

    def relay(out, own, send, recv, over_send, over_recv):
        for k in range(1, pairs):
            here = out.at[source(k)]
            remote(here, here, send.at[k], recv.at[k], (d, s)).wait_recv()
            across(out, over_send, over_recv, k).start()

    def complete(out, own, send, recv, over_send, over_recv):
        for k in range(pairs):
            here = out.at[lax.rem(mate(d) - 2 * k + dp, dp)]
            remote(here, here, over_send.at[k], over_recv.at[k], (d, s)).wait_recv()

    relay(*w_flow)
    for m in range(PARTS):
        slot = slots[m].at[d]
        pl.when(moves)(remote(parts[m], slot, t_send.at[m], t_recv.at[m], (to_d, to_s)).wait_recv)
        pl.when(jnp.logical_not(moves))(stays[m].wait)
        for k in range(1, pairs):
            spread(slots[m], slot, p_send.at[m], p_recv.at[m], k).start()
        across(slots[m], q_send.at[m], q_recv.at[m], 0, slot).start()

    complete(*w_flow)

    def relay_parts():
        for flow in part_flows:
            relay(*flow)

    last = seq - 1
    if fused:
        w_all, x_buf, w_sem, x_sem = take(4)
        width, columns = x_buf.shape[1], pre_out.shape[1]
        cut = math.gcd(columns, 512)
        fetch_w = pltpu.make_async_copy(w_out, w_all, w_sem)
        fetch_w.start()
        fetch_w.wait()

        def project(which, k, way):
            here = pl.multiple_of(which * part, part)
            for q in range(pieces):
                pl.when(k == last)(functools.partial(landed, way, last, q))
                fetch = pltpu.make_async_copy(
                    hid_out.at[0, pl.ds(which * part + q * piece, piece)], x_buf.at[pl.ds(q * piece, piece)], x_sem
                )
                fetch.start()
                fetch.wait()
                x = x_buf[pl.ds(q * piece, piece), :].astype(F32)
                inv = lax.rsqrt(jnp.mean(x * x, axis=1, keepdims=True) + norm_eps)
                rows = pl.ds(pl.multiple_of(here + q * piece, piece), piece)
                normed_out[rows, :] = (x * inv * gain_ref[...].astype(F32)).astype(BF)

            def matmul(at, carried):
                cols = pl.ds(pl.multiple_of(at * cut, cut), cut)
                w_rows = w_all.shape[1]
                block = w_all[pl.ds(at * (cut // w_rows), cut // w_rows)].reshape(cut, width)
                pre_out[pl.ds(here, part), cols] = mm(normed_out[pl.ds(here, part), :], block, NT).astype(BF)
                return carried

            lax.fori_loop(0, columns // cut, matmul, 0)

        def visit(m, carried):
            k = (m + 1) // 2
            way = lax.rem(m, 2)
            which = jnp.where(way == 0, s - k, s + k)
            pl.when(m == 2 * seq - 3)(relay_parts)

            @pl.when(jnp.logical_and(which >= 0, which < seq))
            def _():
                project(which, k, way)

            return carried

        lax.fori_loop(0, 2 * seq - 1, visit, 0)
    else:
        for q in range(pieces):
            for way in range(2):
                pl.when(s - last >= 0 if way == 0 else s + last < seq)(functools.partial(landed, way, last, q))
        relay_parts()

    for flow in part_flows:
        complete(*flow)
    for out, own, send, recv, over_send, over_recv in [w_flow, *part_flows]:
        for k in range(pairs):
            across(out, over_send, over_recv, k, own).wait_send()
        for k in range(1, pairs):
            spread(out, own, send, recv, k).wait_send()
    for k in range(seq - 1):
        for q in range(pieces):
            for way in range(2):
                pl.when(can_send(way, k))(hop(way, k, q).wait_send)
    for m in range(PARTS):
        pl.when(moves)(transfers[m].wait_send)


def fits_whole(seqs, length, width, channels):
    return seqs == 1 and length % 256 == 0 and length * (width + channels) + channels * width <= 6 << 20


def gather(hidden, weight, parts, norm_gain, collective_id=0):
    dp, seq = lax.axis_size("dp"), lax.axis_size("seq")
    seqs, part, width = hidden.shape
    columns = weight.shape[0] * dp
    fused = fits_whole(seqs, part * seq, width, columns // 2)
    pieces = 4 if part % 64 == 0 else 1
    dma, vmem, pairs = pltpu.SemaphoreType.DMA, pltpu.VMEM, dp // 2
    shape = jax.ShapeDtypeStruct
    outs = [shape((seqs, part * seq, width), BF), shape((dp,) + weight.shape, BF)]
    outs += [shape((dp,) + member.shape, BF) for member in parts]
    scratch = [dma((2, seq, pieces)), dma((2, seq, pieces))] + [dma((pairs,))] * 4
    scratch += [dma((PARTS, pairs))] * 4 + [dma((PARTS,)), dma((PARTS,)), dma((2 + PARTS,))]
    ins, in_specs = [hidden, weight, *parts], any_specs(2 + PARTS)
    out_specs = any_specs(2 + PARTS)
    if fused:
        ins.append(norm_gain.reshape(1, width))
        in_specs = in_specs + [pl.BlockSpec(memory_space=pltpu.VMEM)]
        outs += [shape((part * seq, width), BF), shape((part * seq, columns), BF)]
        scratch += [
            vmem((dp,) + weight.shape, BF), vmem((part, width), BF), dma, dma,
        ]
        out_specs = out_specs + [pl.BlockSpec(memory_space=pltpu.VMEM)] * 2
    out = pl.pallas_call(
        functools.partial(gather_kernel, dp, seq, fused),
        in_specs=in_specs,
        out_specs=out_specs,
        out_shape=outs,
        scratch_shapes=scratch,
        compiler_params=pltpu.CompilerParams(
            collective_id=collective_id, has_side_effects=True, vmem_limit_bytes=44 << 20
        ),
        name="gather_in",
    )(*ins)
    hidden = out[0].reshape(-1, width)
    w_in = out[1].reshape(columns, width)
    if fused:
        return hidden, w_in, out[2 : 2 + PARTS], out[-2], out[-1]
    x = hidden.astype(F32)
    inv = lax.rsqrt(jnp.mean(x * x, axis=1, keepdims=True) + norm_eps)
    normed = (x * inv * norm_gain.astype(F32)).astype(BF)
    return hidden, w_in, out[2:], normed, mm(normed, w_in, NT).astype(BF)


def added(ref, *others):
    total = ref[...].astype(F32)
    for other in others:
        total = total + other[...].astype(F32)
    return total


def scatter_kernel(dp, seq, count, fused, *refs):
    refs = list(refs)

    def take(count):
        out = refs[:count]
        del refs[:count]
        return out

    if fused:
        dx_ref, dz_ref, normed_ref, w_ref, full_ref = take(5)
        dn_ref = gw_ref = None
    else:
        dn_ref, gw_ref, gain_ref = take(3)
    parts = take(count)
    hid_ref, cot_ref, scale_ref = take(3)
    out_ref, gw_out = take(2)
    part_outs = take(count)
    gain_out = take(1)[0]
    own, come, gw_own, gw_x, gw_r = take(5)
    p_own, p_x, p_r, p_fin = take(count), take(count), take(count), take(count)
    g_in, g_one, g_x, g_r, g_z, g_a, g_b = take(7)
    z_load, z_send, z_recv, w_load, wx_send, wx_recv, w_send, w_recv = take(8)
    p_load, px_send, px_recv, p_send, p_recv, t_send, t_recv, gx_sem, g_send, g_recv, gz_send, gz_recv = take(12)

    d, s = place()
    seqs, part, width = out_ref.shape
    pieces = z_send.shape[1]
    piece = part // pieces
    pairs = dp // 2
    mine, odd = d // 2, lax.rem(d, 2)
    to_d, to_s = backward_home(d, s, seq)
    from_d, from_s = forward_home(d, s, seq)
    moves = jnp.logical_or(to_d != d, to_s != s)

    if fused:
        d_pre, normed, w_all, x_buf, gw_give, f_sem, x_sem = take(7)
        channels = dx_ref.shape[1]
        loads = [
            pltpu.make_async_copy(dx_ref, d_pre.at[:, pl.ds(0, channels)], f_sem.at[0]),
            pltpu.make_async_copy(dz_ref, d_pre.at[:, pl.ds(channels, channels)], f_sem.at[1]),
            pltpu.make_async_copy(w_ref, w_all, f_sem.at[2]),
            pltpu.make_async_copy(normed_ref, normed, f_sem.at[3]),
        ]
        for copy in loads:
            copy.start()

    for k in range(1, seq):
        greet((d, lax.rem(s + k, seq)))
    for k in range(1, pairs):
        greet((lax.rem(d + 2 * k, dp), s))
    greet((mate(d), s))
    greet((to_d, to_s), moves)
    greet((from_d, from_s), moves)
    pl.semaphore_wait(pltpu.get_barrier_semaphore(), seq - 1 + pairs + jnp.where(moves, 2, 0))

    def swap(src, dst, send, recv, j):
        return remote(src, dst.at[j], send.at[j], recv.at[j], (mate(d), s))

    def part_swap(m, j):
        return swap(parts[m].at[2 * j + 1 - odd], p_x[m], px_send.at[m], px_recv.at[m], j)

    def part_fetch(m, j):
        return pltpu.make_async_copy(parts[m].at[2 * j + odd], p_own[m].at[j], p_load.at[m, j])

    for m in range(count):
        for j in range(pairs):
            part_swap(m, j).start()
            part_fetch(m, j).start()

    if fused:
        for copy in loads[:3]:
            copy.wait()
        g_in[...] = jnp.zeros_like(g_in)
        w_rows = gw_own.shape[1]
        half_width = width // 2

        def chunk_of(i):
            return jnp.where(lax.rem(i, 2) == 0, seq - 1 - i // 2, i // 2)

        def dn_tasks(first, last):
            def run(i, carried):
                r = chunk_of(i)
                rows = pl.ds(pl.multiple_of(r * part, part), part)
                for at in range(2):
                    cols = pl.ds(at * half_width, half_width)
                    own[r, 0, :, cols] = mm(d_pre[rows, :], w_all[:, cols], NN).astype(BF)
                return carried

            lax.fori_loop(first, last, run, 0)

        def gain_tasks(first, last):
            def run(i, carried):
                r = chunk_of(i)
                fetch = pltpu.make_async_copy(full_ref.at[pl.ds(pl.multiple_of(r * part, part), part)], x_buf, x_sem)
                fetch.start()
                fetch.wait()

                def fold(at, carried):
                    some = pl.ds(pl.multiple_of(at * 64, 64), 64)
                    x = x_buf[some, :].astype(F32)
                    inv = lax.rsqrt(jnp.mean(x * x, axis=1, keepdims=True) + norm_eps)
                    weighted = own[r, 0, some, :].astype(F32) * (x * inv)
                    g_in[...] += jnp.sum(weighted.reshape(8, 8, width), axis=0)
                    return carried

                return lax.fori_loop(0, part // 64, fold, carried)

            lax.fori_loop(first, last, run, 0)

        def gw_task(dest, out, j):
            cols = pl.ds(pl.multiple_of(dest * w_rows, w_rows), w_rows)
            for at in range(2):
                some = pl.ds(at * half_width, half_width)
                out[j, :, some] = mm(d_pre[:, cols], normed[:, some], TN).astype(BF)

        def gw_swap(j):
            return swap(gw_give.at[j], gw_x, wx_send, wx_recv, j)

        def gw_away():
            def run(j, carried):
                gw_task(2 * j + 1 - odd, gw_give, j)
                gw_swap(j).start()
                return carried

            lax.fori_loop(0, pairs, run, 0)

        def gw_home():
            def run(k, carried):
                j = lax.rem(mine + 1 + k, pairs)
                gw_task(2 * j + odd, gw_own, j)
                return carried

            lax.fori_loop(0, pairs, run, 0)

        def gw_ready(j):
            pass
    else:
        def gw_swap(j):
            return swap(gw_ref.at[2 * j + 1 - odd], gw_x, wx_send, wx_recv, j)

        def gw_fetch(j):
            return pltpu.make_async_copy(gw_ref.at[2 * j + odd], gw_own.at[j], w_load.at[j])

        def chunk(r):
            return pltpu.make_async_copy(dn_ref.at[:, pl.ds(r * part, part), :], own.at[r], z_load.at[r])

        for r in range(seq):
            chunk(r).start()
        for j in range(pairs):
            gw_swap(j).start()
            gw_fetch(j).start()
        for r in range(seq):
            chunk(r).wait()
        g_in[...] = gain_ref[...]

        def gw_ready(j):
            gw_fetch(j).wait()

    def give(way, r, q):
        rows = pl.ds(q * piece, piece)
        slot = r if way == 0 else jnp.where(s - 1 == r, seq, r)
        near = s + 1 if way == 0 else s - 1
        return remote(own.at[r, :, rows, :], come.at[slot, :, rows, :], z_send.at[r, q], z_recv.at[slot, q], (d, near))

    def landed(slot, q):
        rows = pl.ds(q * piece, piece)
        here = come.at[slot, :, rows, :]
        remote(here, here, z_send.at[0, q], z_recv.at[slot, q], (d, s)).wait_recv()

    def begin():
        for q in range(pieces):
            pl.when(s == 0)(give(0, seq - 1, q).start)
            pl.when(s == seq - 1)(give(1, 0, q).start)

    def hop(turn, q):
        rows = pl.ds(q * piece, piece)
        for way in range(2):
            far = s if way == 0 else seq - 1 - s
            i = turn - far
            r = seq - 1 - i if way == 0 else i
            before = r + 1 if way == 0 else r - 1
            sends = jnp.logical_and(i >= 0, s < r if way == 0 else s > r)

            @pl.when(jnp.logical_and(sends, far > 0))
            def _():
                landed(r, q)
                own[r, :, rows, :] = added(own.at[r, :, rows, :], come.at[r, :, rows, :]).astype(BF)

            pl.when(jnp.logical_and(sends, i > 0))(give(way, before, q).wait_send)
            pl.when(jnp.logical_and(sends, far + i > 0))(give(way, r, q).start)

    def onward(part_own, part_r, send, recv, k):
        j = lax.rem(mine + k, pairs)
        return remote(part_own.at[j], part_r.at[k - 1], send.at[k], recv.at[k], (lax.rem(d + 2 * k, dp), s))

    def part_onward(m, k):
        return onward(p_own[m], p_r[m], p_send.at[m], p_recv.at[m], k)

    def gw_onward(k):
        return onward(gw_own, gw_r, w_send, w_recv, k)

    def part_join():
        for m in range(count):
            for k in range(1, pairs + 1):
                j = lax.rem(mine + k, pairs)
                part_fetch(m, j).wait()
                part_swap(m, j).wait_recv()
                if k < pairs:
                    p_own[m][j] = added(p_own[m].at[j], p_x[m].at[j]).astype(BF)
                    part_onward(m, k).start()

    def gw_join():
        for k in range(1, pairs + 1):
            j = lax.rem(mine + k, pairs)
            gw_ready(j)
            gw_swap(j).wait_recv()
            if k < pairs:
                gw_own[j] = added(gw_own.at[j], gw_x.at[j]).astype(BF)
                gw_onward(k).start()

    gain_swap = remote(g_one, g_x, gx_sem.at[0], gx_sem.at[1], (mate(d), s))

    def gain_near(k):
        return remote(g_a, g_r.at[k - 1], g_send.at[k], g_recv.at[k], (lax.rem(d + 2 * k, dp), s))

    def gain_far(k):
        return remote(g_b, g_z.at[k - 1], gz_send.at[k], gz_recv.at[k], (d, lax.rem(s + k, seq)))

    def gain_middle():
        gain_swap.wait_recv()
        g_a[...] = g_one[...] + g_x[...]
        for k in range(1, pairs):
            gain_near(k).start()

    def gain_last():
        for k in range(1, pairs):
            gain_near(k).wait_recv()
        g_b[...] = added(g_a, *[g_r.at[k] for k in range(pairs - 1)])
        for k in range(1, seq):
            gain_far(k).start()

    backs = [remote(p_fin[m], part_outs[m], t_send.at[m], t_recv.at[m], (to_d, to_s)) for m in range(count)]
    stays = [pltpu.make_async_copy(p_fin[m], part_outs[m], t_send.at[count + m]) for m in range(count)]

    def part_finish():
        for m in range(count):
            for k in range(1, pairs):
                part_onward(m, k).wait_recv()
            rest = [p_r[m].at[k] for k in range(pairs - 1)]
            p_fin[m][...] = added(p_own[m].at[mine], p_x[m].at[mine], *rest).astype(BF)
            pl.when(moves)(backs[m].start)
            pl.when(jnp.logical_not(moves))(stays[m].start)

    if fused:
        dn_tasks(0, 2)
        begin()
        part_join()
        loads[3].wait()
        gw_away()
        gw_home()
        gw_join()
        gain_tasks(0, 2)
        dn_tasks(2, seq)
        gain_tasks(2, seq)
    else:
        begin()
        part_join()
        gw_join()
    g_one[...] = jnp.sum(g_in[...], axis=0, keepdims=True)
    gain_swap.start()
    later = [gain_middle, gain_last, part_finish]
    for i in range(seq - 1):
        for q in range(pieces):
            hop(i, q)
            if later and q == pieces - 1:
                later.pop(0)()
    for task in later:
        task()

    for k in range(1, pairs):
        gw_onward(k).wait_recv()
    gw_out[...] = added(gw_own.at[mine], gw_x.at[mine], *[gw_r.at[k] for k in range(pairs - 1)])
    for k in range(1, seq):
        gain_far(k).wait_recv()
    gain_out[...] = added(g_b, *[g_z.at[k] for k in range(seq - 1)])

    some = math.gcd(piece, 64)
    for q in range(pieces):
        pl.when(s > 0)(functools.partial(landed, s, q))
        pl.when(s < seq - 1)(functools.partial(landed, seq, q))

        def settle(at, carried):
            rows = pl.ds(pl.multiple_of(q * piece + at * some, some), some)
            from_left = jnp.where(s > 0, come[s, :, rows, :].astype(F32), 0.0)
            from_right = jnp.where(s < seq - 1, come[seq, :, rows, :].astype(F32), 0.0)
            total = own[s, :, rows, :].astype(F32) + from_left + from_right
            x = hid_ref[:, rows, :].astype(F32)
            inv = lax.rsqrt(jnp.mean(x * x, axis=2, keepdims=True) + norm_eps)
            scaled = total * scale_ref[...].astype(F32)[None]
            out_ref[:, rows, :] = (
                cot_ref[:, rows, :].astype(F32)
                + inv * scaled
                - x * (inv * inv * inv) * jnp.mean(x * scaled, axis=2, keepdims=True)
            ).astype(BF)
            return carried

        lax.fori_loop(0, piece // some, settle, 0)

    for q in range(pieces):
        pl.when(s < seq - 1)(give(0, s + 1, q).wait_send)
        pl.when(s > 0)(give(1, s - 1, q).wait_send)
    gain_swap.wait_send()
    for j in range(pairs):
        gw_swap(j).wait_send()
        for m in range(count):
            part_swap(m, j).wait_send()
    for k in range(1, pairs):
        gw_onward(k).wait_send()
        gain_near(k).wait_send()
        for m in range(count):
            part_onward(m, k).wait_send()
    for k in range(1, seq):
        gain_far(k).wait_send()
    for m in range(count):
        pl.when(moves)(backs[m].wait_send)
        pl.when(moves)(remote(p_fin[m], part_outs[m], t_send.at[m], t_recv.at[m], (to_d, to_s)).wait_recv)
        pl.when(jnp.logical_not(moves))(stays[m].wait)


def scatter(d_x, d_z, normed, w_in, hidden, parts, hidden_in, cotangent, norm_gain, collective_id=1):
    dp, seq = lax.axis_size("dp"), lax.axis_size("seq")
    seqs, part, width = hidden_in.shape
    tokens, channels = d_x.shape
    w_rows = 2 * channels // dp
    fused = fits_whole(seqs, part * seq, width, channels)
    pieces = 4 if part % 64 == 0 else 1
    pairs, count = dp // 2, len(parts)
    dma, vmem, shape = pltpu.SemaphoreType.DMA, pltpu.VMEM, jax.ShapeDtypeStruct
    here = pl.BlockSpec(memory_space=pltpu.VMEM)
    if fused:
        ins, in_specs = [d_x, d_z, normed, w_in, hidden], any_specs(5)
        extra = [
            vmem((tokens, 2 * channels), BF), vmem((tokens, width), BF), vmem((2 * channels, width), BF),
            vmem((part, width), BF), vmem((pairs, w_rows, width), BF), dma((4,)), dma,
        ]
    else:
        d_pre = jnp.concatenate([d_x, d_z], axis=1)
        x = hidden.astype(F32)
        d_normed = mm(d_pre, w_in, NN)
        inv = lax.rsqrt(jnp.mean(x * x, axis=1, keepdims=True) + norm_eps)
        gain = jnp.pad(jnp.sum(d_normed * x * inv, axis=0)[None], ((0, 7), (0, 0)))
        ins = [
            d_normed.astype(BF).reshape(seqs, -1, width),
            mm(d_pre, normed, TN).astype(BF).reshape(dp, w_rows, width), gain,
        ]
        in_specs, extra = any_specs(2) + [here], []
    part_shapes = [member.shape[1:] for member in parts]
    token_shape, one = (seqs, part, width), (1, width)

    def each(count):
        return [vmem((count,) + member, BF) for member in part_shapes]

    out = pl.pallas_call(
        functools.partial(scatter_kernel, dp, seq, len(parts), fused),
        in_specs=in_specs + any_specs(count) + [here] * 3,
        out_specs=[here] * (3 + count),
        out_shape=[shape(token_shape, BF), shape((w_rows, width), F32)]
        + [shape(member, BF) for member in part_shapes]
        + [shape(one, F32)],
        scratch_shapes=[
            vmem((seq,) + token_shape, BF), vmem((seq + 1,) + token_shape, BF),
            vmem((pairs, w_rows, width), BF), vmem((pairs, w_rows, width), BF), vmem((pairs - 1, w_rows, width), BF),
            *each(pairs), *each(pairs), *each(pairs - 1), *[vmem(member, BF) for member in part_shapes],
            vmem((8, width), F32), vmem(one, F32), vmem(one, F32), vmem((pairs - 1,) + one, F32),
            vmem((seq - 1,) + one, F32), vmem(one, F32), vmem(one, F32),
            dma((seq,)), dma((seq, pieces)), dma((seq + 1, pieces)),
            dma((pairs,)), dma((pairs,)), dma((pairs,)), dma((pairs,)), dma((pairs,)),
            *[dma((count, pairs))] * 5, dma((2 * count,)), dma((count,)),
            dma((2,)), dma((pairs,)), dma((pairs,)), dma((seq,)), dma((seq,)),
            *extra,
        ],
        compiler_params=pltpu.CompilerParams(
            collective_id=collective_id, has_side_effects=True, vmem_limit_bytes=63 << 20
        ),
        name="scatter_out",
    )(*ins, *parts, hidden_in, cotangent, norm_gain.reshape(1, width))
    return out[0], out[1], out[2 : 2 + count], out[-1].reshape(width)


def reduce_kernel(dp, seq, grads, *refs):
    refs = list(refs)

    def take(count):
        out = refs[:count]
        del refs[:count]
        return out

    wide_ref, thin_ref = take(2)
    g_ref = take(1)[0] if grads else None
    wide_out, thin_out = take(2)
    g_out = take(1)[0] if grads else None
    wide_x, thin_x, wide_s, thin_s = take(4)
    xw_send, xw_recv, xt_send, xt_recv, sw_send, sw_recv, st_send, st_recv = take(8)
    d, s = place()
    rows = wide_ref.shape[0] // seq
    pairs = dp // 2
    mine, odd = d // 2, lax.rem(d, 2)
    for k in range(1, seq):
        greet((d, lax.rem(s + k, seq)))
    if grads:
        for k in range(1, pairs):
            greet((lax.rem(d + 2 * k, dp), s))
        greet((mate(d), s))
    pl.semaphore_wait(pltpu.get_barrier_semaphore(), seq - 1 + (pairs if grads else 0))

    def piece(ref, which):
        return ref.at[pl.ds(pl.multiple_of(which * rows, rows), rows)]

    def ask(k):
        to = lax.rem(s + k, seq)
        return (
            remote(piece(wide_ref, to), wide_x.at[k - 1], xw_send.at[k - 1], xw_recv.at[k - 1], (d, to)),
            remote(thin_ref.at[to], thin_x.at[k - 1], xt_send.at[k - 1], xt_recv.at[k - 1], (d, to)),
        )

    def tell(k):
        to = lax.rem(s + k, seq)
        return (
            remote(wide_s, piece(wide_out, s), sw_send.at[k - 1], sw_recv.at[k - 1], (d, to)),
            remote(thin_s, thin_out.at[s], st_send.at[k - 1], st_recv.at[k - 1], (d, to)),
        )

    def told(k):
        source = lax.rem(s - k + seq, seq)
        return (
            remote(wide_s, piece(wide_out, source), sw_send.at[k - 1], sw_recv.at[k - 1], (d, s)),
            remote(thin_s, thin_out.at[source], st_send.at[k - 1], st_recv.at[k - 1], (d, s)),
        )

    order = sorted(range(1, seq), key=lambda k: -min(k, seq - k))
    for k in order:
        for copy in ask(k):
            copy.start()
    if grads:
        g_own, g_x, g_r, g_load, gx_send, gx_recv, g_send, g_recv = take(8)

        def swap(j):
            return remote(g_ref.at[2 * j + 1 - odd], g_x.at[j], gx_send.at[j], gx_recv.at[j], (mate(d), s))

        def fetch(j):
            return pltpu.make_async_copy(g_ref.at[2 * j + odd], g_own.at[j], g_load.at[j])

        def onward(k):
            to = lax.rem(d + 2 * k, dp)
            return remote(g_own.at[to // 2], g_r.at[k - 1], g_send.at[k], g_recv.at[k], (to, s))

        for j in range(pairs):
            swap(j).start()
            fetch(j).start()
        for k in range(1, pairs + 1):
            j = lax.rem(mine + k, pairs)
            fetch(j).wait()
            swap(j).wait_recv()
            if k < pairs:
                g_own[j] = added(g_own.at[j], g_x.at[j]).astype(BF)
                onward(k).start()
    for k in order:
        for copy in ask(k):
            copy.wait_recv()
    start = pl.ds(pl.multiple_of(s * rows, rows), rows)
    total = wide_ref[start, :].astype(F32)
    thin = thin_ref[s]
    for k in range(seq - 1):
        total = total + wide_x[k].astype(F32)
        thin = thin + thin_x[k]
    wide_s[...] = total.astype(BF)
    thin_s[...] = thin
    for k in order:
        for copy in tell(k):
            copy.start()
    wide_out[start, :] = total.astype(BF)
    thin_out[s] = thin
    if grads:
        for k in range(1, pairs):
            onward(k).wait_recv()
        g_out[...] = added(g_own.at[mine], g_x.at[mine], *[g_r.at[k] for k in range(pairs - 1)]).astype(BF)
        for j in range(pairs):
            swap(j).wait_send()
        for k in range(1, pairs):
            onward(k).wait_send()
    for k in order:
        for copy in told(k):
            copy.wait_recv()
    for k in order:
        for copy in ask(k) + tell(k):
            copy.wait_send()


def reduce_over_seq(wide_part, thin_part, collective_id, grads=None):
    dp, seq = lax.axis_size("dp"), lax.axis_size("seq")
    tokens, cols = wide_part.shape
    thin_part = jnp.swapaxes(thin_part.reshape(-1, seq, tokens // seq), 0, 1)
    dma, vmem, shape = pltpu.SemaphoreType.DMA, pltpu.VMEM, jax.ShapeDtypeStruct
    here = pl.BlockSpec(memory_space=pltpu.VMEM)
    rows, few, pairs = tokens // seq, thin_part.shape[1:], dp // 2
    ins, in_specs = [wide_part.astype(BF), thin_part], [here] * 2
    outs = [shape((tokens, cols), BF), shape(thin_part.shape, F32)]
    scratch = [
        vmem((seq - 1, rows, cols), BF), vmem((seq - 1,) + few, F32), vmem((rows, cols), BF), vmem(few, F32),
    ] + [dma((seq - 1,))] * 8
    if grads is not None:
        ins, in_specs = ins + [grads], in_specs + any_specs(1)
        outs.append(shape(grads.shape[1:], BF))
        scratch += [vmem((pairs,) + grads.shape[1:], BF)] * 2 + [vmem((pairs - 1,) + grads.shape[1:], BF)]
        scratch += [dma((pairs,))] * 5
    out = pl.pallas_call(
        functools.partial(reduce_kernel, dp, seq, grads is not None),
        in_specs=in_specs,
        out_specs=[here] * len(outs),
        out_shape=outs,
        scratch_shapes=scratch,
        compiler_params=pltpu.CompilerParams(
            collective_id=collective_id, has_side_effects=True, vmem_limit_bytes=24 << 20
        ),
        name="reduce_seq",
    )(*ins)
    return (out[0], jnp.swapaxes(out[1], 0, 1).reshape(-1, tokens)) + tuple(out[2:])


def homes_back(dp, seq):
    pairs = []
    for d in range(dp):
        for s in range(seq):
            home_d, home_s = 2 * (d // 2) + s % 2, (seq // 2) * (d % 2) + s // 2
            pairs.append((home_d * seq + home_s, d * seq + s))
    return pairs


def local(
    hidden_in,
    doc_lengths,
    norm_gain,
    in_weight,
    conv_weight,
    conv_bias,
    x_weight,
    dt_weight,
    dt_bias,
    skip_gain,
    out_weight,
    out_cotangent,
):
    seqs, part_len, width = hidden_in.shape
    dp, seq = lax.axis_size("dp"), lax.axis_size("seq")
    length = part_len * seq
    tokens = seqs * length
    rows = out_weight.shape[0]
    channels = rows * dp
    lag_max = KCONV - 1

    vectors = [conv_weight, conv_bias[None], dt_bias[None], skip_gain[None]]
    vectors = jnp.pad(jnp.concatenate(vectors, axis=0), ((0, 16 - KCONV - 3), (0, 0)))
    parts = [out_weight, x_weight, dt_weight, vectors]
    hidden, w_in, parts, normed, pre = gather(hidden_in, in_weight, parts, norm_gain)
    cot, pre = lax.optimization_barrier((out_cotangent, pre))
    cot = lax.all_gather(cot, "seq", axis=1, tiled=True).reshape(tokens, width)

    w_out, w_x, w_dt = (part.reshape(channels, part.shape[2]) for part in parts[:3])
    vectors = jnp.swapaxes(parts[3], 0, 1).reshape(16, channels).astype(F32)
    taps, conv_shift, rate_shift, skip = vectors[:KCONV], vectors[KCONV], vectors[KCONV + 1], vectors[KCONV + 2]

    begins, places = token_begins(doc_lengths, length)
    keep = (places[None, :] != begins).astype(F32).reshape(tokens, 1)
    valid = [(places[None, :] - (lag_max - w) >= begins)[:, :, None] for w in range(KCONV)]

    x_inner = pre[:, :channels].reshape(seqs, length, channels)

    padded = jnp.pad(x_inner, ((0, 0), (lag_max, 0), (0, 0)))
    conv_sum = jnp.broadcast_to(conv_shift, (seqs, length, channels))
    for w in range(KCONV):
        window = padded[:, w : w + length, :].astype(F32)
        conv_sum = conv_sum + jnp.where(valid[w], window * taps[w], 0.0)
    conv_flat = conv_sum.reshape(tokens, channels)
    xc_low = jax.nn.silu(conv_flat).astype(BF)
    rate, thin = reduce_over_seq(mm(xc_low, w_x[:, :R], NN), mm(w_x[:, R:], xc_low, ((0,), (1,))), 2)
    key, query = thin[:N].T, thin[N:].T
    key_lanes, query_lanes = (
        jnp.broadcast_to(part.astype(BF)[:, :, None], (tokens, N, LANES)) for part in (key, query)
    )
    ksum = jnp.sum(key * key, axis=1, keepdims=True)
    keep_lanes = jnp.broadcast_to(keep, (tokens, LANES))
    ksum_lanes = jnp.broadcast_to(ksum, (tokens, LANES))
    vectors = jnp.pad(jnp.stack([rate_shift, skip]), ((0, 6), (0, 0)))
    states, y_full, gated = scan_forward(
        seqs, length, xc_low, pre, rate, key_lanes, query_lanes, keep_lanes, ksum_lanes, w_dt, vectors
    )
    branch = mm(gated, w_out, NN).astype(BF).reshape(seqs, length, width)
    branch = lax.psum_scatter(branch, "seq", scatter_dimension=1, tiled=True)
    output = (hidden_in.astype(F32) + branch.astype(F32)).astype(BF)

    d_z, rest, dq, dk, d_norm, d_row, grad_dt, sums = scan_backward(
        seqs, length, mm(cot, w_out, NT), y_full, xc_low, pre, rate, key_lanes, query_lanes, keep_lanes, ksum_lanes, w_dt, vectors, states
    )
    dq, dk = dq.reshape(tokens, N), dk.reshape(tokens, N)
    d_norm = -jnp.sum(d_norm, axis=1, keepdims=True)
    d_keys = dk + 2.0 * key * d_norm
    grad_out = mm(gated, cot, TN).astype(BF).reshape(dp, rows, width)
    d_row, thin, grad_out = reduce_over_seq(d_row, jnp.concatenate([d_keys.T, dq.T], axis=0), 3, grad_out)
    grad_out = lax.ppermute(grad_out, ("dp", "seq"), homes_back(dp, seq))
    d_proj = jnp.concatenate([d_row, thin.T.astype(BF)], axis=1)
    d_conv_out = mm(d_proj, w_x, NT) + rest
    d_conv = (d_conv_out * silu_slope(conv_flat)).reshape(seqs, length, channels)

    tap_grads = []
    d_x_inner = jnp.zeros((seqs, length, channels), F32)
    for w in range(KCONV):
        lag = lag_max - w
        window = padded[:, w : w + length, :].astype(F32)
        masked = jnp.where(valid[w], d_conv, 0.0)
        tap_grads.append(jnp.sum(masked * window, axis=(0, 1)))
        d_x_inner = d_x_inner + jnp.pad(masked, ((0, 0), (0, lag), (0, 0)))[:, lag:, :] * taps[w]
    vector_grads = jnp.stack(
        tap_grads + [jnp.sum(d_conv, axis=(0, 1)), jnp.sum(sums[:8], axis=0), jnp.sum(sums[8:], axis=0)], axis=0
    )
    vector_grads = jnp.pad(vector_grads, ((0, 16 - KCONV - 3), (0, 0))).reshape(16, dp, rows)
    grads = [part.astype(BF).reshape(dp, rows, -1) for part in (mm(xc_low, d_proj, TN), grad_dt)]
    grads.append(jnp.swapaxes(vector_grads, 0, 1).astype(BF))
    grad_in, grad_in_weight, grads, grad_norm_gain = scatter(
        d_x_inner.reshape(tokens, channels).astype(BF), d_z, normed, w_in, hidden, grads,
        hidden_in, out_cotangent, norm_gain,
    )
    grad_x, grad_dt, grad_vectors = (part.astype(F32) for part in grads)
    grad_out_weight = grad_out.astype(F32)
    return (
        output,
        grad_in,
        grad_norm_gain,
        grad_in_weight,
        grad_vectors[:KCONV],
        grad_vectors[KCONV],
        grad_x,
        grad_dt,
        grad_vectors[KCONV + 1],
        grad_vectors[KCONV + 2],
        grad_out_weight,
    )


def solution(mesh):
    both = ("dp", "seq")
    tokens = P("dp", "seq", None)
    matrix, vector = P(both, None), P(both)
    return jax.shard_map(
        local,
        mesh=mesh,
        in_specs=(
            tokens, P("dp", None), P(), matrix, P(None, both), vector,
            matrix, matrix, vector, vector, matrix, tokens,
        ),
        out_specs=(
            tokens, tokens, P(), matrix, P(None, both), vector,
            matrix, matrix, vector, vector, matrix,
        ),
        check_vma=False,
    )
```

```python
import functools
import math

import jax
import jax.numpy as jnp
from jax import lax
from jax.experimental import pallas as pl
from jax.experimental.pallas import tpu as pltpu
from jax.sharding import PartitionSpec as P

N = 16
R = 128
KCONV = 4
CHUNK = 16
LANES = 128
GROUP = 1024
BLOCK = 128

norm_eps = 1e-05
BF = jnp.bfloat16
F32 = jnp.float32


def silu_slope(pre_value):
    sigmoid_of = jax.nn.sigmoid(pre_value)
    return sigmoid_of * (1.0 + pre_value * (1.0 - sigmoid_of))


def token_begins(lengths, position_count):
    doc_ends = jnp.cumsum(lengths, axis=1)
    doc_starts = doc_ends - lengths
    places = jnp.arange(position_count, dtype=jnp.int32)
    inside = doc_starts[:, None, :] <= places[None, :, None]
    return (jnp.max(jnp.where(inside, doc_starts[:, None, :], 0), axis=2), places)


def mm(left, right, dims):
    return lax.dot_general(left, right, (dims, ((), ())), preferred_element_type=F32)


NN = ((1,), (0,))
NT = ((1,), (1,))
TN = ((0,), (0,))


def row(ref, i, lane):
    return jnp.broadcast_to(ref[i : i + 1, pl.ds(lane, LANES)], (8, LANES))


def wide(ref, rows, count):
    value = ref[rows, :]
    return jnp.concatenate([value] * (count // LANES), axis=1)


def merge(even, odd, stride):
    low = lax.broadcasted_iota(jnp.int32, (8, LANES), 0) % (2 * stride) < stride
    if stride == 4:
        return jnp.where(low, even, odd) + pltpu.roll(jnp.where(low, odd, even), 4, 0)
    return jnp.where(low, even + pltpu.roll(even, 8 - stride, 0), odd + pltpu.roll(odd, stride, 0))


def collect(stack, value, descending):
    level = 0
    while stack and stack[-1][0] == level:
        other = stack.pop()[1]
        value = merge(value, other, 1 << level) if descending else merge(other, value, 1 << level)
        level += 1
    stack.append((level, value))


def each_chunk(tokens, channels, body):
    group = math.gcd(channels, 512)

    def run(k, carried):
        rows = pl.ds(pl.multiple_of(k * CHUNK, CHUNK), CHUNK)
        for first in range(0, channels, group):
            body(rows, pl.ds(first, group), first)
        return carried

    lax.fori_loop(0, tokens // CHUNK, run, 0)


def load_carry(carry, tiles):
    out = []
    for lane in tiles:
        out += [carry[0:8, pl.ds(lane, LANES)], carry[8:16, pl.ds(lane, LANES)]]
    return tuple(out)


def store_carry(carry, tiles, values):
    for j, lane in enumerate(tiles):
        carry[0:8, pl.ds(lane, LANES)] = values[2 * j]
        carry[8:16, pl.ds(lane, LANES)] = values[2 * j + 1]


def halves(value):
    return [value[0:8], value[8:16]]


def token(keys, queries, keeps, i):
    return row(keeps, i, 0), halves(keys[i].astype(F32)), halves(queries[i].astype(F32))


def lane_groups(channels):
    group = math.gcd(channels, GROUP)
    return [list(range(first, first + group, LANES)) for first in range(0, channels, group)]


def forward_kernel(
    xc_ref, z_ref, rate_ref, key_ref, query_ref, keep_ref, ksum_ref, wdt_ref, vec_ref,
    s_ref, y_ref, gated_ref, step, inj, carry,
):
    @pl.when(pl.program_id(1) == 0)
    def _():
        carry[...] = jnp.zeros_like(carry)

    tokens, channels = xc_ref.shape
    step[...] = mm(rate_ref[...], wdt_ref[...], NT)

    def prepare(rows, cols, first):
        beta = jax.nn.sigmoid(step[rows, cols] + vec_ref[0:1, cols])
        eps = beta / (1.0 + beta * wide(ksum_ref, rows, cols.size))
        step[rows, cols] = eps
        inj[rows, cols] = eps * xc_ref[rows, cols].astype(F32)

    each_chunk(tokens, channels, prepare)
    for tiles in lane_groups(channels):

        def chunk(k, state):
            state = list(state)
            base = pl.multiple_of(k * CHUNK, CHUNK)
            steps, injs, keeps, keys, queries = (
                r.at[pl.ds(base, CHUNK)] for r in (step, inj, keep_ref, key_ref, query_ref)
            )
            saved = s_ref.at[pl.ds(pl.multiple_of(k * CHUNK * N, CHUNK * N), CHUNK * N)]
            stacks = [[] for _ in tiles]
            for i in range(CHUNK):
                keep, key, query = token(keys, queries, keeps, i)
                ksq = [keep * key[h] * key[h] for h in range(2)]
                for j, lane in enumerate(tiles):
                    eps, push = row(steps, i, lane), row(injs, i, lane)
                    for h in range(2):
                        state[2 * j + h] = (keep - eps * ksq[h]) * state[2 * j + h] + push * key[h]
                    both = jnp.concatenate([state[2 * j], state[2 * j + 1]], axis=0)
                    saved[i * N : (i + 1) * N, pl.ds(lane, LANES)] = both.astype(BF)
                    collect(stacks[j], state[2 * j] * query[0] + state[2 * j + 1] * query[1], False)
                    if i % 8 == 7:
                        y_ref[pl.ds(pl.multiple_of(base + i - 7, 8), 8), pl.ds(lane, LANES)] = stacks[j].pop()[1]
            return tuple(state)

        store_carry(carry, tiles, lax.fori_loop(0, tokens // CHUNK, chunk, load_carry(carry, tiles)))

    def emit(rows, cols, first):
        y_full = y_ref[rows, cols] + vec_ref[1:2, cols] * xc_ref[rows, cols].astype(F32)
        y_ref[rows, cols] = y_full
        z = z_ref[rows, cols].astype(F32)
        gated_ref[rows, cols] = (y_full * (z * jax.nn.sigmoid(z))).astype(BF)

    each_chunk(tokens, channels, emit)


def backward_kernel(
    dg_ref, y_ref, xc_ref, z_ref, rate_ref, key_ref, query_ref, keep_ref, ksum_ref, wdt_ref, vec_ref, s_ref, before_ref,
    dz_ref, rest_ref, dq_ref, dk_ref, dnorm_ref, drow_ref, gdt_ref, sums_ref,
    step, inj, dy, mix, pull, beta, drate, carry, acc_q, acc_k,
):
    turn = pl.program_id(1)
    tokens, channels = xc_ref.shape
    chunks = tokens // CHUNK

    @pl.when(jnp.logical_and(pl.program_id(0) == 0, turn == 0))
    def _():
        gdt_ref[...] = jnp.zeros_like(gdt_ref)
        sums_ref[...] = jnp.zeros_like(sums_ref)

    @pl.when(turn == 0)
    def _():
        carry[...] = jnp.zeros_like(carry)

    beta[...] = mm(rate_ref[...], wdt_ref[...], NT)

    def prepare(rows, cols, first):
        rate_beta = jax.nn.sigmoid(beta[rows, cols] + vec_ref[0:1, cols])
        eps = rate_beta / (1.0 + rate_beta * wide(ksum_ref, rows, cols.size))
        beta[rows, cols] = rate_beta
        step[rows, cols] = eps
        xc = xc_ref[rows, cols].astype(F32)
        inj[rows, cols] = eps * xc
        z = z_ref[rows, cols].astype(F32)
        sig = jax.nn.sigmoid(z)
        d_gated = dg_ref[rows, cols]
        d_y = d_gated * (z * sig)
        dy[rows, cols] = d_y
        dz_ref[rows, cols] = (d_gated * y_ref[rows, cols] * (sig * (1.0 + z * (1.0 - sig)))).astype(BF)
        weighted = d_y * xc
        sums_ref[8:16, cols] += weighted[0:8] + weighted[8:16]

    each_chunk(tokens, channels, prepare)
    for tiles in lane_groups(channels):
        start = tiles[0] == 0

        def chunk(back, carried):
            k = chunks - 1 - back
            pulled, now = list(carried[0]), list(carried[1])
            base = pl.multiple_of(k * CHUNK, CHUNK)
            steps, injs, dys, keeps, keys, queries = (
                r.at[pl.ds(base, CHUNK)] for r in (step, inj, dy, keep_ref, key_ref, query_ref)
            )
            stacks = [([], []) for _ in tiles]
            for i in reversed(range(CHUNK)):
                keep, key, query = token(keys, queries, keeps, i)
                kept = [keep * key[h] for h in range(2)]
                ksq = [kept[h] * key[h] for h in range(2)]
                if i > 0:
                    before = pl.ds(pl.multiple_of((base + i) * N - N, N), N)
                else:
                    before = pl.ds(pl.multiple_of(jnp.maximum(base * N - N, 0), N), N)
                seen, plain, scaled = [0.0, 0.0], [0.0, 0.0], [0.0, 0.0]
                for j, lane in enumerate(tiles):
                    eps, push, d_y = row(steps, i, lane), row(injs, i, lane), row(dys, i, lane)
                    prior = s_ref[before, pl.ds(lane, LANES)]
                    if i == 0:
                        prior = jnp.where(k > 0, prior, before_ref[:, pl.ds(lane, LANES)])
                    prior = halves(prior.astype(F32))
                    by_key, by_square = [], []
                    for h in range(2):
                        at = 2 * j + h
                        grad = pulled[at] + d_y * query[h]
                        pulled[at] = (keep - eps * ksq[h]) * grad
                        keyed = eps * (grad * key[h])
                        prod = keyed * prior[h]
                        seen[h] += now[at] * d_y
                        plain[h] += grad * push
                        scaled[h] += prod
                        by_key.append(keyed)
                        by_square.append(prod * kept[h])
                        now[at] = prior[h]
                    collect(stacks[j][0], by_key[0] + by_key[1], True)
                    collect(stacks[j][1], by_square[0] + by_square[1], True)
                    if i % 8 == 0:
                        rows = pl.ds(pl.multiple_of(base + i, 8), 8)
                        mix[rows, pl.ds(lane, LANES)] = stacks[j][0].pop()[1]
                        pull[rows, pl.ds(lane, LANES)] = stacks[j][1].pop()[1]
                for ref, parts in ((acc_q, seen), (acc_k, [plain[h] - 2.0 * keep * scaled[h] for h in range(2)])):
                    for h in range(2):
                        rows = pl.ds(pl.multiple_of((base + i) * N + 8 * h, 8), 8)
                        if start:
                            ref[rows, :] = parts[h]
                        else:
                            ref[rows, :] += parts[h]
            return (tuple(pulled), tuple(now))

        now = []
        for lane in tiles:
            now += halves(s_ref[tokens * N - N : tokens * N, pl.ds(lane, LANES)].astype(F32))
        pulled, now = lax.fori_loop(0, chunks, chunk, (load_carry(carry, tiles), tuple(now)))
        store_carry(carry, tiles, pulled)

    ones = jnp.ones((LANES, LANES), BF)
    diagonal = lax.broadcasted_iota(jnp.int32, (LANES, LANES), 0) == (
        lax.broadcasted_iota(jnp.int32, (LANES, LANES), 1)
    )
    for out, ref in ((dq_ref, acc_q), (dk_ref, acc_k)):
        for first in range(0, tokens * N, LANES):
            sums = mm(ref[first : first + LANES, :].astype(BF), ones, NN)
            at = first // LANES
            out[at : at + 1, :] = jnp.sum(jnp.where(diagonal, sums, 0.0), axis=0, keepdims=True)

    def settle(rows, cols, first):
        rate_beta, eps = beta[rows, cols], step[rows, cols]
        through = mix[rows, cols]
        change = through * xc_ref[rows, cols].astype(F32) - pull[rows, cols]
        inverse = 1.0 / (1.0 + rate_beta * wide(ksum_ref, rows, cols.size))
        low = (change * inverse * (1.0 - rate_beta)).astype(BF)
        drate[rows, cols] = low
        lowered = low.astype(F32)
        sums_ref[0:8, cols] += lowered[0:8] + lowered[8:16]
        rest_ref[rows, cols] = through + vec_ref[1:2, cols] * dy[rows, cols]
        square = change * eps
        total = square[:, 0:LANES]
        for lane in range(LANES, cols.size, LANES):
            total = total + square[:, lane : lane + LANES]
        if first == 0:
            dnorm_ref[rows, :] = total
        else:
            dnorm_ref[rows, :] += total

    each_chunk(tokens, channels, settle)
    drow_ref[...] = mm(drate[...], wdt_ref[...], NN)
    gdt_ref[...] += mm(drate[...], rate_ref[...], TN)


def scan_blocks(length):
    block = math.gcd(length, BLOCK)
    return block, length // block


def row_spec(rows, cols, when, col=0):
    return pl.BlockSpec((rows, cols), lambda b, t: (when(b, t), col))


def spread_spec(block, when):
    return pl.BlockSpec((block, N, LANES), lambda b, t: (when(b, t), 0, 0))


def whole(array):
    return pl.BlockSpec(array.shape, lambda b, t: (0, 0), pipeline_mode=pl.Buffered(1))


def scan_forward(seqs, length, xc, pre, rate, key_lanes, query_lanes, keep_lanes, ksum_lanes, w_dt, vectors):
    tokens, channels = xc.shape
    block, blocks = scan_blocks(length)

    def at(b, t):
        return b * blocks + t

    rows = row_spec(block, channels, at)
    lanes = row_spec(block, LANES, at)
    vmem = pltpu.VMEM
    return pl.pallas_call(
        forward_kernel,
        grid=(seqs, blocks),
        in_specs=[
            rows, row_spec(block, channels, at, 1), row_spec(block, R, at),
            spread_spec(block, at), spread_spec(block, at), lanes, lanes, whole(w_dt), whole(vectors),
        ],
        out_specs=[row_spec(block * N, channels, at), rows, rows],
        out_shape=[
            jax.ShapeDtypeStruct((tokens * N, channels), BF),
            jax.ShapeDtypeStruct((tokens, channels), F32),
            jax.ShapeDtypeStruct((tokens, channels), BF),
        ],
        scratch_shapes=[vmem((block, channels), F32), vmem((block, channels), F32), vmem((N, channels), F32)],
        cost_estimate=pl.CostEstimate(
            flops=tokens * channels * N * 60, bytes_accessed=tokens * channels * 44, transcendentals=0
        ),
        compiler_params=pltpu.CompilerParams(vmem_limit_bytes=46 << 20),
        name="scan_forward",
    )(xc, pre, rate, key_lanes, query_lanes, keep_lanes, ksum_lanes, w_dt, vectors)


def scan_backward(seqs, length, d_gated, y, xc, pre, rate, key_lanes, query_lanes, keep_lanes, ksum_lanes, w_dt, vectors, states):
    tokens, channels = xc.shape
    block, blocks = scan_blocks(length)

    def at(b, t):
        return b * blocks + blocks - 1 - t

    def prior(b, t):
        return (jnp.maximum(at(b, t) * block - 1, 0), 0)

    rows = row_spec(block, channels, at)
    lanes = row_spec(block, LANES, at)
    flat = row_spec(block * N // LANES, LANES, at)
    vmem = pltpu.VMEM
    wide_f32 = vmem((block, channels), F32)
    return pl.pallas_call(
        backward_kernel,
        grid=(seqs, blocks),
        in_specs=[
            rows, rows, rows, row_spec(block, channels, at, 1), row_spec(block, R, at),
            spread_spec(block, at), spread_spec(block, at), lanes, lanes, whole(w_dt), whole(vectors),
            row_spec(block * N, channels, at), pl.BlockSpec((N, channels), prior),
        ],
        out_specs=[
            rows, rows, flat, flat, lanes, row_spec(block, R, at),
            pl.BlockSpec((channels, R), lambda b, t: (0, 0)), pl.BlockSpec((16, channels), lambda b, t: (0, 0)),
        ],
        out_shape=[
            jax.ShapeDtypeStruct((tokens, channels), BF),
            jax.ShapeDtypeStruct((tokens, channels), F32),
            jax.ShapeDtypeStruct((tokens * N // LANES, LANES), F32),
            jax.ShapeDtypeStruct((tokens * N // LANES, LANES), F32),
            jax.ShapeDtypeStruct((tokens, LANES), F32),
            jax.ShapeDtypeStruct((tokens, R), F32),
            jax.ShapeDtypeStruct((channels, R), F32),
            jax.ShapeDtypeStruct((16, channels), F32),
        ],
        scratch_shapes=[
            wide_f32, wide_f32, wide_f32, wide_f32, wide_f32, wide_f32, vmem((block, channels), BF),
            vmem((N, channels), F32), vmem((block * N, LANES), F32), vmem((block * N, LANES), F32),
        ],
        cost_estimate=pl.CostEstimate(
            flops=tokens * channels * N * 100, bytes_accessed=tokens * channels * 56, transcendentals=0
        ),
        compiler_params=pltpu.CompilerParams(vmem_limit_bytes=54 << 20),
        name="scan_backward",
    )(d_gated, y, xc, pre, rate, key_lanes, query_lanes, keep_lanes, ksum_lanes, w_dt, vectors, states, states)


MESH = pl.DeviceIdType.MESH


def any_specs(count):
    return [pl.BlockSpec(memory_space=pl.ANY)] * count


def place():
    return lax.axis_index("dp"), lax.axis_index("seq")


def mate(d):
    return d + 1 - 2 * lax.rem(d, 2)


def forward_home(d, s, seq):
    return 2 * (d // 2) + lax.rem(s, 2), (seq // 2) * lax.rem(d, 2) + s // 2


def backward_home(d, s, seq):
    return 2 * (d // 2) + s // (seq // 2), 2 * lax.rem(s, seq // 2) + lax.rem(d, 2)


def remote(src, dst, send, recv, device):
    return pltpu.make_async_remote_copy(
        src_ref=src, dst_ref=dst, send_sem=send, recv_sem=recv, device_id=device, device_id_type=MESH
    )


def greet(device, here=True):
    barrier = pltpu.get_barrier_semaphore()

    def tell():
        pl.semaphore_signal(barrier, inc=1, device_id=device, device_id_type=MESH)

    if here is True:
        tell()
    else:
        pl.when(here)(tell)


PARTS = 4


def gather_kernel(dp, seq, fused, *refs):
    refs = list(refs)

    def take(count):
        out = refs[:count]
        del refs[:count]
        return out

    hid_ref, w_ref = take(2)
    parts = take(PARTS)
    gain_ref = take(1)[0] if fused else None
    hid_out, w_out = take(2)
    slots = take(PARTS)
    normed_out, pre_out = take(2) if fused else (None, None)
    z_send, z_recv, w_send, w_recv, f_send, f_recv, p_send, p_recv, q_send, q_recv, t_send, t_recv, own_sem = take(13)
    d, s = place()
    part = hid_ref.shape[1]
    pieces = z_send.shape[2]
    piece = part // pieces
    pairs = dp // 2
    to_d, to_s = forward_home(d, s, seq)
    from_d, from_s = backward_home(d, s, seq)
    moves = jnp.logical_or(to_d != d, to_s != s)

    greet((d, s - 1), s > 0)
    greet((d, s + 1), s < seq - 1)
    for k in range(1, pairs):
        greet((lax.rem(d + 2 * k, dp), s))
    greet((mate(d), s))
    greet((to_d, to_s), moves)
    greet((from_d, from_s), moves)
    count = pairs + jnp.where(s > 0, 1, 0) + jnp.where(s < seq - 1, 1, 0) + jnp.where(moves, 2, 0)
    pl.semaphore_wait(pltpu.get_barrier_semaphore(), count)

    def shard(which, q):
        return hid_out.at[:, pl.ds(which * part + q * piece, piece), :]

    def hop(way, k, q):
        which = s - k if way == 0 else s + k
        src = hid_ref.at[:, pl.ds(q * piece, piece), :] if k == 0 else shard(which, q)
        near = s + 1 if way == 0 else s - 1
        return remote(src, shard(which, q), z_send.at[way, k, q], z_recv.at[way, k, q], (d, near))

    def can_send(way, k):
        if way == 0:
            return jnp.logical_and(s - k >= 0, s < seq - 1)
        return jnp.logical_and(s + k < seq, s > 0)

    def landed(way, k, q):
        which = jnp.where(way == 0, s - k, s + k)
        here = shard(which, q)
        remote(here, here, z_send.at[way, k - 1, q], z_recv.at[way, k - 1, q], (d, s)).wait_recv()

    def spread(out, own, send, recv, k):
        return remote(own, out.at[d], send.at[k], recv.at[k], (lax.rem(d + 2 * k, dp), s))

    def source(k):
        return lax.rem(d - 2 * k + dp, dp)

    def across(out, send, recv, k, own=None):
        return remote(own if k == 0 else out.at[source(k)], out.at[source(k)], send.at[k], recv.at[k], (mate(d), s))

    for q in range(pieces):
        for way in range(2):
            pl.when(can_send(way, 0))(hop(way, 0, q).start)
    transfers = [remote(parts[m], slots[m].at[to_d], t_send.at[m], t_recv.at[m], (to_d, to_s)) for m in range(PARTS)]
    stays = [pltpu.make_async_copy(parts[m], slots[m].at[d], own_sem.at[2 + m]) for m in range(PARTS)]
    for m in range(PARTS):
        pl.when(moves)(transfers[m].start)
        pl.when(jnp.logical_not(moves))(stays[m].start)
    for k in range(1, pairs):
        spread(w_out, w_ref, w_send, w_recv, k).start()
    across(w_out, f_send, f_recv, 0, w_ref).start()
    own_w = pltpu.make_async_copy(w_ref, w_out.at[d], own_sem.at[0])
    own_h = pltpu.make_async_copy(hid_ref, hid_out.at[:, pl.ds(s * part, part), :], own_sem.at[1])
    own_w.start()
    own_h.start()

    for k in range(1, seq - 1):
        for q in range(pieces):
            for way in range(2):
                pl.when(s - k >= 0 if way == 0 else s + k < seq)(functools.partial(landed, way, k, q))
                pl.when(can_send(way, k))(hop(way, k, q).start)
    own_w.wait()
    own_h.wait()
    w_flow = (w_out, w_ref, w_send, w_recv, f_send, f_recv)
    part_flows = [
        (slots[m], slots[m].at[d], p_send.at[m], p_recv.at[m], q_send.at[m], q_recv.at[m]) for m in range(PARTS)
    ]

    def relay(out, own, send, recv, over_send, over_recv):
        for k in range(1, pairs):
            here = out.at[source(k)]
            remote(here, here, send.at[k], recv.at[k], (d, s)).wait_recv()
            across(out, over_send, over_recv, k).start()

    def complete(out, own, send, recv, over_send, over_recv):
        for k in range(pairs):
            here = out.at[lax.rem(mate(d) - 2 * k + dp, dp)]
            remote(here, here, over_send.at[k], over_recv.at[k], (d, s)).wait_recv()

    relay(*w_flow)
    for m in range(PARTS):
        slot = slots[m].at[d]
        pl.when(moves)(remote(parts[m], slot, t_send.at[m], t_recv.at[m], (to_d, to_s)).wait_recv)
        pl.when(jnp.logical_not(moves))(stays[m].wait)
        for k in range(1, pairs):
            spread(slots[m], slot, p_send.at[m], p_recv.at[m], k).start()
        across(slots[m], q_send.at[m], q_recv.at[m], 0, slot).start()

    complete(*w_flow)

    def relay_parts():
        for flow in part_flows:
            relay(*flow)

    last = seq - 1
    if fused:
        w_all, x_buf, w_sem, x_sem = take(4)
        width, columns = x_buf.shape[1], pre_out.shape[1]
        cut = math.gcd(columns, 512)
        fetch_w = pltpu.make_async_copy(w_out, w_all, w_sem)
        fetch_w.start()
        fetch_w.wait()

        def project(which, k, way):
            here = pl.multiple_of(which * part, part)
            for q in range(pieces):
                pl.when(k == last)(functools.partial(landed, way, last, q))
                fetch = pltpu.make_async_copy(
                    hid_out.at[0, pl.ds(which * part + q * piece, piece)], x_buf.at[pl.ds(q * piece, piece)], x_sem
                )
                fetch.start()
                fetch.wait()
                x = x_buf[pl.ds(q * piece, piece), :].astype(F32)
                inv = lax.rsqrt(jnp.mean(x * x, axis=1, keepdims=True) + norm_eps)
                rows = pl.ds(pl.multiple_of(here + q * piece, piece), piece)
                normed_out[rows, :] = (x * inv * gain_ref[...].astype(F32)).astype(BF)

            def matmul(at, carried):
                cols = pl.ds(pl.multiple_of(at * cut, cut), cut)
                w_rows = w_all.shape[1]
                block = w_all[pl.ds(at * (cut // w_rows), cut // w_rows)].reshape(cut, width)
                pre_out[pl.ds(here, part), cols] = mm(normed_out[pl.ds(here, part), :], block, NT).astype(BF)
                return carried

            lax.fori_loop(0, columns // cut, matmul, 0)

        def visit(m, carried):
            k = (m + 1) // 2
            way = lax.rem(m, 2)
            which = jnp.where(way == 0, s - k, s + k)
            pl.when(m == 2 * seq - 3)(relay_parts)

            @pl.when(jnp.logical_and(which >= 0, which < seq))
            def _():
                project(which, k, way)

            return carried

        lax.fori_loop(0, 2 * seq - 1, visit, 0)
    else:
        for q in range(pieces):
            for way in range(2):
                pl.when(s - last >= 0 if way == 0 else s + last < seq)(functools.partial(landed, way, last, q))
        relay_parts()

    for flow in part_flows:
        complete(*flow)
    for out, own, send, recv, over_send, over_recv in [w_flow, *part_flows]:
        for k in range(pairs):
            across(out, over_send, over_recv, k, own).wait_send()
        for k in range(1, pairs):
            spread(out, own, send, recv, k).wait_send()
    for k in range(seq - 1):
        for q in range(pieces):
            for way in range(2):
                pl.when(can_send(way, k))(hop(way, k, q).wait_send)
    for m in range(PARTS):
        pl.when(moves)(transfers[m].wait_send)


def fits_whole(seqs, length, width, channels):
    return seqs == 1 and length % 256 == 0 and length * (width + channels) + channels * width <= 6 << 20


def gather(hidden, weight, parts, norm_gain, collective_id=0):
    dp, seq = lax.axis_size("dp"), lax.axis_size("seq")
    seqs, part, width = hidden.shape
    columns = weight.shape[0] * dp
    fused = fits_whole(seqs, part * seq, width, columns // 2)
    pieces = 4 if part % 64 == 0 else 1
    dma, vmem, pairs = pltpu.SemaphoreType.DMA, pltpu.VMEM, dp // 2
    shape = jax.ShapeDtypeStruct
    outs = [shape((seqs, part * seq, width), BF), shape((dp,) + weight.shape, BF)]
    outs += [shape((dp,) + member.shape, BF) for member in parts]
    scratch = [dma((2, seq, pieces)), dma((2, seq, pieces))] + [dma((pairs,))] * 4
    scratch += [dma((PARTS, pairs))] * 4 + [dma((PARTS,)), dma((PARTS,)), dma((2 + PARTS,))]
    ins, in_specs = [hidden, weight, *parts], any_specs(2 + PARTS)
    out_specs = any_specs(2 + PARTS)
    if fused:
        ins.append(norm_gain.reshape(1, width))
        in_specs = in_specs + [pl.BlockSpec(memory_space=pltpu.VMEM)]
        outs += [shape((part * seq, width), BF), shape((part * seq, columns), BF)]
        scratch += [
            vmem((dp,) + weight.shape, BF), vmem((part, width), BF), dma, dma,
        ]
        out_specs = out_specs + [pl.BlockSpec(memory_space=pltpu.VMEM)] * 2
    out = pl.pallas_call(
        functools.partial(gather_kernel, dp, seq, fused),
        in_specs=in_specs,
        out_specs=out_specs,
        out_shape=outs,
        scratch_shapes=scratch,
        compiler_params=pltpu.CompilerParams(
            collective_id=collective_id, has_side_effects=True, vmem_limit_bytes=44 << 20
        ),
        name="gather_in",
    )(*ins)
    hidden = out[0].reshape(-1, width)
    w_in = out[1].reshape(columns, width)
    if fused:
        return hidden, w_in, out[2 : 2 + PARTS], out[-2], out[-1]
    x = hidden.astype(F32)
    inv = lax.rsqrt(jnp.mean(x * x, axis=1, keepdims=True) + norm_eps)
    normed = (x * inv * norm_gain.astype(F32)).astype(BF)
    return hidden, w_in, out[2:], normed, mm(normed, w_in, NT).astype(BF)


def added(ref, *others):
    total = ref[...].astype(F32)
    for other in others:
        total = total + other[...].astype(F32)
    return total


def scatter_kernel(dp, seq, count, fused, *refs):
    refs = list(refs)

    def take(count):
        out = refs[:count]
        del refs[:count]
        return out

    if fused:
        dx_ref, dz_ref, normed_ref, w_ref, full_ref = take(5)
        dn_ref = gw_ref = None
    else:
        dn_ref, gw_ref, gain_ref = take(3)
    parts = take(count)
    hid_ref, cot_ref, scale_ref = take(3)
    out_ref, gw_out = take(2)
    part_outs = take(count)
    gain_out = take(1)[0]
    own, come, gw_own, gw_x, gw_r = take(5)
    p_own, p_x, p_r, p_fin = take(count), take(count), take(count), take(count)
    g_in, g_one, g_x, g_r, g_z, g_a, g_b = take(7)
    z_load, z_send, z_recv, w_load, wx_send, wx_recv, w_send, w_recv = take(8)
    p_load, px_send, px_recv, p_send, p_recv, t_send, t_recv, gx_sem, g_send, g_recv, gz_send, gz_recv = take(12)

    d, s = place()
    seqs, part, width = out_ref.shape
    pieces = z_send.shape[1]
    piece = part // pieces
    pairs = dp // 2
    mine, odd = d // 2, lax.rem(d, 2)
    to_d, to_s = backward_home(d, s, seq)
    from_d, from_s = forward_home(d, s, seq)
    moves = jnp.logical_or(to_d != d, to_s != s)

    if fused:
        d_pre, normed, w_all, x_buf, gw_give, f_sem, x_sem = take(7)
        channels = dx_ref.shape[1]
        loads = [
            pltpu.make_async_copy(dx_ref, d_pre.at[:, pl.ds(0, channels)], f_sem.at[0]),
            pltpu.make_async_copy(dz_ref, d_pre.at[:, pl.ds(channels, channels)], f_sem.at[1]),
            pltpu.make_async_copy(w_ref, w_all, f_sem.at[2]),
            pltpu.make_async_copy(normed_ref, normed, f_sem.at[3]),
        ]
        for copy in loads:
            copy.start()

    for k in range(1, seq):
        greet((d, lax.rem(s + k, seq)))
    for k in range(1, pairs):
        greet((lax.rem(d + 2 * k, dp), s))
    greet((mate(d), s))
    greet((to_d, to_s), moves)
    greet((from_d, from_s), moves)
    pl.semaphore_wait(pltpu.get_barrier_semaphore(), seq - 1 + pairs + jnp.where(moves, 2, 0))

    def swap(src, dst, send, recv, j):
        return remote(src, dst.at[j], send.at[j], recv.at[j], (mate(d), s))

    def part_swap(m, j):
        return swap(parts[m].at[2 * j + 1 - odd], p_x[m], px_send.at[m], px_recv.at[m], j)

    def part_fetch(m, j):
        return pltpu.make_async_copy(parts[m].at[2 * j + odd], p_own[m].at[j], p_load.at[m, j])

    for m in range(count):
        for j in range(pairs):
            part_swap(m, j).start()
            part_fetch(m, j).start()

    if fused:
        for copy in loads[:3]:
            copy.wait()
        g_in[...] = jnp.zeros_like(g_in)
        w_rows = gw_own.shape[1]
        half_width = width // 2

        def chunk_of(i):
            return jnp.where(lax.rem(i, 2) == 0, seq - 1 - i // 2, i // 2)

        def dn_tasks(first, last):
            def run(i, carried):
                r = chunk_of(i)
                rows = pl.ds(pl.multiple_of(r * part, part), part)
                for at in range(2):
                    cols = pl.ds(at * half_width, half_width)
                    own[r, 0, :, cols] = mm(d_pre[rows, :], w_all[:, cols], NN).astype(BF)
                return carried

            lax.fori_loop(first, last, run, 0)

        def gain_tasks(first, last):
            def run(i, carried):
                r = chunk_of(i)
                fetch = pltpu.make_async_copy(full_ref.at[pl.ds(pl.multiple_of(r * part, part), part)], x_buf, x_sem)
                fetch.start()
                fetch.wait()

                def fold(at, carried):
                    some = pl.ds(pl.multiple_of(at * 64, 64), 64)
                    x = x_buf[some, :].astype(F32)
                    inv = lax.rsqrt(jnp.mean(x * x, axis=1, keepdims=True) + norm_eps)
                    weighted = own[r, 0, some, :].astype(F32) * (x * inv)
                    g_in[...] += jnp.sum(weighted.reshape(8, 8, width), axis=0)
                    return carried

                return lax.fori_loop(0, part // 64, fold, carried)

            lax.fori_loop(first, last, run, 0)

        def gw_task(dest, out, j):
            cols = pl.ds(pl.multiple_of(dest * w_rows, w_rows), w_rows)
            for at in range(2):
                some = pl.ds(at * half_width, half_width)
                out[j, :, some] = mm(d_pre[:, cols], normed[:, some], TN).astype(BF)

        def gw_swap(j):
            return swap(gw_give.at[j], gw_x, wx_send, wx_recv, j)

        def gw_away():
            def run(j, carried):
                gw_task(2 * j + 1 - odd, gw_give, j)
                gw_swap(j).start()
                return carried

            lax.fori_loop(0, pairs, run, 0)

        def gw_home():
            def run(k, carried):
                j = lax.rem(mine + 1 + k, pairs)
                gw_task(2 * j + odd, gw_own, j)
                return carried

            lax.fori_loop(0, pairs, run, 0)

        def gw_ready(j):
            pass
    else:
        def gw_swap(j):
            return swap(gw_ref.at[2 * j + 1 - odd], gw_x, wx_send, wx_recv, j)

        def gw_fetch(j):
            return pltpu.make_async_copy(gw_ref.at[2 * j + odd], gw_own.at[j], w_load.at[j])

        def chunk(r):
            return pltpu.make_async_copy(dn_ref.at[:, pl.ds(r * part, part), :], own.at[r], z_load.at[r])

        for r in range(seq):
            chunk(r).start()
        for j in range(pairs):
            gw_swap(j).start()
            gw_fetch(j).start()
        for r in range(seq):
            chunk(r).wait()
        g_in[...] = gain_ref[...]

        def gw_ready(j):
            gw_fetch(j).wait()

    def give(way, r, q):
        rows = pl.ds(q * piece, piece)
        slot = r if way == 0 else jnp.where(s - 1 == r, seq, r)
        near = s + 1 if way == 0 else s - 1
        return remote(own.at[r, :, rows, :], come.at[slot, :, rows, :], z_send.at[r, q], z_recv.at[slot, q], (d, near))

    def landed(slot, q):
        rows = pl.ds(q * piece, piece)
        here = come.at[slot, :, rows, :]
        remote(here, here, z_send.at[0, q], z_recv.at[slot, q], (d, s)).wait_recv()

    def begin():
        for q in range(pieces):
            pl.when(s == 0)(give(0, seq - 1, q).start)
            pl.when(s == seq - 1)(give(1, 0, q).start)

    def hop(turn, q):
        rows = pl.ds(q * piece, piece)
        for way in range(2):
            far = s if way == 0 else seq - 1 - s
            i = turn - far
            r = seq - 1 - i if way == 0 else i
            before = r + 1 if way == 0 else r - 1
            sends = jnp.logical_and(i >= 0, s < r if way == 0 else s > r)

            @pl.when(jnp.logical_and(sends, far > 0))
            def _():
                landed(r, q)
                own[r, :, rows, :] = added(own.at[r, :, rows, :], come.at[r, :, rows, :]).astype(BF)

            pl.when(jnp.logical_and(sends, i > 0))(give(way, before, q).wait_send)
            pl.when(jnp.logical_and(sends, far + i > 0))(give(way, r, q).start)

    def onward(part_own, part_r, send, recv, k):
        j = lax.rem(mine + k, pairs)
        return remote(part_own.at[j], part_r.at[k - 1], send.at[k], recv.at[k], (lax.rem(d + 2 * k, dp), s))

    def part_onward(m, k):
        return onward(p_own[m], p_r[m], p_send.at[m], p_recv.at[m], k)

    def gw_onward(k):
        return onward(gw_own, gw_r, w_send, w_recv, k)

    def part_join():
        for m in range(count):
            for k in range(1, pairs + 1):
                j = lax.rem(mine + k, pairs)
                part_fetch(m, j).wait()
                part_swap(m, j).wait_recv()
                if k < pairs:
                    p_own[m][j] = added(p_own[m].at[j], p_x[m].at[j]).astype(BF)
                    part_onward(m, k).start()

    def gw_join():
        for k in range(1, pairs + 1):
            j = lax.rem(mine + k, pairs)
            gw_ready(j)
            gw_swap(j).wait_recv()
            if k < pairs:
                gw_own[j] = added(gw_own.at[j], gw_x.at[j]).astype(BF)
                gw_onward(k).start()

    gain_swap = remote(g_one, g_x, gx_sem.at[0], gx_sem.at[1], (mate(d), s))

    def gain_near(k):
        return remote(g_a, g_r.at[k - 1], g_send.at[k], g_recv.at[k], (lax.rem(d + 2 * k, dp), s))

    def gain_far(k):
        return remote(g_b, g_z.at[k - 1], gz_send.at[k], gz_recv.at[k], (d, lax.rem(s + k, seq)))

    def gain_middle():
        gain_swap.wait_recv()
        g_a[...] = g_one[...] + g_x[...]
        for k in range(1, pairs):
            gain_near(k).start()

    def gain_last():
        for k in range(1, pairs):
            gain_near(k).wait_recv()
        g_b[...] = added(g_a, *[g_r.at[k] for k in range(pairs - 1)])
        for k in range(1, seq):
            gain_far(k).start()

    backs = [remote(p_fin[m], part_outs[m], t_send.at[m], t_recv.at[m], (to_d, to_s)) for m in range(count)]
    stays = [pltpu.make_async_copy(p_fin[m], part_outs[m], t_send.at[count + m]) for m in range(count)]

    def part_finish():
        for m in range(count):
            for k in range(1, pairs):
                part_onward(m, k).wait_recv()
            rest = [p_r[m].at[k] for k in range(pairs - 1)]
            p_fin[m][...] = added(p_own[m].at[mine], p_x[m].at[mine], *rest).astype(BF)
            pl.when(moves)(backs[m].start)
            pl.when(jnp.logical_not(moves))(stays[m].start)

    if fused:
        dn_tasks(0, 2)
        begin()
        part_join()
        loads[3].wait()
        gw_away()
        gw_home()
        gw_join()
        gain_tasks(0, 2)
        dn_tasks(2, seq)
        gain_tasks(2, seq)
    else:
        begin()
        part_join()
        gw_join()
    g_one[...] = jnp.sum(g_in[...], axis=0, keepdims=True)
    gain_swap.start()
    later = [gain_middle, gain_last, part_finish]
    for i in range(seq - 1):
        for q in range(pieces):
            hop(i, q)
            if later and q == pieces - 1:
                later.pop(0)()
    for task in later:
        task()

    for k in range(1, pairs):
        gw_onward(k).wait_recv()
    gw_out[...] = added(gw_own.at[mine], gw_x.at[mine], *[gw_r.at[k] for k in range(pairs - 1)])
    for k in range(1, seq):
        gain_far(k).wait_recv()
    gain_out[...] = added(g_b, *[g_z.at[k] for k in range(seq - 1)])

    some = math.gcd(piece, 64)
    for q in range(pieces):
        pl.when(s > 0)(functools.partial(landed, s, q))
        pl.when(s < seq - 1)(functools.partial(landed, seq, q))

        def settle(at, carried):
            rows = pl.ds(pl.multiple_of(q * piece + at * some, some), some)
            from_left = jnp.where(s > 0, come[s, :, rows, :].astype(F32), 0.0)
            from_right = jnp.where(s < seq - 1, come[seq, :, rows, :].astype(F32), 0.0)
            total = own[s, :, rows, :].astype(F32) + from_left + from_right
            x = hid_ref[:, rows, :].astype(F32)
            inv = lax.rsqrt(jnp.mean(x * x, axis=2, keepdims=True) + norm_eps)
            scaled = total * scale_ref[...].astype(F32)[None]
            out_ref[:, rows, :] = (
                cot_ref[:, rows, :].astype(F32)
                + inv * scaled
                - x * (inv * inv * inv) * jnp.mean(x * scaled, axis=2, keepdims=True)
            ).astype(BF)
            return carried

        lax.fori_loop(0, piece // some, settle, 0)

    for q in range(pieces):
        pl.when(s < seq - 1)(give(0, s + 1, q).wait_send)
        pl.when(s > 0)(give(1, s - 1, q).wait_send)
    gain_swap.wait_send()
    for j in range(pairs):
        gw_swap(j).wait_send()
        for m in range(count):
            part_swap(m, j).wait_send()
    for k in range(1, pairs):
        gw_onward(k).wait_send()
        gain_near(k).wait_send()
        for m in range(count):
            part_onward(m, k).wait_send()
    for k in range(1, seq):
        gain_far(k).wait_send()
    for m in range(count):
        pl.when(moves)(backs[m].wait_send)
        pl.when(moves)(remote(p_fin[m], part_outs[m], t_send.at[m], t_recv.at[m], (to_d, to_s)).wait_recv)
        pl.when(jnp.logical_not(moves))(stays[m].wait)


def scatter(d_x, d_z, normed, w_in, hidden, parts, hidden_in, cotangent, norm_gain, collective_id=1):
    dp, seq = lax.axis_size("dp"), lax.axis_size("seq")
    seqs, part, width = hidden_in.shape
    tokens, channels = d_x.shape
    w_rows = 2 * channels // dp
    fused = fits_whole(seqs, part * seq, width, channels)
    pieces = 4 if part % 64 == 0 else 1
    pairs, count = dp // 2, len(parts)
    dma, vmem, shape = pltpu.SemaphoreType.DMA, pltpu.VMEM, jax.ShapeDtypeStruct
    here = pl.BlockSpec(memory_space=pltpu.VMEM)
    if fused:
        ins, in_specs = [d_x, d_z, normed, w_in, hidden], any_specs(5)
        extra = [
            vmem((tokens, 2 * channels), BF), vmem((tokens, width), BF), vmem((2 * channels, width), BF),
            vmem((part, width), BF), vmem((pairs, w_rows, width), BF), dma((4,)), dma,
        ]
    else:
        d_pre = jnp.concatenate([d_x, d_z], axis=1)
        x = hidden.astype(F32)
        d_normed = mm(d_pre, w_in, NN)
        inv = lax.rsqrt(jnp.mean(x * x, axis=1, keepdims=True) + norm_eps)
        gain = jnp.pad(jnp.sum(d_normed * x * inv, axis=0)[None], ((0, 7), (0, 0)))
        ins = [
            d_normed.astype(BF).reshape(seqs, -1, width),
            mm(d_pre, normed, TN).astype(BF).reshape(dp, w_rows, width), gain,
        ]
        in_specs, extra = any_specs(2) + [here], []
    part_shapes = [member.shape[1:] for member in parts]
    token_shape, one = (seqs, part, width), (1, width)

    def each(count):
        return [vmem((count,) + member, BF) for member in part_shapes]

    out = pl.pallas_call(
        functools.partial(scatter_kernel, dp, seq, len(parts), fused),
        in_specs=in_specs + any_specs(count) + [here] * 3,
        out_specs=[here] * (3 + count),
        out_shape=[shape(token_shape, BF), shape((w_rows, width), F32)]
        + [shape(member, BF) for member in part_shapes]
        + [shape(one, F32)],
        scratch_shapes=[
            vmem((seq,) + token_shape, BF), vmem((seq + 1,) + token_shape, BF),
            vmem((pairs, w_rows, width), BF), vmem((pairs, w_rows, width), BF), vmem((pairs - 1, w_rows, width), BF),
            *each(pairs), *each(pairs), *each(pairs - 1), *[vmem(member, BF) for member in part_shapes],
            vmem((8, width), F32), vmem(one, F32), vmem(one, F32), vmem((pairs - 1,) + one, F32),
            vmem((seq - 1,) + one, F32), vmem(one, F32), vmem(one, F32),
            dma((seq,)), dma((seq, pieces)), dma((seq + 1, pieces)),
            dma((pairs,)), dma((pairs,)), dma((pairs,)), dma((pairs,)), dma((pairs,)),
            *[dma((count, pairs))] * 5, dma((2 * count,)), dma((count,)),
            dma((2,)), dma((pairs,)), dma((pairs,)), dma((seq,)), dma((seq,)),
            *extra,
        ],
        compiler_params=pltpu.CompilerParams(
            collective_id=collective_id, has_side_effects=True, vmem_limit_bytes=63 << 20
        ),
        name="scatter_out",
    )(*ins, *parts, hidden_in, cotangent, norm_gain.reshape(1, width))
    return out[0], out[1], out[2 : 2 + count], out[-1].reshape(width)


def reduce_kernel(dp, seq, grads, *refs):
    refs = list(refs)

    def take(count):
        out = refs[:count]
        del refs[:count]
        return out

    wide_ref, thin_ref = take(2)
    g_ref = take(1)[0] if grads else None
    wide_out, thin_out = take(2)
    g_out = take(1)[0] if grads else None
    wide_x, thin_x, wide_s, thin_s = take(4)
    xw_send, xw_recv, xt_send, xt_recv, sw_send, sw_recv, st_send, st_recv = take(8)
    d, s = place()
    rows = wide_ref.shape[0] // seq
    pairs = dp // 2
    mine, odd = d // 2, lax.rem(d, 2)
    for k in range(1, seq):
        greet((d, lax.rem(s + k, seq)))
    if grads:
        for k in range(1, pairs):
            greet((lax.rem(d + 2 * k, dp), s))
        greet((mate(d), s))
    pl.semaphore_wait(pltpu.get_barrier_semaphore(), seq - 1 + (pairs if grads else 0))

    def piece(ref, which):
        return ref.at[pl.ds(pl.multiple_of(which * rows, rows), rows)]

    def ask(k):
        to = lax.rem(s + k, seq)
        return (
            remote(piece(wide_ref, to), wide_x.at[k - 1], xw_send.at[k - 1], xw_recv.at[k - 1], (d, to)),
            remote(thin_ref.at[to], thin_x.at[k - 1], xt_send.at[k - 1], xt_recv.at[k - 1], (d, to)),
        )

    def tell(k):
        to = lax.rem(s + k, seq)
        return (
            remote(wide_s, piece(wide_out, s), sw_send.at[k - 1], sw_recv.at[k - 1], (d, to)),
            remote(thin_s, thin_out.at[s], st_send.at[k - 1], st_recv.at[k - 1], (d, to)),
        )

    def told(k):
        source = lax.rem(s - k + seq, seq)
        return (
            remote(wide_s, piece(wide_out, source), sw_send.at[k - 1], sw_recv.at[k - 1], (d, s)),
            remote(thin_s, thin_out.at[source], st_send.at[k - 1], st_recv.at[k - 1], (d, s)),
        )

    order = sorted(range(1, seq), key=lambda k: -min(k, seq - k))
    for k in order:
        for copy in ask(k):
            copy.start()
    if grads:
        g_own, g_x, g_r, g_load, gx_send, gx_recv, g_send, g_recv = take(8)

        def swap(j):
            return remote(g_ref.at[2 * j + 1 - odd], g_x.at[j], gx_send.at[j], gx_recv.at[j], (mate(d), s))

        def fetch(j):
            return pltpu.make_async_copy(g_ref.at[2 * j + odd], g_own.at[j], g_load.at[j])

        def onward(k):
            to = lax.rem(d + 2 * k, dp)
            return remote(g_own.at[to // 2], g_r.at[k - 1], g_send.at[k], g_recv.at[k], (to, s))

        for j in range(pairs):
            swap(j).start()
            fetch(j).start()
        for k in range(1, pairs + 1):
            j = lax.rem(mine + k, pairs)
            fetch(j).wait()
            swap(j).wait_recv()
            if k < pairs:
                g_own[j] = added(g_own.at[j], g_x.at[j]).astype(BF)
                onward(k).start()
    for k in order:
        for copy in ask(k):
            copy.wait_recv()
    start = pl.ds(pl.multiple_of(s * rows, rows), rows)
    total = wide_ref[start, :].astype(F32)
    thin = thin_ref[s]
    for k in range(seq - 1):
        total = total + wide_x[k].astype(F32)
        thin = thin + thin_x[k]
    wide_s[...] = total.astype(BF)
    thin_s[...] = thin
    for k in order:
        for copy in tell(k):
            copy.start()
    wide_out[start, :] = total.astype(BF)
    thin_out[s] = thin
    if grads:
        for k in range(1, pairs):
            onward(k).wait_recv()
        g_out[...] = added(g_own.at[mine], g_x.at[mine], *[g_r.at[k] for k in range(pairs - 1)]).astype(BF)
        for j in range(pairs):
            swap(j).wait_send()
        for k in range(1, pairs):
            onward(k).wait_send()
    for k in order:
        for copy in told(k):
            copy.wait_recv()
    for k in order:
        for copy in ask(k) + tell(k):
            copy.wait_send()


def reduce_over_seq(wide_part, thin_part, collective_id, grads=None):
    dp, seq = lax.axis_size("dp"), lax.axis_size("seq")
    tokens, cols = wide_part.shape
    thin_part = jnp.swapaxes(thin_part.reshape(-1, seq, tokens // seq), 0, 1)
    dma, vmem, shape = pltpu.SemaphoreType.DMA, pltpu.VMEM, jax.ShapeDtypeStruct
    here = pl.BlockSpec(memory_space=pltpu.VMEM)
    rows, few, pairs = tokens // seq, thin_part.shape[1:], dp // 2
    ins, in_specs = [wide_part.astype(BF), thin_part], [here] * 2
    outs = [shape((tokens, cols), BF), shape(thin_part.shape, F32)]
    scratch = [
        vmem((seq - 1, rows, cols), BF), vmem((seq - 1,) + few, F32), vmem((rows, cols), BF), vmem(few, F32),
    ] + [dma((seq - 1,))] * 8
    if grads is not None:
        ins, in_specs = ins + [grads], in_specs + any_specs(1)
        outs.append(shape(grads.shape[1:], BF))
        scratch += [vmem((pairs,) + grads.shape[1:], BF)] * 2 + [vmem((pairs - 1,) + grads.shape[1:], BF)]
        scratch += [dma((pairs,))] * 5
    out = pl.pallas_call(
        functools.partial(reduce_kernel, dp, seq, grads is not None),
        in_specs=in_specs,
        out_specs=[here] * len(outs),
        out_shape=outs,
        scratch_shapes=scratch,
        compiler_params=pltpu.CompilerParams(
            collective_id=collective_id, has_side_effects=True, vmem_limit_bytes=24 << 20
        ),
        name="reduce_seq",
    )(*ins)
    return (out[0], jnp.swapaxes(out[1], 0, 1).reshape(-1, tokens)) + tuple(out[2:])


def homes_back(dp, seq):
    pairs = []
    for d in range(dp):
        for s in range(seq):
            home_d, home_s = 2 * (d // 2) + s % 2, (seq // 2) * (d % 2) + s // 2
            pairs.append((home_d * seq + home_s, d * seq + s))
    return pairs


def local(
    hidden_in,
    doc_lengths,
    norm_gain,
    in_weight,
    conv_weight,
    conv_bias,
    x_weight,
    dt_weight,
    dt_bias,
    skip_gain,
    out_weight,
    out_cotangent,
):
    seqs, part_len, width = hidden_in.shape
    dp, seq = lax.axis_size("dp"), lax.axis_size("seq")
    length = part_len * seq
    tokens = seqs * length
    rows = out_weight.shape[0]
    channels = rows * dp
    lag_max = KCONV - 1

    vectors = [conv_weight, conv_bias[None], dt_bias[None], skip_gain[None]]
    vectors = jnp.pad(jnp.concatenate(vectors, axis=0), ((0, 16 - KCONV - 3), (0, 0)))
    parts = [out_weight, x_weight, dt_weight, vectors]
    hidden, w_in, parts, normed, pre = gather(hidden_in, in_weight, parts, norm_gain)
    cot, pre = lax.optimization_barrier((out_cotangent, pre))
    cot = lax.all_gather(cot, "seq", axis=1, tiled=True).reshape(tokens, width)

    w_out, w_x, w_dt = (part.reshape(channels, part.shape[2]) for part in parts[:3])
    vectors = jnp.swapaxes(parts[3], 0, 1).reshape(16, channels).astype(F32)
    taps, conv_shift, rate_shift, skip = vectors[:KCONV], vectors[KCONV], vectors[KCONV + 1], vectors[KCONV + 2]

    begins, places = token_begins(doc_lengths, length)
    keep = (places[None, :] != begins).astype(F32).reshape(tokens, 1)
    valid = [(places[None, :] - (lag_max - w) >= begins)[:, :, None] for w in range(KCONV)]

    x_inner = pre[:, :channels].reshape(seqs, length, channels)

    padded = jnp.pad(x_inner, ((0, 0), (lag_max, 0), (0, 0)))
    conv_sum = jnp.broadcast_to(conv_shift, (seqs, length, channels))
    for w in range(KCONV):
        window = padded[:, w : w + length, :].astype(F32)
        conv_sum = conv_sum + jnp.where(valid[w], window * taps[w], 0.0)
    conv_flat = conv_sum.reshape(tokens, channels)
    xc_low = jax.nn.silu(conv_flat).astype(BF)
    rate, thin = reduce_over_seq(mm(xc_low, w_x[:, :R], NN), mm(w_x[:, R:], xc_low, ((0,), (1,))), 2)
    key, query = thin[:N].T, thin[N:].T
    key_lanes, query_lanes = (
        jnp.broadcast_to(part.astype(BF)[:, :, None], (tokens, N, LANES)) for part in (key, query)
    )
    ksum = jnp.sum(key * key, axis=1, keepdims=True)
    keep_lanes = jnp.broadcast_to(keep, (tokens, LANES))
    ksum_lanes = jnp.broadcast_to(ksum, (tokens, LANES))
    vectors = jnp.pad(jnp.stack([rate_shift, skip]), ((0, 6), (0, 0)))
    states, y_full, gated = scan_forward(
        seqs, length, xc_low, pre, rate, key_lanes, query_lanes, keep_lanes, ksum_lanes, w_dt, vectors
    )
    branch = mm(gated, w_out, NN).astype(BF).reshape(seqs, length, width)
    branch = lax.psum_scatter(branch, "seq", scatter_dimension=1, tiled=True)
    output = (hidden_in.astype(F32) + branch.astype(F32)).astype(BF)

    d_z, rest, dq, dk, d_norm, d_row, grad_dt, sums = scan_backward(
        seqs, length, mm(cot, w_out, NT), y_full, xc_low, pre, rate, key_lanes, query_lanes, keep_lanes, ksum_lanes, w_dt, vectors, states
    )
    dq, dk = dq.reshape(tokens, N), dk.reshape(tokens, N)
    d_norm = -jnp.sum(d_norm, axis=1, keepdims=True)
    d_keys = dk + 2.0 * key * d_norm
    grad_out = mm(gated, cot, TN).astype(BF).reshape(dp, rows, width)
    d_row, thin, grad_out = reduce_over_seq(d_row, jnp.concatenate([d_keys.T, dq.T], axis=0), 3, grad_out)
    grad_out = lax.ppermute(grad_out, ("dp", "seq"), homes_back(dp, seq))
    d_proj = jnp.concatenate([d_row, thin.T.astype(BF)], axis=1)
    d_conv_out = mm(d_proj, w_x, NT) + rest
    d_conv = (d_conv_out * silu_slope(conv_flat)).reshape(seqs, length, channels)

    tap_grads = []
    d_x_inner = jnp.zeros((seqs, length, channels), F32)
    for w in range(KCONV):
        lag = lag_max - w
        window = padded[:, w : w + length, :].astype(F32)
        masked = jnp.where(valid[w], d_conv, 0.0)
        tap_grads.append(jnp.sum(masked * window, axis=(0, 1)))
        d_x_inner = d_x_inner + jnp.pad(masked, ((0, 0), (0, lag), (0, 0)))[:, lag:, :] * taps[w]
    vector_grads = jnp.stack(
        tap_grads + [jnp.sum(d_conv, axis=(0, 1)), jnp.sum(sums[:8], axis=0), jnp.sum(sums[8:], axis=0)], axis=0
    )
    vector_grads = jnp.pad(vector_grads, ((0, 16 - KCONV - 3), (0, 0))).reshape(16, dp, rows)
    grads = [part.astype(BF).reshape(dp, rows, -1) for part in (mm(xc_low, d_proj, TN), grad_dt)]
    grads.append(jnp.swapaxes(vector_grads, 0, 1).astype(BF))
    grad_in, grad_in_weight, grads, grad_norm_gain = scatter(
        d_x_inner.reshape(tokens, channels).astype(BF), d_z, normed, w_in, hidden, grads,
        hidden_in, out_cotangent, norm_gain,
    )
    grad_x, grad_dt, grad_vectors = (part.astype(F32) for part in grads)
    grad_out_weight = grad_out.astype(F32)
    return (
        output,
        grad_in,
        grad_norm_gain,
        grad_in_weight,
        grad_vectors[:KCONV],
        grad_vectors[KCONV],
        grad_x,
        grad_dt,
        grad_vectors[KCONV + 1],
        grad_vectors[KCONV + 2],
        grad_out_weight,
    )


def solution(mesh):
    both = ("dp", "seq")
    tokens = P("dp", "seq", None)
    matrix, vector = P(both, None), P(both)
    return jax.shard_map(
        local,
        mesh=mesh,
        in_specs=(
            tokens, P("dp", None), P(), matrix, P(None, both), vector,
            matrix, matrix, vector, vector, matrix, tokens,
        ),
        out_specs=(
            tokens, tokens, P(), matrix, P(None, both), vector,
            matrix, matrix, vector, vector, matrix,
        ),
        check_vma=False,
    )
```
